32 devices in a mesh: dp: 8 (over z, x), mlp: 4 (over y, core).
Axes of the slice: x: 2, y: 2, z: 4, core: 2. Of those that a mesh axis runs over, the one named last changes fastest.
Arguments:
- tokens: bfloat16 [32768, 768], P(('dp', 'mlp')), may hold values from -6 to 6
- cotangent: bfloat16 [32768, 768], P(('dp', 'mlp')), may hold values from -6 to 6
- vectors: float32 [14, 768], replicated
- vector_moments: float32 [14, 768], replicated, may hold values from 819.2 to 26214.4
- decays: float32 [2], replicated, may hold values from 0.9 to 0.98
- owner: int32 [4, 3], replicated, may hold values from 0 to 7, as said below
- master_slots: float32 [8, 4, 768, 768], P('dp', 'mlp'), as said below
- left_slots: float32 [8, 4, 768, 768], P('dp', 'mlp'), as said below
- right_slots: float32 [8, 4, 768, 768], P('dp', 'mlp'), as said below
- left_roots: float32 [8, 4, 768, 768], P('dp', 'mlp'), as said below
- right_roots: float32 [8, 4, 768, 768], P('dp', 'mlp'), as said below
- grid_height: int32 [128], P(('dp', 'mlp')), may hold values from 8 to 24, as said below
- grid_width: int32 [128], P(('dp', 'mlp')), may hold values from 8 to 24, as said below
- patch_rows: int32 [32768], P(('dp', 'mlp')), may hold values from 0 to 23, as said below
- patch_cols: int32 [32768], P(('dp', 'mlp')), may hold values from 0 to 23, as said below
- segment: int32 [32768], P(('dp', 'mlp')), may hold values from 0 to 3, as said below
Outputs:
- output: bfloat16 [32768, 768], P(('dp', 'mlp'))
- input_grad: float32 [32768, 768], P(('dp', 'mlp'))
- slot_grads: float32 [8, 4, 768, 768], P('dp', 'mlp')
- new_left: float32 [8, 4, 768, 768], P('dp', 'mlp')
- new_right: float32 [8, 4, 768, 768], P('dp', 'mlp')
- new_master: float32 [8, 4, 768, 768], P('dp', 'mlp')
- vector_grads: float32 [14, 768], P(None, 'mlp')
- new_vector_moments: float32 [14, 768], P(None, 'mlp')
- new_vectors: float32 [14, 768], P(None, 'mlp')
The draws below stay inside these ranges and needn't reach their ends.
Inputs may be any that keep to these rules, and one draw needn't show every extreme that they name: `owner`: the entries of a row differ; block kind 0 of row m is the m-th of the query, key, value and output projections, kind 1 the m-th 768 columns of the up projection, kind 2 the m-th 768 rows of the down projection. `master_slots`: slot (owner[m,k], m) holds block kind k of row m; the other slots are unused. `left_slots`: symmetric and positive definite. `right_slots`: symmetric and positive definite. `left_roots`: symmetric and positive definite. `right_roots`: symmetric and positive definite. `grid_height`: each image is 16 patches along one side; the other sides of one device's images add up to 64. `grid_width`: as grid_height. `patch_rows`: each device's patches hold its images whole, one after another in the order of their numbers, each in raster order. `patch_cols`: as patch_rows. `segment`: never falls within a device's patches.
All inputs are finite; a program needn't handle non-finite values.
Results may differ from the reference program's by a relative error of at most 0.014.
Values may be sent and summed in bfloat16 or wider, within the bound.
A program may use at most 192 MiB of HBM per device.

```python
import math
import jax
import jax.numpy as jnp
from jax import lax

D = 768
HEADS = 12
FF = 3072
GRID_BASE = 16
IMG_DEV = 4
TOK_DEV = 1024
TOKENS = 32768
VEC_ROWS = 14
N_DP = 8
N_MLP = 4


def draw_owner(key, part):
    base = jax.random.fold_in(key, 11)
    row_keys = jax.random.split(base, N_MLP)
    chosen = jax.vmap(lambda row_key: jax.random.permutation(row_key, N_DP)[:3])(row_keys)
    return chosen.astype(jnp.int32)


def identity_plus(noise_key, leading):
    shape_all = leading + (D, D)
    noise = jax.random.normal(noise_key, shape_all, jnp.float32)
    noise = (noise + jnp.swapaxes(noise, -1, -2)) * (0.25 / math.sqrt(2.0 * D))
    diagonal_ones = (jnp.arange(D)[:, None] == jnp.arange(D)[None, :]).astype(jnp.float32)
    return diagonal_ones + noise


def slot_scale(scale_key, lower, upper):
    return jnp.exp(jax.random.uniform(scale_key, (N_DP, N_MLP, 1, 1), jnp.float32, math.log(lower), math.log(upper)))


def draw_left_slots(key, part):
    level = 0.05 * TOKENS * D
    return level * slot_scale(jax.random.fold_in(key, 41), 1.0, 4.0) * identity_plus(jax.random.fold_in(key, 42), (N_DP, N_MLP))


def draw_right_slots(key, part):
    level = 0.05 * TOKENS * D
    return level * slot_scale(jax.random.fold_in(key, 43), 1.0, 4.0) * identity_plus(jax.random.fold_in(key, 44), (N_DP, N_MLP))


def draw_left_roots(key, part):
    level = (0.05 * TOKENS * D) ** (-0.25)
    return level * slot_scale(jax.random.fold_in(key, 45), 0.7, 1.4) * identity_plus(jax.random.fold_in(key, 46), (N_DP, N_MLP))


def draw_right_roots(key, part):
    level = (0.05 * TOKENS * D) ** (-0.25)
    return level * slot_scale(jax.random.fold_in(key, 47), 0.7, 1.4) * identity_plus(jax.random.fold_in(key, 48), (N_DP, N_MLP))


def draw_master_slots(key, part):
    owner_table = draw_owner(key, part)
    shape_all = (N_DP, N_MLP, D, D)
    values = jax.random.normal(jax.random.fold_in(key, 21), shape_all, jnp.float32)
    output_slot = (jnp.arange(N_DP)[:, None] == owner_table[3, 0]) & (jnp.arange(N_MLP)[None, :] == 3)
    factor = jnp.where(output_slot, 4.0, 1.0)
    return values * (factor[:, :, None, None] / math.sqrt(D))


def draw_vectors(key, part):
    rows_all = 10 + FF // D
    common = jax.random.normal(jax.random.fold_in(key, 51), (rows_all, D), jnp.float32)
    row_index = jnp.arange(rows_all)[:, None]
    gains = 1.0 + 0.15 * common
    biases = 0.3 * common
    half_width = D // 2
    magnitude = jnp.exp(jax.random.uniform(jax.random.fold_in(key, 52), (half_width,), jnp.float32, math.log(0.02), 0.0))
    heading = jax.random.uniform(jax.random.fold_in(key, 53), (half_width,), jnp.float32, -math.pi, math.pi)
    freq_line = jnp.concatenate([magnitude * jnp.cos(heading), magnitude * jnp.sin(heading)])
    result = jnp.where((row_index == 0) | (row_index == 6), gains, biases)
    return jnp.where(row_index == rows_all - 1, freq_line[None, :], result)


def geometry(key):
    base = jax.random.fold_in(key, 31)
    devices = TOKENS // TOK_DEV
    pairs = IMG_DEV // 2
    half_base = GRID_BASE // 2
    delta = jax.random.randint(jax.random.fold_in(base, 1), (devices, pairs), -half_base, half_base + 1)
    delta = delta.at[:, 0].set(half_base)
    longs = jnp.concatenate([GRID_BASE + delta, GRID_BASE - delta], axis=1)
    perm_keys = jax.random.split(jax.random.fold_in(base, 2), devices)
    orders = jax.vmap(lambda perm_key: jax.random.permutation(perm_key, IMG_DEV))(perm_keys)
    longs = jnp.take_along_axis(longs, orders, axis=1)
    flips = jax.random.randint(jax.random.fold_in(base, 3), (devices, IMG_DEV), 0, 2)
    heights = jnp.where(flips == 1, GRID_BASE, longs)
    widths = jnp.where(flips == 1, longs, GRID_BASE)
    areas = longs * GRID_BASE
    ends = jnp.cumsum(areas, axis=1)
    starts = ends - areas
    places = jnp.arange(TOK_DEV, dtype=jnp.int32)
    seg_ids = jnp.sum((places[None, :, None] >= ends[:, None, :]).astype(jnp.int32), axis=2)
    start_of = jnp.take_along_axis(starts, seg_ids, axis=1)
    width_of = jnp.take_along_axis(widths, seg_ids, axis=1)
    local = places[None, :] - start_of
    return (heights.reshape(-1).astype(jnp.int32), widths.reshape(-1).astype(jnp.int32), seg_ids.reshape(-1).astype(jnp.int32), (local // width_of).reshape(-1).astype(jnp.int32), (local % width_of).reshape(-1).astype(jnp.int32))


def draw_grid_height(key, part):
    return geometry(key)[0]


def draw_grid_width(key, part):
    return geometry(key)[1]


def draw_segment(key, part):
    return geometry(key)[2]


def draw_patch_rows(key, part):
    return geometry(key)[3]


def draw_patch_cols(key, part):
    return geometry(key)[4]


def steps_of(rng, extent, shards, least, high):
    loudness, own = 1.0, jax.random.fold_in(rng, 6)
    for dim, parts in shards:
        draws = jnp.exp(jax.random.uniform(jax.random.fold_in(own, dim), (parts,), jnp.float32, least / len(shards), high / len(shards)))
        loudness = loudness * jnp.repeat(draws, extent[dim] // parts).reshape([-1 if axis == dim else 1 for axis in range(len(extent))])
    return loudness


def bell_draw(rng, shape, deviation, bound, cuts=(), kind=jnp.bfloat16):
    values = jax.random.normal(rng, shape, jnp.float32) * deviation
    if len(cuts) > 0:
        values = steps_of(rng, shape, cuts, -0.22, 0.18) * values
    return jnp.clip(values, min=-bound, max=bound).astype(kind)


def setup_inputs(seed: int = 0) -> dict:
    key_list = jax.random.split(jax.random.key(seed), 17)
    tokens = bell_draw(key_list[0], (TOKENS, D), 1.0, 6.0, ((0, 32),))
    cotangent = bell_draw(key_list[1], (TOKENS, D), 1.0, 6.0, ((0, 32),))
    vectors = draw_vectors(jax.random.fold_in(key_list[16], 71), 0)
    vector_moments = jnp.clip(jnp.exp(jax.random.uniform(key_list[3], (VEC_ROWS, D), jnp.float32, math.log(819.2), math.log(26214.4))), 819.2, 26214.4)
    decays = jnp.clip(jax.random.uniform(key_list[4], (2,), jnp.float32, 0.9, 0.98), 0.9, 0.98)
    owner = draw_owner(jax.random.fold_in(key_list[16], 71), 0)
    master_slots = draw_master_slots(jax.random.fold_in(key_list[16], 71), 0)
    left_slots = draw_left_slots(jax.random.fold_in(key_list[16], 71), 0)
    right_slots = draw_right_slots(jax.random.fold_in(key_list[16], 71), 0)
    left_roots = draw_left_roots(jax.random.fold_in(key_list[16], 71), 0)
    right_roots = draw_right_roots(jax.random.fold_in(key_list[16], 71), 0)
    grid_height = draw_grid_height(jax.random.fold_in(key_list[16], 71), 0)
    grid_width = draw_grid_width(jax.random.fold_in(key_list[16], 71), 0)
    patch_rows = draw_patch_rows(jax.random.fold_in(key_list[16], 71), 0)
    patch_cols = draw_patch_cols(jax.random.fold_in(key_list[16], 71), 0)
    segment = draw_segment(jax.random.fold_in(key_list[16], 71), 0)
    return dict(tokens=tokens, cotangent=cotangent, vectors=vectors, vector_moments=vector_moments, decays=decays, owner=owner, master_slots=master_slots, left_slots=left_slots, right_slots=right_slots, left_roots=left_roots, right_roots=right_roots, grid_height=grid_height, grid_width=grid_width, patch_rows=patch_rows, patch_cols=patch_cols, segment=segment)


NORM_EPSILON = 1e-06
GRAFT_EPSILON = 1e-06
STEP_EPSILON = 1e-08
RATE_MATRIX = 0.04
RATE_VECTOR = 0.02
MASKED_SCORE = -1e+30

@jax.custom_vjp
def low(v):
    return lax.optimization_barrier(v.astype(jnp.bfloat16)).astype(jnp.float32)

@jax.custom_vjp
def low_back(v):
    return v

def low_keep(v):
    return (low(v), None)

def low_pass(kept, grad):
    return (grad,)

def back_keep(v):
    return (v, None)

def back_low(kept, grad):
    return (low(grad),)
low.defvjp(low_keep, low_pass)
low_back.defvjp(back_keep, back_low)

def precise_dot(left_side, right_side):
    return jnp.dot(left_side, right_side, precision=lax.Precision.HIGHEST)

def layer_norm(values, gain_row, shift_row):
    centred = values - lax.optimization_barrier(jnp.mean(values, axis=-1, keepdims=True))
    spread = lax.optimization_barrier(jnp.mean(centred * centred, axis=-1, keepdims=True))
    return centred * lax.rsqrt(spread + NORM_EPSILON) * gain_row + shift_row

def rotate_pairs(flat_values, freq_row, rows_pos, cols_pos):
    tokens_here = flat_values.shape[0]
    values = flat_values.reshape(tokens_here, HEADS, -1)
    half_size = values.shape[-1] // 2
    middle = freq_row.shape[0] // 2
    freq_cols = freq_row[:middle].reshape(HEADS, half_size)
    freq_rows = freq_row[middle:].reshape(HEADS, half_size)
    angle_grid = rows_pos[:, None, None] * freq_rows[None] + cols_pos[:, None, None] * freq_cols[None]
    cosine = jnp.cos(angle_grid)
    sine_part = jnp.sin(angle_grid)
    first_half = values[..., :half_size]
    second = values[..., half_size:]
    turned = jnp.concatenate([first_half * cosine - second * sine_part, second * cosine + first_half * sine_part], axis=-1)
    return turned.reshape(tokens_here, -1)

def patch_positions(segment_ids, heights_in, widths_in, rows_in, cols_in):
    images_here = heights_in.shape[0]
    matches = segment_ids[:, None] == jnp.arange(images_here, dtype=jnp.int32)[None, :]
    heights = lax.optimization_barrier(jnp.sum(jnp.where(matches, heights_in[None, :], 0), axis=1)).astype(jnp.float32)
    widths = lax.optimization_barrier(jnp.sum(jnp.where(matches, widths_in[None, :], 0), axis=1)).astype(jnp.float32)
    rows_pos = rows_in.astype(jnp.float32) * GRID_BASE / heights
    cols_pos = cols_in.astype(jnp.float32) * GRID_BASE / widths
    return (rows_pos, cols_pos)

def group_layer(inputs, rows_pos, cols_pos, segment_ids, weights, vector_rows):
    query_weight, key_weight, value_weight, out_weight, up_weight, down_weight = weights
    tokens_here = inputs.shape[0]
    groups_mlp = FF // D
    normed = low(layer_norm(inputs, vector_rows[0], vector_rows[1]))
    query = low_back(precise_dot(normed, query_weight) + vector_rows[2])
    keyed = low_back(precise_dot(normed, key_weight) + vector_rows[3])
    valued = low(low_back(precise_dot(normed, value_weight) + vector_rows[4]))
    freq_row = vector_rows[9 + groups_mlp]
    query_rot = low(rotate_pairs(query, freq_row, rows_pos, cols_pos)).reshape(tokens_here, HEADS, -1)
    key_rot = low(rotate_pairs(keyed, freq_row, rows_pos, cols_pos)).reshape(tokens_here, HEADS, -1)
    value_heads = valued.reshape(tokens_here, HEADS, -1)
    score_scale = 1.0 / math.sqrt(D // HEADS)
    scores = low_back(jnp.einsum('qhd,khd->hqk', query_rot, key_rot, precision=lax.Precision.HIGHEST) * score_scale)
    same_image = segment_ids[:, None] == segment_ids[None, :]
    scores = jnp.where(same_image[None], scores, MASKED_SCORE)
    weights_low = low(jax.nn.softmax(scores, axis=-1))
    attended = jnp.einsum('hqk,khd->qhd', weights_low, value_heads, precision=lax.Precision.HIGHEST).reshape(tokens_here, -1)
    attended = low(low_back(attended))
    branch_one = low_back(precise_dot(attended, out_weight) + vector_rows[5])
    middle = inputs + branch_one
    normed_two = low(layer_norm(middle, vector_rows[6], vector_rows[7]))
    up_bias = vector_rows[8:8 + groups_mlp].reshape(-1)
    pre_act = low_back(precise_dot(normed_two, up_weight) + up_bias)
    activation = low(jax.nn.gelu(pre_act, approximate=False))
    branch_two = low_back(precise_dot(activation, down_weight) + vector_rows[8 + groups_mlp])
    return middle + branch_two

def reference(tokens, cotangent, vectors, vector_moments, decays, owner, master_slots, left_slots, right_slots, left_roots, right_roots, grid_height, grid_width, patch_rows, patch_cols, segment):
    groups = TOKENS // TOK_DEV

    def picked(block_kind):
        return jnp.stack([master_slots[owner[column, block_kind], column] for column in range(N_MLP)])
    attention_master = picked(0)
    up_master = picked(1)
    down_master = picked(2)
    segment_groups = segment.reshape(groups, TOK_DEV)
    rows_pos, cols_pos = jax.vmap(patch_positions)(segment_groups, grid_height.reshape(groups, -1), grid_width.reshape(groups, -1), patch_rows.reshape(groups, TOK_DEV), patch_cols.reshape(groups, TOK_DEV))

    def forward(inputs, attention_blocks, up_blocks, down_blocks, vector_rows):
        weights = (low(attention_blocks[0]), low(attention_blocks[1]), low(attention_blocks[2]), low(attention_blocks[3]), low(jnp.transpose(up_blocks, (1, 0, 2)).reshape(D, -1)), low(down_blocks.reshape(-1, D)))

        def one_group(pieces):
            return group_layer(pieces[0], pieces[1], pieces[2], pieces[3], weights, vector_rows)
        checked = jax.checkpoint(one_group)

        def scan_step(carry, pieces):
            return (carry, checked(pieces))
        _, outputs = lax.scan(scan_step, jnp.zeros((), jnp.float32), (inputs.reshape(groups, TOK_DEV, D), rows_pos, cols_pos, segment_groups))
        return outputs.reshape(TOKENS, D)
    result, pullback = jax.vjp(forward, tokens.astype(jnp.float32), attention_master, up_master, down_master, vectors)
    grad_input, grad_attention, grad_up, grad_down, grad_vectors = pullback(cotangent.astype(jnp.float32))
    decay_matrix = decays[0]
    slot_grads = jnp.zeros_like(master_slots)
    new_left = left_slots
    new_right = right_slots
    new_master = master_slots
    for column in range(N_MLP):
        for block_kind, grad_stack in enumerate((grad_attention, grad_up, grad_down)):
            holder = owner[column, block_kind]
            gradient = grad_stack[column]
            left_next = decay_matrix * left_slots[holder, column] + (1.0 - decay_matrix) * precise_dot(gradient, gradient.T)
            right_next = decay_matrix * right_slots[holder, column] + (1.0 - decay_matrix) * precise_dot(gradient.T, gradient)
            direction = precise_dot(precise_dot(left_roots[holder, column], gradient), right_roots[holder, column])
            normed_step = direction * lax.rsqrt(jnp.mean(direction * direction) + GRAFT_EPSILON)
            slot_grads = slot_grads.at[holder, column].set(gradient)
            new_left = new_left.at[holder, column].set(left_next)
            new_right = new_right.at[holder, column].set(right_next)
            new_master = new_master.at[holder, column].set(master_slots[holder, column] - RATE_MATRIX * normed_step)
    decay_vector = decays[1]
    moments_next = decay_vector * vector_moments + (1.0 - decay_vector) * grad_vectors * grad_vectors
    vectors_next = vectors - RATE_VECTOR * grad_vectors / (jnp.sqrt(moments_next) + STEP_EPSILON)
    return (result.astype(jnp.bfloat16), grad_input, slot_grads, new_left, new_right, new_master, grad_vectors, moments_next, vectors_next)
```

```python
import functools
import math

import jax
import jax.numpy as jnp
from jax import lax
from jax.experimental import pallas as pl
from jax.experimental.pallas import tpu as pltpu
from jax.sharding import PartitionSpec as P

HEADS = 12
GRID_BASE = 16
NORM_EPSILON = 1e-06
GRAFT_EPSILON = 1e-06
STEP_EPSILON = 1e-08
RATE_MATRIX = 0.04
RATE_VECTOR = 0.02
MASK_SHIFT = -(2.0**100)
BLOCK = 128
TILE = 256
F32 = jnp.float32
BF = jnp.bfloat16
VMEM_LIMIT = 60 * 1024 * 1024


def dot(left, right, left_dim, right_dim, precision=None):
    return lax.dot_general(
        left,
        right,
        (((left_dim,), (right_dim,)), ((), ())),
        preferred_element_type=F32,
        precision=precision,
    )


def normed(values):
    mean = jnp.mean(values, axis=-1, keepdims=True)
    centred = values - mean
    spread = jnp.mean(centred * centred, axis=-1, keepdims=True)
    scale = lax.rsqrt(spread + NORM_EPSILON)
    return centred * scale, scale


def norm_back(grad, unit, scale, gain):
    scaled = grad * gain
    first = jnp.mean(scaled, axis=-1, keepdims=True)
    second = jnp.mean(scaled * unit, axis=-1, keepdims=True)
    return scale * (scaled - first - unit * second)


def fold_rows(values):
    return jnp.sum(values.reshape(values.shape[0] // 8, 8, values.shape[1]), axis=0)


def project_kernel(
    x_ref, pos_ref, vec_ref, turned_ref, weight_ref,
    n1_ref, q_ref, k_ref, v_ref, cos_ref, sin_ref, qmark_ref, kmark_ref,
):
    unit, _ = normed(x_ref[...].astype(F32))
    n1 = (unit * vec_ref[0:1, :] + vec_ref[1:2, :]).astype(BF)
    n1t = n1.T
    n1_ref[...] = n1t
    px = pos_ref[0:1, :]
    py = pos_ref[1:2, :]
    half = cos_ref.shape[0]
    last = turned_ref.shape[1] - 1
    angle = turned_ref[half:, last:] * py + turned_ref[:half, last:] * px
    cosine = jnp.cos(angle)
    sine = jnp.sin(angle)
    cos_ref[...] = cosine
    sin_ref[...] = sine
    seg = pos_ref[2:3, :].astype(jnp.int32)
    row = lax.broadcasted_iota(jnp.int32, qmark_ref.shape, 0)
    qmark_ref[...] = jnp.where(row == seg, 1.0, 0.0).astype(BF)
    kmark_ref[...] = jnp.where(row == seg, 0.0, MASK_SHIFT).astype(BF)
    part = half // HEADS
    for index, (out, scale) in enumerate(((q_ref, 0.125), (k_ref, 1.0))):
        flat = dot(weight_ref[index], n1t, 0, 0) + turned_ref[:, 2 + index : 3 + index]
        for head in range(HEADS):
            low, mid = 2 * part * head, 2 * part * head + part
            a = flat[low:mid]
            b = flat[mid : mid + part]
            c = cosine[part * head : part * (head + 1)]
            s = sine[part * head : part * (head + 1)]
            out[low:mid, :] = (a * c - b * s).astype(BF) * jnp.asarray(scale, BF)
            out[mid : mid + part, :] = (b * c + a * s).astype(BF) * jnp.asarray(scale, BF)
    v_ref[...] = (dot(weight_ref[2], n1t, 0, 0) + turned_ref[:, 4:5]).astype(BF)


def project(x, pos, vec, turned, weights):
    rows, width = x.shape
    half = width // 2
    whole = lambda a: pl.BlockSpec(a.shape, lambda i: (0,) * a.ndim)
    col = lambda n: pl.BlockSpec((n, TILE), lambda i: (0, i))
    out = lambda n, d: jax.ShapeDtypeStruct((n, rows), d)
    return pl.pallas_call(
        project_kernel,
        grid=(rows // TILE,),
        in_specs=[
            pl.BlockSpec((TILE, width), lambda i: (i, 0)),
            col(8),
            whole(vec),
            whole(turned),
            whole(weights),
        ],
        out_specs=[col(width)] * 4 + [col(half)] * 2 + [col(16)] * 2,
        out_shape=[out(width, BF)] * 4 + [out(half, F32)] * 2 + [out(16, BF)] * 2,
        compiler_params=pltpu.CompilerParams(vmem_limit_bytes=VMEM_LIMIT),
        name="project",
    )(x, pos, vec, turned, weights)


def key_window(height_ref, width_ref, block):
    first = block * BLOCK
    last = first + BLOCK - 1
    start = jnp.int32(0)
    low = jnp.int32(0)
    high = jnp.int32(0)
    for image in range(height_ref.shape[0]):
        end = start + height_ref[image] * width_ref[image]
        low = jnp.where((start <= first) & (first < end), start, low)
        high = jnp.where((start <= last) & (last < end), end, high)
        start = end
    base = low // BLOCK
    return base, (high + BLOCK - 1) // BLOCK - base


def attend_kernel(height_ref, width_ref, q_ref, k_ref, v_ref, qmark_ref, kmark_ref, o_ref, log_ref):
    tokens = q_ref.shape[1]
    blocks = tokens // BLOCK
    size = q_ref.shape[0] // HEADS
    group = 4

    def one(block, part, base, count):
        here = pl.ds(pl.multiple_of(block * BLOCK, BLOCK), BLOCK)
        keys = pl.ds(pl.multiple_of(base * BLOCK, BLOCK), BLOCK * count)
        qmark = qmark_ref[:, here]
        kmark = kmark_ref[:, keys]
        for j in range(group):
            head = part * group + j
            rows = pl.ds(pl.multiple_of(head * size, size), size)
            q = jnp.concatenate([q_ref[rows, here], qmark], axis=0)
            k = jnp.concatenate([k_ref[rows, keys], kmark], axis=0)
            scores = dot(k, q, 0, 0)
            peak = jnp.max(scores, axis=0, keepdims=True)
            powers = jnp.exp(scores - peak)
            total = jnp.sum(powers, axis=0, keepdims=True)
            mixed = dot(v_ref[rows, keys], powers.astype(BF), 1, 0)
            o_ref[rows, here] = (mixed * (1.0 / total)).astype(BF)
            log_ref[pl.ds(pl.multiple_of(head * 8, 8), 8), here] = jnp.broadcast_to(
                peak + jnp.log(total), (8, BLOCK)
            )

    def step(block, carry):
        base, count = key_window(height_ref, width_ref, block)
        for n in range(1, blocks + 1):

            @pl.when(count == n)
            def _():
                def inner(part, c):
                    one(block, part, base, n)
                    return c

                lax.fori_loop(0, HEADS // group, inner, 0)

        return carry

    lax.fori_loop(0, blocks, step, 0)


def attend(heights, widths, q, k, v, qmark, kmark):
    smem = pl.BlockSpec(memory_space=pltpu.SMEM)
    vmem = pl.BlockSpec(memory_space=pltpu.VMEM)
    return pl.pallas_call(
        attend_kernel,
        in_specs=[smem, smem] + [vmem] * 5,
        out_specs=[vmem, vmem],
        out_shape=[
            jax.ShapeDtypeStruct(q.shape, BF),
            jax.ShapeDtypeStruct((8 * HEADS, q.shape[1]), F32),
        ],
        compiler_params=pltpu.CompilerParams(vmem_limit_bytes=VMEM_LIMIT),
        name="attend",
    )(heights, widths, q, k, v, qmark, kmark)


def attend_back_kernel(
    height_ref, width_ref, q_ref, k_ref, v_ref, qmark_ref, kmark_ref, log_ref, do_ref,
    pos_ref, cos_ref, sin_ref,
    dq_ref, dk_ref, dv_ref, freq_ref, bias_ref,
    gq_ref, gk_ref, gv_ref, turn_ref,
):
    tokens = q_ref.shape[1]
    blocks = tokens // BLOCK
    size = q_ref.shape[0] // HEADS
    half = size // 2
    group = 2
    gk_ref[...] = jnp.zeros_like(gk_ref)
    gv_ref[...] = jnp.zeros_like(gv_ref)

    def one(block, part, base, count):
        here = pl.ds(pl.multiple_of(block * BLOCK, BLOCK), BLOCK)
        keys = pl.ds(pl.multiple_of(base * BLOCK, BLOCK), BLOCK * count)
        qmark = qmark_ref[:, here]
        kmark = kmark_ref[:, keys]
        for j in range(group):
            head = part * group + j
            rows = pl.ds(pl.multiple_of(head * size, size), size)
            q = q_ref[rows, here]
            k = k_ref[rows, keys]
            do = do_ref[rows, here]
            scores = dot(
                jnp.concatenate([k, kmark], axis=0), jnp.concatenate([q, qmark], axis=0), 0, 0
            )
            log_row = log_ref[pl.ds(pl.multiple_of(head * 8, 8), 8), here][0:1]
            probs = jnp.exp(scores - log_row)
            dp = dot(v_ref[rows, keys], do, 0, 0)
            inner = jnp.sum(probs * dp, axis=0, keepdims=True)
            ds = (probs * (dp - inner)).astype(BF)
            gq_ref[rows, here] = dot(k, ds, 1, 0) * 0.125
            gk_ref[rows, keys] += dot(q, ds, 1, 1)
            gv_ref[rows, keys] += dot(do, probs.astype(BF), 1, 1)

    def step(block, carry):
        base, count = key_window(height_ref, width_ref, block)
        for n in range(1, blocks + 1):

            @pl.when(count == n)
            def _():
                def inner(part, c):
                    one(block, part, base, n)
                    return c

                lax.fori_loop(0, HEADS // group, inner, 0)

        return carry

    lax.fori_loop(0, blocks, step, 0)

    def unturn(head, carry):
        low = pl.ds(pl.multiple_of(head * size, size), half)
        high = pl.ds(pl.multiple_of(head * size + half, half), half)
        table = pl.ds(pl.multiple_of(head * half, half), half)
        c = cos_ref[table, :]
        s = sin_ref[table, :]
        turn = None
        for grad_ref, rot_ref, scale, out_ref in (
            (gq_ref, q_ref, 8.0, dq_ref),
            (gk_ref, k_ref, 1.0, dk_ref),
        ):
            ga = grad_ref[low, :]
            gb = grad_ref[high, :]
            out_ref[low, :] = (ga * c + gb * s).astype(BF)
            out_ref[high, :] = (gb * c - ga * s).astype(BF)
            ra = rot_ref[low, :].astype(F32) * scale
            rb = rot_ref[high, :].astype(F32) * scale
            piece = gb * ra - ga * rb
            turn = piece if turn is None else turn + piece
        turn_ref[table, :] = turn
        both = pl.ds(pl.multiple_of(head * size, size), size)
        dv_ref[both, :] = gv_ref[both, :].astype(BF)
        return carry

    lax.fori_loop(0, HEADS, unturn, 0)
    freq_ref[...] = dot(pos_ref[...], turn_ref[...], 1, 1, lax.Precision.HIGHEST)
    ones = jnp.ones((8, tokens), BF)
    for index, ref in enumerate((dq_ref, dk_ref, dv_ref)):
        bias_ref[8 * index : 8 * index + 8, :] = dot(ones, ref[...], 1, 1)


def attend_back(heights, widths, q, k, v, qmark, kmark, log_totals, do, pos, cosine, sine):
    smem = pl.BlockSpec(memory_space=pltpu.SMEM)
    vmem = pl.BlockSpec(memory_space=pltpu.VMEM)
    width, tokens = q.shape
    return pl.pallas_call(
        attend_back_kernel,
        in_specs=[smem, smem] + [vmem] * 10,
        out_specs=[vmem] * 5,
        out_shape=[jax.ShapeDtypeStruct(q.shape, BF)] * 3
        + [
            jax.ShapeDtypeStruct((8, width // 2), F32),
            jax.ShapeDtypeStruct((24, width), F32),
        ],
        scratch_shapes=[pltpu.VMEM(q.shape, F32)] * 3 + [pltpu.VMEM((width // 2, tokens), F32)],
        compiler_params=pltpu.CompilerParams(vmem_limit_bytes=VMEM_LIMIT),
        name="attend_back",
    )(heights, widths, q, k, v, qmark, kmark, log_totals, do, pos, cosine, sine)


def middle_kernel(
    x_ref, g_ref, o_ref, vec_ref, wo_ref, up_ref, down_ref,
    y_ref, dh_ref, do_ref, dwo_ref, dup_ref, ddown_ref, rows_ref, dc_ref,
    h_ref, n2_ref, n2t_ref, acc_ref, dn_ref, a_ref, dz_ref, dr_ref,
):
    groups = vec_ref.shape[0] - 10
    step = pl.program_id(0)
    tokens, width = x_ref.shape
    tiles = tokens // TILE

    def tile(i):
        return pl.ds(pl.multiple_of(i * TILE, TILE), TILE)

    @pl.when(step == 0)
    def _():
        def first(i, c):
            t = tile(i)
            branch = dot(o_ref[:, t], wo_ref[...], 0, 0) + vec_ref[5:6, :]
            h = x_ref[t, :].astype(F32) + branch
            h_ref[t, :] = h
            unit, _ = normed(h)
            n2 = (unit * vec_ref[6:7, :] + vec_ref[7:8, :]).astype(BF)
            n2_ref[t, :] = n2
            n2t_ref[:, t] = n2.T
            acc_ref[t, :] = h + vec_ref[8 + groups : 9 + groups, :]
            dn_ref[t, :] = jnp.zeros((TILE, width), F32)
            return c

        lax.fori_loop(0, tiles, first, 0)

    up_bias = vec_ref[pl.ds(8 + step, 1), :]

    def second(i, c):
        t = tile(i)
        z = dot(n2_ref[t, :], up_ref[0], 1, 0) + up_bias
        cdf = 0.5 * (1.0 + lax.erf(z * math.sqrt(0.5)))
        a = (z * cdf).astype(BF)
        a_ref[t, :] = a
        acc_ref[t, :] += dot(a, down_ref[0], 1, 0)
        da = dot(g_ref[t, :], down_ref[0], 1, 1)
        slope = cdf + z * (jnp.exp(-0.5 * z * z) * (1.0 / math.sqrt(2.0 * math.pi)))
        dz = (da * slope).astype(BF)
        dz_ref[t, :] = dz
        dn_ref[t, :] += dot(dz, up_ref[0], 1, 1)
        return c

    lax.fori_loop(0, tiles, second, 0)
    dc_ref[0] = dot(jnp.ones((8, tokens), BF), dz_ref[...], 1, 0)
    dup_ref[0] = dot(n2t_ref[...], dz_ref[...], 1, 0).astype(BF)
    ddown_ref[0] = dot(a_ref[...], g_ref[...], 0, 0).astype(BF)

    @pl.when(step == groups - 1)
    def _():
        rows_ref[...] = jnp.zeros_like(rows_ref)

        def third(i, c):
            t = tile(i)
            y_ref[t, :] = acc_ref[t, :].astype(BF)
            g = g_ref[t, :].astype(F32)
            unit, scale = normed(h_ref[t, :])
            dn = dn_ref[t, :]
            dh = g + norm_back(dn, unit, scale, vec_ref[6:7, :])
            dh_ref[t, :] = dh
            dr = dh.astype(BF)
            dr_ref[t, :] = dr
            do_ref[:, t] = dot(wo_ref[...], dr, 1, 1).astype(BF)
            rows_ref[0:8, :] += fold_rows(dr.astype(F32))
            rows_ref[8:16, :] += fold_rows(dn * unit)
            rows_ref[16:24, :] += fold_rows(dn)
            rows_ref[24:32, :] += fold_rows(g)
            return c

        lax.fori_loop(0, tiles, third, 0)
        dwo_ref[...] = dot(o_ref[...], dr_ref[...], 1, 0).astype(BF)


def middle_part(x, g, o, vec, wo, up, down):
    tokens, width = x.shape
    groups = up.shape[0]
    whole = lambda s: pl.BlockSpec(s, lambda i: (0,) * len(s))
    block = pl.BlockSpec((1, width, width), lambda i: (i, 0, 0))
    return pl.pallas_call(
        middle_kernel,
        grid=(groups,),
        in_specs=[
            whole(x.shape),
            whole(g.shape),
            whole(o.shape),
            whole(vec.shape),
            whole(wo.shape),
            block,
            block,
        ],
        out_specs=[
            whole((tokens, width)),
            whole((tokens, width)),
            whole((width, tokens)),
            whole((width, width)),
            block,
            block,
            whole((32, width)),
            pl.BlockSpec((1, 8, width), lambda i: (i, 0, 0)),
        ],
        out_shape=[
            jax.ShapeDtypeStruct((tokens, width), BF),
            jax.ShapeDtypeStruct((tokens, width), F32),
            jax.ShapeDtypeStruct((width, tokens), BF),
            jax.ShapeDtypeStruct((width, width), BF),
            jax.ShapeDtypeStruct((groups, width, width), BF),
            jax.ShapeDtypeStruct((groups, width, width), BF),
            jax.ShapeDtypeStruct((32, width), F32),
            jax.ShapeDtypeStruct((groups, 8, width), F32),
        ],
        scratch_shapes=[
            pltpu.VMEM((tokens, width), F32),
            pltpu.VMEM((tokens, width), BF),
            pltpu.VMEM((width, tokens), BF),
            pltpu.VMEM((tokens, width), F32),
            pltpu.VMEM((tokens, width), F32),
            pltpu.VMEM((tokens, width), BF),
            pltpu.VMEM((tokens, width), BF),
            pltpu.VMEM((tokens, width), BF),
        ],
        compiler_params=pltpu.CompilerParams(vmem_limit_bytes=VMEM_LIMIT),
        name="middle",
    )(x, g, o, vec, wo, up, down)


def final_kernel(
    x_ref, dh_ref, n1_ref, dq_ref, dk_ref, dv_ref, vec_ref, weight_ref,
    dx_ref, dw_ref, rows_ref,
):
    tokens, width = x_ref.shape
    for index, ref in enumerate((dq_ref, dk_ref, dv_ref)):
        dw_ref[index] = dot(n1_ref[...], ref[...], 1, 1).astype(BF)
    rows_ref[...] = jnp.zeros_like(rows_ref)

    def loop(i, c):
        t = pl.ds(pl.multiple_of(i * TILE, TILE), TILE)
        dn = dot(dq_ref[:, t], weight_ref[0], 0, 1)
        dn += dot(dk_ref[:, t], weight_ref[1], 0, 1)
        dn += dot(dv_ref[:, t], weight_ref[2], 0, 1)
        unit, scale = normed(x_ref[t, :].astype(F32))
        dx_ref[t, :] = dh_ref[t, :] + norm_back(dn, unit, scale, vec_ref[0:1, :])
        rows_ref[0:8, :] += fold_rows(dn * unit)
        rows_ref[8:16, :] += fold_rows(dn)
        return c

    lax.fori_loop(0, tokens // TILE, loop, 0)


def final_part(x, dh, n1, dq, dk, dv, vec, weights):
    tokens, width = x.shape
    vmem = pl.BlockSpec(memory_space=pltpu.VMEM)
    return pl.pallas_call(
        final_kernel,
        in_specs=[vmem] * 8,
        out_specs=[vmem] * 3,
        out_shape=[
            jax.ShapeDtypeStruct((tokens, width), F32),
            jax.ShapeDtypeStruct((3, width, width), BF),
            jax.ShapeDtypeStruct((16, width), F32),
        ],
        compiler_params=pltpu.CompilerParams(vmem_limit_bytes=VMEM_LIMIT),
        name="final",
    )(x, dh, n1, dq, dk, dv, vec, weights)


def halves(values):
    high = values.astype(BF)
    return high, (values - high.astype(F32)).astype(BF)


def dot_fine(left, right):
    left_high, left_low = halves(left)
    right_high, right_low = halves(right)
    return (
        dot(left_high, right_low, 1, 0)
        + dot(left_low, right_high, 1, 0)
        + dot(left_high, right_high, 1, 0)
    )


def update_kernel(
    keep_ref, decay_ref, grad_ref, left_ref, right_ref, lroot_ref, rroot_ref, master_ref,
    slot_ref, newleft_ref, newright_ref, newmaster_ref,
):
    @pl.when(keep_ref[0] == 0)
    def _():
        slot_ref[...] = jnp.zeros_like(slot_ref)
        newleft_ref[...] = left_ref[...]
        newright_ref[...] = right_ref[...]
        newmaster_ref[...] = master_ref[...]

    @pl.when(keep_ref[0] != 0)
    def _():
        decay = decay_ref[0]
        grad = grad_ref[...].astype(F32)
        slot_ref[...] = grad
        low = grad.astype(BF)
        newleft_ref[...] = decay * left_ref[...] + (1.0 - decay) * dot(low, low, 1, 1)
        newright_ref[...] = decay * right_ref[...] + (1.0 - decay) * dot(low, low, 0, 0)
        inner = dot_fine(lroot_ref[...], grad)
        direction = dot_fine(inner, rroot_ref[...])
        size = direction.shape[0] * direction.shape[1]
        mean = jnp.sum(direction * direction, keepdims=True) * (1.0 / size)
        newmaster_ref[...] = master_ref[...] - RATE_MATRIX * direction * lax.rsqrt(
            mean + GRAFT_EPSILON
        )


def update(owns, decays, grad, left, right, lroot, rroot, master):
    smem = pl.BlockSpec(memory_space=pltpu.SMEM)
    vmem = pl.BlockSpec(memory_space=pltpu.VMEM)
    return pl.pallas_call(
        update_kernel,
        in_specs=[smem, smem] + [vmem] * 6,
        out_specs=[vmem] * 4,
        out_shape=[jax.ShapeDtypeStruct(left.shape, F32)] * 4,
        compiler_params=pltpu.CompilerParams(vmem_limit_bytes=VMEM_LIMIT),
        name="update",
    )(owns, decays, grad, left, right, lroot, rroot, master)


def positions(segment, heights, widths, patch_rows, patch_cols):
    images = heights.shape[0]
    matches = segment[None, :] == jnp.arange(images, dtype=jnp.int32)[:, None]
    tall = jnp.sum(jnp.where(matches, heights[:, None], 0), axis=0).astype(F32)
    wide = jnp.sum(jnp.where(matches, widths[:, None], 0), axis=0).astype(F32)
    py = patch_rows.astype(F32) * GRID_BASE / tall
    px = patch_cols.astype(F32) * GRID_BASE / wide
    zero = jnp.zeros_like(px)
    return jnp.stack([px, py, segment.astype(F32), zero, zero, zero, zero, zero])


def local(
    tokens, cotangent, vectors, vector_moments, decays, owner, master_slots, left_slots,
    right_slots, left_roots, right_roots, grid_height, grid_width, patch_rows, patch_cols, segment,
):
    dp_index = lax.axis_index("dp")
    mlp_index = lax.axis_index("mlp")
    n_dp = lax.axis_size("dp")
    n_mlp = lax.axis_size("mlp")
    width = tokens.shape[1]
    share = width // n_dp
    owner_row = jnp.take(owner, mlp_index, axis=0)
    holds = owner_row == dp_index
    master = master_slots[0, 0]
    pieces = lax.all_to_all(master.astype(BF).reshape(n_dp, share, width), "dp", 0, 0, tiled=True)
    mine = jnp.take(pieces, owner_row, axis=0)
    every = lax.all_gather(mine[None], ("dp", "mlp"), axis=0, tiled=True)
    blocks = every.reshape(n_dp, n_mlp, 3, share, width).transpose(2, 1, 0, 3, 4)
    blocks = blocks.reshape(3, n_mlp, width, width)
    attention = blocks[0]
    turned = vectors.T
    pos = positions(segment, grid_height, grid_width, patch_rows, patch_cols)
    n1t, q, k, v, cosine, sine, qmark, kmark = project(tokens, pos, vectors, turned, attention)
    o, log_totals = attend(grid_height, grid_width, q, k, v, qmark, kmark)
    output, dh, do, dwo, dup, ddown, mid_rows, dc = middle_part(
        tokens, cotangent, o, vectors, attention[3], blocks[1], blocks[2]
    )
    dq, dk, dv, freq, bias = attend_back(
        grid_height, grid_width, q, k, v, qmark, kmark, log_totals, do, pos, cosine, sine
    )
    input_grad, dwqkv, fin_rows = final_part(tokens, dh, n1t, dq, dk, dv, vectors, attention)

    attention_grads = jnp.concatenate([dwqkv, dwo[None]], axis=0)
    grads = jnp.stack([attention_grads, dup, ddown], axis=1)
    grads = grads.reshape(n_mlp, 3, n_dp, share, width).transpose(2, 0, 1, 3, 4)
    grads = grads.reshape(n_dp * n_mlp * 3, share, width)
    reduced = lax.psum_scatter(grads, ("dp", "mlp"), scatter_dimension=0, tiled=True)
    takers = owner_row[None, :] == jnp.arange(n_dp, dtype=jnp.int32)[:, None]
    kind_of = jnp.sum(jnp.where(takers, jnp.arange(3, dtype=jnp.int32)[None, :], 0), axis=1)
    gradient = lax.all_to_all(jnp.take(reduced, kind_of, axis=0), "dp", 0, 0, tiled=True)
    gradient = gradient.reshape(width, width)
    owns = jnp.any(holds).astype(jnp.int32).reshape(1)
    slot_grad, left_out, right_out, master_out = update(
        owns, decays, gradient, left_slots[0, 0], right_slots[0, 0], left_roots[0, 0],
        right_roots[0, 0], master,
    )

    eights = lambda rows: jnp.sum(rows.reshape(-1, 8, width), axis=1)
    fin = eights(fin_rows)
    mid = eights(mid_rows)
    local_vectors = jnp.concatenate(
        [
            fin,
            bias[0::8],
            mid[0:3],
            dc[:, 0, :],
            mid[3:4],
            freq[0:2].reshape(1, width),
        ],
        axis=0,
    )
    total = lax.psum(local_vectors, ("dp", "mlp"))
    cut = width // n_mlp
    own = lambda table: lax.dynamic_slice_in_dim(table, mlp_index * cut, cut, 1)
    grad_share = own(total)
    decay = decays[1]
    moment_next = decay * own(vector_moments) + (1.0 - decay) * grad_share * grad_share
    vector_next = own(vectors) - RATE_VECTOR * grad_share / (jnp.sqrt(moment_next) + STEP_EPSILON)
    lift = lambda a: a[None, None]
    return (
        output, input_grad, lift(slot_grad), lift(left_out), lift(right_out), lift(master_out),
        grad_share, moment_next, vector_next,
    )


def solution(mesh):
    both = P(("dp", "mlp"))
    flat = P(("dp", "mlp"), None)
    slots = P("dp", "mlp", None, None)
    split = P(None, "mlp")
    return jax.shard_map(
        local,
        mesh=mesh,
        in_specs=(flat, flat, P(), P(), P(), P(), slots, slots, slots, slots, slots)
        + (both,) * 5,
        out_specs=(flat, flat, slots, slots, slots, slots, split, split, split),
        check_vma=False,
    )
```

```python
import functools
import math

import jax
import jax.numpy as jnp
from jax import lax
from jax.experimental import pallas as pl
from jax.experimental.pallas import tpu as pltpu
from jax.sharding import PartitionSpec as P

HEADS = 12
GRID_BASE = 16
NORM_EPSILON = 1e-06
GRAFT_EPSILON = 1e-06
STEP_EPSILON = 1e-08
RATE_MATRIX = 0.04
RATE_VECTOR = 0.02
MASK_SHIFT = -(2.0**100)
BLOCK = 128
TILE = 256
F32 = jnp.float32
BF = jnp.bfloat16
VMEM_LIMIT = 60 * 1024 * 1024


def dot(left, right, left_dim, right_dim, precision=None):
    return lax.dot_general(
        left,
        right,
        (((left_dim,), (right_dim,)), ((), ())),
        preferred_element_type=F32,
        precision=precision,
    )


def normed(values):
    mean = jnp.mean(values, axis=-1, keepdims=True)
    centred = values - mean
    spread = jnp.mean(centred * centred, axis=-1, keepdims=True)
    scale = lax.rsqrt(spread + NORM_EPSILON)
    return centred * scale, scale


def norm_back(grad, unit, scale, gain):
    scaled = grad * gain
    first = jnp.mean(scaled, axis=-1, keepdims=True)
    second = jnp.mean(scaled * unit, axis=-1, keepdims=True)
    return scale * (scaled - first - unit * second)


def fold_rows(values):
    return jnp.sum(values.reshape(values.shape[0] // 8, 8, values.shape[1]), axis=0)


def place():
    d = lax.axis_index("dp")
    m = lax.axis_index("mlp")
    return d // 2, d % 2, m // 2, m % 2


def at(z, x, y, c):
    return (2 * z + x, 2 * y + c)


def greet(peers):
    barrier = pltpu.get_barrier_semaphore()
    for peer in peers:
        pl.semaphore_signal(barrier, inc=1, device_id=peer, device_id_type=pl.DeviceIdType.MESH)
    pl.semaphore_wait(barrier, len(peers))


class Mail:
    def __init__(self, sems):
        self.sems = sems
        self.sent = []

    def send(self, source, target, arrival, peer):
        copy = pltpu.make_async_remote_copy(
            src_ref=source,
            dst_ref=target,
            send_sem=self.sems.at[len(self.sent)],
            recv_sem=arrival,
            device_id=peer,
            device_id_type=pl.DeviceIdType.MESH,
        )
        copy.start()
        self.sent.append(copy)

    def finish(self):
        for copy in self.sent:
            copy.wait_send()


def arrived(target, arrival):
    pltpu.make_async_copy(target, target, arrival).wait()


def enter_kernel(
    owner_ref, slot_ref, x_ref, pos_ref, vec_ref, turned_ref,
    n1_ref, q_ref, k_ref, v_ref, cos_ref, sin_ref, qmark_ref, kmark_ref, weight_ref, zone_ref,
    land_ref, mine_ref, att_ref, zland_ref,
    land_sem, zone_sem, att_sem, send_sem, local_sem,
):
    z, x, y, c = place()
    m = 2 * y + c
    d = 2 * z + x
    n_dp = land_ref.shape[0]
    right_x, right_y, partner = at(z, 1 - x, y, c), at(z, x, 1 - y, c), at(z, x, y, 1 - c)
    dp_peers = [((d + off) % n_dp, m) for off in range(1, n_dp)]
    greet(dp_peers + [right_y, partner])
    mail = Mail(send_sem)
    own = pltpu.make_async_copy(slot_ref.at[d], land_ref.at[d], local_sem.at[0])
    own.start()
    for peer in dp_peers:
        mail.send(slot_ref.at[peer[0]], land_ref.at[d], land_sem.at[d], peer)

    tokens = x_ref.shape[0]
    half = cos_ref.shape[0]
    last = turned_ref.shape[1] - 1
    tiles = tokens // TILE

    def prepare(i, carry):
        t = pl.ds(pl.multiple_of(i * TILE, TILE), TILE)
        unit, _ = normed(x_ref[t, :].astype(F32))
        n1_ref[:, t] = (unit * vec_ref[0:1, :] + vec_ref[1:2, :]).astype(BF).T
        angle = turned_ref[half:, last:] * pos_ref[1:2, t] + turned_ref[:half, last:] * pos_ref[0:1, t]
        cos_ref[:, t] = jnp.cos(angle)
        sin_ref[:, t] = jnp.sin(angle)
        seg = pos_ref[2:3, t].astype(jnp.int32)
        row = lax.broadcasted_iota(jnp.int32, (qmark_ref.shape[0], TILE), 0)
        qmark_ref[:, t] = jnp.where(row == seg, 1.0, 0.0).astype(BF)
        kmark_ref[:, t] = jnp.where(row == seg, 0.0, MASK_SHIFT).astype(BF)
        return carry

    lax.fori_loop(0, tiles, prepare, 0)

    own.wait()
    for off in range(1, n_dp):
        source = (d + off) % n_dp
        arrived(land_ref.at[source], land_sem.at[source])
    for kind in range(3):
        mine_ref[kind] = land_ref[owner_ref[m, kind]]

    def spread_z(source, target, sem):
        for off in range(1, 4):
            mail.send(source, target, sem, at((z + off) % 4, x, y, c))

    spread_z(mine_ref.at[0], att_ref.at[m, d], att_sem.at[m, d])
    for peer in (right_x, right_y, partner):
        mail.send(mine_ref.at[0], att_ref.at[m, d], att_sem.at[m, d], peer)
    keep = pltpu.make_async_copy(mine_ref.at[0], att_ref.at[m, d], local_sem.at[1])
    keep.start()
    for off in (1, 3, 2):
        e = 2 * ((z + off) % 4) + x
        arrived(att_ref.at[m, e], att_sem.at[m, e])
        for peer in (right_x, right_y, partner):
            mail.send(att_ref.at[m, e], att_ref.at[m, e], att_sem.at[m, e], peer)
    keeps = []
    for kind in range(2):
        spread_z(mine_ref.at[1 + kind], zland_ref.at[kind, z], zone_sem.at[kind, z])
        copy = pltpu.make_async_copy(
            mine_ref.at[1 + kind], zland_ref.at[kind, z], local_sem.at[2 + kind]
        )
        copy.start()
        keeps.append(copy)
    m_y = 2 * (1 - y) + c
    for part in range(4):
        e = 2 * part + 1 - x
        arrived(att_ref.at[m, e], att_sem.at[m, e])
        if part < 2:
            mail.send(att_ref.at[m, e], att_ref.at[m, e], att_sem.at[m, e], right_y)
        mail.send(att_ref.at[m, e], att_ref.at[m, e], att_sem.at[m, e], partner)
        f = 2 * part + x
        arrived(att_ref.at[m_y, f], att_sem.at[m_y, f])
        if part >= 2:
            mail.send(att_ref.at[m_y, f], att_ref.at[m_y, f], att_sem.at[m_y, f], right_x)
        mail.send(att_ref.at[m_y, f], att_ref.at[m_y, f], att_sem.at[m_y, f], partner)
    for part in range(4):
        e = 2 * part + 1 - x
        arrived(att_ref.at[m_y, e], att_sem.at[m_y, e])
        mail.send(att_ref.at[m_y, e], att_ref.at[m_y, e], att_sem.at[m_y, e], partner)
    for step in range(2):
        other = 2 * step + 1 - c
        for e in range(n_dp):
            arrived(att_ref.at[other, e], att_sem.at[other, e])
    keep.wait()
    out = pltpu.make_async_copy(att_ref, weight_ref, local_sem.at[4])
    out.start()

    part = half // HEADS
    width = x_ref.shape[1]

    def weight(index):
        return att_ref[index].reshape(width, width)

    def rotate(i, carry):
        t = pl.ds(pl.multiple_of(i * TILE, TILE), TILE)
        n1t = n1_ref[:, t]
        cosine = cos_ref[:, t]
        sine = sin_ref[:, t]
        for index, (ref, scale) in enumerate(((q_ref, 0.125), (k_ref, 1.0))):
            flat = dot(weight(index), n1t, 0, 0) + turned_ref[:, 2 + index : 3 + index]
            for head in range(HEADS):
                low, mid = 2 * part * head, 2 * part * head + part
                a = flat[low:mid]
                b = flat[mid : mid + part]
                cs = cosine[part * head : part * (head + 1)]
                sn = sine[part * head : part * (head + 1)]
                ref[low:mid, t] = (a * cs - b * sn).astype(BF) * jnp.asarray(scale, BF)
                ref[mid : mid + part, t] = (b * cs + a * sn).astype(BF) * jnp.asarray(scale, BF)
        v_ref[:, t] = (dot(weight(2), n1t, 0, 0) + turned_ref[:, 4:5]).astype(BF)
        return carry

    lax.fori_loop(0, tiles, rotate, 0)
    for kind in range(2):
        keeps[kind].wait()
        for off in range(1, 4):
            e = (z + off) % 4
            arrived(zland_ref.at[kind, e], zone_sem.at[kind, e])
    last_out = pltpu.make_async_copy(zland_ref, zone_ref, local_sem.at[5])
    last_out.start()
    out.wait()
    last_out.wait()
    mail.finish()


def enter(owner, slot, x, pos, vec, turned):
    rows, width = x.shape
    half = width // 2
    n_dp, share, _ = slot.shape
    n_mlp = owner.shape[0]
    smem = pl.BlockSpec(memory_space=pltpu.SMEM)
    vmem = pl.BlockSpec(memory_space=pltpu.VMEM)
    hbm = pl.BlockSpec(memory_space=pl.ANY)
    out = lambda n, dtype: jax.ShapeDtypeStruct((n, rows), dtype)
    return pl.pallas_call(
        enter_kernel,
        in_specs=[smem, hbm, vmem, vmem, vmem, vmem],
        out_specs=[vmem] * 8 + [hbm] * 2,
        out_shape=[out(width, BF)] * 4
        + [out(half, F32)] * 2
        + [out(16, BF)] * 2
        + [
            jax.ShapeDtypeStruct((n_mlp, n_dp, share, width), BF),
            jax.ShapeDtypeStruct((2, 4, share, width), BF),
        ],
        scratch_shapes=[
            pltpu.VMEM((n_dp, share, width), BF),
            pltpu.VMEM((3, share, width), BF),
            pltpu.VMEM((n_mlp, n_dp, share, width), BF),
            pltpu.VMEM((2, 4, share, width), BF),
            pltpu.SemaphoreType.DMA((n_dp,)),
            pltpu.SemaphoreType.DMA((2, 4)),
            pltpu.SemaphoreType.DMA((n_mlp, n_dp)),
            pltpu.SemaphoreType.DMA((64,)),
            pltpu.SemaphoreType.DMA((6,)),
        ],
        compiler_params=pltpu.CompilerParams(
            vmem_limit_bytes=VMEM_LIMIT, collective_id=0, has_side_effects=True
        ),
        name="enter",
    )(owner, slot, x, pos, vec, turned)


def fill_kernel(
    zone_ref, xzone_ref, yzone_ref, up_ref, down_ref, land_sem, send_sem, local_sem
):
    z, x, y, c = place()
    m = 2 * y + c
    m_y = 2 * (1 - y) + c
    right_x, right_y, partner = at(z, 1 - x, y, c), at(z, x, 1 - y, c), at(z, x, y, 1 - c)
    greet([right_x, right_y, partner])
    mail = Mail(send_sem)
    kept = []
    outs = (up_ref, down_ref)
    for kind in range(2):
        to = outs[kind]
        sem = land_sem.at[kind]
        for part in range(4):
            own, from_x, from_y = 2 * part + x, 2 * part + 1 - x, 2 * part + x
            if part < 2:
                mail.send(xzone_ref.at[kind, part], to.at[m, from_x], sem.at[m, from_x], right_y)
            else:
                mail.send(yzone_ref.at[kind, part], to.at[m_y, from_y], sem.at[m_y, from_y], right_x)
            for ref, column, e in ((zone_ref, m, own), (xzone_ref, m, from_x), (yzone_ref, m_y, from_y)):
                mail.send(ref.at[kind, part], to.at[column, e], sem.at[column, e], partner)
                copy = pltpu.make_async_copy(
                    ref.at[kind, part], to.at[column, e], local_sem.at[len(kept)]
                )
                copy.start()
                kept.append(copy)
    for kind in range(2):
        to = outs[kind]
        sem = land_sem.at[kind]
        for part in range(4):
            e = 2 * part + 1 - x
            arrived(to.at[m_y, e], sem.at[m_y, e])
            mail.send(to.at[m_y, e], to.at[m_y, e], sem.at[m_y, e], partner)
    for kind in range(2):
        to = outs[kind]
        sem = land_sem.at[kind]
        for step in range(2):
            other = 2 * step + 1 - c
            for e in range(8):
                arrived(to.at[other, e], sem.at[other, e])
    for copy in kept:
        copy.wait()
    mail.finish()


def fill(zone, xzone, yzone):
    share, width = zone.shape[2:]
    hbm = pl.BlockSpec(memory_space=pl.ANY)
    vmem = pl.BlockSpec(memory_space=pltpu.VMEM)
    return pl.pallas_call(
        fill_kernel,
        in_specs=[hbm] * 3,
        out_specs=[vmem] * 2,
        out_shape=[jax.ShapeDtypeStruct((4, 8, share, width), BF)] * 2,
        scratch_shapes=[
            pltpu.SemaphoreType.DMA((2, 4, 8)),
            pltpu.SemaphoreType.DMA((48,)),
            pltpu.SemaphoreType.DMA((24,)),
        ],
        compiler_params=pltpu.CompilerParams(
            vmem_limit_bytes=VMEM_LIMIT, collective_id=1, has_side_effects=True
        ),
        name="fill",
    )(zone, xzone, yzone)


def leave_kernel(
    owner_ref, att_ref, up_ref, down_ref, small_ref,
    grad_ref, total_ref,
    part_ref, near_ref, fromx_ref, fromy_ref, diagx_ref, diagy_ref, zone_ref, done_ref, pack_ref,
    side_ref, sums_ref,
    near_sem, x_sem, y_sem, dx_sem, dy_sem, z_sem, grad_sem, side_sem, send_sem, local_sem,
):
    z, x, y, c = place()
    m = 2 * y + c
    d = 2 * z + x
    n_dp = grad_ref.shape[0]
    right_x, right_y, partner = at(z, 1 - x, y, c), at(z, x, 1 - y, c), at(z, x, y, 1 - c)
    dp_peers = [((d + off) % n_dp, m) for off in range(1, n_dp)]
    greet(dp_peers + [right_y, partner])
    mail = Mail(send_sem)
    sources = (att_ref, up_ref, down_ref)
    loads = []
    for kind in range(3):
        for step in range(2):
            mail.send(
                sources[kind].at[2 * step + 1 - c],
                near_ref.at[kind, step],
                near_sem.at[kind, step],
                partner,
            )
            load = pltpu.make_async_copy(
                sources[kind].at[2 * step + c], part_ref.at[kind, step], local_sem.at[len(loads)]
            )
            load.start()
            loads.append(load)
    sums_ref[0] = small_ref[...]
    for hop, peer in enumerate((partner, right_x, right_y)):
        mail.send(sums_ref.at[hop], side_ref.at[hop], side_sem.at[hop], peer)
        arrived(side_ref.at[hop], side_sem.at[hop])
        sums_ref[hop + 1] = sums_ref[hop] + side_ref[hop]
    for off in range(1, 4):
        mail.send(
            sums_ref.at[3], side_ref.at[3 + z], side_sem.at[3 + z], at((z + off) % 4, x, y, c)
        )
    side_ref[3 + z] = sums_ref[3]

    def add(a, b):
        return (a.astype(F32) + b.astype(F32)).astype(BF)

    for kind in range(3):
        for step in range(2):
            loads[2 * kind + step].wait()
            arrived(near_ref.at[kind, step], near_sem.at[kind, step])

            def summed(e, carry):
                part_ref[kind, step, e] = add(part_ref[kind, step, e], near_ref[kind, step, e])
                return carry

            lax.fori_loop(0, n_dp, summed, 0)
        for part in range(2):
            mail.send(
                part_ref.at[kind, 1 - y, 2 * part + 1 - x], diagy_ref.at[kind, part],
                dy_sem.at[kind, part], right_y,
            )
            mail.send(
                part_ref.at[kind, 1 - y, 2 * (2 + part) + 1 - x], diagx_ref.at[kind, part],
                dx_sem.at[kind, part], right_x,
            )
            mail.send(
                part_ref.at[kind, y, 2 * (2 + part) + 1 - x], fromx_ref.at[kind, 2 + part],
                x_sem.at[kind, 2 + part], right_x,
            )
            mail.send(
                part_ref.at[kind, 1 - y, 2 * part + x], fromy_ref.at[kind, part],
                y_sem.at[kind, part], right_y,
            )
    for kind in range(3):
        for part in range(2):
            arrived(diagy_ref.at[kind, part], dy_sem.at[kind, part])
            e = 2 * part + 1 - x
            part_ref[kind, y, e] = add(part_ref[kind, y, e], diagy_ref[kind, part])
            mail.send(
                part_ref.at[kind, y, e], fromx_ref.at[kind, part], x_sem.at[kind, part], right_x
            )
            arrived(diagx_ref.at[kind, part], dx_sem.at[kind, part])
            f = 2 * (2 + part) + x
            part_ref[kind, 1 - y, f] = add(part_ref[kind, 1 - y, f], diagx_ref[kind, part])
            mail.send(
                part_ref.at[kind, 1 - y, f], fromy_ref.at[kind, 2 + part],
                y_sem.at[kind, 2 + part], right_y,
            )
    for kind in range(3):
        for part in (2, 3, 0, 1):
            arrived(fromx_ref.at[kind, part], x_sem.at[kind, part])
            arrived(fromy_ref.at[kind, part], y_sem.at[kind, part])
        for off in (1, 2, 3, 0):
            to = (z + off) % 4
            e = 2 * to + x
            part_ref[kind, y, e] = (
                part_ref[kind, y, e].astype(F32)
                + fromx_ref[kind, to].astype(F32)
                + fromy_ref[kind, to].astype(F32)
            ).astype(BF)
            if off:
                mail.send(
                    part_ref.at[kind, y, e], zone_ref.at[kind, z], z_sem.at[kind, z],
                    at(to, x, y, c),
                )
    for kind in range(3):
        total = part_ref[kind, y, d].astype(F32)
        for off in range(1, 4):
            e = (z + off) % 4
            arrived(zone_ref.at[kind, e], z_sem.at[kind, e])
            total = total + zone_ref[kind, e].astype(F32)
        done_ref[kind] = total.astype(BF)
    for off in (3, 4, 5, 2, 6, 1, 7):
        e = (d + off) % n_dp
        kind = jnp.where(owner_ref[m, 1] == e, 1, jnp.where(owner_ref[m, 2] == e, 2, 0))
        pack_ref[e] = done_ref[kind]
        mail.send(pack_ref.at[e], grad_ref.at[d], grad_sem.at[d], (e, m))
    kind = jnp.where(owner_ref[m, 1] == d, 1, jnp.where(owner_ref[m, 2] == d, 2, 0))
    grad_ref[d] = done_ref[kind]
    for off in range(1, 4):
        e = (z + off) % 4
        arrived(side_ref.at[3 + e], side_sem.at[3 + e])
    total_ref[...] = (side_ref[3] + side_ref[4]) + (side_ref[5] + side_ref[6])
    for off in range(1, n_dp):
        e = (d + off) % n_dp
        arrived(grad_ref.at[e], grad_sem.at[e])
    mail.finish()


def leave(owner, att, up, down, small):
    n_mlp, n_dp, share, width = att.shape
    smem = pl.BlockSpec(memory_space=pltpu.SMEM)
    vmem = pl.BlockSpec(memory_space=pltpu.VMEM)
    hbm = pl.BlockSpec(memory_space=pl.ANY)
    dma = pltpu.SemaphoreType.DMA
    return pl.pallas_call(
        leave_kernel,
        in_specs=[smem, hbm, hbm, hbm, vmem],
        out_specs=[vmem, vmem],
        out_shape=[
            jax.ShapeDtypeStruct((n_dp, share, width), BF),
            jax.ShapeDtypeStruct(small.shape, F32),
        ],
        scratch_shapes=[
            pltpu.VMEM((3, 2, n_dp, share, width), BF),
            pltpu.VMEM((3, 2, n_dp, share, width), BF),
            pltpu.VMEM((3, 4, share, width), BF),
            pltpu.VMEM((3, 4, share, width), BF),
            pltpu.VMEM((3, 2, share, width), BF),
            pltpu.VMEM((3, 2, share, width), BF),
            pltpu.VMEM((3, 4, share, width), BF),
            pltpu.VMEM((3, share, width), BF),
            pltpu.VMEM((n_dp, share, width), BF),
            pltpu.VMEM((7,) + small.shape, F32),
            pltpu.VMEM((4,) + small.shape, F32),
            dma((3, 2)), dma((3, 4)), dma((3, 4)), dma((3, 2)), dma((3, 2)), dma((3, 4)),
            dma((n_dp,)), dma((7,)), dma((64,)), dma((6,)),
        ],
        compiler_params=pltpu.CompilerParams(
            vmem_limit_bytes=VMEM_LIMIT, collective_id=2, has_side_effects=True
        ),
        name="leave",
    )(owner, att, up, down, small)


def project_kernel(
    x_ref, pos_ref, vec_ref, turned_ref, weight_ref,
    n1_ref, q_ref, k_ref, v_ref, cos_ref, sin_ref, qmark_ref, kmark_ref,
):
    unit, _ = normed(x_ref[...].astype(F32))
    n1 = (unit * vec_ref[0:1, :] + vec_ref[1:2, :]).astype(BF)
    n1t = n1.T
    n1_ref[...] = n1t
    px = pos_ref[0:1, :]
    py = pos_ref[1:2, :]
    half = cos_ref.shape[0]
    last = turned_ref.shape[1] - 1
    angle = turned_ref[half:, last:] * py + turned_ref[:half, last:] * px
    cosine = jnp.cos(angle)
    sine = jnp.sin(angle)
    cos_ref[...] = cosine
    sin_ref[...] = sine
    seg = pos_ref[2:3, :].astype(jnp.int32)
    row = lax.broadcasted_iota(jnp.int32, qmark_ref.shape, 0)
    qmark_ref[...] = jnp.where(row == seg, 1.0, 0.0).astype(BF)
    kmark_ref[...] = jnp.where(row == seg, 0.0, MASK_SHIFT).astype(BF)
    part = half // HEADS
    for index, (out, scale) in enumerate(((q_ref, 0.125), (k_ref, 1.0))):
        flat = dot(weight_ref[index], n1t, 0, 0) + turned_ref[:, 2 + index : 3 + index]
        for head in range(HEADS):
            low, mid = 2 * part * head, 2 * part * head + part
            a = flat[low:mid]
            b = flat[mid : mid + part]
            c = cosine[part * head : part * (head + 1)]
            s = sine[part * head : part * (head + 1)]
            out[low:mid, :] = (a * c - b * s).astype(BF) * jnp.asarray(scale, BF)
            out[mid : mid + part, :] = (b * c + a * s).astype(BF) * jnp.asarray(scale, BF)
    v_ref[...] = (dot(weight_ref[2], n1t, 0, 0) + turned_ref[:, 4:5]).astype(BF)


def project(x, pos, vec, turned, weights):
    rows, width = x.shape
    half = width // 2
    whole = lambda a: pl.BlockSpec(a.shape, lambda i: (0,) * a.ndim)
    col = lambda n: pl.BlockSpec((n, TILE), lambda i: (0, i))
    out = lambda n, d: jax.ShapeDtypeStruct((n, rows), d)
    return pl.pallas_call(
        project_kernel,
        grid=(rows // TILE,),
        in_specs=[
            pl.BlockSpec((TILE, width), lambda i: (i, 0)),
            col(8),
            whole(vec),
            whole(turned),
            whole(weights),
        ],
        out_specs=[col(width)] * 4 + [col(half)] * 2 + [col(16)] * 2,
        out_shape=[out(width, BF)] * 4 + [out(half, F32)] * 2 + [out(16, BF)] * 2,
        compiler_params=pltpu.CompilerParams(vmem_limit_bytes=VMEM_LIMIT),
        name="project",
    )(x, pos, vec, turned, weights)


def key_window(height_ref, width_ref, block):
    first = block * BLOCK
    last = first + BLOCK - 1
    start = jnp.int32(0)
    low = jnp.int32(0)
    high = jnp.int32(0)
    for image in range(height_ref.shape[0]):
        end = start + height_ref[image] * width_ref[image]
        low = jnp.where((start <= first) & (first < end), start, low)
        high = jnp.where((start <= last) & (last < end), end, high)
        start = end
    base = low // BLOCK
    return base, (high + BLOCK - 1) // BLOCK - base


def attend_kernel(height_ref, width_ref, q_ref, k_ref, v_ref, qmark_ref, kmark_ref, o_ref, log_ref):
    tokens = q_ref.shape[1]
    blocks = tokens // BLOCK
    size = q_ref.shape[0] // HEADS
    group = 4

    def one(block, part, base, count):
        here = pl.ds(pl.multiple_of(block * BLOCK, BLOCK), BLOCK)
        keys = pl.ds(pl.multiple_of(base * BLOCK, BLOCK), BLOCK * count)
        qmark = qmark_ref[:, here]
        kmark = kmark_ref[:, keys]
        for j in range(group):
            head = part * group + j
            rows = pl.ds(pl.multiple_of(head * size, size), size)
            q = jnp.concatenate([q_ref[rows, here], qmark], axis=0)
            k = jnp.concatenate([k_ref[rows, keys], kmark], axis=0)
            scores = dot(k, q, 0, 0)
            peak = jnp.max(scores, axis=0, keepdims=True)
            powers = jnp.exp(scores - peak)
            total = jnp.sum(powers, axis=0, keepdims=True)
            mixed = dot(v_ref[rows, keys], powers.astype(BF), 1, 0)
            o_ref[rows, here] = (mixed * (1.0 / total)).astype(BF)
            log_ref[pl.ds(pl.multiple_of(head * 8, 8), 8), here] = jnp.broadcast_to(
                peak + jnp.log(total), (8, BLOCK)
            )

    def step(block, carry):
        base, count = key_window(height_ref, width_ref, block)
        for n in range(1, blocks + 1):

            @pl.when(count == n)
            def _():
                def inner(part, c):
                    one(block, part, base, n)
                    return c

                lax.fori_loop(0, HEADS // group, inner, 0)

        return carry

    lax.fori_loop(0, blocks, step, 0)


def attend(heights, widths, q, k, v, qmark, kmark):
    smem = pl.BlockSpec(memory_space=pltpu.SMEM)
    vmem = pl.BlockSpec(memory_space=pltpu.VMEM)
    return pl.pallas_call(
        attend_kernel,
        in_specs=[smem, smem] + [vmem] * 5,
        out_specs=[vmem, vmem],
        out_shape=[
            jax.ShapeDtypeStruct(q.shape, BF),
            jax.ShapeDtypeStruct((8 * HEADS, q.shape[1]), F32),
        ],
        compiler_params=pltpu.CompilerParams(vmem_limit_bytes=VMEM_LIMIT),
        name="attend",
    )(heights, widths, q, k, v, qmark, kmark)


def attend_back_kernel(
    height_ref, width_ref, q_ref, k_ref, v_ref, qmark_ref, kmark_ref, log_ref, do_ref,
    pos_ref, cos_ref, sin_ref,
    dq_ref, dk_ref, dv_ref, freq_ref, bias_ref,
    gq_ref, gk_ref, gv_ref, turn_ref,
):
    tokens = q_ref.shape[1]
    blocks = tokens // BLOCK
    size = q_ref.shape[0] // HEADS
    half = size // 2
    group = 2
    gk_ref[...] = jnp.zeros_like(gk_ref)
    gv_ref[...] = jnp.zeros_like(gv_ref)

    def one(block, part, base, count):
        here = pl.ds(pl.multiple_of(block * BLOCK, BLOCK), BLOCK)
        keys = pl.ds(pl.multiple_of(base * BLOCK, BLOCK), BLOCK * count)
        qmark = qmark_ref[:, here]
        kmark = kmark_ref[:, keys]
        for j in range(group):
            head = part * group + j
            rows = pl.ds(pl.multiple_of(head * size, size), size)
            q = q_ref[rows, here]
            k = k_ref[rows, keys]
            do = do_ref[rows, here]
            scores = dot(
                jnp.concatenate([k, kmark], axis=0), jnp.concatenate([q, qmark], axis=0), 0, 0
            )
            log_row = log_ref[pl.ds(pl.multiple_of(head * 8, 8), 8), here][0:1]
            probs = jnp.exp(scores - log_row)
            dp = dot(v_ref[rows, keys], do, 0, 0)
            inner = jnp.sum(probs * dp, axis=0, keepdims=True)
            ds = (probs * (dp - inner)).astype(BF)
            gq_ref[rows, here] = dot(k, ds, 1, 0) * 0.125
            gk_ref[rows, keys] += dot(q, ds, 1, 1)
            gv_ref[rows, keys] += dot(do, probs.astype(BF), 1, 1)

    def step(block, carry):
        base, count = key_window(height_ref, width_ref, block)
        for n in range(1, blocks + 1):

            @pl.when(count == n)
            def _():
                def inner(part, c):
                    one(block, part, base, n)
                    return c

                lax.fori_loop(0, HEADS // group, inner, 0)

        return carry

    lax.fori_loop(0, blocks, step, 0)

    def unturn(head, carry):
        low = pl.ds(pl.multiple_of(head * size, size), half)
        high = pl.ds(pl.multiple_of(head * size + half, half), half)
        table = pl.ds(pl.multiple_of(head * half, half), half)
        c = cos_ref[table, :]
        s = sin_ref[table, :]
        turn = None
        for grad_ref, rot_ref, scale, out_ref in (
            (gq_ref, q_ref, 8.0, dq_ref),
            (gk_ref, k_ref, 1.0, dk_ref),
        ):
            ga = grad_ref[low, :]
            gb = grad_ref[high, :]
            out_ref[low, :] = (ga * c + gb * s).astype(BF)
            out_ref[high, :] = (gb * c - ga * s).astype(BF)
            ra = rot_ref[low, :].astype(F32) * scale
            rb = rot_ref[high, :].astype(F32) * scale
            piece = gb * ra - ga * rb
            turn = piece if turn is None else turn + piece
        turn_ref[table, :] = turn
        both = pl.ds(pl.multiple_of(head * size, size), size)
        dv_ref[both, :] = gv_ref[both, :].astype(BF)
        return carry

    lax.fori_loop(0, HEADS, unturn, 0)
    freq_ref[...] = dot(pos_ref[...], turn_ref[...], 1, 1, lax.Precision.HIGHEST)
    ones = jnp.ones((8, tokens), BF)
    for index, ref in enumerate((dq_ref, dk_ref, dv_ref)):
        bias_ref[8 * index : 8 * index + 8, :] = dot(ones, ref[...], 1, 1)


def attend_back(heights, widths, q, k, v, qmark, kmark, log_totals, do, pos, cosine, sine):
    smem = pl.BlockSpec(memory_space=pltpu.SMEM)
    vmem = pl.BlockSpec(memory_space=pltpu.VMEM)
    width, tokens = q.shape
    return pl.pallas_call(
        attend_back_kernel,
        in_specs=[smem, smem] + [vmem] * 10,
        out_specs=[vmem] * 5,
        out_shape=[jax.ShapeDtypeStruct(q.shape, BF)] * 3
        + [
            jax.ShapeDtypeStruct((8, width // 2), F32),
            jax.ShapeDtypeStruct((24, width), F32),
        ],
        scratch_shapes=[pltpu.VMEM(q.shape, F32)] * 3 + [pltpu.VMEM((width // 2, tokens), F32)],
        compiler_params=pltpu.CompilerParams(vmem_limit_bytes=VMEM_LIMIT),
        name="attend_back",
    )(heights, widths, q, k, v, qmark, kmark, log_totals, do, pos, cosine, sine)


def middle_kernel(
    x_ref, g_ref, o_ref, vec_ref, wo_ref, up_ref, down_ref,
    y_ref, dh_ref, do_ref, dwo_ref, dup_ref, ddown_ref, rows_ref, dc_ref,
    h_ref, n2_ref, n2t_ref, acc_ref, dn_ref, a_ref, dz_ref, dr_ref,
):
    groups = vec_ref.shape[0] - 10
    step = pl.program_id(0)
    tokens, width = x_ref.shape
    tiles = tokens // TILE

    def tile(i):
        return pl.ds(pl.multiple_of(i * TILE, TILE), TILE)

    @pl.when(step == 0)
    def _():
        def first(i, c):
            t = tile(i)
            branch = dot(o_ref[:, t], wo_ref[...], 0, 0) + vec_ref[5:6, :]
            h = x_ref[t, :].astype(F32) + branch
            h_ref[t, :] = h
            unit, _ = normed(h)
            n2 = (unit * vec_ref[6:7, :] + vec_ref[7:8, :]).astype(BF)
            n2_ref[t, :] = n2
            n2t_ref[:, t] = n2.T
            acc_ref[t, :] = h + vec_ref[8 + groups : 9 + groups, :]
            dn_ref[t, :] = jnp.zeros((TILE, width), F32)
            return c

        lax.fori_loop(0, tiles, first, 0)

    up_bias = vec_ref[pl.ds(8 + step, 1), :]

    def second(i, c):
        t = tile(i)
        z = dot(n2_ref[t, :], up_ref[0], 1, 0) + up_bias
        cdf = 0.5 * (1.0 + lax.erf(z * math.sqrt(0.5)))
        a = (z * cdf).astype(BF)
        a_ref[t, :] = a
        acc_ref[t, :] += dot(a, down_ref[0], 1, 0)
        da = dot(g_ref[t, :], down_ref[0], 1, 1)
        slope = cdf + z * (jnp.exp(-0.5 * z * z) * (1.0 / math.sqrt(2.0 * math.pi)))
        dz = (da * slope).astype(BF)
        dz_ref[t, :] = dz
        dn_ref[t, :] += dot(dz, up_ref[0], 1, 1)
        return c

    lax.fori_loop(0, tiles, second, 0)
    dc_ref[0] = dot(jnp.ones((8, tokens), BF), dz_ref[...], 1, 0)
    dup_ref[0] = dot(n2t_ref[...], dz_ref[...], 1, 0).astype(BF)
    ddown_ref[0] = dot(a_ref[...], g_ref[...], 0, 0).astype(BF)

    @pl.when(step == groups - 1)
    def _():
        rows_ref[...] = jnp.zeros_like(rows_ref)

        def third(i, c):
            t = tile(i)
            y_ref[t, :] = acc_ref[t, :].astype(BF)
            g = g_ref[t, :].astype(F32)
            unit, scale = normed(h_ref[t, :])
            dn = dn_ref[t, :]
            dh = g + norm_back(dn, unit, scale, vec_ref[6:7, :])
            dh_ref[t, :] = dh
            dr = dh.astype(BF)
            dr_ref[t, :] = dr
            do_ref[:, t] = dot(wo_ref[...], dr, 1, 1).astype(BF)
            rows_ref[0:8, :] += fold_rows(dr.astype(F32))
            rows_ref[8:16, :] += fold_rows(dn * unit)
            rows_ref[16:24, :] += fold_rows(dn)
            rows_ref[24:32, :] += fold_rows(g)
            return c

        lax.fori_loop(0, tiles, third, 0)
        dwo_ref[...] = dot(o_ref[...], dr_ref[...], 1, 0).astype(BF)


def middle_part(x, g, o, vec, wo, up, down):
    tokens, width = x.shape
    groups = up.shape[0]
    whole = lambda s: pl.BlockSpec(s, lambda i: (0,) * len(s))
    block = pl.BlockSpec((1, width, width), lambda i: (i, 0, 0))
    return pl.pallas_call(
        middle_kernel,
        grid=(groups,),
        in_specs=[
            whole(x.shape),
            whole(g.shape),
            whole(o.shape),
            whole(vec.shape),
            whole(wo.shape),
            block,
            block,
        ],
        out_specs=[
            whole((tokens, width)),
            whole((tokens, width)),
            whole((width, tokens)),
            whole((width, width)),
            block,
            block,
            whole((32, width)),
            pl.BlockSpec((1, 8, width), lambda i: (i, 0, 0)),
        ],
        out_shape=[
            jax.ShapeDtypeStruct((tokens, width), BF),
            jax.ShapeDtypeStruct((tokens, width), F32),
            jax.ShapeDtypeStruct((width, tokens), BF),
            jax.ShapeDtypeStruct((width, width), BF),
            jax.ShapeDtypeStruct((groups, width, width), BF),
            jax.ShapeDtypeStruct((groups, width, width), BF),
            jax.ShapeDtypeStruct((32, width), F32),
            jax.ShapeDtypeStruct((groups, 8, width), F32),
        ],
        scratch_shapes=[
            pltpu.VMEM((tokens, width), F32),
            pltpu.VMEM((tokens, width), BF),
            pltpu.VMEM((width, tokens), BF),
            pltpu.VMEM((tokens, width), F32),
            pltpu.VMEM((tokens, width), F32),
            pltpu.VMEM((tokens, width), BF),
            pltpu.VMEM((tokens, width), BF),
            pltpu.VMEM((tokens, width), BF),
        ],
        compiler_params=pltpu.CompilerParams(vmem_limit_bytes=VMEM_LIMIT),
        name="middle",
    )(x, g, o, vec, wo, up, down)


def final_kernel(
    x_ref, dh_ref, n1_ref, dq_ref, dk_ref, dv_ref, vec_ref, weight_ref, dwo_ref,
    dx_ref, dw_ref, rows_ref,
):
    tokens, width = x_ref.shape
    dw_ref[3] = dwo_ref[...]
    for index, ref in enumerate((dq_ref, dk_ref, dv_ref)):
        dw_ref[index] = dot(n1_ref[...], ref[...], 1, 1).astype(BF)
    rows_ref[...] = jnp.zeros_like(rows_ref)

    def loop(i, c):
        t = pl.ds(pl.multiple_of(i * TILE, TILE), TILE)
        dn = dot(dq_ref[:, t], weight_ref[0], 0, 1)
        dn += dot(dk_ref[:, t], weight_ref[1], 0, 1)
        dn += dot(dv_ref[:, t], weight_ref[2], 0, 1)
        unit, scale = normed(x_ref[t, :].astype(F32))
        dx_ref[t, :] = dh_ref[t, :] + norm_back(dn, unit, scale, vec_ref[0:1, :])
        rows_ref[0:8, :] += fold_rows(dn * unit)
        rows_ref[8:16, :] += fold_rows(dn)
        return c

    lax.fori_loop(0, tokens // TILE, loop, 0)


def final_part(x, dh, n1, dq, dk, dv, vec, weights, dwo):
    tokens, width = x.shape
    vmem = pl.BlockSpec(memory_space=pltpu.VMEM)
    return pl.pallas_call(
        final_kernel,
        in_specs=[vmem] * 9,
        out_specs=[vmem] * 3,
        out_shape=[
            jax.ShapeDtypeStruct((tokens, width), F32),
            jax.ShapeDtypeStruct((4, width, width), BF),
            jax.ShapeDtypeStruct((16, width), F32),
        ],
        compiler_params=pltpu.CompilerParams(vmem_limit_bytes=VMEM_LIMIT),
        name="final",
    )(x, dh, n1, dq, dk, dv, vec, weights, dwo)


def halves(values):
    high = values.astype(BF)
    return high, (values - high.astype(F32)).astype(BF)


def dot_fine(left, right):
    left_high, left_low = halves(left)
    right_high, right_low = halves(right)
    return (
        dot(left_high, right_low, 1, 0)
        + dot(left_low, right_high, 1, 0)
        + dot(left_high, right_high, 1, 0)
    )


def update_kernel(
    keep_ref, decay_ref, grad_ref, left_ref, right_ref, lroot_ref, rroot_ref, master_ref,
    slot_ref, newleft_ref, newright_ref, newmaster_ref,
):
    @pl.when(keep_ref[0] == 0)
    def _():
        slot_ref[...] = jnp.zeros_like(slot_ref)
        newleft_ref[...] = left_ref[...]
        newright_ref[...] = right_ref[...]
        newmaster_ref[...] = master_ref[...]

    @pl.when(keep_ref[0] != 0)
    def _():
        decay = decay_ref[0]
        grad = grad_ref[...].astype(F32)
        slot_ref[...] = grad
        low = grad.astype(BF)
        newleft_ref[...] = decay * left_ref[...] + (1.0 - decay) * dot(low, low, 1, 1)
        newright_ref[...] = decay * right_ref[...] + (1.0 - decay) * dot(low, low, 0, 0)
        inner = dot_fine(lroot_ref[...], grad)
        direction = dot_fine(inner, rroot_ref[...])
        size = direction.shape[0] * direction.shape[1]
        mean = jnp.sum(direction * direction, keepdims=True) * (1.0 / size)
        newmaster_ref[...] = master_ref[...] - RATE_MATRIX * direction * lax.rsqrt(
            mean + GRAFT_EPSILON
        )


def update(owns, decays, grad, left, right, lroot, rroot, master):
    smem = pl.BlockSpec(memory_space=pltpu.SMEM)
    vmem = pl.BlockSpec(memory_space=pltpu.VMEM)
    return pl.pallas_call(
        update_kernel,
        in_specs=[smem, smem] + [vmem] * 6,
        out_specs=[vmem] * 4,
        out_shape=[jax.ShapeDtypeStruct(left.shape, F32)] * 4,
        compiler_params=pltpu.CompilerParams(vmem_limit_bytes=VMEM_LIMIT),
        name="update",
    )(owns, decays, grad, left, right, lroot, rroot, master)


def positions(segment, heights, widths, patch_rows, patch_cols):
    images = heights.shape[0]
    matches = segment[None, :] == jnp.arange(images, dtype=jnp.int32)[:, None]
    tall = jnp.sum(jnp.where(matches, heights[:, None], 0), axis=0).astype(F32)
    wide = jnp.sum(jnp.where(matches, widths[:, None], 0), axis=0).astype(F32)
    py = patch_rows.astype(F32) * GRID_BASE / tall
    px = patch_cols.astype(F32) * GRID_BASE / wide
    zero = jnp.zeros_like(px)
    return jnp.stack([px, py, segment.astype(F32), zero, zero, zero, zero, zero])


def local(
    tokens, cotangent, vectors, vector_moments, decays, owner, master_slots, left_slots,
    right_slots, left_roots, right_roots, grid_height, grid_width, patch_rows, patch_cols, segment,
):
    dp_index = lax.axis_index("dp")
    mlp_index = lax.axis_index("mlp")
    n_dp = lax.axis_size("dp")
    n_mlp = lax.axis_size("mlp")
    width = tokens.shape[1]
    share = width // n_dp
    owner_row = jnp.take(owner, mlp_index, axis=0)
    holds = owner_row == dp_index
    owns = jnp.any(holds).astype(jnp.int32).reshape(1)
    master = master_slots[0, 0]
    slot = master.astype(BF).reshape(n_dp, share, width)
    turned = vectors.T
    pos = positions(segment, grid_height, grid_width, patch_rows, patch_cols)
    direct = n_dp == 8 and n_mlp == 4
    if direct:
        n1t, q, k, v, cosine, sine, qmark, kmark, attention, zone = enter(
            owner, slot, tokens, pos, vectors, turned
        )
        attention = attention.reshape(n_mlp, width, width)
        xzone = lax.ppermute(zone, "dp", [(i, i ^ 1) for i in range(n_dp)])
        yzone = lax.ppermute(zone, "mlp", [(i, i ^ 2) for i in range(n_mlp)])
    else:
        pieces = lax.all_to_all(slot, "dp", 0, 0, tiled=True)
        mine = jnp.take(pieces, owner_row, axis=0)
        every = lax.all_gather(mine[None], ("dp", "mlp"), axis=0, tiled=True)
        blocks = every.reshape(n_dp, n_mlp, 3, share, width).transpose(2, 1, 0, 3, 4)
        attention, up, down = blocks.reshape(3, n_mlp, width, width)
        n1t, q, k, v, cosine, sine, qmark, kmark = project(tokens, pos, vectors, turned, attention)
    o, log_totals = attend(grid_height, grid_width, q, k, v, qmark, kmark)
    if direct:
        up, down = (w.reshape(n_mlp, width, width) for w in fill(zone, xzone, yzone))
    output, dh, do, dwo, dup, ddown, mid_rows, dc = middle_part(
        tokens, cotangent, o, vectors, attention[3], up, down
    )
    dq, dk, dv, freq, bias = attend_back(
        grid_height, grid_width, q, k, v, qmark, kmark, log_totals, do, pos, cosine, sine
    )
    input_grad, datt, fin_rows = final_part(
        tokens, dh, n1t, dq, dk, dv, vectors, attention, dwo
    )
    eights = lambda rows: jnp.sum(rows.reshape(-1, 8, width), axis=1)
    fin = eights(fin_rows)
    mid = eights(mid_rows)
    small = jnp.concatenate(
        [fin, bias[0::8], mid[0:3], dc[:, 0, :], mid[3:4], freq[0:2].reshape(1, width)],
        axis=0,
    )
    if direct:
        fine = (n_mlp, n_dp, share, width)
        gradient, total = leave(
            owner, datt.reshape(fine), dup.reshape(fine), ddown.reshape(fine), small
        )
    else:
        grads = jnp.stack([datt, dup, ddown], axis=1)
        grads = grads.reshape(n_mlp, 3, n_dp, share, width).transpose(2, 0, 1, 3, 4)
        grads = grads.reshape(n_dp * n_mlp * 3, share, width)
        reduced = lax.psum_scatter(grads, ("dp", "mlp"), scatter_dimension=0, tiled=True)
        takers = owner_row[None, :] == jnp.arange(n_dp, dtype=jnp.int32)[:, None]
        kind_of = jnp.sum(jnp.where(takers, jnp.arange(3, dtype=jnp.int32)[None, :], 0), axis=1)
        gradient = lax.all_to_all(jnp.take(reduced, kind_of, axis=0), "dp", 0, 0, tiled=True)
        total = lax.psum(small, ("dp", "mlp"))
    gradient = gradient.reshape(width, width)
    slot_grad, left_out, right_out, master_out = update(
        owns, decays, gradient, left_slots[0, 0], right_slots[0, 0], left_roots[0, 0],
        right_roots[0, 0], master,
    )

    cut = width // n_mlp
    own = lambda table: lax.dynamic_slice_in_dim(table, mlp_index * cut, cut, 1)
    grad_share = own(total)
    decay = decays[1]
    moment_next = decay * own(vector_moments) + (1.0 - decay) * grad_share * grad_share
    vector_next = own(vectors) - RATE_VECTOR * grad_share / (jnp.sqrt(moment_next) + STEP_EPSILON)
    lift = lambda a: a[None, None]
    return (
        output, input_grad, lift(slot_grad), lift(left_out), lift(right_out), lift(master_out),
        grad_share, moment_next, vector_next,
    )


def solution(mesh):
    both = P(("dp", "mlp"))
    flat = P(("dp", "mlp"), None)
    slots = P("dp", "mlp", None, None)
    split = P(None, "mlp")
    return jax.shard_map(
        local,
        mesh=mesh,
        in_specs=(flat, flat, P(), P(), P(), P(), slots, slots, slots, slots, slots)
        + (both,) * 5,
        out_specs=(flat, flat, slots, slots, slots, slots, split, split, split),
        check_vma=False,
    )
```

```python
import functools
import math

import jax
import jax.numpy as jnp
from jax import lax
from jax.experimental import pallas as pl
from jax.experimental.pallas import tpu as pltpu
from jax.sharding import PartitionSpec as P

HEADS = 12
GRID_BASE = 16
NORM_EPSILON = 1e-06
GRAFT_EPSILON = 1e-06
STEP_EPSILON = 1e-08
RATE_MATRIX = 0.04
RATE_VECTOR = 0.02
MASK_SHIFT = -(2.0**100)
BLOCK = 128
TILE = 256
PARTS = 2
F32 = jnp.float32
BF = jnp.bfloat16
VMEM_LIMIT = 60 * 1024 * 1024


def dot(left, right, left_dim, right_dim, precision=None):
    return lax.dot_general(
        left,
        right,
        (((left_dim,), (right_dim,)), ((), ())),
        preferred_element_type=F32,
        precision=precision,
    )


def normed(values):
    mean = jnp.mean(values, axis=-1, keepdims=True)
    centred = values - mean
    spread = jnp.mean(centred * centred, axis=-1, keepdims=True)
    scale = lax.rsqrt(spread + NORM_EPSILON)
    return centred * scale, scale


def norm_back(grad, unit, scale, gain):
    scaled = grad * gain
    first = jnp.mean(scaled, axis=-1, keepdims=True)
    second = jnp.mean(scaled * unit, axis=-1, keepdims=True)
    return scale * (scaled - first - unit * second)


def fold_rows(values):
    return jnp.sum(values.reshape(values.shape[0] // 8, 8, values.shape[1]), axis=0)


def place():
    d = lax.axis_index("dp")
    m = lax.axis_index("mlp")
    return d // 2, d % 2, m // 2, m % 2


def at(z, x, y, c):
    return (2 * z + x, 2 * y + c)


def greet(peers):
    barrier = pltpu.get_barrier_semaphore()
    for peer in peers:
        pl.semaphore_signal(barrier, inc=1, device_id=peer, device_id_type=pl.DeviceIdType.MESH)
    pl.semaphore_wait(barrier, len(peers))


class Mail:
    def __init__(self, sems):
        self.sems = sems
        self.like = []

    def send(self, source, target, arrival, peer, like):
        slot = len(self.like)
        pltpu.make_async_remote_copy(
            src_ref=source,
            dst_ref=target,
            send_sem=self.sems.at[slot],
            recv_sem=arrival,
            device_id=peer,
            device_id_type=pl.DeviceIdType.MESH,
        ).start()
        self.like.append(like)
        return slot

    def settle(self, slot):
        arrived(self.like[slot], self.sems.at[slot])
        self.like[slot] = None

    def finish(self):
        for slot, like in enumerate(self.like):
            if like is not None:
                self.settle(slot)


def arrived(target, arrival):
    pltpu.make_async_copy(target, target, arrival).wait()


def enter_kernel(
    owner_ref, slot_ref, x_ref, pos_ref, vec_ref, turned_ref,
    n1_ref, q_ref, k_ref, v_ref, cos_ref, sin_ref, qmark_ref, kmark_ref, weight_ref, zone_ref,
    land_ref, mine_ref, att_ref, zland_ref,
    land_sem, zone_sem, att_sem, send_sem, local_sem,
):
    z, x, y, c = place()
    m = 2 * y + c
    d = 2 * z + x
    n_dp = land_ref.shape[0]
    right_x, right_y, partner = at(z, 1 - x, y, c), at(z, x, 1 - y, c), at(z, x, y, 1 - c)
    dp_peers = [((d + off) % n_dp, m) for off in range(1, n_dp)]
    greet(dp_peers + [right_y, partner])
    mail = Mail(send_sem)
    piece = mine_ref.at[0]
    own = pltpu.make_async_copy(slot_ref.at[d], land_ref.at[d], local_sem.at[0])
    own.start()
    for peer in dp_peers:
        mail.send(slot_ref.at[peer[0]], land_ref.at[d], land_sem.at[d], peer, piece)

    tokens = x_ref.shape[0]
    half = cos_ref.shape[0]
    last = turned_ref.shape[1] - 1
    tiles = tokens // TILE

    def prepare(i, carry):
        t = pl.ds(pl.multiple_of(i * TILE, TILE), TILE)
        unit, _ = normed(x_ref[t, :].astype(F32))
        n1_ref[:, t] = (unit * vec_ref[0:1, :] + vec_ref[1:2, :]).astype(BF).T
        angle = turned_ref[half:, last:] * pos_ref[1:2, t] + turned_ref[:half, last:] * pos_ref[0:1, t]
        cos_ref[:, t] = jnp.cos(angle)
        sin_ref[:, t] = jnp.sin(angle)
        seg = pos_ref[2:3, t].astype(jnp.int32)
        row = lax.broadcasted_iota(jnp.int32, (qmark_ref.shape[0], TILE), 0)
        qmark_ref[:, t] = jnp.where(row == seg, 1.0, 0.0).astype(BF)
        kmark_ref[:, t] = jnp.where(row == seg, 0.0, MASK_SHIFT).astype(BF)
        return carry

    lax.fori_loop(0, tiles, prepare, 0)

    own.wait()
    for off in range(1, n_dp):
        source = (d + off) % n_dp
        arrived(land_ref.at[source], land_sem.at[source])
    for kind in range(3):
        mine_ref[kind] = land_ref[owner_ref[m, kind]]

    def spread_z(source, target, sem):
        for off in range(1, 4):
            mail.send(source, target, sem, at((z + off) % 4, x, y, c), piece)

    spread_z(mine_ref.at[0], att_ref.at[m, d], att_sem.at[m, d])
    for peer in (right_x, right_y, partner):
        mail.send(mine_ref.at[0], att_ref.at[m, d], att_sem.at[m, d], peer, piece)
    keep = pltpu.make_async_copy(mine_ref.at[0], att_ref.at[m, d], local_sem.at[1])
    keep.start()
    for off in (1, 3, 2):
        e = 2 * ((z + off) % 4) + x
        arrived(att_ref.at[m, e], att_sem.at[m, e])
        for peer in (right_x, right_y, partner):
            mail.send(att_ref.at[m, e], att_ref.at[m, e], att_sem.at[m, e], peer, piece)
    keeps = []
    for kind in range(2):
        spread_z(mine_ref.at[1 + kind], zland_ref.at[kind, z], zone_sem.at[kind, z])
        copy = pltpu.make_async_copy(
            mine_ref.at[1 + kind], zland_ref.at[kind, z], local_sem.at[2 + kind]
        )
        copy.start()
        keeps.append(copy)
    m_y = 2 * (1 - y) + c
    for part in range(4):
        e = 2 * part + 1 - x
        arrived(att_ref.at[m, e], att_sem.at[m, e])
        if part < 2:
            mail.send(att_ref.at[m, e], att_ref.at[m, e], att_sem.at[m, e], right_y, piece)
        mail.send(att_ref.at[m, e], att_ref.at[m, e], att_sem.at[m, e], partner, piece)
        f = 2 * part + x
        arrived(att_ref.at[m_y, f], att_sem.at[m_y, f])
        if part >= 2:
            mail.send(att_ref.at[m_y, f], att_ref.at[m_y, f], att_sem.at[m_y, f], right_x, piece)
        mail.send(att_ref.at[m_y, f], att_ref.at[m_y, f], att_sem.at[m_y, f], partner, piece)
    for part in range(4):
        e = 2 * part + 1 - x
        arrived(att_ref.at[m_y, e], att_sem.at[m_y, e])
        mail.send(att_ref.at[m_y, e], att_ref.at[m_y, e], att_sem.at[m_y, e], partner, piece)
    for step in range(2):
        other = 2 * step + 1 - c
        for e in range(n_dp):
            arrived(att_ref.at[other, e], att_sem.at[other, e])
    keep.wait()
    out = pltpu.make_async_copy(att_ref, weight_ref, local_sem.at[4])
    out.start()

    part = half // HEADS
    width = x_ref.shape[1]

    def weight(index):
        return att_ref[index].reshape(width, width)

    def rotate(i, carry):
        t = pl.ds(pl.multiple_of(i * TILE, TILE), TILE)
        n1t = n1_ref[:, t]
        cosine = cos_ref[:, t]
        sine = sin_ref[:, t]
        for index, (ref, scale) in enumerate(((q_ref, 0.125), (k_ref, 1.0))):
            flat = dot(weight(index), n1t, 0, 0) + turned_ref[:, 2 + index : 3 + index]
            for head in range(HEADS):
                low, mid = 2 * part * head, 2 * part * head + part
                a = flat[low:mid]
                b = flat[mid : mid + part]
                cs = cosine[part * head : part * (head + 1)]
                sn = sine[part * head : part * (head + 1)]
                ref[low:mid, t] = (a * cs - b * sn).astype(BF) * jnp.asarray(scale, BF)
                ref[mid : mid + part, t] = (b * cs + a * sn).astype(BF) * jnp.asarray(scale, BF)
        v_ref[:, t] = (dot(weight(2), n1t, 0, 0) + turned_ref[:, 4:5]).astype(BF)
        return carry

    lax.fori_loop(0, tiles, rotate, 0)
    for kind in range(2):
        keeps[kind].wait()
        for off in range(1, 4):
            e = (z + off) % 4
            arrived(zland_ref.at[kind, e], zone_sem.at[kind, e])
    last_out = pltpu.make_async_copy(zland_ref, zone_ref, local_sem.at[5])
    last_out.start()
    out.wait()
    last_out.wait()
    mail.finish()


def enter(owner, slot, x, pos, vec, turned):
    rows, width = x.shape
    half = width // 2
    n_dp, share, _ = slot.shape
    n_mlp = owner.shape[0]
    smem = pl.BlockSpec(memory_space=pltpu.SMEM)
    vmem = pl.BlockSpec(memory_space=pltpu.VMEM)
    hbm = pl.BlockSpec(memory_space=pl.ANY)
    out = lambda n, dtype: jax.ShapeDtypeStruct((n, rows), dtype)
    return pl.pallas_call(
        enter_kernel,
        in_specs=[smem, hbm, vmem, vmem, vmem, vmem],
        out_specs=[vmem] * 8 + [hbm] * 2,
        out_shape=[out(width, BF)] * 4
        + [out(half, F32)] * 2
        + [out(16, BF)] * 2
        + [
            jax.ShapeDtypeStruct((n_mlp, n_dp, share, width), BF),
            jax.ShapeDtypeStruct((2, 4, share, width), BF),
        ],
        scratch_shapes=[
            pltpu.VMEM((n_dp, share, width), BF),
            pltpu.VMEM((3, share, width), BF),
            pltpu.VMEM((n_mlp, n_dp, share, width), BF),
            pltpu.VMEM((2, 4, share, width), BF),
            pltpu.SemaphoreType.DMA((n_dp,)),
            pltpu.SemaphoreType.DMA((2, 4)),
            pltpu.SemaphoreType.DMA((n_mlp, n_dp)),
            pltpu.SemaphoreType.DMA((64,)),
            pltpu.SemaphoreType.DMA((6,)),
        ],
        compiler_params=pltpu.CompilerParams(
            vmem_limit_bytes=VMEM_LIMIT, collective_id=0, has_side_effects=True
        ),
        name="enter",
    )(owner, slot, x, pos, vec, turned)


def project_kernel(
    x_ref, pos_ref, vec_ref, turned_ref, weight_ref,
    n1_ref, q_ref, k_ref, v_ref, cos_ref, sin_ref, qmark_ref, kmark_ref,
):
    unit, _ = normed(x_ref[...].astype(F32))
    n1 = (unit * vec_ref[0:1, :] + vec_ref[1:2, :]).astype(BF)
    n1t = n1.T
    n1_ref[...] = n1t
    px = pos_ref[0:1, :]
    py = pos_ref[1:2, :]
    half = cos_ref.shape[0]
    last = turned_ref.shape[1] - 1
    angle = turned_ref[half:, last:] * py + turned_ref[:half, last:] * px
    cosine = jnp.cos(angle)
    sine = jnp.sin(angle)
    cos_ref[...] = cosine
    sin_ref[...] = sine
    seg = pos_ref[2:3, :].astype(jnp.int32)
    row = lax.broadcasted_iota(jnp.int32, qmark_ref.shape, 0)
    qmark_ref[...] = jnp.where(row == seg, 1.0, 0.0).astype(BF)
    kmark_ref[...] = jnp.where(row == seg, 0.0, MASK_SHIFT).astype(BF)
    part = half // HEADS
    for index, (out, scale) in enumerate(((q_ref, 0.125), (k_ref, 1.0))):
        flat = dot(weight_ref[index], n1t, 0, 0) + turned_ref[:, 2 + index : 3 + index]
        for head in range(HEADS):
            low, mid = 2 * part * head, 2 * part * head + part
            a = flat[low:mid]
            b = flat[mid : mid + part]
            c = cosine[part * head : part * (head + 1)]
            s = sine[part * head : part * (head + 1)]
            out[low:mid, :] = (a * c - b * s).astype(BF) * jnp.asarray(scale, BF)
            out[mid : mid + part, :] = (b * c + a * s).astype(BF) * jnp.asarray(scale, BF)
    v_ref[...] = (dot(weight_ref[2], n1t, 0, 0) + turned_ref[:, 4:5]).astype(BF)


def project(x, pos, vec, turned, weights):
    rows, width = x.shape
    half = width // 2
    whole = lambda a: pl.BlockSpec(a.shape, lambda i: (0,) * a.ndim)
    col = lambda n: pl.BlockSpec((n, TILE), lambda i: (0, i))
    out = lambda n, d: jax.ShapeDtypeStruct((n, rows), d)
    return pl.pallas_call(
        project_kernel,
        grid=(rows // TILE,),
        in_specs=[
            pl.BlockSpec((TILE, width), lambda i: (i, 0)),
            col(8),
            whole(vec),
            whole(turned),
            whole(weights),
        ],
        out_specs=[col(width)] * 4 + [col(half)] * 2 + [col(16)] * 2,
        out_shape=[out(width, BF)] * 4 + [out(half, F32)] * 2 + [out(16, BF)] * 2,
        compiler_params=pltpu.CompilerParams(vmem_limit_bytes=VMEM_LIMIT),
        name="project",
    )(x, pos, vec, turned, weights)


def key_window(height_ref, width_ref, block):
    first = block * BLOCK
    last = first + BLOCK - 1
    start = jnp.int32(0)
    low = jnp.int32(0)
    high = jnp.int32(0)
    for image in range(height_ref.shape[0]):
        end = start + height_ref[image] * width_ref[image]
        low = jnp.where((start <= first) & (first < end), start, low)
        high = jnp.where((start <= last) & (last < end), end, high)
        start = end
    base = low // BLOCK
    return base, (high + BLOCK - 1) // BLOCK - base


def attend_kernel(height_ref, width_ref, q_ref, k_ref, v_ref, qmark_ref, kmark_ref, o_ref, log_ref):
    tokens = q_ref.shape[1]
    blocks = tokens // BLOCK
    size = q_ref.shape[0] // HEADS
    group = 4

    def one(block, part, base, count):
        here = pl.ds(pl.multiple_of(block * BLOCK, BLOCK), BLOCK)
        keys = pl.ds(pl.multiple_of(base * BLOCK, BLOCK), BLOCK * count)
        qmark = qmark_ref[:, here]
        kmark = kmark_ref[:, keys]
        for j in range(group):
            head = part * group + j
            rows = pl.ds(pl.multiple_of(head * size, size), size)
            q = jnp.concatenate([q_ref[rows, here], qmark], axis=0)
            k = jnp.concatenate([k_ref[rows, keys], kmark], axis=0)
            scores = dot(k, q, 0, 0)
            peak = jnp.max(scores, axis=0, keepdims=True)
            powers = jnp.exp(scores - peak)
            total = jnp.sum(powers, axis=0, keepdims=True)
            mixed = dot(v_ref[rows, keys], powers.astype(BF), 1, 0)
            o_ref[rows, here] = (mixed * (1.0 / total)).astype(BF)
            log_ref[pl.ds(pl.multiple_of(head * 8, 8), 8), here] = jnp.broadcast_to(
                peak + jnp.log(total), (8, BLOCK)
            )

    def step(block, carry):
        base, count = key_window(height_ref, width_ref, block)
        for n in range(1, blocks + 1):

            @pl.when(count == n)
            def _():
                def inner(part, c):
                    one(block, part, base, n)
                    return c

                lax.fori_loop(0, HEADS // group, inner, 0)

        return carry

    lax.fori_loop(0, blocks, step, 0)


def attend(heights, widths, q, k, v, qmark, kmark):
    smem = pl.BlockSpec(memory_space=pltpu.SMEM)
    vmem = pl.BlockSpec(memory_space=pltpu.VMEM)
    return pl.pallas_call(
        attend_kernel,
        in_specs=[smem, smem] + [vmem] * 5,
        out_specs=[vmem, vmem],
        out_shape=[
            jax.ShapeDtypeStruct(q.shape, BF),
            jax.ShapeDtypeStruct((8 * HEADS, q.shape[1]), F32),
        ],
        compiler_params=pltpu.CompilerParams(vmem_limit_bytes=VMEM_LIMIT),
        name="attend",
    )(heights, widths, q, k, v, qmark, kmark)


def attend_back_kernel(
    height_ref, width_ref, q_ref, k_ref, v_ref, qmark_ref, kmark_ref, log_ref, do_ref,
    pos_ref, cos_ref, sin_ref,
    dq_ref, dk_ref, dv_ref, freq_ref, bias_ref,
    gq_ref, gk_ref, gv_ref, turn_ref,
):
    tokens = q_ref.shape[1]
    blocks = tokens // BLOCK
    heads = log_ref.shape[0] // 8
    size = q_ref.shape[0] // heads
    half = size // 2
    group = 2
    gk_ref[...] = jnp.zeros_like(gk_ref)
    gv_ref[...] = jnp.zeros_like(gv_ref)

    def one(block, part, base, count):
        here = pl.ds(pl.multiple_of(block * BLOCK, BLOCK), BLOCK)
        keys = pl.ds(pl.multiple_of(base * BLOCK, BLOCK), BLOCK * count)
        qmark = qmark_ref[:, here]
        kmark = kmark_ref[:, keys]
        for j in range(group):
            head = part * group + j
            rows = pl.ds(pl.multiple_of(head * size, size), size)
            q = q_ref[rows, here]
            k = k_ref[rows, keys]
            do = do_ref[rows, here]
            scores = dot(
                jnp.concatenate([k, kmark], axis=0), jnp.concatenate([q, qmark], axis=0), 0, 0
            )
            log_row = log_ref[pl.ds(pl.multiple_of(head * 8, 8), 8), here][0:1]
            probs = jnp.exp(scores - log_row)
            dp = dot(v_ref[rows, keys], do, 0, 0)
            inner = jnp.sum(probs * dp, axis=0, keepdims=True)
            ds = (probs * (dp - inner)).astype(BF)
            gq_ref[rows, here] = dot(k, ds, 1, 0) * 0.125
            gk_ref[rows, keys] += dot(q, ds, 1, 1)
            gv_ref[rows, keys] += dot(do, probs.astype(BF), 1, 1)

    def step(block, carry):
        base, count = key_window(height_ref, width_ref, block)
        for n in range(1, blocks + 1):

            @pl.when(count == n)
            def _():
                def inner(part, c):
                    one(block, part, base, n)
                    return c

                lax.fori_loop(0, heads // group, inner, 0)

        return carry

    lax.fori_loop(0, blocks, step, 0)

    def unturn(head, carry):
        low = pl.ds(pl.multiple_of(head * size, size), half)
        high = pl.ds(pl.multiple_of(head * size + half, half), half)
        table = pl.ds(pl.multiple_of(head * half, half), half)
        c = cos_ref[table, :]
        s = sin_ref[table, :]
        turn = None
        for grad_ref, rot_ref, scale, out_ref in (
            (gq_ref, q_ref, 8.0, dq_ref),
            (gk_ref, k_ref, 1.0, dk_ref),
        ):
            ga = grad_ref[low, :]
            gb = grad_ref[high, :]
            out_ref[low, :] = (ga * c + gb * s).astype(BF)
            out_ref[high, :] = (gb * c - ga * s).astype(BF)
            ra = rot_ref[low, :].astype(F32) * scale
            rb = rot_ref[high, :].astype(F32) * scale
            piece = gb * ra - ga * rb
            turn = piece if turn is None else turn + piece
        turn_ref[table, :] = turn
        both = pl.ds(pl.multiple_of(head * size, size), size)
        dv_ref[both, :] = gv_ref[both, :].astype(BF)
        return carry

    lax.fori_loop(0, heads, unturn, 0)
    freq_ref[...] = dot(pos_ref[...], turn_ref[...], 1, 1, lax.Precision.HIGHEST)
    ones = jnp.ones((8, tokens), BF)
    for index, ref in enumerate((dq_ref, dk_ref, dv_ref)):
        bias_ref[8 * index : 8 * index + 8, :] = dot(ones, ref[...], 1, 1)


def attend_back(heights, widths, q, k, v, qmark, kmark, log_totals, do, pos, cosine, sine, part):
    smem = pl.BlockSpec(memory_space=pltpu.SMEM)
    width, tokens = q.shape
    half = width // PARTS
    cut = lambda a: pl.BlockSpec((a.shape[0] // PARTS, tokens), lambda i: (part, 0))
    whole = lambda a: pl.BlockSpec(a.shape, lambda i: (0, 0))
    out = lambda n, cols, dtype: jax.ShapeDtypeStruct((n, cols), dtype)
    outs = [out(half, tokens, BF)] * 3 + [out(8, half // 2, F32), out(24, half, F32)]
    return pl.pallas_call(
        attend_back_kernel,
        grid=(1,),
        in_specs=[smem, smem, cut(q), cut(k), cut(v), whole(qmark), whole(kmark), cut(log_totals)]
        + [cut(do), whole(pos), cut(cosine), cut(sine)],
        out_specs=[whole(a) for a in outs],
        out_shape=outs,
        scratch_shapes=[pltpu.VMEM((half, tokens), F32)] * 3
        + [pltpu.VMEM((half // 2, tokens), F32)],
        compiler_params=pltpu.CompilerParams(vmem_limit_bytes=VMEM_LIMIT),
        name="attend_back",
    )(heights, widths, q, k, v, qmark, kmark, log_totals, do, pos, cosine, sine)


def middle_kernel(
    x_ref, g_ref, o_ref, vec_ref, wo_ref, up_ref, down_ref,
    y_ref, dh_ref, do_ref, dwo_ref, dup_ref, ddown_ref, rows_ref, dc_ref,
    h_ref, n2_ref, n2t_ref, acc_ref, dn_ref, a_ref, dz_ref, dr_ref,
):
    groups = vec_ref.shape[0] - 10
    step = pl.program_id(0)
    tokens, width = x_ref.shape
    tiles = tokens // TILE

    def tile(i):
        return pl.ds(pl.multiple_of(i * TILE, TILE), TILE)

    @pl.when(step == 0)
    def _():
        def first(i, c):
            t = tile(i)
            branch = dot(o_ref[:, t], wo_ref[...], 0, 0) + vec_ref[5:6, :]
            h = x_ref[t, :].astype(F32) + branch
            h_ref[t, :] = h
            unit, _ = normed(h)
            n2 = (unit * vec_ref[6:7, :] + vec_ref[7:8, :]).astype(BF)
            n2_ref[t, :] = n2
            n2t_ref[:, t] = n2.T
            acc_ref[t, :] = h + vec_ref[8 + groups : 9 + groups, :]
            dn_ref[t, :] = jnp.zeros((TILE, width), F32)
            return c

        lax.fori_loop(0, tiles, first, 0)

    up_bias = vec_ref[pl.ds(8 + step, 1), :]

    def second(i, c):
        t = tile(i)
        z = dot(n2_ref[t, :], up_ref[0], 1, 0) + up_bias
        cdf = 0.5 * (1.0 + lax.erf(z * math.sqrt(0.5)))
        a = (z * cdf).astype(BF)
        a_ref[t, :] = a
        acc_ref[t, :] += dot(a, down_ref[0], 1, 0)
        da = dot(g_ref[t, :], down_ref[0], 1, 1)
        slope = cdf + z * (jnp.exp(-0.5 * z * z) * (1.0 / math.sqrt(2.0 * math.pi)))
        dz = (da * slope).astype(BF)
        dz_ref[t, :] = dz
        dn_ref[t, :] += dot(dz, up_ref[0], 1, 1)
        return c

    lax.fori_loop(0, tiles, second, 0)
    dc_ref[0] = dot(jnp.ones((8, tokens), BF), dz_ref[...], 1, 0)
    dup_ref[0] = dot(n2t_ref[...], dz_ref[...], 1, 0).astype(BF)
    ddown_ref[0] = dot(a_ref[...], g_ref[...], 0, 0).astype(BF)

    @pl.when(step == groups - 1)
    def _():
        rows_ref[...] = jnp.zeros_like(rows_ref)

        def third(i, c):
            t = tile(i)
            y_ref[t, :] = acc_ref[t, :].astype(BF)
            g = g_ref[t, :].astype(F32)
            unit, scale = normed(h_ref[t, :])
            dn = dn_ref[t, :]
            dh = g + norm_back(dn, unit, scale, vec_ref[6:7, :])
            dh_ref[t, :] = dh
            dr = dh.astype(BF)
            dr_ref[t, :] = dr
            do_ref[:, t] = dot(wo_ref[...], dr, 1, 1).astype(BF)
            rows_ref[0:8, :] += fold_rows(dr.astype(F32))
            rows_ref[8:16, :] += fold_rows(dn * unit)
            rows_ref[16:24, :] += fold_rows(dn)
            rows_ref[24:32, :] += fold_rows(g)
            return c

        lax.fori_loop(0, tiles, third, 0)
        dwo_ref[...] = dot(o_ref[...], dr_ref[...], 1, 0).astype(BF)


def middle_part(x, g, o, vec, wo, up, down):
    tokens, width = x.shape
    groups = up.shape[0]
    whole = lambda s: pl.BlockSpec(s, lambda i: (0,) * len(s))
    block = pl.BlockSpec((1, width, width), lambda i: (i, 0, 0))
    return pl.pallas_call(
        middle_kernel,
        grid=(groups,),
        in_specs=[
            whole(x.shape),
            whole(g.shape),
            whole(o.shape),
            whole(vec.shape),
            whole(wo.shape),
            block,
            block,
        ],
        out_specs=[
            whole((tokens, width)),
            whole((tokens, width)),
            whole((width, tokens)),
            whole((width, width)),
            block,
            block,
            whole((32, width)),
            pl.BlockSpec((1, 8, width), lambda i: (i, 0, 0)),
        ],
        out_shape=[
            jax.ShapeDtypeStruct((tokens, width), BF),
            jax.ShapeDtypeStruct((tokens, width), F32),
            jax.ShapeDtypeStruct((width, tokens), BF),
            jax.ShapeDtypeStruct((width, width), BF),
            jax.ShapeDtypeStruct((groups, width, width), BF),
            jax.ShapeDtypeStruct((groups, width, width), BF),
            jax.ShapeDtypeStruct((32, width), F32),
            jax.ShapeDtypeStruct((groups, 8, width), F32),
        ],
        scratch_shapes=[
            pltpu.VMEM((tokens, width), F32),
            pltpu.VMEM((tokens, width), BF),
            pltpu.VMEM((width, tokens), BF),
            pltpu.VMEM((tokens, width), F32),
            pltpu.VMEM((tokens, width), F32),
            pltpu.VMEM((tokens, width), BF),
            pltpu.VMEM((tokens, width), BF),
            pltpu.VMEM((tokens, width), BF),
        ],
        compiler_params=pltpu.CompilerParams(vmem_limit_bytes=VMEM_LIMIT),
        name="middle",
    )(x, g, o, vec, wo, up, down)


def final_kernel(
    x_ref, dh_ref, n1_ref, dq_ref, dk_ref, dv_ref, vec_ref, weight_ref, dwo_ref,
    dx_ref, dw_ref, rows_ref,
):
    tokens, width = x_ref.shape
    dw_ref[3] = dwo_ref[...]
    for index, ref in enumerate((dq_ref, dk_ref, dv_ref)):
        dw_ref[index] = dot(n1_ref[...], ref[...], 1, 1).astype(BF)
    rows_ref[...] = jnp.zeros_like(rows_ref)

    def loop(i, c):
        t = pl.ds(pl.multiple_of(i * TILE, TILE), TILE)
        dn = dot(dq_ref[:, t], weight_ref[0], 0, 1)
        dn += dot(dk_ref[:, t], weight_ref[1], 0, 1)
        dn += dot(dv_ref[:, t], weight_ref[2], 0, 1)
        unit, scale = normed(x_ref[t, :].astype(F32))
        dx_ref[t, :] = dh_ref[t, :] + norm_back(dn, unit, scale, vec_ref[0:1, :])
        rows_ref[0:8, :] += fold_rows(dn * unit)
        rows_ref[8:16, :] += fold_rows(dn)
        return c

    lax.fori_loop(0, tokens // TILE, loop, 0)


def final_part(x, dh, n1, dq, dk, dv, vec, weights, dwo):
    tokens, width = x.shape
    vmem = pl.BlockSpec(memory_space=pltpu.VMEM)
    return pl.pallas_call(
        final_kernel,
        in_specs=[vmem] * 9,
        out_specs=[vmem] * 3,
        out_shape=[
            jax.ShapeDtypeStruct((tokens, width), F32),
            jax.ShapeDtypeStruct((4, width, width), BF),
            jax.ShapeDtypeStruct((16, width), F32),
        ],
        compiler_params=pltpu.CompilerParams(vmem_limit_bytes=VMEM_LIMIT),
        name="final",
    )(x, dh, n1, dq, dk, dv, vec, weights, dwo)


def center_kernel(
    x_ref, g_ref, o_ref, vec_ref, weight_ref, zone_ref, xzone_ref, yzone_ref,
    y_ref, dh_ref, do_ref, dwo_ref, rows_ref, dc_ref, upgo_ref, upstay_ref, downgo_ref, downstay_ref,
    h_ref, n2_ref, n2t_ref, acc_ref, dn_ref, a_ref, dz_ref, wo_ref, w_ref, near_ref,
    land_sem, near_sem, send_sem, local_sem, out_sem,
):
    z, x, y, c = place()
    m = 2 * y + c
    m_y = 2 * (1 - y) + c
    right_x, right_y, partner = at(z, 1 - x, y, c), at(z, x, 1 - y, c), at(z, x, y, 1 - c)
    tokens, width = x_ref.shape
    tiles = tokens // TILE
    n_dp = w_ref.shape[2]
    fetch = pltpu.make_async_copy(weight_ref.at[3], wo_ref, local_sem.at[24])
    fetch.start()
    greet([right_x, right_y, partner])
    mail = Mail(send_sem)
    piece = w_ref.at[0, 0, 0]
    column_like = near_ref.at[0, 0]
    kept = []
    for kind in range(2):
        to = w_ref.at[kind]
        sem = land_sem.at[kind]
        for part in range(4):
            own, from_x = 2 * part + x, 2 * part + 1 - x
            if part < 2:
                mail.send(xzone_ref.at[kind, part], to.at[m, from_x], sem.at[m, from_x], right_y, piece)
            else:
                mail.send(yzone_ref.at[kind, part], to.at[m_y, own], sem.at[m_y, own], right_x, piece)
    for ref, column, shift in ((zone_ref, m, 0), (xzone_ref, m, 1), (yzone_ref, m_y, 0)):
        for kind in range(2):
            to = w_ref.at[kind]
            sem = land_sem.at[kind]
            for part in range(4):
                e = 2 * part + (x + shift) % 2
                mail.send(ref.at[kind, part], to.at[column, e], sem.at[column, e], partner, piece)
                copy = pltpu.make_async_copy(
                    ref.at[kind, part], to.at[column, e], local_sem.at[len(kept)]
                )
                copy.start()
                kept.append(copy)

    def tile(i):
        return pl.ds(pl.multiple_of(i * TILE, TILE), TILE)

    fetch.wait()
    wo = wo_ref.reshape(width, width)

    def first(i, carry):
        t = tile(i)
        branch = dot(o_ref[:, t], wo[...], 0, 0) + vec_ref[5:6, :]
        h = x_ref[t, :].astype(F32) + branch
        h_ref[t, :] = h
        unit, _ = normed(h)
        n2 = (unit * vec_ref[6:7, :] + vec_ref[7:8, :]).astype(BF)
        n2_ref[t, :] = n2
        n2t_ref[:, t] = n2.T
        acc_ref[t, :] = h + vec_ref[12:13, :]
        dn_ref[t, :] = jnp.zeros((TILE, width), F32)
        return carry

    lax.fori_loop(0, tiles, first, 0)
    for copy in kept:
        copy.wait()
    forwards = []

    def work(step, carry):
        column = 2 * ((y + step // 2) % 2) + (c + (step + 1) // 2) % 2

        @pl.when(step == 1)
        def _():
            for kind in range(2):
                sem = land_sem.at[kind]
                for part in range(4):
                    e = 2 * part + 1 - x
                    arrived(w_ref.at[kind, m_y, e], sem.at[m_y, e])
                    forwards.append(
                        mail.send(
                            w_ref.at[kind, m_y, e], w_ref.at[kind, m_y, e], sem.at[m_y, e], partner, piece
                        )
                    )
                for e in range(n_dp):
                    arrived(w_ref.at[kind, 2 * y + 1 - c, e], sem.at[2 * y + 1 - c, e])

        @pl.when(step == 2)
        def _():
            for kind in range(2):
                for e in range(n_dp):
                    other = 2 * (1 - y) + 1 - c
                    arrived(w_ref.at[kind, other, e], land_sem.at[kind, other, e])
            for slot in forwards:
                arrived(w_ref.at[0, 0, 0], send_sem.at[slot])
                mail.like[slot] = None

        up = w_ref.at[0, column].reshape(width, width)
        down = w_ref.at[1, column].reshape(width, width)
        up_bias = vec_ref[pl.ds(8 + column, 1), :]

        def second(i, c):
            t = tile(i)
            zed = dot(n2_ref[t, :], up[...], 1, 0) + up_bias
            cdf = 0.5 * (1.0 + lax.erf(zed * math.sqrt(0.5)))
            a = (zed * cdf).astype(BF)
            a_ref[t, :] = a
            acc_ref[t, :] += dot(a, down[...], 1, 0)
            da = dot(g_ref[t, :], down[...], 1, 1)
            slope = cdf + zed * (jnp.exp(-0.5 * zed * zed) * (1.0 / math.sqrt(2.0 * math.pi)))
            dz = (da * slope).astype(BF)
            dz_ref[t, :] = dz
            dn_ref[t, :] += dot(dz, up[...], 1, 1)
            return c

        lax.fori_loop(0, tiles, second, 0)
        dc_ref[column] = dot(jnp.ones((8, tokens), BF), dz_ref[...], 1, 0)
        up[...] = dot(n2t_ref[...], dz_ref[...], 1, 0).astype(BF)
        down[...] = dot(a_ref[...], g_ref[...], 0, 0).astype(BF)
        for s, row in ((1, y), (2, 1 - y)):

            @pl.when(step == s)
            def _():
                for kind in range(2):
                    mail.send(
                        w_ref.at[kind, 2 * row + 1 - c], near_ref.at[kind, row],
                        near_sem.at[kind, row], partner, column_like,
                    )

        return carry

    lax.fori_loop(0, 4, work, 0)

    outs = []

    def emit(source, target):
        copy = pltpu.make_async_copy(source, target, out_sem.at[len(outs)])
        copy.start()
        outs.append(copy)

    for row in (y, 1 - y):
        for kind in range(2):
            arrived(near_ref.at[kind, row], near_sem.at[kind, row])

            def summed(e, carry):
                total = w_ref[kind, 2 * row + c, e].astype(F32) + near_ref[kind, row, e].astype(F32)
                near_ref[kind, row, e] = total.astype(BF)
                return carry

            lax.fori_loop(0, n_dp, summed, 0)
    for row in range(2):
        for part in range(4):
            emit(near_ref.at[0, row, 2 * part + 1 - x], upgo_ref.at[row, part])
            emit(near_ref.at[0, row, 2 * part + x], upstay_ref.at[row, part])
    emit(near_ref.at[1, 1 - y], downgo_ref)
    emit(near_ref.at[1, y], downstay_ref)

    rows_ref[...] = jnp.zeros_like(rows_ref)

    def third(i, carry):
        t = tile(i)
        y_ref[t, :] = acc_ref[t, :].astype(BF)
        g = g_ref[t, :].astype(F32)
        unit, scale = normed(h_ref[t, :])
        dn = dn_ref[t, :]
        dh = g + norm_back(dn, unit, scale, vec_ref[6:7, :])
        dh_ref[t, :] = dh
        dr = dh.astype(BF)
        a_ref[t, :] = dr
        do_ref[:, t] = dot(wo[...], dr, 1, 1).astype(BF)
        rows_ref[0:8, :] += fold_rows(dr.astype(F32))
        rows_ref[8:16, :] += fold_rows(dn * unit)
        rows_ref[16:24, :] += fold_rows(dn)
        rows_ref[24:32, :] += fold_rows(g)
        return carry

    lax.fori_loop(0, tiles, third, 0)
    dwo_ref[...] = dot(o_ref[...], a_ref[...], 1, 0).astype(BF)
    for copy in outs:
        copy.wait()
    mail.finish()


def center(x, g, o, vec, weights, zone, xzone, yzone):
    tokens, width = x.shape
    n_mlp, n_dp, share, _ = weights.shape
    vmem = pl.BlockSpec(memory_space=pltpu.VMEM)
    hbm = pl.BlockSpec(memory_space=pl.ANY)
    shape = jax.ShapeDtypeStruct
    dma = pltpu.SemaphoreType.DMA
    return pl.pallas_call(
        center_kernel,
        in_specs=[vmem] * 4 + [hbm] * 4,
        out_specs=[vmem] * 6 + [hbm] * 4,
        out_shape=[
            shape((tokens, width), BF),
            shape((tokens, width), F32),
            shape((width, tokens), BF),
            shape((width, width), BF),
            shape((32, width), F32),
            shape((n_mlp, 8, width), F32),
        ]
        + [shape((2, 4, share, width), BF)] * 2
        + [shape((n_dp, share, width), BF)] * 2,
        scratch_shapes=[
            pltpu.VMEM((tokens, width), F32),
            pltpu.VMEM((tokens, width), BF),
            pltpu.VMEM((width, tokens), BF),
            pltpu.VMEM((tokens, width), F32),
            pltpu.VMEM((tokens, width), F32),
            pltpu.VMEM((tokens, width), BF),
            pltpu.VMEM((tokens, width), BF),
            pltpu.VMEM((n_dp, share, width), BF),
            pltpu.VMEM((2, n_mlp, n_dp, share, width), BF),
            pltpu.VMEM((2, 2, n_dp, share, width), BF),
            dma((2, n_mlp, n_dp)), dma((2, 2)), dma((48,)), dma((25,)), dma((18,)),
        ],
        compiler_params=pltpu.CompilerParams(
            vmem_limit_bytes=VMEM_LIMIT, collective_id=1, has_side_effects=True
        ),
        name="center",
    )(x, g, o, vec, weights, zone, xzone, yzone)


def added(*values):
    total = values[0].astype(F32)
    for value in values[1:]:
        total = total + value.astype(F32)
    return total.astype(BF)


def merge_kernel(
    upstay_ref, upgot_ref, downstay_ref, downgot_ref, upgo_out, upstay_out, downgo_out, downstay_out
):
    _, x, y, _ = place()
    for part in range(4):
        upgo_out[part] = added(upstay_ref[1 - y, part], upgot_ref[1 - y, part])
        upstay_out[part] = added(upstay_ref[y, part], upgot_ref[y, part])
        e = 2 * part + 1 - x
        downgo_out[part] = added(downstay_ref[e], downgot_ref[e])
        f = 2 * part + x
        downstay_out[part] = added(downstay_ref[f], downgot_ref[f])


def merge(upstay, upgot, downstay, downgot):
    vmem = pl.BlockSpec(memory_space=pltpu.VMEM)
    return pl.pallas_call(
        merge_kernel,
        in_specs=[vmem] * 4,
        out_specs=[vmem] * 4,
        out_shape=[jax.ShapeDtypeStruct((4,) + upstay.shape[2:], BF)] * 4,
        compiler_params=pltpu.CompilerParams(vmem_limit_bytes=VMEM_LIMIT),
        name="merge",
    )(upstay, upgot, downstay, downgot)


def leave_kernel(
    owner_ref, n1_ref, dq0_ref, dq1_ref, dk0_ref, dk1_ref, dv0_ref, dv1_ref, vec_ref, small_ref,
    upstay_ref, upgot_ref, downstay_ref, downgot_ref, x_hbm, dh_hbm, weight_hbm, dwo_hbm,
    dx_ref, grad_ref, total_ref,
    x_ref, dh_ref, weight_ref, rows_ref,
    dw_ref, near_ref, fromx_ref, fromy_ref, diagx_ref, diagy_ref, third_ref, zone_ref, done_ref,
    pack_ref, side_ref, sums_ref,
    near_sem, x_sem, y_sem, dx_sem, dy_sem, z_sem, grad_sem, side_sem, send_sem, local_sem,
):
    z, x, y, c = place()
    m = 2 * y + c
    d = 2 * z + x
    n_dp = grad_ref.shape[0]
    right_x, right_y, partner = at(z, 1 - x, y, c), at(z, x, 1 - y, c), at(z, x, y, 1 - c)
    dp_peers = [((d + off) % n_dp, m) for off in range(1, n_dp)]
    tokens, width = x_ref.shape
    loads = []
    for source, target in (
        (dwo_hbm, dw_ref.at[3]), (x_hbm, x_ref), (dh_hbm, dh_ref), (weight_hbm, weight_ref)
    ):
        load = pltpu.make_async_copy(source, target, local_sem.at[len(loads)])
        load.start()
        loads.append(load)
    greet(dp_peers + [right_y, partner])
    mail = Mail(send_sem)
    piece = pack_ref.at[0]
    for kind, (stay_ref, got_ref) in enumerate(
        ((upstay_ref, upgot_ref), (downstay_ref, downgot_ref))
    ):
        for off in (2, 1, 3, 0):
            to = (z + off) % 4
            third_ref[1 + kind, to] = added(stay_ref[to], got_ref[to])
            if off:
                mail.send(
                    third_ref.at[1 + kind, to], zone_ref.at[1 + kind, z], z_sem.at[1 + kind, z],
                    at(to, x, y, c), piece,
                )

    pairs = ((dq0_ref, dq1_ref), (dk0_ref, dk1_ref), (dv0_ref, dv1_ref))
    half = width // PARTS
    for index, pair in enumerate(pairs):
        out = dw_ref.at[index].reshape(width, width)
        for part, ref in enumerate(pair):
            out[:, part * half : (part + 1) * half] = dot(n1_ref[...], ref[...], 1, 1).astype(BF)
    loads[0].wait()
    for step in range(2):
        mail.send(
            dw_ref.at[2 * step + 1 - c], near_ref.at[step], near_sem.at[step], partner,
            near_ref.at[0],
        )
    for load in loads[1:]:
        load.wait()
    rows_ref[...] = jnp.zeros_like(rows_ref)
    flat = [weight_ref.at[index].reshape(width, width) for index in range(3)]

    def back(i, carry):
        t = pl.ds(pl.multiple_of(i * TILE, TILE), TILE)
        dn = jnp.zeros((TILE, width), F32)
        for index, pair in enumerate(pairs):
            for part, ref in enumerate(pair):
                dn += dot(ref[:, t], flat[index][:, part * half : (part + 1) * half], 0, 1)
        unit, scale = normed(x_ref[t, :].astype(F32))
        dx_ref[t, :] = dh_ref[t, :] + norm_back(dn, unit, scale, vec_ref[0:1, :])
        rows_ref[0:8, :] += fold_rows(dn * unit)
        rows_ref[8:16, :] += fold_rows(dn)
        return carry

    lax.fori_loop(0, 1, back, 0)
    for row in (0, 1):
        arrived(near_ref.at[row], near_sem.at[row])

        def summed(e, carry):
            near_ref[row, e] = added(near_ref[row, e], dw_ref[2 * row + c, e])
            return carry

        lax.fori_loop(0, n_dp, summed, 0)
    for part in range(2):
        mail.send(
            near_ref.at[1 - y, 2 * part + 1 - x], diagy_ref.at[part], dy_sem.at[part], right_y, piece
        )
        mail.send(
            near_ref.at[1 - y, 2 * (2 + part) + 1 - x], diagx_ref.at[part], dx_sem.at[part],
            right_x, piece,
        )
    for part in range(2):
        mail.send(
            near_ref.at[y, 2 * (2 + part) + 1 - x], fromx_ref.at[2 + part], x_sem.at[2 + part],
            right_x, piece,
        )
        mail.send(near_ref.at[1 - y, 2 * part + x], fromy_ref.at[part], y_sem.at[part], right_y, piece)
    lax.fori_loop(1, 3, back, 0)
    for part in range(2):
        arrived(diagy_ref.at[part], dy_sem.at[part])
        e = 2 * part + 1 - x
        diagy_ref[part] = added(near_ref[y, e], diagy_ref[part])
        mail.send(diagy_ref.at[part], fromx_ref.at[part], x_sem.at[part], right_x, piece)
        arrived(diagx_ref.at[part], dx_sem.at[part])
        f = 2 * (2 + part) + x
        diagx_ref[part] = added(near_ref[1 - y, f], diagx_ref[part])
        mail.send(diagx_ref.at[part], fromy_ref.at[2 + part], y_sem.at[2 + part], right_y, piece)
    lax.fori_loop(3, tokens // TILE, back, 0)

    sums_ref[0] = small_ref[...]
    sums_ref[0, 0:1, :] = jnp.sum(rows_ref[0:8, :], axis=0, keepdims=True)
    sums_ref[0, 1:2, :] = jnp.sum(rows_ref[8:16, :], axis=0, keepdims=True)

    def hop(index, peer):
        mail.send(
            sums_ref.at[index], side_ref.at[index], side_sem.at[index], peer, sums_ref.at[0]
        )

    def landed(index):
        arrived(side_ref.at[index], side_sem.at[index])
        sums_ref[index + 1] = sums_ref[index] + side_ref[index]

    hop(0, partner)
    for kind in (1, 2):
        total = third_ref[kind, z].astype(F32)
        for off in range(1, 4):
            e = (z + off) % 4
            arrived(zone_ref.at[kind, e], z_sem.at[kind, e])
            total = total + zone_ref[kind, e].astype(F32)
        done_ref[kind] = total.astype(BF)
    landed(0)
    hop(1, right_x)
    for part in (2, 3, 0, 1):
        arrived(fromx_ref.at[part], x_sem.at[part])
        arrived(fromy_ref.at[part], y_sem.at[part])
    for off in (2, 1, 3, 0):
        to = (z + off) % 4
        third_ref[0, to] = added(near_ref[y, 2 * to + x], fromx_ref[to], fromy_ref[to])
        if off:
            mail.send(
                third_ref.at[0, to], zone_ref.at[0, z], z_sem.at[0, z], at(to, x, y, c), piece
            )
    landed(1)
    hop(2, right_y)
    landed(2)
    for off in range(1, 4):
        mail.send(
            sums_ref.at[3], side_ref.at[3 + z], side_sem.at[3 + z], at((z + off) % 4, x, y, c),
            sums_ref.at[0],
        )
    side_ref[3 + z] = sums_ref[3]
    total = third_ref[0, z].astype(F32)
    for off in range(1, 4):
        e = (z + off) % 4
        arrived(zone_ref.at[0, e], z_sem.at[0, e])
        total = total + zone_ref[0, e].astype(F32)
    done_ref[0] = total.astype(BF)
    for off in (3, 4, 5, 2, 6, 1, 7):
        e = (d + off) % n_dp
        kind = jnp.where(owner_ref[m, 1] == e, 1, jnp.where(owner_ref[m, 2] == e, 2, 0))
        pack_ref[e] = done_ref[kind]
        mail.send(pack_ref.at[e], grad_ref.at[d], grad_sem.at[d], (e, m), piece)
    kind = jnp.where(owner_ref[m, 1] == d, 1, jnp.where(owner_ref[m, 2] == d, 2, 0))
    grad_ref[d] = done_ref[kind]
    for off in range(1, 4):
        e = (z + off) % 4
        arrived(side_ref.at[3 + e], side_sem.at[3 + e])
    total_ref[...] = (side_ref[3] + side_ref[4]) + (side_ref[5] + side_ref[6])
    for off in range(1, n_dp):
        e = (d + off) % n_dp
        arrived(grad_ref.at[e], grad_sem.at[e])
    mail.finish()


def leave(owner, x, dh, n1, flows, vec, weights, dwo, small, rest):
    tokens, width = x.shape
    n_mlp, n_dp, share, _ = weights.shape
    smem = pl.BlockSpec(memory_space=pltpu.SMEM)
    vmem = pl.BlockSpec(memory_space=pltpu.VMEM)
    hbm = pl.BlockSpec(memory_space=pl.ANY)
    dma = pltpu.SemaphoreType.DMA
    part = lambda *lead: pltpu.VMEM(lead + (share, width), BF)
    flat = [ref for pair in flows for ref in pair]
    return pl.pallas_call(
        leave_kernel,
        in_specs=[smem] + [vmem] * 13 + [hbm] * 4,
        out_specs=[vmem] * 3,
        out_shape=[
            jax.ShapeDtypeStruct((tokens, width), F32),
            jax.ShapeDtypeStruct((n_dp, share, width), BF),
            jax.ShapeDtypeStruct(small.shape, F32),
        ],
        scratch_shapes=[
            pltpu.VMEM((tokens, width), BF),
            pltpu.VMEM((tokens, width), F32),
            part(n_mlp, n_dp),
            pltpu.VMEM((16, width), F32),
            part(n_mlp, n_dp), part(2, n_dp), part(4), part(4), part(2), part(2), part(3, 4),
            part(3, 4), part(3), part(n_dp),
            pltpu.VMEM((7,) + small.shape, F32),
            pltpu.VMEM((4,) + small.shape, F32),
            dma((2,)), dma((4,)), dma((4,)), dma((2,)), dma((2,)), dma((3, 4)),
            dma((n_dp,)), dma((7,)), dma((48,)), dma((4,)),
        ],
        compiler_params=pltpu.CompilerParams(
            vmem_limit_bytes=VMEM_LIMIT, collective_id=2, has_side_effects=True
        ),
        name="leave",
    )(
        owner, n1, *flat, vec, small, *rest, x, dh, weights,
        dwo.reshape(n_dp, share, width),
    )


def halves(values):
    high = values.astype(BF)
    return high, (values - high.astype(F32)).astype(BF)


def dot_fine(left, right):
    left_high, left_low = halves(left)
    right_high, right_low = halves(right)
    return (
        dot(left_high, right_low, 1, 0)
        + dot(left_low, right_high, 1, 0)
        + dot(left_high, right_high, 1, 0)
    )


def update_kernel(
    keep_ref, decay_ref, grad_ref, left_ref, right_ref, lroot_ref, rroot_ref, master_ref,
    slot_ref, newleft_ref, newright_ref, newmaster_ref,
):
    @pl.when(keep_ref[0] == 0)
    def _():
        slot_ref[...] = jnp.zeros_like(slot_ref)
        newleft_ref[...] = left_ref[...]
        newright_ref[...] = right_ref[...]
        newmaster_ref[...] = master_ref[...]

    @pl.when(keep_ref[0] != 0)
    def _():
        decay = decay_ref[0]
        grad = grad_ref[...].astype(F32)
        slot_ref[...] = grad
        low = grad.astype(BF)
        newleft_ref[...] = decay * left_ref[...] + (1.0 - decay) * dot(low, low, 1, 1)
        newright_ref[...] = decay * right_ref[...] + (1.0 - decay) * dot(low, low, 0, 0)
        inner = dot_fine(lroot_ref[...], grad)
        direction = dot_fine(inner, rroot_ref[...])
        size = direction.shape[0] * direction.shape[1]
        mean = jnp.sum(direction * direction, keepdims=True) * (1.0 / size)
        newmaster_ref[...] = master_ref[...] - RATE_MATRIX * direction * lax.rsqrt(
            mean + GRAFT_EPSILON
        )


def update(owns, decays, grad, left, right, lroot, rroot, master):
    smem = pl.BlockSpec(memory_space=pltpu.SMEM)
    vmem = pl.BlockSpec(memory_space=pltpu.VMEM)
    return pl.pallas_call(
        update_kernel,
        in_specs=[smem, smem] + [vmem] * 6,
        out_specs=[vmem] * 4,
        out_shape=[jax.ShapeDtypeStruct(left.shape, F32)] * 4,
        compiler_params=pltpu.CompilerParams(vmem_limit_bytes=VMEM_LIMIT),
        name="update",
    )(owns, decays, grad, left, right, lroot, rroot, master)


def positions(segment, heights, widths, patch_rows, patch_cols):
    images = heights.shape[0]
    matches = segment[None, :] == jnp.arange(images, dtype=jnp.int32)[:, None]
    tall = jnp.sum(jnp.where(matches, heights[:, None], 0), axis=0).astype(F32)
    wide = jnp.sum(jnp.where(matches, widths[:, None], 0), axis=0).astype(F32)
    py = patch_rows.astype(F32) * GRID_BASE / tall
    px = patch_cols.astype(F32) * GRID_BASE / wide
    zero = jnp.zeros_like(px)
    return jnp.stack([px, py, segment.astype(F32), zero, zero, zero, zero, zero])


def local(
    tokens, cotangent, vectors, vector_moments, decays, owner, master_slots, left_slots,
    right_slots, left_roots, right_roots, grid_height, grid_width, patch_rows, patch_cols, segment,
):
    dp_index = lax.axis_index("dp")
    mlp_index = lax.axis_index("mlp")
    n_dp = lax.axis_size("dp")
    n_mlp = lax.axis_size("mlp")
    width = tokens.shape[1]
    share = width // n_dp
    owner_row = jnp.take(owner, mlp_index, axis=0)
    holds = owner_row == dp_index
    owns = jnp.any(holds).astype(jnp.int32).reshape(1)
    master = master_slots[0, 0]
    slot = master.astype(BF).reshape(n_dp, share, width)
    turned = vectors.T
    pos = positions(segment, grid_height, grid_width, patch_rows, patch_cols)
    direct = n_dp == 8 and n_mlp == 4
    if direct:
        n1t, q, k, v, cosine, sine, qmark, kmark, attention, zone = enter(
            owner, slot, tokens, pos, vectors, turned
        )
        over_x = [(i, i ^ 1) for i in range(n_dp)]
        over_y = [(i, i ^ 2) for i in range(n_mlp)]
        xzone = lax.ppermute(zone, "dp", over_x)
        yzone = lax.ppermute(zone, "mlp", over_y)
    else:
        pieces = lax.all_to_all(slot, "dp", 0, 0, tiled=True)
        mine = jnp.take(pieces, owner_row, axis=0)
        every = lax.all_gather(mine[None], ("dp", "mlp"), axis=0, tiled=True)
        blocks = every.reshape(n_dp, n_mlp, 3, share, width).transpose(2, 1, 0, 3, 4)
        attention, up, down = blocks.reshape(3, n_mlp, width, width)
        n1t, q, k, v, cosine, sine, qmark, kmark = project(tokens, pos, vectors, turned, attention)
    o, log_totals = attend(grid_height, grid_width, q, k, v, qmark, kmark)
    fine = (n_mlp, n_dp, share, width)
    back = functools.partial(attend_back, grid_height, grid_width)
    if direct:
        output, dh, do, dwo, mid_rows, dc, upgo, upstay, downgo, downstay = center(
            tokens, cotangent, o, vectors, attention, zone, xzone, yzone
        )
        upgot = lax.ppermute(upgo, "dp", over_x)
        downgot = lax.ppermute(downgo, "mlp", over_y)
        first = back(q, k, v, qmark, kmark, log_totals, do, pos, cosine, sine, 0)
        first, upgot, downgot = lax.optimization_barrier((first, upgot, downgot))
        upgo, upstay, downgo, downstay = merge(upstay, upgot, downstay, downgot)
        upgot = lax.ppermute(upgo, "mlp", over_y)
        downgot = lax.ppermute(downgo, "dp", over_x)
        do, upstay, downstay = lax.optimization_barrier((do, upstay, downstay))
    else:
        output, dh, do, dwo, dup, ddown, mid_rows, dc = middle_part(
            tokens, cotangent, o, vectors, attention[3], up, down
        )
        first = back(q, k, v, qmark, kmark, log_totals, do, pos, cosine, sine, 0)
    second = back(q, k, v, qmark, kmark, log_totals, do, pos, cosine, sine, 1)
    both = list(zip(first, second))
    freq = jnp.concatenate(both[3], axis=1)[0:2].reshape(1, width)
    bias = jnp.concatenate(both[4], axis=1)[0::8]
    eights = lambda rows: jnp.sum(rows.reshape(-1, 8, width), axis=1)
    mid = eights(mid_rows)
    tail = [bias, mid[0:3], dc[:, 0, :], mid[3:4], freq]
    if direct:
        small = jnp.concatenate([jnp.zeros((2, width), F32)] + tail, axis=0)
        input_grad, gradient, total = leave(
            owner, tokens, dh, n1t, both[0:3], vectors, attention.reshape(fine), dwo, small,
            (upstay, upgot, downstay, downgot),
        )
    else:
        dq, dk, dv = (jnp.concatenate(pair, axis=0) for pair in both[0:3])
        input_grad, datt, fin_rows = final_part(
            tokens, dh, n1t, dq, dk, dv, vectors, attention, dwo
        )
        grads = jnp.stack([datt, dup, ddown], axis=1)
        grads = grads.reshape(n_mlp, 3, n_dp, share, width).transpose(2, 0, 1, 3, 4)
        grads = grads.reshape(n_dp * n_mlp * 3, share, width)
        reduced = lax.psum_scatter(grads, ("dp", "mlp"), scatter_dimension=0, tiled=True)
        takers = owner_row[None, :] == jnp.arange(n_dp, dtype=jnp.int32)[:, None]
        kind_of = jnp.sum(jnp.where(takers, jnp.arange(3, dtype=jnp.int32)[None, :], 0), axis=1)
        gradient = lax.all_to_all(jnp.take(reduced, kind_of, axis=0), "dp", 0, 0, tiled=True)
        total = lax.psum(jnp.concatenate([eights(fin_rows)] + tail, axis=0), ("dp", "mlp"))
    gradient = gradient.reshape(width, width)
    slot_grad, left_out, right_out, master_out = update(
        owns, decays, gradient, left_slots[0, 0], right_slots[0, 0], left_roots[0, 0],
        right_roots[0, 0], master,
    )

    cut = width // n_mlp
    own = lambda table: lax.dynamic_slice_in_dim(table, mlp_index * cut, cut, 1)
    grad_share = own(total)
    decay = decays[1]
    moment_next = decay * own(vector_moments) + (1.0 - decay) * grad_share * grad_share
    vector_next = own(vectors) - RATE_VECTOR * grad_share / (jnp.sqrt(moment_next) + STEP_EPSILON)
    lift = lambda a: a[None, None]
    return (
        output, input_grad, lift(slot_grad), lift(left_out), lift(right_out), lift(master_out),
        grad_share, moment_next, vector_next,
    )


def solution(mesh):
    both = P(("dp", "mlp"))
    flat = P(("dp", "mlp"), None)
    slots = P("dp", "mlp", None, None)
    split = P(None, "mlp")
    return jax.shard_map(
        local,
        mesh=mesh,
        in_specs=(flat, flat, P(), P(), P(), P(), slots, slots, slots, slots, slots)
        + (both,) * 5,
        out_specs=(flat, flat, slots, slots, slots, slots, split, split, split),
        check_vma=False,
    )
```

```python
import functools
import math

import jax
import jax.numpy as jnp
from jax import lax
from jax.experimental import pallas as pl
from jax.experimental.pallas import tpu as pltpu
from jax.sharding import PartitionSpec as P

HEADS = 12
GRID_BASE = 16
NORM_EPSILON = 1e-06
GRAFT_EPSILON = 1e-06
STEP_EPSILON = 1e-08
RATE_MATRIX = 0.04
RATE_VECTOR = 0.02
MASK_SHIFT = -(2.0**100)
BLOCK = 128
TILE = 256
PARTS = 2
WINDOW = 6
F32 = jnp.float32
BF = jnp.bfloat16
VMEM_LIMIT = 60 * 1024 * 1024


def dot(left, right, left_dim, right_dim, precision=None):
    return lax.dot_general(
        left,
        right,
        (((left_dim,), (right_dim,)), ((), ())),
        preferred_element_type=F32,
        precision=precision,
    )


def normed(values):
    mean = jnp.mean(values, axis=-1, keepdims=True)
    centred = values - mean
    spread = jnp.mean(centred * centred, axis=-1, keepdims=True)
    scale = lax.rsqrt(spread + NORM_EPSILON)
    return centred * scale, scale


def norm_back(grad, unit, scale, gain):
    scaled = grad * gain
    first = jnp.mean(scaled, axis=-1, keepdims=True)
    second = jnp.mean(scaled * unit, axis=-1, keepdims=True)
    return scale * (scaled - first - unit * second)


def fold_rows(values):
    return jnp.sum(values.reshape(values.shape[0] // 8, 8, values.shape[1]), axis=0)


def place():
    d = lax.axis_index("dp")
    m = lax.axis_index("mlp")
    return d // 2, d % 2, m // 2, m % 2


def at(z, x, y, c):
    return (2 * z + x, 2 * y + c)


def greet(peers):
    barrier = pltpu.get_barrier_semaphore()
    for peer in peers:
        pl.semaphore_signal(barrier, inc=1, device_id=peer, device_id_type=pl.DeviceIdType.MESH)
    pl.semaphore_wait(barrier, len(peers))


class Mail:
    def __init__(self, sems):
        self.sems = sems
        self.like = []

    def send(self, source, target, arrival, peer, like):
        slot = len(self.like)
        pltpu.make_async_remote_copy(
            src_ref=source,
            dst_ref=target,
            send_sem=self.sems.at[slot],
            recv_sem=arrival,
            device_id=peer,
            device_id_type=pl.DeviceIdType.MESH,
        ).start()
        self.like.append(like)
        return slot

    def settle(self, slot):
        arrived(self.like[slot], self.sems.at[slot])
        self.like[slot] = None

    def finish(self):
        for slot, like in enumerate(self.like):
            if like is not None:
                self.settle(slot)


def arrived(target, arrival):
    pltpu.make_async_copy(target, target, arrival).wait()


def enter_kernel(
    owner_ref, slot_hbm, x_ref, pos_ref, vec_ref, turned_ref,
    n1_ref, q_ref, k_ref, v_ref, cos_ref, sin_ref, qmark_ref, kmark_ref, weight_ref, zone_ref,
    raw_ref, slot_ref, cross_ref, chain_ref, att_ref, zland_ref,
    cross_sem, chain_sem, relay_sem, att_sem, send_sem, local_sem,
):
    z, x, y, c = place()
    m = 2 * y + c
    n_dp = slot_ref.shape[0]
    right_x, right_y, partner = at(z, 1 - x, y, c), at(z, x, 1 - y, c), at(z, x, y, 1 - c)
    own = pltpu.make_async_copy(slot_hbm, raw_ref, local_sem.at[0])
    own.start()
    greet([right_x, right_y, partner, at((z + 1) % 4, x, y, c), at((z + 3) % 4, x, y, c)])
    mail = Mail(send_sem)
    piece = slot_ref.at[0]
    own.wait()
    for part in range(4):
        e = 2 * part + 1 - x
        slot_ref[e] = raw_ref[e].astype(BF)
        mail.send(slot_ref.at[e], cross_ref.at[part], cross_sem.at[part], right_x, piece)
    for part in range(4):
        e = 2 * part + x
        slot_ref[e] = raw_ref[e].astype(BF)

    tokens = x_ref.shape[0]
    half = cos_ref.shape[0]
    last = turned_ref.shape[1] - 1
    tiles = tokens // TILE

    def prepare(i, carry):
        t = pl.ds(pl.multiple_of(i * TILE, TILE), TILE)
        unit, _ = normed(x_ref[t, :].astype(F32))
        n1_ref[:, t] = (unit * vec_ref[0:1, :] + vec_ref[1:2, :]).astype(BF).T
        angle = turned_ref[half:, last:] * pos_ref[1:2, t] + turned_ref[:half, last:] * pos_ref[0:1, t]
        cos_ref[:, t] = jnp.cos(angle)
        sin_ref[:, t] = jnp.sin(angle)
        seg = pos_ref[2:3, t].astype(jnp.int32)
        row = lax.broadcasted_iota(jnp.int32, (qmark_ref.shape[0], TILE), 0)
        qmark_ref[:, t] = jnp.where(row == seg, 1.0, 0.0).astype(BF)
        kmark_ref[:, t] = jnp.where(row == seg, 0.0, MASK_SHIFT).astype(BF)
        return carry

    lax.fori_loop(0, tiles // 2, prepare, 0)

    edge = z % 3 == 0
    inner = z % 3 != 0
    far = z // 2
    near = 1 - far

    def relay(direction, kind, part):
        ref = chain_ref.at[direction, kind, part]
        return pltpu.make_async_remote_copy(
            src_ref=ref,
            dst_ref=ref,
            send_sem=relay_sem.at[direction, kind, part],
            recv_sem=chain_sem.at[direction, kind, part],
            device_id=at(z + 1 - 2 * direction, x, y, c),
            device_id_type=pl.DeviceIdType.MESH,
        )

    def merged(direction, kind, part, opening):
        ref = chain_ref.at[direction, kind, part]
        home = owner_ref[m, kind]
        value = lax.select(home % 2 == x, slot_ref[2 * part + x], cross_ref[part])
        if not opening:
            arrived(ref, chain_sem.at[direction, kind, part])
            value = lax.select(home // 2 == z, value, ref[...])
        ref[...] = value

    def crossed(part):
        arrived(cross_ref.at[part], cross_sem.at[part])

    def outward(kind, part):
        merged(far, kind, part, False)
        relay(far, kind, part).start()

    def inward(kind, part):
        merged(near, kind, part, False)

        @pl.when(inner)
        def _():
            relay(near, kind, part).start()

        return lax.select(
            owner_ref[m, kind] // 2 <= z, chain_ref[0, kind, part], chain_ref[1, kind, part]
        )

    def bring(part):
        e = 2 * part + x
        att_ref[m, e] = inward(0, part)
        for peer in (right_x, right_y, partner):
            mail.send(att_ref.at[m, e], att_ref.at[m, e], att_sem.at[m, e], peer, piece)

    @pl.when(edge)
    def _():
        def opening(part, carry):
            crossed(part)
            merged(far, 0, part, True)
            relay(far, 0, part).start()
            return carry

        lax.fori_loop(0, 4, opening, 0)

        def rest(s, carry):
            merged(far, 1 + s // 4, s % 4, True)
            relay(far, 1 + s // 4, s % 4).start()
            return carry

        lax.fori_loop(0, 8, rest, 0)

    def early(part):
        @pl.when(inner)
        def _():
            crossed(part)
            outward(0, part)

    early(0)
    early(1)
    bring(0)
    early(2)
    bring(1)
    early(3)
    bring(2)
    bring(3)
    lax.fori_loop(tiles // 2, tiles, prepare, 0)

    def ahead(s):
        @pl.when(inner)
        def _():
            outward(1 + s // 4, s % 4)

    def keep(s):
        zland_ref[s // 4, s % 4] = inward(1 + s // 4, s % 4)

    m_y = 2 * (1 - y) + c
    for part in range(4):
        e = 2 * part + 1 - x
        arrived(att_ref.at[m, e], att_sem.at[m, e])
        if part < 2:
            mail.send(att_ref.at[m, e], att_ref.at[m, e], att_sem.at[m, e], right_y, piece)
        mail.send(att_ref.at[m, e], att_ref.at[m, e], att_sem.at[m, e], partner, piece)
        f = 2 * part + x
        arrived(att_ref.at[m_y, f], att_sem.at[m_y, f])
        if part >= 2:
            mail.send(att_ref.at[m_y, f], att_ref.at[m_y, f], att_sem.at[m_y, f], right_x, piece)
        mail.send(att_ref.at[m_y, f], att_ref.at[m_y, f], att_sem.at[m_y, f], partner, piece)
        ahead(part)
        if part:
            keep(part - 1)
    for part in range(4):
        e = 2 * part + 1 - x
        arrived(att_ref.at[m_y, e], att_sem.at[m_y, e])
        mail.send(att_ref.at[m_y, e], att_ref.at[m_y, e], att_sem.at[m_y, e], partner, piece)
    for step in range(2):
        other = 2 * step + 1 - c
        for e in range(n_dp):
            arrived(att_ref.at[other, e], att_sem.at[other, e])
    out = pltpu.make_async_copy(att_ref, weight_ref, local_sem.at[1])
    out.start()

    part = half // HEADS
    width = x_ref.shape[1]

    def weight(index):
        return att_ref[index].reshape(width, width)

    def rotate(i, carry):
        ahead(4 + i)
        keep(3 + i)
        t = pl.ds(pl.multiple_of(i * TILE, TILE), TILE)
        n1t = n1_ref[:, t]
        cosine = cos_ref[:, t]
        sine = sin_ref[:, t]
        for index, (ref, scale) in enumerate(((q_ref, 0.125), (k_ref, 1.0))):
            flat = dot(weight(index), n1t, 0, 0) + turned_ref[:, 2 + index : 3 + index]
            for head in range(HEADS):
                low, mid = 2 * part * head, 2 * part * head + part
                a = flat[low:mid]
                b = flat[mid : mid + part]
                cs = cosine[part * head : part * (head + 1)]
                sn = sine[part * head : part * (head + 1)]
                ref[low:mid, t] = (a * cs - b * sn).astype(BF) * jnp.asarray(scale, BF)
                ref[mid : mid + part, t] = (b * cs + a * sn).astype(BF) * jnp.asarray(scale, BF)
        v_ref[:, t] = (dot(weight(2), n1t, 0, 0) + turned_ref[:, 4:5]).astype(BF)
        return carry

    lax.fori_loop(0, tiles, rotate, 0)
    keep(7)
    last_out = pltpu.make_async_copy(zland_ref, zone_ref, local_sem.at[2])
    last_out.start()
    mail.finish()
    for kind in range(3):
        for step in range(4):
            arrived(piece, relay_sem.at[far, kind, step])

            @pl.when(inner)
            def _():
                arrived(piece, relay_sem.at[near, kind, step])

    out.wait()
    last_out.wait()


def enter(owner, slot, x, pos, vec, turned):
    rows, width = x.shape
    half = width // 2
    n_dp, share, _ = slot.shape
    n_mlp = owner.shape[0]
    smem = pl.BlockSpec(memory_space=pltpu.SMEM)
    vmem = pl.BlockSpec(memory_space=pltpu.VMEM)
    hbm = pl.BlockSpec(memory_space=pl.ANY)
    out = lambda n, dtype: jax.ShapeDtypeStruct((n, rows), dtype)
    return pl.pallas_call(
        enter_kernel,
        in_specs=[smem, hbm, vmem, vmem, vmem, vmem],
        out_specs=[vmem] * 8 + [hbm] * 2,
        out_shape=[out(width, BF)] * 4
        + [out(half, F32)] * 2
        + [out(16, BF)] * 2
        + [
            jax.ShapeDtypeStruct((n_mlp, n_dp, share, width), BF),
            jax.ShapeDtypeStruct((2, 4, share, width), BF),
        ],
        scratch_shapes=[
            pltpu.VMEM((n_dp, share, width), F32),
            pltpu.VMEM((n_dp, share, width), BF),
            pltpu.VMEM((4, share, width), BF),
            pltpu.VMEM((2, 3, 4, share, width), BF),
            pltpu.VMEM((n_mlp, n_dp, share, width), BF),
            pltpu.VMEM((2, 4, share, width), BF),
            pltpu.SemaphoreType.DMA((4,)),
            pltpu.SemaphoreType.DMA((2, 3, 4)),
            pltpu.SemaphoreType.DMA((2, 3, 4)),
            pltpu.SemaphoreType.DMA((n_mlp, n_dp)),
            pltpu.SemaphoreType.DMA((48,)),
            pltpu.SemaphoreType.DMA((3,)),
        ],
        compiler_params=pltpu.CompilerParams(
            vmem_limit_bytes=VMEM_LIMIT, collective_id=0, has_side_effects=True
        ),
        name="enter",
    )(owner, slot, x, pos, vec, turned)


def project_kernel(
    x_ref, pos_ref, vec_ref, turned_ref, weight_ref,
    n1_ref, q_ref, k_ref, v_ref, cos_ref, sin_ref, qmark_ref, kmark_ref,
):
    unit, _ = normed(x_ref[...].astype(F32))
    n1 = (unit * vec_ref[0:1, :] + vec_ref[1:2, :]).astype(BF)
    n1t = n1.T
    n1_ref[...] = n1t
    px = pos_ref[0:1, :]
    py = pos_ref[1:2, :]
    half = cos_ref.shape[0]
    last = turned_ref.shape[1] - 1
    angle = turned_ref[half:, last:] * py + turned_ref[:half, last:] * px
    cosine = jnp.cos(angle)
    sine = jnp.sin(angle)
    cos_ref[...] = cosine
    sin_ref[...] = sine
    seg = pos_ref[2:3, :].astype(jnp.int32)
    row = lax.broadcasted_iota(jnp.int32, qmark_ref.shape, 0)
    qmark_ref[...] = jnp.where(row == seg, 1.0, 0.0).astype(BF)
    kmark_ref[...] = jnp.where(row == seg, 0.0, MASK_SHIFT).astype(BF)
    part = half // HEADS
    for index, (out, scale) in enumerate(((q_ref, 0.125), (k_ref, 1.0))):
        flat = dot(weight_ref[index], n1t, 0, 0) + turned_ref[:, 2 + index : 3 + index]
        for head in range(HEADS):
            low, mid = 2 * part * head, 2 * part * head + part
            a = flat[low:mid]
            b = flat[mid : mid + part]
            c = cosine[part * head : part * (head + 1)]
            s = sine[part * head : part * (head + 1)]
            out[low:mid, :] = (a * c - b * s).astype(BF) * jnp.asarray(scale, BF)
            out[mid : mid + part, :] = (b * c + a * s).astype(BF) * jnp.asarray(scale, BF)
    v_ref[...] = (dot(weight_ref[2], n1t, 0, 0) + turned_ref[:, 4:5]).astype(BF)


def project(x, pos, vec, turned, weights):
    rows, width = x.shape
    half = width // 2
    whole = lambda a: pl.BlockSpec(a.shape, lambda i: (0,) * a.ndim)
    col = lambda n: pl.BlockSpec((n, TILE), lambda i: (0, i))
    out = lambda n, d: jax.ShapeDtypeStruct((n, rows), d)
    return pl.pallas_call(
        project_kernel,
        grid=(rows // TILE,),
        in_specs=[
            pl.BlockSpec((TILE, width), lambda i: (i, 0)),
            col(8),
            whole(vec),
            whole(turned),
            whole(weights),
        ],
        out_specs=[col(width)] * 4 + [col(half)] * 2 + [col(16)] * 2,
        out_shape=[out(width, BF)] * 4 + [out(half, F32)] * 2 + [out(16, BF)] * 2,
        compiler_params=pltpu.CompilerParams(vmem_limit_bytes=VMEM_LIMIT),
        name="project",
    )(x, pos, vec, turned, weights)


def key_window(height_ref, width_ref, block):
    first = block * BLOCK
    last = first + BLOCK - 1
    start = jnp.int32(0)
    low = jnp.int32(0)
    high = jnp.int32(0)
    for image in range(height_ref.shape[0]):
        end = start + height_ref[image] * width_ref[image]
        low = jnp.where((start <= first) & (first < end), start, low)
        high = jnp.where((start <= last) & (last < end), end, high)
        start = end
    base = low // BLOCK
    return base, (high + BLOCK - 1) // BLOCK - base


def attend_kernel(height_ref, width_ref, q_ref, k_ref, v_ref, qmark_ref, kmark_ref, o_ref, log_ref):
    tokens = q_ref.shape[1]
    blocks = tokens // BLOCK
    size = q_ref.shape[0] // HEADS
    group = 4

    def one(block, part, base, count):
        here = pl.ds(pl.multiple_of(block * BLOCK, BLOCK), BLOCK)
        keys = pl.ds(pl.multiple_of(base * BLOCK, BLOCK), BLOCK * count)
        qmark = qmark_ref[:, here]
        kmark = kmark_ref[:, keys]
        for j in range(group):
            head = part * group + j
            rows = pl.ds(pl.multiple_of(head * size, size), size)
            q = jnp.concatenate([q_ref[rows, here], qmark], axis=0)
            k = jnp.concatenate([k_ref[rows, keys], kmark], axis=0)
            scores = dot(k, q, 0, 0)
            peak = jnp.max(scores, axis=0, keepdims=True)
            powers = jnp.exp(scores - peak)
            total = jnp.sum(powers, axis=0, keepdims=True)
            mixed = dot(v_ref[rows, keys], powers.astype(BF), 1, 0)
            o_ref[rows, here] = (mixed * (1.0 / total)).astype(BF)
            log_ref[pl.ds(pl.multiple_of(head * 8, 8), 8), here] = jnp.broadcast_to(
                peak + jnp.log(total), (8, BLOCK)
            )

    def step(block, carry):
        base, count = key_window(height_ref, width_ref, block)
        for n in range(1, min(blocks, WINDOW) + 1):

            @pl.when(count == n)
            def _():
                def inner(part, c):
                    one(block, part, base, n)
                    return c

                lax.fori_loop(0, HEADS // group, inner, 0)

        return carry

    lax.fori_loop(0, blocks, step, 0)


def attend(heights, widths, q, k, v, qmark, kmark):
    smem = pl.BlockSpec(memory_space=pltpu.SMEM)
    vmem = pl.BlockSpec(memory_space=pltpu.VMEM)
    return pl.pallas_call(
        attend_kernel,
        in_specs=[smem, smem] + [vmem] * 5,
        out_specs=[vmem, vmem],
        out_shape=[
            jax.ShapeDtypeStruct(q.shape, BF),
            jax.ShapeDtypeStruct((8 * HEADS, q.shape[1]), F32),
        ],
        compiler_params=pltpu.CompilerParams(vmem_limit_bytes=VMEM_LIMIT),
        name="attend",
    )(heights, widths, q, k, v, qmark, kmark)


def attend_back_kernel(
    height_ref, width_ref, q_ref, k_ref, v_ref, qmark_ref, kmark_ref, log_ref, do_ref,
    pos_ref, cos_ref, sin_ref,
    dq_ref, dk_ref, dv_ref, freq_ref, bias_ref,
    gq_ref, gk_ref, gv_ref, turn_ref,
):
    tokens = q_ref.shape[1]
    blocks = tokens // BLOCK
    heads = log_ref.shape[0] // 8
    size = q_ref.shape[0] // heads
    half = size // 2
    group = 2
    gk_ref[...] = jnp.zeros_like(gk_ref)
    gv_ref[...] = jnp.zeros_like(gv_ref)

    def one(block, part, base, count):
        here = pl.ds(pl.multiple_of(block * BLOCK, BLOCK), BLOCK)
        keys = pl.ds(pl.multiple_of(base * BLOCK, BLOCK), BLOCK * count)
        qmark = qmark_ref[:, here]
        kmark = kmark_ref[:, keys]
        for j in range(group):
            head = part * group + j
            rows = pl.ds(pl.multiple_of(head * size, size), size)
            q = q_ref[rows, here]
            k = k_ref[rows, keys]
            do = do_ref[rows, here]
            scores = dot(
                jnp.concatenate([k, kmark], axis=0), jnp.concatenate([q, qmark], axis=0), 0, 0
            )
            log_row = log_ref[pl.ds(pl.multiple_of(head * 8, 8), 8), here][0:1]
            probs = jnp.exp(scores - log_row)
            dp = dot(v_ref[rows, keys], do, 0, 0)
            inner = jnp.sum(probs * dp, axis=0, keepdims=True)
            ds = (probs * (dp - inner)).astype(BF)
            gq_ref[rows, here] = dot(k, ds, 1, 0) * 0.125
            gk_ref[rows, keys] += dot(q, ds, 1, 1)
            gv_ref[rows, keys] += dot(do, probs.astype(BF), 1, 1)

    def step(block, carry):
        base, count = key_window(height_ref, width_ref, block)
        for n in range(1, min(blocks, WINDOW) + 1):

            @pl.when(count == n)
            def _():
                def inner(part, c):
                    one(block, part, base, n)
                    return c

                lax.fori_loop(0, heads // group, inner, 0)

        return carry

    lax.fori_loop(0, blocks, step, 0)

    def unturn(head, carry):
        low = pl.ds(pl.multiple_of(head * size, size), half)
        high = pl.ds(pl.multiple_of(head * size + half, half), half)
        table = pl.ds(pl.multiple_of(head * half, half), half)
        c = cos_ref[table, :]
        s = sin_ref[table, :]
        turn = None
        for grad_ref, rot_ref, scale, out_ref in (
            (gq_ref, q_ref, 8.0, dq_ref),
            (gk_ref, k_ref, 1.0, dk_ref),
        ):
            ga = grad_ref[low, :]
            gb = grad_ref[high, :]
            out_ref[low, :] = (ga * c + gb * s).astype(BF)
            out_ref[high, :] = (gb * c - ga * s).astype(BF)
            ra = rot_ref[low, :].astype(F32) * scale
            rb = rot_ref[high, :].astype(F32) * scale
            piece = gb * ra - ga * rb
            turn = piece if turn is None else turn + piece
        turn_ref[table, :] = turn
        both = pl.ds(pl.multiple_of(head * size, size), size)
        dv_ref[both, :] = gv_ref[both, :].astype(BF)
        return carry

    lax.fori_loop(0, heads, unturn, 0)
    freq_ref[...] = dot(pos_ref[...], turn_ref[...], 1, 1, lax.Precision.HIGHEST)
    ones = jnp.ones((8, tokens), BF)
    for index, ref in enumerate((dq_ref, dk_ref, dv_ref)):
        bias_ref[8 * index : 8 * index + 8, :] = dot(ones, ref[...], 1, 1)


def attend_back(heights, widths, q, k, v, qmark, kmark, log_totals, do, pos, cosine, sine, part):
    smem = pl.BlockSpec(memory_space=pltpu.SMEM)
    width, tokens = q.shape
    half = width // PARTS
    cut = lambda a: pl.BlockSpec((a.shape[0] // PARTS, tokens), lambda i: (part, 0))
    whole = lambda a: pl.BlockSpec(a.shape, lambda i: (0, 0))
    out = lambda n, cols, dtype: jax.ShapeDtypeStruct((n, cols), dtype)
    outs = [out(half, tokens, BF)] * 3 + [out(8, half // 2, F32), out(24, half, F32)]
    return pl.pallas_call(
        attend_back_kernel,
        grid=(1,),
        in_specs=[smem, smem, cut(q), cut(k), cut(v), whole(qmark), whole(kmark), cut(log_totals)]
        + [cut(do), whole(pos), cut(cosine), cut(sine)],
        out_specs=[whole(a) for a in outs],
        out_shape=outs,
        scratch_shapes=[pltpu.VMEM((half, tokens), F32)] * 3
        + [pltpu.VMEM((half // 2, tokens), F32)],
        compiler_params=pltpu.CompilerParams(vmem_limit_bytes=VMEM_LIMIT),
        name="attend_back",
    )(heights, widths, q, k, v, qmark, kmark, log_totals, do, pos, cosine, sine)


def middle_kernel(
    x_ref, g_ref, o_ref, vec_ref, wo_ref, up_ref, down_ref,
    y_ref, dh_ref, do_ref, dwo_ref, dup_ref, ddown_ref, rows_ref, dc_ref,
    h_ref, n2_ref, n2t_ref, acc_ref, dn_ref, a_ref, dz_ref, dr_ref,
):
    groups = vec_ref.shape[0] - 10
    step = pl.program_id(0)
    tokens, width = x_ref.shape
    tiles = tokens // TILE

    def tile(i):
        return pl.ds(pl.multiple_of(i * TILE, TILE), TILE)

    @pl.when(step == 0)
    def _():
        def first(i, c):
            t = tile(i)
            branch = dot(o_ref[:, t], wo_ref[...], 0, 0) + vec_ref[5:6, :]
            h = x_ref[t, :].astype(F32) + branch
            h_ref[t, :] = h
            unit, _ = normed(h)
            n2 = (unit * vec_ref[6:7, :] + vec_ref[7:8, :]).astype(BF)
            n2_ref[t, :] = n2
            n2t_ref[:, t] = n2.T
            acc_ref[t, :] = h + vec_ref[8 + groups : 9 + groups, :]
            dn_ref[t, :] = jnp.zeros((TILE, width), F32)
            return c

        lax.fori_loop(0, tiles, first, 0)

    up_bias = vec_ref[pl.ds(8 + step, 1), :]

    def second(i, c):
        t = tile(i)
        z = dot(n2_ref[t, :], up_ref[0], 1, 0) + up_bias
        cdf = 0.5 * (1.0 + lax.erf(z * math.sqrt(0.5)))
        a = (z * cdf).astype(BF)
        a_ref[t, :] = a
        acc_ref[t, :] += dot(a, down_ref[0], 1, 0)
        da = dot(g_ref[t, :], down_ref[0], 1, 1)
        slope = cdf + z * (jnp.exp(-0.5 * z * z) * (1.0 / math.sqrt(2.0 * math.pi)))
        dz = (da * slope).astype(BF)
        dz_ref[t, :] = dz
        dn_ref[t, :] += dot(dz, up_ref[0], 1, 1)
        return c

    lax.fori_loop(0, tiles, second, 0)
    dc_ref[0] = dot(jnp.ones((8, tokens), BF), dz_ref[...], 1, 0)
    dup_ref[0] = dot(n2t_ref[...], dz_ref[...], 1, 0).astype(BF)
    ddown_ref[0] = dot(a_ref[...], g_ref[...], 0, 0).astype(BF)

    @pl.when(step == groups - 1)
    def _():
        rows_ref[...] = jnp.zeros_like(rows_ref)

        def third(i, c):
            t = tile(i)
            y_ref[t, :] = acc_ref[t, :].astype(BF)
            g = g_ref[t, :].astype(F32)
            unit, scale = normed(h_ref[t, :])
            dn = dn_ref[t, :]
            dh = g + norm_back(dn, unit, scale, vec_ref[6:7, :])
            dh_ref[t, :] = dh
            dr = dh.astype(BF)
            dr_ref[t, :] = dr
            do_ref[:, t] = dot(wo_ref[...], dr, 1, 1).astype(BF)
            rows_ref[0:8, :] += fold_rows(dr.astype(F32))
            rows_ref[8:16, :] += fold_rows(dn * unit)
            rows_ref[16:24, :] += fold_rows(dn)
            rows_ref[24:32, :] += fold_rows(g)
            return c

        lax.fori_loop(0, tiles, third, 0)
        dwo_ref[...] = dot(o_ref[...], dr_ref[...], 1, 0).astype(BF)


def middle_part(x, g, o, vec, wo, up, down):
    tokens, width = x.shape
    groups = up.shape[0]
    whole = lambda s: pl.BlockSpec(s, lambda i: (0,) * len(s))
    block = pl.BlockSpec((1, width, width), lambda i: (i, 0, 0))
    return pl.pallas_call(
        middle_kernel,
        grid=(groups,),
        in_specs=[
            whole(x.shape),
            whole(g.shape),
            whole(o.shape),
            whole(vec.shape),
            whole(wo.shape),
            block,
            block,
        ],
        out_specs=[
            whole((tokens, width)),
            whole((tokens, width)),
            whole((width, tokens)),
            whole((width, width)),
            block,
            block,
            whole((32, width)),
            pl.BlockSpec((1, 8, width), lambda i: (i, 0, 0)),
        ],
        out_shape=[
            jax.ShapeDtypeStruct((tokens, width), BF),
            jax.ShapeDtypeStruct((tokens, width), F32),
            jax.ShapeDtypeStruct((width, tokens), BF),
            jax.ShapeDtypeStruct((width, width), BF),
            jax.ShapeDtypeStruct((groups, width, width), BF),
            jax.ShapeDtypeStruct((groups, width, width), BF),
            jax.ShapeDtypeStruct((32, width), F32),
            jax.ShapeDtypeStruct((groups, 8, width), F32),
        ],
        scratch_shapes=[
            pltpu.VMEM((tokens, width), F32),
            pltpu.VMEM((tokens, width), BF),
            pltpu.VMEM((width, tokens), BF),
            pltpu.VMEM((tokens, width), F32),
            pltpu.VMEM((tokens, width), F32),
            pltpu.VMEM((tokens, width), BF),
            pltpu.VMEM((tokens, width), BF),
            pltpu.VMEM((tokens, width), BF),
        ],
        compiler_params=pltpu.CompilerParams(vmem_limit_bytes=VMEM_LIMIT),
        name="middle",
    )(x, g, o, vec, wo, up, down)


def final_kernel(
    x_ref, dh_ref, n1_ref, dq_ref, dk_ref, dv_ref, vec_ref, weight_ref, dwo_ref,
    dx_ref, dw_ref, rows_ref,
):
    tokens, width = x_ref.shape
    dw_ref[3] = dwo_ref[...]
    for index, ref in enumerate((dq_ref, dk_ref, dv_ref)):
        dw_ref[index] = dot(n1_ref[...], ref[...], 1, 1).astype(BF)
    rows_ref[...] = jnp.zeros_like(rows_ref)

    def loop(i, c):
        t = pl.ds(pl.multiple_of(i * TILE, TILE), TILE)
        dn = dot(dq_ref[:, t], weight_ref[0], 0, 1)
        dn += dot(dk_ref[:, t], weight_ref[1], 0, 1)
        dn += dot(dv_ref[:, t], weight_ref[2], 0, 1)
        unit, scale = normed(x_ref[t, :].astype(F32))
        dx_ref[t, :] = dh_ref[t, :] + norm_back(dn, unit, scale, vec_ref[0:1, :])
        rows_ref[0:8, :] += fold_rows(dn * unit)
        rows_ref[8:16, :] += fold_rows(dn)
        return c

    lax.fori_loop(0, tokens // TILE, loop, 0)


def final_part(x, dh, n1, dq, dk, dv, vec, weights, dwo):
    tokens, width = x.shape
    vmem = pl.BlockSpec(memory_space=pltpu.VMEM)
    return pl.pallas_call(
        final_kernel,
        in_specs=[vmem] * 9,
        out_specs=[vmem] * 3,
        out_shape=[
            jax.ShapeDtypeStruct((tokens, width), F32),
            jax.ShapeDtypeStruct((4, width, width), BF),
            jax.ShapeDtypeStruct((16, width), F32),
        ],
        compiler_params=pltpu.CompilerParams(vmem_limit_bytes=VMEM_LIMIT),
        name="final",
    )(x, dh, n1, dq, dk, dv, vec, weights, dwo)


def center_kernel(
    x_ref, g_ref, o_ref, vec_ref, weight_ref, zone_ref, xzone_ref, yzone_ref,
    y_ref, dh_ref, do_ref, dwo_ref, rows_ref, dc_ref, upgo_ref, upstay_ref, downgo_ref, downstay_ref,
    h_ref, n2_ref, n2t_ref, acc_ref, dn_ref, a_ref, dz_ref, wo_ref, w_ref, near_ref,
    land_sem, near_sem, send_sem, local_sem, out_sem,
):
    z, x, y, c = place()
    m = 2 * y + c
    m_y = 2 * (1 - y) + c
    right_x, right_y, partner = at(z, 1 - x, y, c), at(z, x, 1 - y, c), at(z, x, y, 1 - c)
    tokens, width = x_ref.shape
    tiles = tokens // TILE
    n_dp = w_ref.shape[2]
    fetch = pltpu.make_async_copy(weight_ref.at[3], wo_ref, local_sem.at[24])
    fetch.start()
    greet([right_x, right_y, partner])
    mail = Mail(send_sem)
    piece = w_ref.at[0, 0, 0]
    column_like = near_ref.at[0, 0]
    kept = []
    for kind in range(2):
        to = w_ref.at[kind]
        sem = land_sem.at[kind]
        for part in range(4):
            own, from_x = 2 * part + x, 2 * part + 1 - x
            if part < 2:
                mail.send(xzone_ref.at[kind, part], to.at[m, from_x], sem.at[m, from_x], right_y, piece)
            else:
                mail.send(yzone_ref.at[kind, part], to.at[m_y, own], sem.at[m_y, own], right_x, piece)
    for ref, column, shift in ((zone_ref, m, 0), (xzone_ref, m, 1), (yzone_ref, m_y, 0)):
        for kind in range(2):
            to = w_ref.at[kind]
            sem = land_sem.at[kind]
            for part in range(4):
                e = 2 * part + (x + shift) % 2
                mail.send(ref.at[kind, part], to.at[column, e], sem.at[column, e], partner, piece)
                copy = pltpu.make_async_copy(
                    ref.at[kind, part], to.at[column, e], local_sem.at[len(kept)]
                )
                copy.start()
                kept.append(copy)

    def tile(i):
        return pl.ds(pl.multiple_of(i * TILE, TILE), TILE)

    fetch.wait()
    wo = wo_ref.reshape(width, width)

    def first(i, carry):
        t = tile(i)
        branch = dot(o_ref[:, t], wo[...], 0, 0) + vec_ref[5:6, :]
        h = x_ref[t, :].astype(F32) + branch
        h_ref[t, :] = h
        unit, _ = normed(h)
        n2 = (unit * vec_ref[6:7, :] + vec_ref[7:8, :]).astype(BF)
        n2_ref[t, :] = n2
        n2t_ref[:, t] = n2.T
        acc_ref[t, :] = h + vec_ref[12:13, :]
        dn_ref[t, :] = jnp.zeros((TILE, width), F32)
        return carry

    lax.fori_loop(0, tiles, first, 0)
    for copy in kept:
        copy.wait()
    forwards = []

    def work(step, carry):
        column = 2 * ((y + step // 2) % 2) + (c + (step + 1) // 2) % 2

        @pl.when(step == 1)
        def _():
            for kind in range(2):
                sem = land_sem.at[kind]
                for part in range(4):
                    e = 2 * part + 1 - x
                    arrived(w_ref.at[kind, m_y, e], sem.at[m_y, e])
                    forwards.append(
                        mail.send(
                            w_ref.at[kind, m_y, e], w_ref.at[kind, m_y, e], sem.at[m_y, e], partner, piece
                        )
                    )
                for e in range(n_dp):
                    arrived(w_ref.at[kind, 2 * y + 1 - c, e], sem.at[2 * y + 1 - c, e])

        @pl.when(step == 2)
        def _():
            for kind in range(2):
                for e in range(n_dp):
                    other = 2 * (1 - y) + 1 - c
                    arrived(w_ref.at[kind, other, e], land_sem.at[kind, other, e])
            for slot in forwards:
                arrived(w_ref.at[0, 0, 0], send_sem.at[slot])
                mail.like[slot] = None

        up = w_ref.at[0, column].reshape(width, width)
        down = w_ref.at[1, column].reshape(width, width)
        up_bias = vec_ref[pl.ds(8 + column, 1), :]

        def second(i, c):
            t = tile(i)
            zed = dot(n2_ref[t, :], up[...], 1, 0) + up_bias
            cdf = 0.5 * (1.0 + lax.erf(zed * math.sqrt(0.5)))
            a = (zed * cdf).astype(BF)
            a_ref[t, :] = a
            acc_ref[t, :] += dot(a, down[...], 1, 0)
            da = dot(g_ref[t, :], down[...], 1, 1)
            slope = cdf + zed * (jnp.exp(-0.5 * zed * zed) * (1.0 / math.sqrt(2.0 * math.pi)))
            dz = (da * slope).astype(BF)
            dz_ref[t, :] = dz
            dn_ref[t, :] += dot(dz, up[...], 1, 1)
            return c

        lax.fori_loop(0, tiles, second, 0)
        dc_ref[column] = dot(jnp.ones((8, tokens), BF), dz_ref[...], 1, 0)
        up[...] = dot(n2t_ref[...], dz_ref[...], 1, 0).astype(BF)
        down[...] = dot(a_ref[...], g_ref[...], 0, 0).astype(BF)
        for s, row in ((1, y), (2, 1 - y)):

            @pl.when(step == s)
            def _():
                for kind in range(2):
                    mail.send(
                        w_ref.at[kind, 2 * row + 1 - c], near_ref.at[kind, row],
                        near_sem.at[kind, row], partner, column_like,
                    )

        return carry

    lax.fori_loop(0, 4, work, 0)

    outs = []

    def emit(source, target):
        copy = pltpu.make_async_copy(source, target, out_sem.at[len(outs)])
        copy.start()
        outs.append(copy)

    for row in (y, 1 - y):
        for kind in range(2):
            arrived(near_ref.at[kind, row], near_sem.at[kind, row])

            def summed(e, carry):
                total = w_ref[kind, 2 * row + c, e].astype(F32) + near_ref[kind, row, e].astype(F32)
                near_ref[kind, row, e] = total.astype(BF)
                return carry

            lax.fori_loop(0, n_dp, summed, 0)
    for row in range(2):
        for part in range(4):
            emit(near_ref.at[0, row, 2 * part + 1 - x], upgo_ref.at[row, part])
            emit(near_ref.at[0, row, 2 * part + x], upstay_ref.at[row, part])
    emit(near_ref.at[1, 1 - y], downgo_ref)
    emit(near_ref.at[1, y], downstay_ref)

    rows_ref[...] = jnp.zeros_like(rows_ref)

    def third(i, carry):
        t = tile(i)
        y_ref[t, :] = acc_ref[t, :].astype(BF)
        g = g_ref[t, :].astype(F32)
        unit, scale = normed(h_ref[t, :])
        dn = dn_ref[t, :]
        dh = g + norm_back(dn, unit, scale, vec_ref[6:7, :])
        dh_ref[t, :] = dh
        dr = dh.astype(BF)
        a_ref[t, :] = dr
        do_ref[:, t] = dot(wo[...], dr, 1, 1).astype(BF)
        rows_ref[0:8, :] += fold_rows(dr.astype(F32))
        rows_ref[8:16, :] += fold_rows(dn * unit)
        rows_ref[16:24, :] += fold_rows(dn)
        rows_ref[24:32, :] += fold_rows(g)
        return carry

    lax.fori_loop(0, tiles, third, 0)
    dwo_ref[...] = dot(o_ref[...], a_ref[...], 1, 0).astype(BF)
    for copy in outs:
        copy.wait()
    mail.finish()


def center(x, g, o, vec, weights, zone, xzone, yzone):
    tokens, width = x.shape
    n_mlp, n_dp, share, _ = weights.shape
    vmem = pl.BlockSpec(memory_space=pltpu.VMEM)
    hbm = pl.BlockSpec(memory_space=pl.ANY)
    shape = jax.ShapeDtypeStruct
    dma = pltpu.SemaphoreType.DMA
    return pl.pallas_call(
        center_kernel,
        in_specs=[vmem] * 4 + [hbm] * 4,
        out_specs=[vmem] * 6 + [hbm] * 4,
        out_shape=[
            shape((tokens, width), BF),
            shape((tokens, width), F32),
            shape((width, tokens), BF),
            shape((width, width), BF),
            shape((32, width), F32),
            shape((n_mlp, 8, width), F32),
        ]
        + [shape((2, 4, share, width), BF)] * 2
        + [shape((n_dp, share, width), BF)] * 2,
        scratch_shapes=[
            pltpu.VMEM((tokens, width), F32),
            pltpu.VMEM((tokens, width), BF),
            pltpu.VMEM((width, tokens), BF),
            pltpu.VMEM((tokens, width), F32),
            pltpu.VMEM((tokens, width), F32),
            pltpu.VMEM((tokens, width), BF),
            pltpu.VMEM((tokens, width), BF),
            pltpu.VMEM((n_dp, share, width), BF),
            pltpu.VMEM((2, n_mlp, n_dp, share, width), BF),
            pltpu.VMEM((2, 2, n_dp, share, width), BF),
            dma((2, n_mlp, n_dp)), dma((2, 2)), dma((48,)), dma((25,)), dma((18,)),
        ],
        compiler_params=pltpu.CompilerParams(
            vmem_limit_bytes=VMEM_LIMIT, collective_id=1, has_side_effects=True
        ),
        name="center",
    )(x, g, o, vec, weights, zone, xzone, yzone)


def added(*values):
    total = values[0].astype(F32)
    for value in values[1:]:
        total = total + value.astype(F32)
    return total.astype(BF)


def merge_kernel(
    upstay_ref, upgot_ref, downstay_ref, downgot_ref, upgo_out, upstay_out, downgo_out, downstay_out
):
    _, x, y, _ = place()
    for part in range(4):
        upgo_out[part] = added(upstay_ref[1 - y, part], upgot_ref[1 - y, part])
        upstay_out[part] = added(upstay_ref[y, part], upgot_ref[y, part])
        e = 2 * part + 1 - x
        downgo_out[part] = added(downstay_ref[e], downgot_ref[e])
        f = 2 * part + x
        downstay_out[part] = added(downstay_ref[f], downgot_ref[f])


def merge(upstay, upgot, downstay, downgot):
    vmem = pl.BlockSpec(memory_space=pltpu.VMEM)
    return pl.pallas_call(
        merge_kernel,
        in_specs=[vmem] * 4,
        out_specs=[vmem] * 4,
        out_shape=[jax.ShapeDtypeStruct((4,) + upstay.shape[2:], BF)] * 4,
        compiler_params=pltpu.CompilerParams(vmem_limit_bytes=VMEM_LIMIT),
        name="merge",
    )(upstay, upgot, downstay, downgot)


def leave_kernel(
    owner_ref, n1_ref, dq0_ref, dq1_ref, dk0_ref, dk1_ref, dv0_ref, dv1_ref, vec_ref, small_ref,
    upstay_ref, upgot_ref, downstay_ref, downgot_ref, x_hbm, dh_hbm, weight_hbm, dwo_hbm,
    dx_ref, grad_ref, total_ref,
    x_ref, dh_ref, weight_ref, rows_ref,
    dw_ref, near_ref, fromx_ref, fromy_ref, diagx_ref, diagy_ref, third_ref, chain_ref, done_ref,
    pack_ref, side_ref, sums_ref,
    near_sem, x_sem, y_sem, dx_sem, dy_sem, chain_sem, relay_sem, grad_sem, side_sem, send_sem, local_sem,
):
    z, x, y, c = place()
    m = 2 * y + c
    d = 2 * z + x
    n_dp = grad_ref.shape[0]
    right_x, right_y, partner = at(z, 1 - x, y, c), at(z, x, 1 - y, c), at(z, x, y, 1 - c)
    tokens, width = x_ref.shape
    loads = []
    for source, target in (
        (dwo_hbm, dw_ref.at[3]), (x_hbm, x_ref), (dh_hbm, dh_ref), (weight_hbm, weight_ref)
    ):
        load = pltpu.make_async_copy(source, target, local_sem.at[len(loads)])
        load.start()
        loads.append(load)
    greet([right_x, right_y, partner] + [at((z + off) % 4, x, y, c) for off in range(1, 4)])
    mail = Mail(send_sem)
    piece = pack_ref.at[0]

    edge = z % 3 == 0
    inner = z % 3 != 0
    far = z // 2
    near = 1 - far

    def relay(direction, kind, part):
        ref = chain_ref.at[direction, kind, part]
        return pltpu.make_async_remote_copy(
            src_ref=ref,
            dst_ref=ref,
            send_sem=relay_sem.at[direction, kind, part],
            recv_sem=chain_sem.at[direction, kind, part],
            device_id=at(z + 1 - 2 * direction, x, y, c),
            device_id_type=pl.DeviceIdType.MESH,
        )

    def opening(kind, part):
        chain_ref[far, kind, part] = third_ref[kind, part]
        relay(far, kind, part).start()

    def outward(kind, part):
        ref = chain_ref.at[far, kind, part]
        arrived(ref, chain_sem.at[far, kind, part])
        ref[...] = added(third_ref[kind, part], ref[...])
        relay(far, kind, part).start()

    def inward(kind, part):
        ref = chain_ref.at[near, kind, part]
        arrived(ref, chain_sem.at[near, kind, part])
        total = added(chain_ref[far, kind, part], ref[...])

        @pl.when(inner)
        def _():
            ref[...] = added(third_ref[kind, part], ref[...])
            relay(near, kind, part).start()

        return total

    def ahead(s):
        @pl.when(inner)
        def _():
            outward(1 + s // 4, s % 4)

    def keep(s):
        done_ref[s // 4, s % 4] = inward(1 + s // 4, s % 4)

    for kind, (stay_ref, got_ref) in enumerate(
        ((upstay_ref, upgot_ref), (downstay_ref, downgot_ref))
    ):
        for part in range(4):
            third_ref[1 + kind, part] = added(stay_ref[part], got_ref[part])

    @pl.when(edge)
    def _():
        def rest(s, carry):
            opening(1 + s // 4, s % 4)
            return carry

        lax.fori_loop(0, 8, rest, 0)

    pairs = ((dq0_ref, dq1_ref), (dk0_ref, dk1_ref), (dv0_ref, dv1_ref))
    half = width // PARTS
    for index, pair in enumerate(pairs):
        out = dw_ref.at[index].reshape(width, width)
        for part, ref in enumerate(pair):
            out[:, part * half : (part + 1) * half] = dot(n1_ref[...], ref[...], 1, 1).astype(BF)
    loads[0].wait()
    for step in range(2):
        mail.send(
            dw_ref.at[2 * step + 1 - c], near_ref.at[step], near_sem.at[step], partner,
            near_ref.at[0],
        )
    for load in loads[1:]:
        load.wait()
    rows_ref[...] = jnp.zeros_like(rows_ref)
    flat = [weight_ref.at[index].reshape(width, width) for index in range(3)]

    def back(i, carry):
        ahead(2 + i)
        t = pl.ds(pl.multiple_of(i * TILE, TILE), TILE)
        dn = jnp.zeros((TILE, width), F32)
        for index, pair in enumerate(pairs):
            for part, ref in enumerate(pair):
                dn += dot(ref[:, t], flat[index][:, part * half : (part + 1) * half], 0, 1)
        unit, scale = normed(x_ref[t, :].astype(F32))
        dx_ref[t, :] = dh_ref[t, :] + norm_back(dn, unit, scale, vec_ref[0:1, :])
        rows_ref[0:8, :] += fold_rows(dn * unit)
        rows_ref[8:16, :] += fold_rows(dn)
        keep(i)
        return carry

    ahead(0)
    ahead(1)
    lax.fori_loop(0, 1, back, 0)
    for row in (0, 1):
        arrived(near_ref.at[row], near_sem.at[row])

        def summed(e, carry):
            near_ref[row, e] = added(near_ref[row, e], dw_ref[2 * row + c, e])
            return carry

        lax.fori_loop(0, n_dp, summed, 0)
    for part in range(2):
        mail.send(
            near_ref.at[1 - y, 2 * part + 1 - x], diagy_ref.at[part], dy_sem.at[part], right_y, piece
        )
        mail.send(
            near_ref.at[1 - y, 2 * (2 + part) + 1 - x], diagx_ref.at[part], dx_sem.at[part],
            right_x, piece,
        )
    for part in range(2):
        mail.send(
            near_ref.at[y, 2 * (2 + part) + 1 - x], fromx_ref.at[2 + part], x_sem.at[2 + part],
            right_x, piece,
        )
        mail.send(near_ref.at[1 - y, 2 * part + x], fromy_ref.at[part], y_sem.at[part], right_y, piece)
    lax.fori_loop(1, 3, back, 0)
    for part in range(2):
        arrived(diagy_ref.at[part], dy_sem.at[part])
        e = 2 * part + 1 - x
        diagy_ref[part] = added(near_ref[y, e], diagy_ref[part])
        mail.send(diagy_ref.at[part], fromx_ref.at[part], x_sem.at[part], right_x, piece)
        arrived(diagx_ref.at[part], dx_sem.at[part])
        f = 2 * (2 + part) + x
        diagx_ref[part] = added(near_ref[1 - y, f], diagx_ref[part])
        mail.send(diagx_ref.at[part], fromy_ref.at[2 + part], y_sem.at[2 + part], right_y, piece)
    lax.fori_loop(3, tokens // TILE, back, 0)

    sums_ref[0] = small_ref[...]
    sums_ref[0, 0:1, :] = jnp.sum(rows_ref[0:8, :], axis=0, keepdims=True)
    sums_ref[0, 1:2, :] = jnp.sum(rows_ref[8:16, :], axis=0, keepdims=True)

    def hop(index, peer):
        mail.send(
            sums_ref.at[index], side_ref.at[index], side_sem.at[index], peer, sums_ref.at[0]
        )

    def landed(index):
        arrived(side_ref.at[index], side_sem.at[index])
        sums_ref[index + 1] = sums_ref[index] + side_ref[index]

    hop(0, partner)
    ahead(6)
    keep(4)
    landed(0)
    hop(1, right_x)
    ahead(7)
    keep(5)
    landed(1)
    hop(2, right_y)
    keep(6)
    landed(2)
    for off in range(1, 4):
        mail.send(
            sums_ref.at[3], side_ref.at[3 + z], side_sem.at[3 + z], at((z + off) % 4, x, y, c),
            sums_ref.at[0],
        )
    side_ref[3 + z] = sums_ref[3]
    keep(7)

    def gathered(part):
        arrived(fromx_ref.at[part], x_sem.at[part])
        arrived(fromy_ref.at[part], y_sem.at[part])
        third_ref[0, part] = added(near_ref[y, 2 * part + x], fromx_ref[part], fromy_ref[part])

    def wanted(e, part, first):
        second = lax.select(owner_ref[m, 2] == e, done_ref[1, part], first)
        return lax.select(owner_ref[m, 1] == e, done_ref[0, part], second)

    def close(part):
        first = inward(0, part)
        e = 2 * part + x
        pack_ref[part] = wanted(2 * z + 1 - x, part, first)
        mail.send(pack_ref.at[part], grad_ref.at[e], grad_sem.at[part], right_x, piece)
        grad_ref[e] = wanted(d, part, first)

    @pl.when(edge)
    def _():
        for part in (2, 3, 0, 1):
            gathered(part)
            opening(0, part)

    def early(part):
        @pl.when(inner)
        def _():
            gathered(part)
            outward(0, part)

    early(2)
    early(3)
    close(2)
    early(0)
    close(3)
    early(1)
    close(0)
    close(1)
    for off in range(1, 4):
        e = (z + off) % 4
        arrived(side_ref.at[3 + e], side_sem.at[3 + e])
    total_ref[...] = (side_ref[3] + side_ref[4]) + (side_ref[5] + side_ref[6])
    for part in (2, 3, 0, 1):
        arrived(grad_ref.at[2 * part + 1 - x], grad_sem.at[part])
    mail.finish()
    for kind in range(3):
        for part in range(4):
            arrived(piece, relay_sem.at[far, kind, part])

            @pl.when(inner)
            def _():
                arrived(piece, relay_sem.at[near, kind, part])


def leave(owner, x, dh, n1, flows, vec, weights, dwo, small, rest):
    tokens, width = x.shape
    n_mlp, n_dp, share, _ = weights.shape
    smem = pl.BlockSpec(memory_space=pltpu.SMEM)
    vmem = pl.BlockSpec(memory_space=pltpu.VMEM)
    hbm = pl.BlockSpec(memory_space=pl.ANY)
    dma = pltpu.SemaphoreType.DMA
    part = lambda *lead: pltpu.VMEM(lead + (share, width), BF)
    flat = [ref for pair in flows for ref in pair]
    return pl.pallas_call(
        leave_kernel,
        in_specs=[smem] + [vmem] * 13 + [hbm] * 4,
        out_specs=[vmem] * 3,
        out_shape=[
            jax.ShapeDtypeStruct((tokens, width), F32),
            jax.ShapeDtypeStruct((n_dp, share, width), BF),
            jax.ShapeDtypeStruct(small.shape, F32),
        ],
        scratch_shapes=[
            pltpu.VMEM((tokens, width), BF),
            pltpu.VMEM((tokens, width), F32),
            part(n_mlp, n_dp),
            pltpu.VMEM((16, width), F32),
            part(n_mlp, n_dp), part(2, n_dp), part(4), part(4), part(2), part(2), part(3, 4),
            part(2, 3, 4), part(2, 4), part(4),
            pltpu.VMEM((7,) + small.shape, F32),
            pltpu.VMEM((4,) + small.shape, F32),
            dma((2,)), dma((4,)), dma((4,)), dma((2,)), dma((2,)), dma((2, 3, 4)), dma((2, 3, 4)),
            dma((4,)), dma((7,)), dma((32,)), dma((4,)),
        ],
        compiler_params=pltpu.CompilerParams(
            vmem_limit_bytes=VMEM_LIMIT, collective_id=2, has_side_effects=True
        ),
        name="leave",
    )(
        owner, n1, *flat, vec, small, *rest, x, dh, weights,
        dwo.reshape(n_dp, share, width),
    )


def update_kernel(
    keep_ref, decay_ref, grad_ref, left_hbm, right_hbm, lroot_hbm, rroot_hbm, master_hbm, y_hbm, dx_hbm,
    slot_out, left_out, right_out, master_out, y_out, dx_out,
    left_ref, right_ref, lroot_ref, rroot_ref, master_ref, y_ref, dx_ref, slot_ref, turn_ref,
    in_sem, out_sem,
):
    loads = []
    for source, target in (
        (left_hbm, left_ref), (right_hbm, right_ref), (lroot_hbm, lroot_ref), (rroot_hbm, rroot_ref),
        (master_hbm, master_ref), (y_hbm, y_ref), (dx_hbm, dx_ref),
    ):
        loads.append(pltpu.make_async_copy(source, target, in_sem.at[len(loads)]))
        loads[-1].start()
    outs = []

    def emit(source, target):
        outs.append(pltpu.make_async_copy(source, target, out_sem.at[len(outs)]))
        outs[-1].start()

    held = keep_ref[0] != 0
    decay = decay_ref[0]
    width = grad_ref.shape[0]
    tall = width // 3

    def strip(i):
        return pl.ds(pl.multiple_of(i * tall, tall), tall)

    @pl.when(held)
    def _():
        slot_ref[...] = grad_ref[...].astype(F32)

    @pl.when(jnp.logical_not(held))
    def _():
        slot_ref[...] = jnp.zeros_like(slot_ref)

    emit(slot_ref, slot_out)
    loads[0].wait()

    @pl.when(held)
    def _():
        def rows(i, carry):
            r = strip(i)
            gram = dot(grad_ref[r, :], grad_ref[...], 1, 1)
            left_ref[r, :] = decay * left_ref[r, :] + (1.0 - decay) * gram
            return carry

        lax.fori_loop(0, 3, rows, 0)

    emit(left_ref, left_out)
    loads[1].wait()

    @pl.when(held)
    def _():
        turn_ref[...] = grad_ref[...].T

        def rows(i, carry):
            r = strip(i)
            gram = dot(turn_ref[r, :], grad_ref[...], 1, 0)
            right_ref[r, :] = decay * right_ref[r, :] + (1.0 - decay) * gram
            return carry

        lax.fori_loop(0, 3, rows, 0)

    emit(right_ref, right_out)
    for index, source, target in ((5, y_ref, y_out), (6, dx_ref, dx_out)):
        loads[index].wait()
        emit(source, target)
    for load in loads[2:5]:
        load.wait()

    @pl.when(held)
    def _():
        turn_ref[...] = rroot_ref[...].astype(BF)

        def rows(i, total):
            r = strip(i)
            inner = dot(lroot_ref[r, :].astype(BF), grad_ref[...], 1, 0).astype(BF)
            direction = dot(inner, turn_ref[...], 1, 0)
            lroot_ref[r, :] = direction
            return total + jnp.sum(direction * direction, axis=0, keepdims=True)

        total = jnp.sum(lax.fori_loop(0, 3, rows, jnp.zeros((1, width), F32)), keepdims=True)
        mean = total * (1.0 / (width * width))
        master_ref[...] -= lroot_ref[...] * (RATE_MATRIX * lax.rsqrt(mean + GRAFT_EPSILON))

    emit(master_ref, master_out)
    for copy in outs:
        copy.wait()


def update(owns, decays, grad, left, right, lroot, rroot, master, output, input_grad):
    smem = pl.BlockSpec(memory_space=pltpu.SMEM)
    vmem = pl.BlockSpec(memory_space=pltpu.VMEM)
    hbm = pl.BlockSpec(memory_space=pl.ANY)
    shape = lambda a: jax.ShapeDtypeStruct(a.shape, a.dtype)
    room = lambda a: pltpu.VMEM(a.shape, a.dtype)
    return pl.pallas_call(
        update_kernel,
        in_specs=[smem, smem, vmem] + [hbm] * 7,
        out_specs=[hbm] * 6,
        out_shape=[shape(a) for a in (left, left, right, master, output, input_grad)],
        scratch_shapes=[room(a) for a in (left, right, lroot, rroot, master, output, input_grad, left, grad)]
        + [pltpu.SemaphoreType.DMA((7,)), pltpu.SemaphoreType.DMA((6,))],
        compiler_params=pltpu.CompilerParams(vmem_limit_bytes=VMEM_LIMIT),
        name="update",
    )(owns, decays, grad, left, right, lroot, rroot, master, output, input_grad)


def positions(segment, heights, widths, patch_rows, patch_cols):
    images = heights.shape[0]
    matches = segment[None, :] == jnp.arange(images, dtype=jnp.int32)[:, None]
    tall = jnp.sum(jnp.where(matches, heights[:, None], 0), axis=0).astype(F32)
    wide = jnp.sum(jnp.where(matches, widths[:, None], 0), axis=0).astype(F32)
    py = patch_rows.astype(F32) * GRID_BASE / tall
    px = patch_cols.astype(F32) * GRID_BASE / wide
    zero = jnp.zeros_like(px)
    return jnp.stack([px, py, segment.astype(F32), zero, zero, zero, zero, zero])


def local(
    tokens, cotangent, vectors, vector_moments, decays, owner, master_slots, left_slots,
    right_slots, left_roots, right_roots, grid_height, grid_width, patch_rows, patch_cols, segment,
):
    dp_index = lax.axis_index("dp")
    mlp_index = lax.axis_index("mlp")
    n_dp = lax.axis_size("dp")
    n_mlp = lax.axis_size("mlp")
    width = tokens.shape[1]
    share = width // n_dp
    owner_row = jnp.take(owner, mlp_index, axis=0)
    holds = owner_row == dp_index
    owns = jnp.any(holds).astype(jnp.int32).reshape(1)
    master = master_slots[0, 0]
    turned = vectors.T
    pos = positions(segment, grid_height, grid_width, patch_rows, patch_cols)
    direct = n_dp == 8 and n_mlp == 4
    if direct:
        n1t, q, k, v, cosine, sine, qmark, kmark, attention, zone = enter(
            owner, master.reshape(n_dp, share, width), tokens, pos, vectors, turned
        )
        over_x = [(i, i ^ 1) for i in range(n_dp)]
        over_y = [(i, i ^ 2) for i in range(n_mlp)]
        xzone = lax.ppermute(zone, "dp", over_x)
        yzone = lax.ppermute(zone, "mlp", over_y)
    else:
        slot = master.astype(BF).reshape(n_dp, share, width)
        pieces = lax.all_to_all(slot, "dp", 0, 0, tiled=True)
        mine = jnp.take(pieces, owner_row, axis=0)
        every = lax.all_gather(mine[None], ("dp", "mlp"), axis=0, tiled=True)
        blocks = every.reshape(n_dp, n_mlp, 3, share, width).transpose(2, 1, 0, 3, 4)
        attention, up, down = blocks.reshape(3, n_mlp, width, width)
        n1t, q, k, v, cosine, sine, qmark, kmark = project(tokens, pos, vectors, turned, attention)
    o, log_totals = attend(grid_height, grid_width, q, k, v, qmark, kmark)
    fine = (n_mlp, n_dp, share, width)
    back = functools.partial(attend_back, grid_height, grid_width)
    if direct:
        output, dh, do, dwo, mid_rows, dc, upgo, upstay, downgo, downstay = center(
            tokens, cotangent, o, vectors, attention, zone, xzone, yzone
        )
        upgot = lax.ppermute(upgo, "dp", over_x)
        downgot = lax.ppermute(downgo, "mlp", over_y)
        first = back(q, k, v, qmark, kmark, log_totals, do, pos, cosine, sine, 0)
        first, upgot, downgot = lax.optimization_barrier((first, upgot, downgot))
        upgo, upstay, downgo, downstay = merge(upstay, upgot, downstay, downgot)
        upgot = lax.ppermute(upgo, "mlp", over_y)
        downgot = lax.ppermute(downgo, "dp", over_x)
        do, upstay, downstay = lax.optimization_barrier((do, upstay, downstay))
    else:
        output, dh, do, dwo, dup, ddown, mid_rows, dc = middle_part(
            tokens, cotangent, o, vectors, attention[3], up, down
        )
        first = back(q, k, v, qmark, kmark, log_totals, do, pos, cosine, sine, 0)
    second = back(q, k, v, qmark, kmark, log_totals, do, pos, cosine, sine, 1)
    both = list(zip(first, second))
    freq = jnp.concatenate(both[3], axis=1)[0:2].reshape(1, width)
    bias = jnp.concatenate(both[4], axis=1)[0::8]
    eights = lambda rows: jnp.sum(rows.reshape(-1, 8, width), axis=1)
    mid = eights(mid_rows)
    tail = [bias, mid[0:3], dc[:, 0, :], mid[3:4], freq]
    if direct:
        small = jnp.concatenate([jnp.zeros((2, width), F32)] + tail, axis=0)
        input_grad, gradient, total = leave(
            owner, tokens, dh, n1t, both[0:3], vectors, attention.reshape(fine), dwo, small,
            (upstay, upgot, downstay, downgot),
        )
    else:
        dq, dk, dv = (jnp.concatenate(pair, axis=0) for pair in both[0:3])
        input_grad, datt, fin_rows = final_part(
            tokens, dh, n1t, dq, dk, dv, vectors, attention, dwo
        )
        grads = jnp.stack([datt, dup, ddown], axis=1)
        grads = grads.reshape(n_mlp, 3, n_dp, share, width).transpose(2, 0, 1, 3, 4)
        grads = grads.reshape(n_dp * n_mlp * 3, share, width)
        reduced = lax.psum_scatter(grads, ("dp", "mlp"), scatter_dimension=0, tiled=True)
        takers = owner_row[None, :] == jnp.arange(n_dp, dtype=jnp.int32)[:, None]
        kind_of = jnp.sum(jnp.where(takers, jnp.arange(3, dtype=jnp.int32)[None, :], 0), axis=1)
        gradient = lax.all_to_all(jnp.take(reduced, kind_of, axis=0), "dp", 0, 0, tiled=True)
        total = lax.psum(jnp.concatenate([eights(fin_rows)] + tail, axis=0), ("dp", "mlp"))
    gradient = gradient.reshape(width, width)
    slot_grad, left_out, right_out, master_out, output, input_grad = update(
        owns, decays, gradient, left_slots[0, 0], right_slots[0, 0], left_roots[0, 0],
        right_roots[0, 0], master, output, input_grad,
    )

    cut = width // n_mlp
    own = lambda table: lax.dynamic_slice_in_dim(table, mlp_index * cut, cut, 1)
    grad_share = own(total)
    decay = decays[1]
    moment_next = decay * own(vector_moments) + (1.0 - decay) * grad_share * grad_share
    vector_next = own(vectors) - RATE_VECTOR * grad_share / (jnp.sqrt(moment_next) + STEP_EPSILON)
    lift = lambda a: a[None, None]
    return (
        output, input_grad, lift(slot_grad), lift(left_out), lift(right_out), lift(master_out),
        grad_share, moment_next, vector_next,
    )


def solution(mesh):
    both = P(("dp", "mlp"))
    flat = P(("dp", "mlp"), None)
    slots = P("dp", "mlp", None, None)
    split = P(None, "mlp")
    return jax.shard_map(
        local,
        mesh=mesh,
        in_specs=(flat, flat, P(), P(), P(), P(), slots, slots, slots, slots, slots)
        + (both,) * 5,
        out_specs=(flat, flat, slots, slots, slots, slots, split, split, split),
        check_vma=False,
    )
```

```python
import functools
import math

import jax
import jax.numpy as jnp
from jax import lax
from jax.experimental import pallas as pl
from jax.experimental.pallas import tpu as pltpu
from jax.sharding import PartitionSpec as P

HEADS = 12
GRID_BASE = 16
NORM_EPSILON = 1e-06
GRAFT_EPSILON = 1e-06
STEP_EPSILON = 1e-08
RATE_MATRIX = 0.04
RATE_VECTOR = 0.02
MASK_SHIFT = -(2.0**100)
BLOCK = 128
TILE = 256
PARTS = 2
WINDOW = 6
F32 = jnp.float32
BF = jnp.bfloat16
VMEM_LIMIT = 60 * 1024 * 1024


def dot(left, right, left_dim, right_dim, precision=None):
    return lax.dot_general(
        left,
        right,
        (((left_dim,), (right_dim,)), ((), ())),
        preferred_element_type=F32,
        precision=precision,
    )


def normed(values):
    mean = jnp.mean(values, axis=-1, keepdims=True)
    centred = values - mean
    spread = jnp.mean(centred * centred, axis=-1, keepdims=True)
    scale = lax.rsqrt(spread + NORM_EPSILON)
    return centred * scale, scale


def norm_back(grad, unit, scale, gain):
    scaled = grad * gain
    first = jnp.mean(scaled, axis=-1, keepdims=True)
    second = jnp.mean(scaled * unit, axis=-1, keepdims=True)
    return scale * (scaled - first - unit * second)


def fold_rows(values):
    return jnp.sum(values.reshape(values.shape[0] // 8, 8, values.shape[1]), axis=0)


def place():
    d = lax.axis_index("dp")
    m = lax.axis_index("mlp")
    return d // 2, d % 2, m // 2, m % 2


def at(z, x, y, c):
    return (2 * z + x, 2 * y + c)


def greet(peers):
    barrier = pltpu.get_barrier_semaphore()
    for peer in peers:
        pl.semaphore_signal(barrier, inc=1, device_id=peer, device_id_type=pl.DeviceIdType.MESH)
    pl.semaphore_wait(barrier, len(peers))


class Mail:
    def __init__(self, sems):
        self.sems = sems
        self.like = []

    def send(self, source, target, arrival, peer, like):
        slot = len(self.like)
        pltpu.make_async_remote_copy(
            src_ref=source,
            dst_ref=target,
            send_sem=self.sems.at[slot],
            recv_sem=arrival,
            device_id=peer,
            device_id_type=pl.DeviceIdType.MESH,
        ).start()
        self.like.append(like)
        return slot

    def settle(self, slot):
        arrived(self.like[slot], self.sems.at[slot])
        self.like[slot] = None

    def finish(self):
        for slot, like in enumerate(self.like):
            if like is not None:
                self.settle(slot)


def arrived(target, arrival):
    pltpu.make_async_copy(target, target, arrival).wait()


def enter_kernel(
    owner_ref, slot_hbm, x_ref, pos_ref, vec_ref, turned_ref,
    n1_ref, q_ref, k_ref, v_ref, cos_ref, sin_ref, qmark_ref, kmark_ref, weight_ref, zone_ref,
    raw_ref, slot_ref, cross_ref, chain_ref, att_ref, zland_ref,
    cross_sem, chain_sem, relay_sem, att_sem, send_sem, local_sem,
):
    z, x, y, c = place()
    m = 2 * y + c
    n_dp = slot_ref.shape[0]
    right_x, right_y, partner = at(z, 1 - x, y, c), at(z, x, 1 - y, c), at(z, x, y, 1 - c)
    own = pltpu.make_async_copy(slot_hbm, raw_ref, local_sem.at[0])
    own.start()
    greet([right_x, right_y, partner, at((z + 1) % 4, x, y, c), at((z + 3) % 4, x, y, c)])
    mail = Mail(send_sem)
    piece = slot_ref.at[0]
    own.wait()
    for part in range(4):
        e = 2 * part + 1 - x
        slot_ref[e] = raw_ref[e].astype(BF)
        mail.send(slot_ref.at[e], cross_ref.at[part], cross_sem.at[part], right_x, piece)
    for part in range(4):
        e = 2 * part + x
        slot_ref[e] = raw_ref[e].astype(BF)

    tokens = x_ref.shape[0]
    half = cos_ref.shape[0]
    last = turned_ref.shape[1] - 1
    tiles = tokens // TILE

    def prepare(i, carry):
        t = pl.ds(pl.multiple_of(i * TILE, TILE), TILE)
        unit, _ = normed(x_ref[t, :].astype(F32))
        n1_ref[:, t] = (unit * vec_ref[0:1, :] + vec_ref[1:2, :]).astype(BF).T
        angle = turned_ref[half:, last:] * pos_ref[1:2, t] + turned_ref[:half, last:] * pos_ref[0:1, t]
        cos_ref[:, t] = jnp.cos(angle)
        sin_ref[:, t] = jnp.sin(angle)
        seg = pos_ref[2:3, t].astype(jnp.int32)
        row = lax.broadcasted_iota(jnp.int32, (qmark_ref.shape[0], TILE), 0)
        qmark_ref[:, t] = jnp.where(row == seg, 1.0, 0.0).astype(BF)
        kmark_ref[:, t] = jnp.where(row == seg, 0.0, MASK_SHIFT).astype(BF)
        return carry

    lax.fori_loop(0, tiles // 2, prepare, 0)

    edge = z % 3 == 0
    inner = z % 3 != 0
    far = z // 2
    near = 1 - far

    def relay(direction, kind, part):
        ref = chain_ref.at[direction, kind, part]
        return pltpu.make_async_remote_copy(
            src_ref=ref,
            dst_ref=ref,
            send_sem=relay_sem.at[direction, kind, part],
            recv_sem=chain_sem.at[direction, kind, part],
            device_id=at(z + 1 - 2 * direction, x, y, c),
            device_id_type=pl.DeviceIdType.MESH,
        )

    def merged(direction, kind, part, opening):
        ref = chain_ref.at[direction, kind, part]
        home = owner_ref[m, kind]
        value = lax.select(home % 2 == x, slot_ref[2 * part + x], cross_ref[part])
        if not opening:
            arrived(ref, chain_sem.at[direction, kind, part])
            value = lax.select(home // 2 == z, value, ref[...])
        ref[...] = value

    def crossed(part):
        arrived(cross_ref.at[part], cross_sem.at[part])

    def outward(kind, part):
        merged(far, kind, part, False)
        relay(far, kind, part).start()

    def inward(kind, part):
        merged(near, kind, part, False)

        @pl.when(inner)
        def _():
            relay(near, kind, part).start()

        return lax.select(
            owner_ref[m, kind] // 2 <= z, chain_ref[0, kind, part], chain_ref[1, kind, part]
        )

    def bring(part):
        e = 2 * part + x
        att_ref[m, e] = inward(0, part)
        for peer in (right_x, right_y, partner):
            mail.send(att_ref.at[m, e], att_ref.at[m, e], att_sem.at[m, e], peer, piece)

    @pl.when(edge)
    def _():
        def opening(part, carry):
            crossed(part)
            merged(far, 0, part, True)
            relay(far, 0, part).start()
            return carry

        lax.fori_loop(0, 4, opening, 0)

        def rest(s, carry):
            merged(far, 1 + s // 4, s % 4, True)
            relay(far, 1 + s // 4, s % 4).start()
            return carry

        lax.fori_loop(0, 8, rest, 0)

    def early(part):
        @pl.when(inner)
        def _():
            crossed(part)
            outward(0, part)

    def ahead(s):
        @pl.when(inner)
        def _():
            outward(1 + s // 4, s % 4)

    def keep(s):
        zland_ref[s // 4, s % 4] = inward(1 + s // 4, s % 4)

    m_y = 2 * (1 - y) + c

    def spread(part):
        e = 2 * part + 1 - x
        arrived(att_ref.at[m, e], att_sem.at[m, e])
        if part < 2:
            mail.send(att_ref.at[m, e], att_ref.at[m, e], att_sem.at[m, e], right_y, piece)
        mail.send(att_ref.at[m, e], att_ref.at[m, e], att_sem.at[m, e], partner, piece)
        f = 2 * part + x
        arrived(att_ref.at[m_y, f], att_sem.at[m_y, f])
        if part >= 2:
            mail.send(att_ref.at[m_y, f], att_ref.at[m_y, f], att_sem.at[m_y, f], right_x, piece)
        mail.send(att_ref.at[m_y, f], att_ref.at[m_y, f], att_sem.at[m_y, f], partner, piece)

    early(0)
    early(1)
    bring(0)
    early(2)
    bring(1)
    early(3)
    bring(2)
    ahead(0)
    spread(0)
    bring(3)
    ahead(1)
    spread(1)
    ahead(2)
    keep(0)
    lax.fori_loop(tiles // 2, tiles, prepare, 0)
    spread(2)
    ahead(3)
    keep(1)
    spread(3)
    ahead(4)
    keep(2)
    for part in range(4):
        e = 2 * part + 1 - x
        arrived(att_ref.at[m_y, e], att_sem.at[m_y, e])
        mail.send(att_ref.at[m_y, e], att_ref.at[m_y, e], att_sem.at[m_y, e], partner, piece)
    for step in range(2):
        other = 2 * step + 1 - c
        for e in range(n_dp):
            arrived(att_ref.at[other, e], att_sem.at[other, e])
    out = pltpu.make_async_copy(att_ref, weight_ref, local_sem.at[1])
    out.start()

    part = half // HEADS
    width = x_ref.shape[1]

    def weight(index):
        return att_ref[index].reshape(width, width)

    def rotate(i, carry):
        @pl.when(i < 3)
        def _():
            ahead(5 + i)

        keep(3 + i)
        t = pl.ds(pl.multiple_of(i * TILE, TILE), TILE)
        n1t = n1_ref[:, t]
        cosine = cos_ref[:, t]
        sine = sin_ref[:, t]
        for index, (ref, scale) in enumerate(((q_ref, 0.125), (k_ref, 1.0))):
            flat = dot(weight(index), n1t, 0, 0) + turned_ref[:, 2 + index : 3 + index]
            for head in range(HEADS):
                low, mid = 2 * part * head, 2 * part * head + part
                a = flat[low:mid]
                b = flat[mid : mid + part]
                cs = cosine[part * head : part * (head + 1)]
                sn = sine[part * head : part * (head + 1)]
                ref[low:mid, t] = (a * cs - b * sn).astype(BF) * jnp.asarray(scale, BF)
                ref[mid : mid + part, t] = (b * cs + a * sn).astype(BF) * jnp.asarray(scale, BF)
        v_ref[:, t] = (dot(weight(2), n1t, 0, 0) + turned_ref[:, 4:5]).astype(BF)
        return carry

    lax.fori_loop(0, tiles, rotate, 0)
    keep(7)
    last_out = pltpu.make_async_copy(zland_ref, zone_ref, local_sem.at[2])
    last_out.start()
    mail.finish()
    for kind in range(3):
        for step in range(4):
            arrived(piece, relay_sem.at[far, kind, step])

            @pl.when(inner)
            def _():
                arrived(piece, relay_sem.at[near, kind, step])

    out.wait()
    last_out.wait()


def enter(owner, slot, x, pos, vec, turned):
    rows, width = x.shape
    half = width // 2
    n_dp, share, _ = slot.shape
    n_mlp = owner.shape[0]
    smem = pl.BlockSpec(memory_space=pltpu.SMEM)
    vmem = pl.BlockSpec(memory_space=pltpu.VMEM)
    hbm = pl.BlockSpec(memory_space=pl.ANY)
    out = lambda n, dtype: jax.ShapeDtypeStruct((n, rows), dtype)
    return pl.pallas_call(
        enter_kernel,
        in_specs=[smem, hbm, vmem, vmem, vmem, vmem],
        out_specs=[vmem] * 8 + [hbm] * 2,
        out_shape=[out(width, BF)] * 4
        + [out(half, F32)] * 2
        + [out(16, BF)] * 2
        + [
            jax.ShapeDtypeStruct((n_mlp, n_dp, share, width), BF),
            jax.ShapeDtypeStruct((2, 4, share, width), BF),
        ],
        scratch_shapes=[
            pltpu.VMEM((n_dp, share, width), F32),
            pltpu.VMEM((n_dp, share, width), BF),
            pltpu.VMEM((4, share, width), BF),
            pltpu.VMEM((2, 3, 4, share, width), BF),
            pltpu.VMEM((n_mlp, n_dp, share, width), BF),
            pltpu.VMEM((2, 4, share, width), BF),
            pltpu.SemaphoreType.DMA((4,)),
            pltpu.SemaphoreType.DMA((2, 3, 4)),
            pltpu.SemaphoreType.DMA((2, 3, 4)),
            pltpu.SemaphoreType.DMA((n_mlp, n_dp)),
            pltpu.SemaphoreType.DMA((48,)),
            pltpu.SemaphoreType.DMA((3,)),
        ],
        compiler_params=pltpu.CompilerParams(
            vmem_limit_bytes=VMEM_LIMIT, collective_id=0, has_side_effects=True
        ),
        name="enter",
    )(owner, slot, x, pos, vec, turned)


def project_kernel(
    x_ref, pos_ref, vec_ref, turned_ref, weight_ref,
    n1_ref, q_ref, k_ref, v_ref, cos_ref, sin_ref, qmark_ref, kmark_ref,
):
    unit, _ = normed(x_ref[...].astype(F32))
    n1 = (unit * vec_ref[0:1, :] + vec_ref[1:2, :]).astype(BF)
    n1t = n1.T
    n1_ref[...] = n1t
    px = pos_ref[0:1, :]
    py = pos_ref[1:2, :]
    half = cos_ref.shape[0]
    last = turned_ref.shape[1] - 1
    angle = turned_ref[half:, last:] * py + turned_ref[:half, last:] * px
    cosine = jnp.cos(angle)
    sine = jnp.sin(angle)
    cos_ref[...] = cosine
    sin_ref[...] = sine
    seg = pos_ref[2:3, :].astype(jnp.int32)
    row = lax.broadcasted_iota(jnp.int32, qmark_ref.shape, 0)
    qmark_ref[...] = jnp.where(row == seg, 1.0, 0.0).astype(BF)
    kmark_ref[...] = jnp.where(row == seg, 0.0, MASK_SHIFT).astype(BF)
    part = half // HEADS
    for index, (out, scale) in enumerate(((q_ref, 0.125), (k_ref, 1.0))):
        flat = dot(weight_ref[index], n1t, 0, 0) + turned_ref[:, 2 + index : 3 + index]
        for head in range(HEADS):
            low, mid = 2 * part * head, 2 * part * head + part
            a = flat[low:mid]
            b = flat[mid : mid + part]
            c = cosine[part * head : part * (head + 1)]
            s = sine[part * head : part * (head + 1)]
            out[low:mid, :] = (a * c - b * s).astype(BF) * jnp.asarray(scale, BF)
            out[mid : mid + part, :] = (b * c + a * s).astype(BF) * jnp.asarray(scale, BF)
    v_ref[...] = (dot(weight_ref[2], n1t, 0, 0) + turned_ref[:, 4:5]).astype(BF)


def project(x, pos, vec, turned, weights):
    rows, width = x.shape
    half = width // 2
    whole = lambda a: pl.BlockSpec(a.shape, lambda i: (0,) * a.ndim)
    col = lambda n: pl.BlockSpec((n, TILE), lambda i: (0, i))
    out = lambda n, d: jax.ShapeDtypeStruct((n, rows), d)
    return pl.pallas_call(
        project_kernel,
        grid=(rows // TILE,),
        in_specs=[
            pl.BlockSpec((TILE, width), lambda i: (i, 0)),
            col(8),
            whole(vec),
            whole(turned),
            whole(weights),
        ],
        out_specs=[col(width)] * 4 + [col(half)] * 2 + [col(16)] * 2,
        out_shape=[out(width, BF)] * 4 + [out(half, F32)] * 2 + [out(16, BF)] * 2,
        compiler_params=pltpu.CompilerParams(vmem_limit_bytes=VMEM_LIMIT),
        name="project",
    )(x, pos, vec, turned, weights)


def key_window(height_ref, width_ref, block):
    first = block * BLOCK
    last = first + BLOCK - 1
    start = jnp.int32(0)
    low = jnp.int32(0)
    high = jnp.int32(0)
    for image in range(height_ref.shape[0]):
        end = start + height_ref[image] * width_ref[image]
        low = jnp.where((start <= first) & (first < end), start, low)
        high = jnp.where((start <= last) & (last < end), end, high)
        start = end
    base = low // BLOCK
    return base, (high + BLOCK - 1) // BLOCK - base


def attend_kernel(height_ref, width_ref, q_ref, k_ref, v_ref, qmark_ref, kmark_ref, o_ref, log_ref):
    tokens = q_ref.shape[1]
    blocks = tokens // BLOCK
    size = q_ref.shape[0] // HEADS
    group = 4

    def one(block, part, base, count):
        here = pl.ds(pl.multiple_of(block * BLOCK, BLOCK), BLOCK)
        keys = pl.ds(pl.multiple_of(base * BLOCK, BLOCK), BLOCK * count)
        qmark = qmark_ref[:, here]
        kmark = kmark_ref[:, keys]
        for j in range(group):
            head = part * group + j
            rows = pl.ds(pl.multiple_of(head * size, size), size)
            q = jnp.concatenate([q_ref[rows, here], qmark], axis=0)
            k = jnp.concatenate([k_ref[rows, keys], kmark], axis=0)
            scores = dot(k, q, 0, 0)
            peak = jnp.max(scores, axis=0, keepdims=True)
            powers = jnp.exp(scores - peak)
            total = jnp.sum(powers, axis=0, keepdims=True)
            mixed = dot(v_ref[rows, keys], powers.astype(BF), 1, 0)
            o_ref[rows, here] = (mixed * (1.0 / total)).astype(BF)
            log_ref[pl.ds(pl.multiple_of(head * 8, 8), 8), here] = jnp.broadcast_to(
                peak + jnp.log(total), (8, BLOCK)
            )

    def step(block, carry):
        base, count = key_window(height_ref, width_ref, block)
        for n in range(1, min(blocks, WINDOW) + 1):

            @pl.when(count == n)
            def _():
                def inner(part, c):
                    one(block, part, base, n)
                    return c

                lax.fori_loop(0, HEADS // group, inner, 0)

        return carry

    lax.fori_loop(0, blocks, step, 0)


def attend(heights, widths, q, k, v, qmark, kmark):
    smem = pl.BlockSpec(memory_space=pltpu.SMEM)
    vmem = pl.BlockSpec(memory_space=pltpu.VMEM)
    return pl.pallas_call(
        attend_kernel,
        in_specs=[smem, smem] + [vmem] * 5,
        out_specs=[vmem, vmem],
        out_shape=[
            jax.ShapeDtypeStruct(q.shape, BF),
            jax.ShapeDtypeStruct((8 * HEADS, q.shape[1]), F32),
        ],
        compiler_params=pltpu.CompilerParams(vmem_limit_bytes=VMEM_LIMIT),
        name="attend",
    )(heights, widths, q, k, v, qmark, kmark)


def attend_back_kernel(
    height_ref, width_ref, q_ref, k_ref, v_ref, qmark_ref, kmark_ref, log_ref, do_ref,
    pos_ref, cos_ref, sin_ref,
    dq_ref, dk_ref, dv_ref, freq_ref, bias_ref,
    gq_ref, gk_ref, gv_ref, turn_ref,
):
    tokens = q_ref.shape[1]
    blocks = tokens // BLOCK
    heads = log_ref.shape[0] // 8
    size = q_ref.shape[0] // heads
    half = size // 2
    group = 2
    gk_ref[...] = jnp.zeros_like(gk_ref)
    gv_ref[...] = jnp.zeros_like(gv_ref)

    def one(block, part, base, count):
        here = pl.ds(pl.multiple_of(block * BLOCK, BLOCK), BLOCK)
        keys = pl.ds(pl.multiple_of(base * BLOCK, BLOCK), BLOCK * count)
        qmark = qmark_ref[:, here]
        kmark = kmark_ref[:, keys]
        for j in range(group):
            head = part * group + j
            rows = pl.ds(pl.multiple_of(head * size, size), size)
            q = q_ref[rows, here]
            k = k_ref[rows, keys]
            do = do_ref[rows, here]
            scores = dot(
                jnp.concatenate([k, kmark], axis=0), jnp.concatenate([q, qmark], axis=0), 0, 0
            )
            log_row = log_ref[pl.ds(pl.multiple_of(head * 8, 8), 8), here][0:1]
            probs = jnp.exp(scores - log_row)
            dp = dot(v_ref[rows, keys], do, 0, 0)
            inner = jnp.sum(probs * dp, axis=0, keepdims=True)
            ds = (probs * (dp - inner)).astype(BF)
            gq_ref[rows, here] = dot(k, ds, 1, 0) * 0.125
            gk_ref[rows, keys] += dot(q, ds, 1, 1)
            gv_ref[rows, keys] += dot(do, probs.astype(BF), 1, 1)

    def step(block, carry):
        base, count = key_window(height_ref, width_ref, block)
        for n in range(1, min(blocks, WINDOW) + 1):

            @pl.when(count == n)
            def _():
                def inner(part, c):
                    one(block, part, base, n)
                    return c

                lax.fori_loop(0, heads // group, inner, 0)

        return carry

    lax.fori_loop(0, blocks, step, 0)

    def unturn(head, carry):
        low = pl.ds(pl.multiple_of(head * size, size), half)
        high = pl.ds(pl.multiple_of(head * size + half, half), half)
        table = pl.ds(pl.multiple_of(head * half, half), half)
        c = cos_ref[table, :]
        s = sin_ref[table, :]
        turn = None
        for grad_ref, rot_ref, scale, out_ref in (
            (gq_ref, q_ref, 8.0, dq_ref),
            (gk_ref, k_ref, 1.0, dk_ref),
        ):
            ga = grad_ref[low, :]
            gb = grad_ref[high, :]
            out_ref[low, :] = (ga * c + gb * s).astype(BF)
            out_ref[high, :] = (gb * c - ga * s).astype(BF)
            ra = rot_ref[low, :].astype(F32) * scale
            rb = rot_ref[high, :].astype(F32) * scale
            piece = gb * ra - ga * rb
            turn = piece if turn is None else turn + piece
        turn_ref[table, :] = turn
        both = pl.ds(pl.multiple_of(head * size, size), size)
        dv_ref[both, :] = gv_ref[both, :].astype(BF)
        return carry

    lax.fori_loop(0, heads, unturn, 0)
    freq_ref[...] = dot(pos_ref[...], turn_ref[...], 1, 1, lax.Precision.HIGHEST)
    ones = jnp.ones((8, tokens), BF)
    for index, ref in enumerate((dq_ref, dk_ref, dv_ref)):
        bias_ref[8 * index : 8 * index + 8, :] = dot(ones, ref[...], 1, 1)


def attend_back(heights, widths, q, k, v, qmark, kmark, log_totals, do, pos, cosine, sine, part):
    smem = pl.BlockSpec(memory_space=pltpu.SMEM)
    width, tokens = q.shape
    half = width // PARTS
    cut = lambda a: pl.BlockSpec((a.shape[0] // PARTS, tokens), lambda i: (part, 0))
    whole = lambda a: pl.BlockSpec(a.shape, lambda i: (0, 0))
    out = lambda n, cols, dtype: jax.ShapeDtypeStruct((n, cols), dtype)
    outs = [out(half, tokens, BF)] * 3 + [out(8, half // 2, F32), out(24, half, F32)]
    return pl.pallas_call(
        attend_back_kernel,
        grid=(1,),
        in_specs=[smem, smem, cut(q), cut(k), cut(v), whole(qmark), whole(kmark), cut(log_totals)]
        + [cut(do), whole(pos), cut(cosine), cut(sine)],
        out_specs=[whole(a) for a in outs],
        out_shape=outs,
        scratch_shapes=[pltpu.VMEM((half, tokens), F32)] * 3
        + [pltpu.VMEM((half // 2, tokens), F32)],
        compiler_params=pltpu.CompilerParams(vmem_limit_bytes=VMEM_LIMIT),
        name="attend_back",
    )(heights, widths, q, k, v, qmark, kmark, log_totals, do, pos, cosine, sine)


def middle_kernel(
    x_ref, g_ref, o_ref, vec_ref, wo_ref, up_ref, down_ref,
    y_ref, dh_ref, do_ref, dwo_ref, dup_ref, ddown_ref, rows_ref, dc_ref,
    h_ref, n2_ref, n2t_ref, acc_ref, dn_ref, a_ref, dz_ref, dr_ref,
):
    groups = vec_ref.shape[0] - 10
    step = pl.program_id(0)
    tokens, width = x_ref.shape
    tiles = tokens // TILE

    def tile(i):
        return pl.ds(pl.multiple_of(i * TILE, TILE), TILE)

    @pl.when(step == 0)
    def _():
        def first(i, c):
            t = tile(i)
            branch = dot(o_ref[:, t], wo_ref[...], 0, 0) + vec_ref[5:6, :]
            h = x_ref[t, :].astype(F32) + branch
            h_ref[t, :] = h
            unit, _ = normed(h)
            n2 = (unit * vec_ref[6:7, :] + vec_ref[7:8, :]).astype(BF)
            n2_ref[t, :] = n2
            n2t_ref[:, t] = n2.T
            acc_ref[t, :] = h + vec_ref[8 + groups : 9 + groups, :]
            dn_ref[t, :] = jnp.zeros((TILE, width), F32)
            return c

        lax.fori_loop(0, tiles, first, 0)

    up_bias = vec_ref[pl.ds(8 + step, 1), :]

    def second(i, c):
        t = tile(i)
        z = dot(n2_ref[t, :], up_ref[0], 1, 0) + up_bias
        cdf = 0.5 * (1.0 + lax.erf(z * math.sqrt(0.5)))
        a = (z * cdf).astype(BF)
        a_ref[t, :] = a
        acc_ref[t, :] += dot(a, down_ref[0], 1, 0)
        da = dot(g_ref[t, :], down_ref[0], 1, 1)
        slope = cdf + z * (jnp.exp(-0.5 * z * z) * (1.0 / math.sqrt(2.0 * math.pi)))
        dz = (da * slope).astype(BF)
        dz_ref[t, :] = dz
        dn_ref[t, :] += dot(dz, up_ref[0], 1, 1)
        return c

    lax.fori_loop(0, tiles, second, 0)
    dc_ref[0] = dot(jnp.ones((8, tokens), BF), dz_ref[...], 1, 0)
    dup_ref[0] = dot(n2t_ref[...], dz_ref[...], 1, 0).astype(BF)
    ddown_ref[0] = dot(a_ref[...], g_ref[...], 0, 0).astype(BF)

    @pl.when(step == groups - 1)
    def _():
        rows_ref[...] = jnp.zeros_like(rows_ref)

        def third(i, c):
            t = tile(i)
            y_ref[t, :] = acc_ref[t, :].astype(BF)
            g = g_ref[t, :].astype(F32)
            unit, scale = normed(h_ref[t, :])
            dn = dn_ref[t, :]
            dh = g + norm_back(dn, unit, scale, vec_ref[6:7, :])
            dh_ref[t, :] = dh
            dr = dh.astype(BF)
            dr_ref[t, :] = dr
            do_ref[:, t] = dot(wo_ref[...], dr, 1, 1).astype(BF)
            rows_ref[0:8, :] += fold_rows(dr.astype(F32))
            rows_ref[8:16, :] += fold_rows(dn * unit)
            rows_ref[16:24, :] += fold_rows(dn)
            rows_ref[24:32, :] += fold_rows(g)
            return c

        lax.fori_loop(0, tiles, third, 0)
        dwo_ref[...] = dot(o_ref[...], dr_ref[...], 1, 0).astype(BF)


def middle_part(x, g, o, vec, wo, up, down):
    tokens, width = x.shape
    groups = up.shape[0]
    whole = lambda s: pl.BlockSpec(s, lambda i: (0,) * len(s))
    block = pl.BlockSpec((1, width, width), lambda i: (i, 0, 0))
    return pl.pallas_call(
        middle_kernel,
        grid=(groups,),
        in_specs=[
            whole(x.shape),
            whole(g.shape),
            whole(o.shape),
            whole(vec.shape),
            whole(wo.shape),
            block,
            block,
        ],
        out_specs=[
            whole((tokens, width)),
            whole((tokens, width)),
            whole((width, tokens)),
            whole((width, width)),
            block,
            block,
            whole((32, width)),
            pl.BlockSpec((1, 8, width), lambda i: (i, 0, 0)),
        ],
        out_shape=[
            jax.ShapeDtypeStruct((tokens, width), BF),
            jax.ShapeDtypeStruct((tokens, width), F32),
            jax.ShapeDtypeStruct((width, tokens), BF),
            jax.ShapeDtypeStruct((width, width), BF),
            jax.ShapeDtypeStruct((groups, width, width), BF),
            jax.ShapeDtypeStruct((groups, width, width), BF),
            jax.ShapeDtypeStruct((32, width), F32),
            jax.ShapeDtypeStruct((groups, 8, width), F32),
        ],
        scratch_shapes=[
            pltpu.VMEM((tokens, width), F32),
            pltpu.VMEM((tokens, width), BF),
            pltpu.VMEM((width, tokens), BF),
            pltpu.VMEM((tokens, width), F32),
            pltpu.VMEM((tokens, width), F32),
            pltpu.VMEM((tokens, width), BF),
            pltpu.VMEM((tokens, width), BF),
            pltpu.VMEM((tokens, width), BF),
        ],
        compiler_params=pltpu.CompilerParams(vmem_limit_bytes=VMEM_LIMIT),
        name="middle",
    )(x, g, o, vec, wo, up, down)


def final_kernel(
    x_ref, dh_ref, n1_ref, dq_ref, dk_ref, dv_ref, vec_ref, weight_ref, dwo_ref,
    dx_ref, dw_ref, rows_ref,
):
    tokens, width = x_ref.shape
    dw_ref[3] = dwo_ref[...]
    for index, ref in enumerate((dq_ref, dk_ref, dv_ref)):
        dw_ref[index] = dot(n1_ref[...], ref[...], 1, 1).astype(BF)
    rows_ref[...] = jnp.zeros_like(rows_ref)

    def loop(i, c):
        t = pl.ds(pl.multiple_of(i * TILE, TILE), TILE)
        dn = dot(dq_ref[:, t], weight_ref[0], 0, 1)
        dn += dot(dk_ref[:, t], weight_ref[1], 0, 1)
        dn += dot(dv_ref[:, t], weight_ref[2], 0, 1)
        unit, scale = normed(x_ref[t, :].astype(F32))
        dx_ref[t, :] = dh_ref[t, :] + norm_back(dn, unit, scale, vec_ref[0:1, :])
        rows_ref[0:8, :] += fold_rows(dn * unit)
        rows_ref[8:16, :] += fold_rows(dn)
        return c

    lax.fori_loop(0, tokens // TILE, loop, 0)


def final_part(x, dh, n1, dq, dk, dv, vec, weights, dwo):
    tokens, width = x.shape
    vmem = pl.BlockSpec(memory_space=pltpu.VMEM)
    return pl.pallas_call(
        final_kernel,
        in_specs=[vmem] * 9,
        out_specs=[vmem] * 3,
        out_shape=[
            jax.ShapeDtypeStruct((tokens, width), F32),
            jax.ShapeDtypeStruct((4, width, width), BF),
            jax.ShapeDtypeStruct((16, width), F32),
        ],
        compiler_params=pltpu.CompilerParams(vmem_limit_bytes=VMEM_LIMIT),
        name="final",
    )(x, dh, n1, dq, dk, dv, vec, weights, dwo)


def center_kernel(
    x_ref, g_ref, o_ref, vec_ref, weight_ref, zone_ref, xzone_ref, yzone_ref,
    y_ref, dh_ref, do_ref, dwo_ref, rows_ref, dc_ref, upgo_ref, upstay_ref, downgo_ref, downstay_ref,
    h_ref, n2_ref, n2t_ref, acc_ref, dn_ref, a_ref, dz_ref, wo_ref, w_ref, near_ref,
    land_sem, near_sem, send_sem, local_sem, out_sem,
):
    z, x, y, c = place()
    m = 2 * y + c
    m_y = 2 * (1 - y) + c
    right_x, right_y, partner = at(z, 1 - x, y, c), at(z, x, 1 - y, c), at(z, x, y, 1 - c)
    tokens, width = x_ref.shape
    tiles = tokens // TILE
    n_dp = w_ref.shape[2]
    fetch = pltpu.make_async_copy(weight_ref.at[3], wo_ref, local_sem.at[24])
    fetch.start()
    greet([right_x, right_y, partner])
    mail = Mail(send_sem)
    piece = w_ref.at[0, 0, 0]
    column_like = near_ref.at[0, 0]
    kept = []
    for kind in range(2):
        to = w_ref.at[kind]
        sem = land_sem.at[kind]
        for part in range(4):
            own, from_x = 2 * part + x, 2 * part + 1 - x
            if part < 2:
                mail.send(xzone_ref.at[kind, part], to.at[m, from_x], sem.at[m, from_x], right_y, piece)
            else:
                mail.send(yzone_ref.at[kind, part], to.at[m_y, own], sem.at[m_y, own], right_x, piece)
    for ref, column, shift in ((zone_ref, m, 0), (xzone_ref, m, 1), (yzone_ref, m_y, 0)):
        for kind in range(2):
            to = w_ref.at[kind]
            sem = land_sem.at[kind]
            for part in range(4):
                e = 2 * part + (x + shift) % 2
                mail.send(ref.at[kind, part], to.at[column, e], sem.at[column, e], partner, piece)
                copy = pltpu.make_async_copy(
                    ref.at[kind, part], to.at[column, e], local_sem.at[len(kept)]
                )
                copy.start()
                kept.append(copy)

    def tile(i):
        return pl.ds(pl.multiple_of(i * TILE, TILE), TILE)

    fetch.wait()
    wo = wo_ref.reshape(width, width)

    def first(i, carry):
        t = tile(i)
        branch = dot(o_ref[:, t], wo[...], 0, 0) + vec_ref[5:6, :]
        h = x_ref[t, :].astype(F32) + branch
        h_ref[t, :] = h
        unit, _ = normed(h)
        n2 = (unit * vec_ref[6:7, :] + vec_ref[7:8, :]).astype(BF)
        n2_ref[t, :] = n2
        n2t_ref[:, t] = n2.T
        acc_ref[t, :] = h + vec_ref[12:13, :]
        dn_ref[t, :] = jnp.zeros((TILE, width), F32)
        return carry

    lax.fori_loop(0, tiles, first, 0)
    for copy in kept:
        copy.wait()
    forwards = []

    def work(step, carry):
        column = 2 * ((y + step // 2) % 2) + (c + (step + 1) // 2) % 2

        @pl.when(step == 1)
        def _():
            for kind in range(2):
                sem = land_sem.at[kind]
                for part in range(4):
                    e = 2 * part + 1 - x
                    arrived(w_ref.at[kind, m_y, e], sem.at[m_y, e])
                    forwards.append(
                        mail.send(
                            w_ref.at[kind, m_y, e], w_ref.at[kind, m_y, e], sem.at[m_y, e], partner, piece
                        )
                    )
                for e in range(n_dp):
                    arrived(w_ref.at[kind, 2 * y + 1 - c, e], sem.at[2 * y + 1 - c, e])

        @pl.when(step == 2)
        def _():
            for kind in range(2):
                for e in range(n_dp):
                    other = 2 * (1 - y) + 1 - c
                    arrived(w_ref.at[kind, other, e], land_sem.at[kind, other, e])
            for slot in forwards:
                arrived(w_ref.at[0, 0, 0], send_sem.at[slot])
                mail.like[slot] = None

        up = w_ref.at[0, column].reshape(width, width)
        down = w_ref.at[1, column].reshape(width, width)
        up_bias = vec_ref[pl.ds(8 + column, 1), :]

        def second(i, c):
            t = tile(i)
            zed = dot(n2_ref[t, :], up[...], 1, 0) + up_bias
            cdf = 0.5 * (1.0 + lax.erf(zed * math.sqrt(0.5)))
            a = (zed * cdf).astype(BF)
            a_ref[t, :] = a
            acc_ref[t, :] += dot(a, down[...], 1, 0)
            da = dot(g_ref[t, :], down[...], 1, 1)
            slope = cdf + zed * (jnp.exp(-0.5 * zed * zed) * (1.0 / math.sqrt(2.0 * math.pi)))
            dz = (da * slope).astype(BF)
            dz_ref[t, :] = dz
            dn_ref[t, :] += dot(dz, up[...], 1, 1)
            return c

        lax.fori_loop(0, tiles, second, 0)
        dc_ref[column] = dot(jnp.ones((8, tokens), BF), dz_ref[...], 1, 0)
        up[...] = dot(n2t_ref[...], dz_ref[...], 1, 0).astype(BF)
        down[...] = dot(a_ref[...], g_ref[...], 0, 0).astype(BF)
        for s, row in ((1, y), (2, 1 - y)):

            @pl.when(step == s)
            def _():
                for kind in range(2):
                    mail.send(
                        w_ref.at[kind, 2 * row + 1 - c], near_ref.at[kind, row],
                        near_sem.at[kind, row], partner, column_like,
                    )

        return carry

    lax.fori_loop(0, 4, work, 0)

    outs = []

    def emit(source, target):
        copy = pltpu.make_async_copy(source, target, out_sem.at[len(outs)])
        copy.start()
        outs.append(copy)

    for row in (y, 1 - y):
        for kind in range(2):
            arrived(near_ref.at[kind, row], near_sem.at[kind, row])

            def summed(e, carry):
                total = w_ref[kind, 2 * row + c, e].astype(F32) + near_ref[kind, row, e].astype(F32)
                near_ref[kind, row, e] = total.astype(BF)
                return carry

            lax.fori_loop(0, n_dp, summed, 0)
    for row in range(2):
        for part in range(4):
            emit(near_ref.at[0, row, 2 * part + 1 - x], upgo_ref.at[row, part])
            emit(near_ref.at[0, row, 2 * part + x], upstay_ref.at[row, part])
    emit(near_ref.at[1, 1 - y], downgo_ref)
    emit(near_ref.at[1, y], downstay_ref)

    rows_ref[...] = jnp.zeros_like(rows_ref)

    def third(i, carry):
        t = tile(i)
        y_ref[t, :] = acc_ref[t, :].astype(BF)
        g = g_ref[t, :].astype(F32)
        unit, scale = normed(h_ref[t, :])
        dn = dn_ref[t, :]
        dh = g + norm_back(dn, unit, scale, vec_ref[6:7, :])
        dh_ref[t, :] = dh
        dr = dh.astype(BF)
        a_ref[t, :] = dr
        do_ref[:, t] = dot(wo[...], dr, 1, 1).astype(BF)
        rows_ref[0:8, :] += fold_rows(dr.astype(F32))
        rows_ref[8:16, :] += fold_rows(dn * unit)
        rows_ref[16:24, :] += fold_rows(dn)
        rows_ref[24:32, :] += fold_rows(g)
        return carry

    lax.fori_loop(0, tiles, third, 0)
    dwo_ref[...] = dot(o_ref[...], a_ref[...], 1, 0).astype(BF)
    for copy in outs:
        copy.wait()
    mail.finish()


def center(x, g, o, vec, weights, zone, xzone, yzone):
    tokens, width = x.shape
    n_mlp, n_dp, share, _ = weights.shape
    vmem = pl.BlockSpec(memory_space=pltpu.VMEM)
    hbm = pl.BlockSpec(memory_space=pl.ANY)
    shape = jax.ShapeDtypeStruct
    dma = pltpu.SemaphoreType.DMA
    return pl.pallas_call(
        center_kernel,
        in_specs=[vmem] * 4 + [hbm] * 4,
        out_specs=[vmem] * 6 + [hbm] * 4,
        out_shape=[
            shape((tokens, width), BF),
            shape((tokens, width), F32),
            shape((width, tokens), BF),
            shape((width, width), BF),
            shape((32, width), F32),
            shape((n_mlp, 8, width), F32),
        ]
        + [shape((2, 4, share, width), BF)] * 2
        + [shape((n_dp, share, width), BF)] * 2,
        scratch_shapes=[
            pltpu.VMEM((tokens, width), F32),
            pltpu.VMEM((tokens, width), BF),
            pltpu.VMEM((width, tokens), BF),
            pltpu.VMEM((tokens, width), F32),
            pltpu.VMEM((tokens, width), F32),
            pltpu.VMEM((tokens, width), BF),
            pltpu.VMEM((tokens, width), BF),
            pltpu.VMEM((n_dp, share, width), BF),
            pltpu.VMEM((2, n_mlp, n_dp, share, width), BF),
            pltpu.VMEM((2, 2, n_dp, share, width), BF),
            dma((2, n_mlp, n_dp)), dma((2, 2)), dma((48,)), dma((25,)), dma((18,)),
        ],
        compiler_params=pltpu.CompilerParams(
            vmem_limit_bytes=VMEM_LIMIT, collective_id=1, has_side_effects=True
        ),
        name="center",
    )(x, g, o, vec, weights, zone, xzone, yzone)


def added(*values):
    total = values[0].astype(F32)
    for value in values[1:]:
        total = total + value.astype(F32)
    return total.astype(BF)


def merge_kernel(
    upstay_ref, upgot_ref, downstay_ref, downgot_ref, upgo_out, upstay_out, downgo_out, downstay_out
):
    _, x, y, _ = place()
    for part in range(4):
        upgo_out[part] = added(upstay_ref[1 - y, part], upgot_ref[1 - y, part])
        upstay_out[part] = added(upstay_ref[y, part], upgot_ref[y, part])
        e = 2 * part + 1 - x
        downgo_out[part] = added(downstay_ref[e], downgot_ref[e])
        f = 2 * part + x
        downstay_out[part] = added(downstay_ref[f], downgot_ref[f])


def merge(upstay, upgot, downstay, downgot):
    vmem = pl.BlockSpec(memory_space=pltpu.VMEM)
    return pl.pallas_call(
        merge_kernel,
        in_specs=[vmem] * 4,
        out_specs=[vmem] * 4,
        out_shape=[jax.ShapeDtypeStruct((4,) + upstay.shape[2:], BF)] * 4,
        compiler_params=pltpu.CompilerParams(vmem_limit_bytes=VMEM_LIMIT),
        name="merge",
    )(upstay, upgot, downstay, downgot)


def leave_kernel(
    owner_ref, n1_ref, dq0_ref, dq1_ref, dk0_ref, dk1_ref, dv0_ref, dv1_ref, vec_ref, small_ref,
    upstay_ref, upgot_ref, downstay_ref, downgot_ref, x_hbm, dh_hbm, weight_hbm, dwo_hbm,
    dx_ref, grad_ref, total_ref,
    x_ref, dh_ref, weight_ref, rows_ref,
    dw_ref, near_ref, fromx_ref, fromy_ref, diagx_ref, diagy_ref, third_ref, chain_ref, done_ref,
    pack_ref, side_ref, sums_ref,
    near_sem, x_sem, y_sem, dx_sem, dy_sem, chain_sem, relay_sem, grad_sem, side_sem, send_sem, local_sem,
):
    z, x, y, c = place()
    m = 2 * y + c
    d = 2 * z + x
    n_dp = grad_ref.shape[0]
    right_x, right_y, partner = at(z, 1 - x, y, c), at(z, x, 1 - y, c), at(z, x, y, 1 - c)
    tokens, width = x_ref.shape
    loads = []
    for source, target in (
        (dwo_hbm, dw_ref.at[3]), (x_hbm, x_ref), (dh_hbm, dh_ref), (weight_hbm, weight_ref)
    ):
        load = pltpu.make_async_copy(source, target, local_sem.at[len(loads)])
        load.start()
        loads.append(load)
    greet([right_x, right_y, partner] + [at((z + off) % 4, x, y, c) for off in range(1, 4)])
    mail = Mail(send_sem)
    piece = pack_ref.at[0]

    edge = z % 3 == 0
    inner = z % 3 != 0
    far = z // 2
    near = 1 - far

    def relay(direction, kind, part):
        ref = chain_ref.at[direction, kind, part]
        return pltpu.make_async_remote_copy(
            src_ref=ref,
            dst_ref=ref,
            send_sem=relay_sem.at[direction, kind, part],
            recv_sem=chain_sem.at[direction, kind, part],
            device_id=at(z + 1 - 2 * direction, x, y, c),
            device_id_type=pl.DeviceIdType.MESH,
        )

    def opening(kind, part):
        chain_ref[far, kind, part] = third_ref[kind, part]
        relay(far, kind, part).start()

    def outward(kind, part):
        ref = chain_ref.at[far, kind, part]
        arrived(ref, chain_sem.at[far, kind, part])
        ref[...] = added(third_ref[kind, part], ref[...])
        relay(far, kind, part).start()

    def inward(kind, part):
        ref = chain_ref.at[near, kind, part]
        arrived(ref, chain_sem.at[near, kind, part])
        total = added(chain_ref[far, kind, part], ref[...])

        @pl.when(inner)
        def _():
            ref[...] = added(third_ref[kind, part], ref[...])
            relay(near, kind, part).start()

        return total

    def ahead(s):
        @pl.when(inner)
        def _():
            outward(1 + s // 4, s % 4)

    def keep(s):
        done_ref[s // 4, s % 4] = inward(1 + s // 4, s % 4)

    for kind, (stay_ref, got_ref) in enumerate(
        ((upstay_ref, upgot_ref), (downstay_ref, downgot_ref))
    ):
        for part in range(4):
            third_ref[1 + kind, part] = added(stay_ref[part], got_ref[part])

    @pl.when(edge)
    def _():
        def rest(s, carry):
            opening(1 + s // 4, s % 4)
            return carry

        lax.fori_loop(0, 8, rest, 0)

    pairs = ((dq0_ref, dq1_ref), (dk0_ref, dk1_ref), (dv0_ref, dv1_ref))
    half = width // PARTS
    groups = ((0, 2), (1, 3))
    share = near_ref.shape[2]
    twin = near_ref.at[0, pl.ds(0, 2)]

    def products(group):
        rows = [slice(2 * share * part, 2 * share * (part + 1)) for part in group]
        left = jnp.concatenate([n1_ref[r, :] for r in rows], axis=0)
        for index, pair in enumerate(pairs):
            out = dw_ref.at[index].reshape(width, width)
            for side, ref in enumerate(pair):
                value = dot(left, ref[...], 1, 1).astype(BF)
                for place_in, r in enumerate(rows):
                    out[r, side * half : (side + 1) * half] = value[
                        2 * share * place_in : 2 * share * (place_in + 1)
                    ]

    def pass_over(group):
        for part in group:
            for row in range(2):
                mail.send(
                    dw_ref.at[2 * row + 1 - c, pl.ds(2 * part, 2)], near_ref.at[row, pl.ds(2 * part, 2)],
                    near_sem.at[row, part], partner, twin,
                )

    def summed(group):
        for part in group:
            for row in range(2):
                arrived(twin, near_sem.at[row, part])

            def one(i, carry):
                row, e = i // 2, 2 * part + i % 2
                near_ref[row, e] = added(near_ref[row, e], dw_ref[2 * row + c, e])
                return carry

            lax.fori_loop(0, 4, one, 0)

    def issue(group):
        low, high = group
        mail.send(
            near_ref.at[1 - y, 2 * low + 1 - x], diagy_ref.at[low], dy_sem.at[low], right_y, piece
        )
        mail.send(
            near_ref.at[1 - y, 2 * high + 1 - x], diagx_ref.at[high - 2], dx_sem.at[high - 2],
            right_x, piece,
        )
        mail.send(near_ref.at[1 - y, 2 * low + x], fromy_ref.at[low], y_sem.at[low], right_y, piece)
        mail.send(near_ref.at[y, 2 * high + 1 - x], fromx_ref.at[high], x_sem.at[high], right_x, piece)

    def forward(group):
        low, high = group
        turn = high - 2
        arrived(diagy_ref.at[low], dy_sem.at[low])
        diagy_ref[low] = added(near_ref[y, 2 * low + 1 - x], diagy_ref[low])
        mail.send(diagy_ref.at[low], fromx_ref.at[low], x_sem.at[low], right_x, piece)
        arrived(diagx_ref.at[turn], dx_sem.at[turn])
        diagx_ref[turn] = added(near_ref[1 - y, 2 * high + x], diagx_ref[turn])
        mail.send(diagx_ref.at[turn], fromy_ref.at[high], y_sem.at[high], right_y, piece)

    products(groups[0])
    loads[0].wait()
    pass_over(groups[0])
    products(groups[1])
    pass_over(groups[1])
    for load in loads[1:]:
        load.wait()
    rows_ref[...] = jnp.zeros_like(rows_ref)
    flat = [weight_ref.at[index].reshape(width, width) for index in range(3)]

    def back(i, carry):
        t = pl.ds(pl.multiple_of(i * TILE, TILE), TILE)
        dn = jnp.zeros((TILE, width), F32)
        for index, pair in enumerate(pairs):
            for part, ref in enumerate(pair):
                dn += dot(ref[:, t], flat[index][:, part * half : (part + 1) * half], 0, 1)
        unit, scale = normed(x_ref[t, :].astype(F32))
        dx_ref[t, :] = dh_ref[t, :] + norm_back(dn, unit, scale, vec_ref[0:1, :])
        rows_ref[0:8, :] += fold_rows(dn * unit)
        rows_ref[8:16, :] += fold_rows(dn)
        return carry

    def gathered(part):
        arrived(fromx_ref.at[part], x_sem.at[part])
        arrived(fromy_ref.at[part], y_sem.at[part])
        third_ref[0, part] = added(near_ref[y, 2 * part + x], fromx_ref[part], fromy_ref[part])

    def wanted(e, part, first):
        second = lax.select(owner_ref[m, 2] == e, done_ref[1, part], first)
        return lax.select(owner_ref[m, 1] == e, done_ref[0, part], second)

    def close(part):
        first = inward(0, part)
        e = 2 * part + x
        pack_ref[part] = wanted(2 * z + 1 - x, part, first)
        mail.send(pack_ref.at[part], grad_ref.at[e], grad_sem.at[part], right_x, piece)
        grad_ref[e] = wanted(d, part, first)

    def begin(group):
        @pl.when(edge)
        def _():
            for part in group[::-1]:
                gathered(part)
                opening(0, part)

    def early(part):
        @pl.when(inner)
        def _():
            gathered(part)
            outward(0, part)

    def hop(index, peer):
        mail.send(
            sums_ref.at[index], side_ref.at[index], side_sem.at[index], peer, sums_ref.at[0]
        )

    def landed(index):
        arrived(side_ref.at[index], side_sem.at[index])
        sums_ref[index + 1] = sums_ref[index] + side_ref[index]

    ahead(0)
    summed(groups[0])
    issue(groups[0])
    ahead(1)
    lax.fori_loop(0, 1, back, 0)
    summed(groups[1])
    ahead(2)
    keep(0)
    forward(groups[0])
    issue(groups[1])

    def middle(i, carry):
        ahead(2 + i)
        keep(i)
        return back(i, carry)

    lax.fori_loop(1, 3, middle, 0)
    begin(groups[0])
    lax.fori_loop(3, tokens // TILE, middle, 0)

    sums_ref[0] = small_ref[...]
    sums_ref[0, 0:1, :] = jnp.sum(rows_ref[0:8, :], axis=0, keepdims=True)
    sums_ref[0, 1:2, :] = jnp.sum(rows_ref[8:16, :], axis=0, keepdims=True)
    hop(0, partner)
    forward(groups[1])
    ahead(6)
    keep(4)
    landed(0)
    hop(1, right_x)
    ahead(7)
    keep(5)
    landed(1)
    hop(2, right_y)
    begin(groups[1])
    keep(6)
    landed(2)
    for off in range(1, 4):
        mail.send(
            sums_ref.at[3], side_ref.at[3 + z], side_sem.at[3 + z], at((z + off) % 4, x, y, c),
            sums_ref.at[0],
        )
    side_ref[3 + z] = sums_ref[3]
    early(2)
    keep(7)
    early(0)
    close(2)
    early(3)
    close(0)
    early(1)
    close(3)
    close(1)
    for off in range(1, 4):
        e = (z + off) % 4
        arrived(side_ref.at[3 + e], side_sem.at[3 + e])
    total_ref[...] = (side_ref[3] + side_ref[4]) + (side_ref[5] + side_ref[6])
    for part in (2, 3, 0, 1):
        arrived(grad_ref.at[2 * part + 1 - x], grad_sem.at[part])
    mail.finish()
    for kind in range(3):
        for part in range(4):
            arrived(piece, relay_sem.at[far, kind, part])

            @pl.when(inner)
            def _():
                arrived(piece, relay_sem.at[near, kind, part])


def leave(owner, x, dh, n1, flows, vec, weights, dwo, small, rest):
    tokens, width = x.shape
    n_mlp, n_dp, share, _ = weights.shape
    smem = pl.BlockSpec(memory_space=pltpu.SMEM)
    vmem = pl.BlockSpec(memory_space=pltpu.VMEM)
    hbm = pl.BlockSpec(memory_space=pl.ANY)
    dma = pltpu.SemaphoreType.DMA
    part = lambda *lead: pltpu.VMEM(lead + (share, width), BF)
    flat = [ref for pair in flows for ref in pair]
    return pl.pallas_call(
        leave_kernel,
        in_specs=[smem] + [vmem] * 13 + [hbm] * 4,
        out_specs=[vmem] * 3,
        out_shape=[
            jax.ShapeDtypeStruct((tokens, width), F32),
            jax.ShapeDtypeStruct((n_dp, share, width), BF),
            jax.ShapeDtypeStruct(small.shape, F32),
        ],
        scratch_shapes=[
            pltpu.VMEM((tokens, width), BF),
            pltpu.VMEM((tokens, width), F32),
            part(n_mlp, n_dp),
            pltpu.VMEM((16, width), F32),
            part(n_mlp, n_dp), part(2, n_dp), part(4), part(4), part(2), part(2), part(3, 4),
            part(2, 3, 4), part(2, 4), part(4),
            pltpu.VMEM((7,) + small.shape, F32),
            pltpu.VMEM((4,) + small.shape, F32),
            dma((2, 4)), dma((4,)), dma((4,)), dma((2,)), dma((2,)), dma((2, 3, 4)), dma((2, 3, 4)),
            dma((4,)), dma((7,)), dma((32,)), dma((4,)),
        ],
        compiler_params=pltpu.CompilerParams(
            vmem_limit_bytes=VMEM_LIMIT, collective_id=2, has_side_effects=True
        ),
        name="leave",
    )(
        owner, n1, *flat, vec, small, *rest, x, dh, weights,
        dwo.reshape(n_dp, share, width),
    )


def update_kernel(
    keep_ref, decay_ref, grad_ref, left_hbm, right_hbm, lroot_hbm, rroot_hbm, master_hbm, y_hbm, dx_hbm,
    slot_out, left_out, right_out, master_out, y_out, dx_out,
    left_ref, right_ref, lroot_ref, rroot_ref, master_ref, y_ref, dx_ref, slot_ref, turn_ref,
    in_sem, out_sem,
):
    loads = []
    for source, target in (
        (left_hbm, left_ref), (right_hbm, right_ref), (lroot_hbm, lroot_ref), (rroot_hbm, rroot_ref),
        (master_hbm, master_ref), (y_hbm, y_ref), (dx_hbm, dx_ref),
    ):
        loads.append(pltpu.make_async_copy(source, target, in_sem.at[len(loads)]))
        loads[-1].start()
    outs = []

    def emit(source, target):
        outs.append(pltpu.make_async_copy(source, target, out_sem.at[len(outs)]))
        outs[-1].start()

    held = keep_ref[0] != 0
    decay = decay_ref[0]
    width = grad_ref.shape[0]
    tall = width // 3

    def strip(i):
        return pl.ds(pl.multiple_of(i * tall, tall), tall)

    @pl.when(held)
    def _():
        slot_ref[...] = grad_ref[...].astype(F32)

    @pl.when(jnp.logical_not(held))
    def _():
        slot_ref[...] = jnp.zeros_like(slot_ref)

    emit(slot_ref, slot_out)
    loads[0].wait()

    @pl.when(held)
    def _():
        def rows(i, carry):
            r = strip(i)
            gram = dot(grad_ref[r, :], grad_ref[...], 1, 1)
            left_ref[r, :] = decay * left_ref[r, :] + (1.0 - decay) * gram
            return carry

        lax.fori_loop(0, 3, rows, 0)

    emit(left_ref, left_out)
    loads[1].wait()

    @pl.when(held)
    def _():
        turn_ref[...] = grad_ref[...].T

        def rows(i, carry):
            r = strip(i)
            gram = dot(turn_ref[r, :], grad_ref[...], 1, 0)
            right_ref[r, :] = decay * right_ref[r, :] + (1.0 - decay) * gram
            return carry

        lax.fori_loop(0, 3, rows, 0)

    emit(right_ref, right_out)
    for index, source, target in ((5, y_ref, y_out), (6, dx_ref, dx_out)):
        loads[index].wait()
        emit(source, target)
    for load in loads[2:5]:
        load.wait()

    @pl.when(held)
    def _():
        turn_ref[...] = rroot_ref[...].astype(BF)

        def rows(i, total):
            r = strip(i)
            inner = dot(lroot_ref[r, :].astype(BF), grad_ref[...], 1, 0).astype(BF)
            direction = dot(inner, turn_ref[...], 1, 0)
            lroot_ref[r, :] = direction
            return total + jnp.sum(direction * direction, axis=0, keepdims=True)

        total = jnp.sum(lax.fori_loop(0, 3, rows, jnp.zeros((1, width), F32)), keepdims=True)
        mean = total * (1.0 / (width * width))
        master_ref[...] -= lroot_ref[...] * (RATE_MATRIX * lax.rsqrt(mean + GRAFT_EPSILON))

    emit(master_ref, master_out)
    for copy in outs:
        copy.wait()


def update(owns, decays, grad, left, right, lroot, rroot, master, output, input_grad):
    smem = pl.BlockSpec(memory_space=pltpu.SMEM)
    vmem = pl.BlockSpec(memory_space=pltpu.VMEM)
    hbm = pl.BlockSpec(memory_space=pl.ANY)
    shape = lambda a: jax.ShapeDtypeStruct(a.shape, a.dtype)
    room = lambda a: pltpu.VMEM(a.shape, a.dtype)
    return pl.pallas_call(
        update_kernel,
        in_specs=[smem, smem, vmem] + [hbm] * 7,
        out_specs=[hbm] * 6,
        out_shape=[shape(a) for a in (left, left, right, master, output, input_grad)],
        scratch_shapes=[room(a) for a in (left, right, lroot, rroot, master, output, input_grad, left, grad)]
        + [pltpu.SemaphoreType.DMA((7,)), pltpu.SemaphoreType.DMA((6,))],
        compiler_params=pltpu.CompilerParams(vmem_limit_bytes=VMEM_LIMIT),
        name="update",
    )(owns, decays, grad, left, right, lroot, rroot, master, output, input_grad)


def positions(segment, heights, widths, patch_rows, patch_cols):
    images = heights.shape[0]
    matches = segment[None, :] == jnp.arange(images, dtype=jnp.int32)[:, None]
    tall = jnp.sum(jnp.where(matches, heights[:, None], 0), axis=0).astype(F32)
    wide = jnp.sum(jnp.where(matches, widths[:, None], 0), axis=0).astype(F32)
    py = patch_rows.astype(F32) * GRID_BASE / tall
    px = patch_cols.astype(F32) * GRID_BASE / wide
    zero = jnp.zeros_like(px)
    return jnp.stack([px, py, segment.astype(F32), zero, zero, zero, zero, zero])


def local(
    tokens, cotangent, vectors, vector_moments, decays, owner, master_slots, left_slots,
    right_slots, left_roots, right_roots, grid_height, grid_width, patch_rows, patch_cols, segment,
):
    dp_index = lax.axis_index("dp")
    mlp_index = lax.axis_index("mlp")
    n_dp = lax.axis_size("dp")
    n_mlp = lax.axis_size("mlp")
    width = tokens.shape[1]
    share = width // n_dp
    owner_row = jnp.take(owner, mlp_index, axis=0)
    holds = owner_row == dp_index
    owns = jnp.any(holds).astype(jnp.int32).reshape(1)
    master = master_slots[0, 0]
    turned = vectors.T
    pos = positions(segment, grid_height, grid_width, patch_rows, patch_cols)
    direct = n_dp == 8 and n_mlp == 4
    if direct:
        n1t, q, k, v, cosine, sine, qmark, kmark, attention, zone = enter(
            owner, master.reshape(n_dp, share, width), tokens, pos, vectors, turned
        )
        over_x = [(i, i ^ 1) for i in range(n_dp)]
        over_y = [(i, i ^ 2) for i in range(n_mlp)]
        xzone = lax.ppermute(zone, "dp", over_x)
        yzone = lax.ppermute(zone, "mlp", over_y)
    else:
        slot = master.astype(BF).reshape(n_dp, share, width)
        pieces = lax.all_to_all(slot, "dp", 0, 0, tiled=True)
        mine = jnp.take(pieces, owner_row, axis=0)
        every = lax.all_gather(mine[None], ("dp", "mlp"), axis=0, tiled=True)
        blocks = every.reshape(n_dp, n_mlp, 3, share, width).transpose(2, 1, 0, 3, 4)
        attention, up, down = blocks.reshape(3, n_mlp, width, width)
        n1t, q, k, v, cosine, sine, qmark, kmark = project(tokens, pos, vectors, turned, attention)
    o, log_totals = attend(grid_height, grid_width, q, k, v, qmark, kmark)
    fine = (n_mlp, n_dp, share, width)
    back = functools.partial(attend_back, grid_height, grid_width)
    if direct:
        output, dh, do, dwo, mid_rows, dc, upgo, upstay, downgo, downstay = center(
            tokens, cotangent, o, vectors, attention, zone, xzone, yzone
        )
        upgot = lax.ppermute(upgo, "dp", over_x)
        downgot = lax.ppermute(downgo, "mlp", over_y)
        first = back(q, k, v, qmark, kmark, log_totals, do, pos, cosine, sine, 0)
        first, upgot, downgot = lax.optimization_barrier((first, upgot, downgot))
        upgo, upstay, downgo, downstay = merge(upstay, upgot, downstay, downgot)
        upgot = lax.ppermute(upgo, "mlp", over_y)
        downgot = lax.ppermute(downgo, "dp", over_x)
        do, upstay, downstay = lax.optimization_barrier((do, upstay, downstay))
    else:
        output, dh, do, dwo, dup, ddown, mid_rows, dc = middle_part(
            tokens, cotangent, o, vectors, attention[3], up, down
        )
        first = back(q, k, v, qmark, kmark, log_totals, do, pos, cosine, sine, 0)
    second = back(q, k, v, qmark, kmark, log_totals, do, pos, cosine, sine, 1)
    both = list(zip(first, second))
    freq = jnp.concatenate(both[3], axis=1)[0:2].reshape(1, width)
    bias = jnp.concatenate(both[4], axis=1)[0::8]
    eights = lambda rows: jnp.sum(rows.reshape(-1, 8, width), axis=1)
    mid = eights(mid_rows)
    tail = [bias, mid[0:3], dc[:, 0, :], mid[3:4], freq]
    if direct:
        small = jnp.concatenate([jnp.zeros((2, width), F32)] + tail, axis=0)
        input_grad, gradient, total = leave(
            owner, tokens, dh, n1t, both[0:3], vectors, attention.reshape(fine), dwo, small,
            (upstay, upgot, downstay, downgot),
        )
    else:
        dq, dk, dv = (jnp.concatenate(pair, axis=0) for pair in both[0:3])
        input_grad, datt, fin_rows = final_part(
            tokens, dh, n1t, dq, dk, dv, vectors, attention, dwo
        )
        grads = jnp.stack([datt, dup, ddown], axis=1)
        grads = grads.reshape(n_mlp, 3, n_dp, share, width).transpose(2, 0, 1, 3, 4)
        grads = grads.reshape(n_dp * n_mlp * 3, share, width)
        reduced = lax.psum_scatter(grads, ("dp", "mlp"), scatter_dimension=0, tiled=True)
        takers = owner_row[None, :] == jnp.arange(n_dp, dtype=jnp.int32)[:, None]
        kind_of = jnp.sum(jnp.where(takers, jnp.arange(3, dtype=jnp.int32)[None, :], 0), axis=1)
        gradient = lax.all_to_all(jnp.take(reduced, kind_of, axis=0), "dp", 0, 0, tiled=True)
        total = lax.psum(jnp.concatenate([eights(fin_rows)] + tail, axis=0), ("dp", "mlp"))
    gradient = gradient.reshape(width, width)
    slot_grad, left_out, right_out, master_out, output, input_grad = update(
        owns, decays, gradient, left_slots[0, 0], right_slots[0, 0], left_roots[0, 0],
        right_roots[0, 0], master, output, input_grad,
    )

    cut = width // n_mlp
    own = lambda table: lax.dynamic_slice_in_dim(table, mlp_index * cut, cut, 1)
    grad_share = own(total)
    decay = decays[1]
    moment_next = decay * own(vector_moments) + (1.0 - decay) * grad_share * grad_share
    vector_next = own(vectors) - RATE_VECTOR * grad_share / (jnp.sqrt(moment_next) + STEP_EPSILON)
    lift = lambda a: a[None, None]
    return (
        output, input_grad, lift(slot_grad), lift(left_out), lift(right_out), lift(master_out),
        grad_share, moment_next, vector_next,
    )


def solution(mesh):
    both = P(("dp", "mlp"))
    flat = P(("dp", "mlp"), None)
    slots = P("dp", "mlp", None, None)
    split = P(None, "mlp")
    return jax.shard_map(
        local,
        mesh=mesh,
        in_specs=(flat, flat, P(), P(), P(), P(), slots, slots, slots, slots, slots)
        + (both,) * 5,
        out_specs=(flat, flat, slots, slots, slots, slots, split, split, split),
        check_vma=False,
    )
```

```python
import functools
import math

import jax
import jax.numpy as jnp
from jax import lax
from jax.experimental import pallas as pl
from jax.experimental.pallas import tpu as pltpu
from jax.sharding import PartitionSpec as P

HEADS = 12
GRID_BASE = 16
NORM_EPSILON = 1e-06
GRAFT_EPSILON = 1e-06
STEP_EPSILON = 1e-08
RATE_MATRIX = 0.04
RATE_VECTOR = 0.02
MASK_SHIFT = -(2.0**100)
BLOCK = 128
TILE = 256
PARTS = 2
WINDOW = 6
F32 = jnp.float32
BF = jnp.bfloat16
VMEM_LIMIT = 60 * 1024 * 1024


def dot(left, right, left_dim, right_dim, precision=None):
    return lax.dot_general(
        left,
        right,
        (((left_dim,), (right_dim,)), ((), ())),
        preferred_element_type=F32,
        precision=precision,
    )


def normed(values):
    mean = jnp.mean(values, axis=-1, keepdims=True)
    centred = values - mean
    spread = jnp.mean(centred * centred, axis=-1, keepdims=True)
    scale = lax.rsqrt(spread + NORM_EPSILON)
    return centred * scale, scale


def norm_back(grad, unit, scale, gain):
    scaled = grad * gain
    first = jnp.mean(scaled, axis=-1, keepdims=True)
    second = jnp.mean(scaled * unit, axis=-1, keepdims=True)
    return scale * (scaled - first - unit * second)


def fold_rows(values):
    return jnp.sum(values.reshape(values.shape[0] // 8, 8, values.shape[1]), axis=0)


def place():
    d = lax.axis_index("dp")
    m = lax.axis_index("mlp")
    return d // 2, d % 2, m // 2, m % 2


def at(z, x, y, c):
    return (2 * z + x, 2 * y + c)


def greet(peers):
    barrier = pltpu.get_barrier_semaphore()
    for peer in peers:
        pl.semaphore_signal(barrier, inc=1, device_id=peer, device_id_type=pl.DeviceIdType.MESH)
    pl.semaphore_wait(barrier, len(peers))


class Mail:
    def __init__(self, sems):
        self.sems = sems
        self.like = []

    def send(self, source, target, arrival, peer, like):
        slot = len(self.like)
        pltpu.make_async_remote_copy(
            src_ref=source,
            dst_ref=target,
            send_sem=self.sems.at[slot],
            recv_sem=arrival,
            device_id=peer,
            device_id_type=pl.DeviceIdType.MESH,
        ).start()
        self.like.append(like)
        return slot

    def settle(self, slot):
        arrived(self.like[slot], self.sems.at[slot])
        self.like[slot] = None

    def finish(self):
        for slot, like in enumerate(self.like):
            if like is not None:
                self.settle(slot)


def arrived(target, arrival):
    pltpu.make_async_copy(target, target, arrival).wait()


def enter_kernel(
    owner_ref, height_ref, width_ref, slot_hbm, x_ref, seg_ref, patch_rows_ref, patch_cols_ref, vec_ref,
    n1_ref, q_ref, k_ref, v_ref, cos_ref, sin_ref, qmark_ref, kmark_ref, pos_ref, weight_ref, zone_ref,
    wide_ref, turned_ref, raw_ref, slot_ref, cross_ref, chain_ref, att_ref, zland_ref,
    cross_sem, chain_sem, relay_sem, att_sem, send_sem, local_sem,
):
    z, x, y, c = place()
    m = 2 * y + c
    n_dp = slot_ref.shape[0]
    right_x, right_y, partner = at(z, 1 - x, y, c), at(z, x, 1 - y, c), at(z, x, y, 1 - c)
    own = pltpu.make_async_copy(slot_hbm, raw_ref, local_sem.at[0])
    own.start()
    greet([right_x, right_y, partner, at((z + 1) % 4, x, y, c), at((z + 3) % 4, x, y, c)])
    mail = Mail(send_sem)
    piece = slot_ref.at[0]
    own.wait()
    for part in range(4):
        e = 2 * part + 1 - x
        slot_ref[e] = raw_ref[e].astype(BF)
        mail.send(slot_ref.at[e], cross_ref.at[part], cross_sem.at[part], right_x, piece)
    for part in range(4):
        e = 2 * part + x
        slot_ref[e] = raw_ref[e].astype(BF)

    tokens = x_ref.shape[0]
    half = cos_ref.shape[0]
    last = vec_ref.shape[0] - 1
    tiles = tokens // TILE
    wide_ref[...] = jnp.zeros_like(wide_ref)
    wide_ref[0 : last + 1, :] = vec_ref[...]
    turned_ref[...] = wide_ref[...].T
    tall = jnp.zeros(seg_ref.shape, F32)
    broad = jnp.zeros(seg_ref.shape, F32)
    for image in range(height_ref.shape[0]):
        match = seg_ref[...] == image
        tall = jnp.where(match, height_ref[image].astype(F32), tall)
        broad = jnp.where(match, width_ref[image].astype(F32), broad)
    pos_ref[...] = jnp.zeros_like(pos_ref)
    pos_ref[0:1, :] = patch_cols_ref[...].astype(F32) * GRID_BASE / broad
    pos_ref[1:2, :] = patch_rows_ref[...].astype(F32) * GRID_BASE / tall
    pos_ref[2:3, :] = seg_ref[...].astype(F32)

    def prepare(i, carry):
        t = pl.ds(pl.multiple_of(i * TILE, TILE), TILE)
        unit, _ = normed(x_ref[t, :].astype(F32))
        n1_ref[:, t] = (unit * vec_ref[0:1, :] + vec_ref[1:2, :]).astype(BF).T
        angle = turned_ref[half:, last : last + 1] * pos_ref[1:2, t] + turned_ref[:half, last : last + 1] * pos_ref[0:1, t]
        cos_ref[:, t] = jnp.cos(angle)
        sin_ref[:, t] = jnp.sin(angle)
        seg = pos_ref[2:3, t].astype(jnp.int32)
        row = lax.broadcasted_iota(jnp.int32, (qmark_ref.shape[0], TILE), 0)
        qmark_ref[:, t] = jnp.where(row == seg, 1.0, 0.0).astype(BF)
        kmark_ref[:, t] = jnp.where(row == seg, 0.0, MASK_SHIFT).astype(BF)
        return carry

    lax.fori_loop(0, tiles // 2, prepare, 0)

    edge = z % 3 == 0
    inner = z % 3 != 0
    far = z // 2
    near = 1 - far

    def relay(direction, kind, part):
        ref = chain_ref.at[direction, kind, part]
        return pltpu.make_async_remote_copy(
            src_ref=ref,
            dst_ref=ref,
            send_sem=relay_sem.at[direction, kind, part],
            recv_sem=chain_sem.at[direction, kind, part],
            device_id=at(z + 1 - 2 * direction, x, y, c),
            device_id_type=pl.DeviceIdType.MESH,
        )

    def merged(direction, kind, part, opening):
        ref = chain_ref.at[direction, kind, part]
        home = owner_ref[m, kind]
        value = lax.select(home % 2 == x, slot_ref[2 * part + x], cross_ref[part])
        if not opening:
            arrived(ref, chain_sem.at[direction, kind, part])
            value = lax.select(home // 2 == z, value, ref[...])
        ref[...] = value

    def crossed(part):
        arrived(cross_ref.at[part], cross_sem.at[part])

    def outward(kind, part):
        merged(far, kind, part, False)
        relay(far, kind, part).start()

    def inward(kind, part):
        merged(near, kind, part, False)

        @pl.when(inner)
        def _():
            relay(near, kind, part).start()

        return lax.select(
            owner_ref[m, kind] // 2 <= z, chain_ref[0, kind, part], chain_ref[1, kind, part]
        )

    def bring(part):
        e = 2 * part + x
        att_ref[m, e] = inward(0, part)
        for peer in (right_x, right_y, partner):
            mail.send(att_ref.at[m, e], att_ref.at[m, e], att_sem.at[m, e], peer, piece)

    @pl.when(edge)
    def _():
        def opening(part, carry):
            crossed(part)
            merged(far, 0, part, True)
            relay(far, 0, part).start()
            return carry

        lax.fori_loop(0, 4, opening, 0)

        def rest(s, carry):
            merged(far, 1 + s // 4, s % 4, True)
            relay(far, 1 + s // 4, s % 4).start()
            return carry

        lax.fori_loop(0, 8, rest, 0)

    def early(part):
        @pl.when(inner)
        def _():
            crossed(part)
            outward(0, part)

    def ahead(s):
        @pl.when(inner)
        def _():
            outward(1 + s // 4, s % 4)

    def keep(s):
        zland_ref[s // 4, s % 4] = inward(1 + s // 4, s % 4)

    m_y = 2 * (1 - y) + c

    def spread(part):
        e = 2 * part + 1 - x
        arrived(att_ref.at[m, e], att_sem.at[m, e])
        if part < 2:
            mail.send(att_ref.at[m, e], att_ref.at[m, e], att_sem.at[m, e], right_y, piece)
        mail.send(att_ref.at[m, e], att_ref.at[m, e], att_sem.at[m, e], partner, piece)
        f = 2 * part + x
        arrived(att_ref.at[m_y, f], att_sem.at[m_y, f])
        if part >= 2:
            mail.send(att_ref.at[m_y, f], att_ref.at[m_y, f], att_sem.at[m_y, f], right_x, piece)
        mail.send(att_ref.at[m_y, f], att_ref.at[m_y, f], att_sem.at[m_y, f], partner, piece)

    early(0)
    early(1)
    bring(0)
    early(2)
    bring(1)
    early(3)
    bring(2)
    ahead(0)
    spread(0)
    bring(3)
    ahead(1)
    spread(1)
    ahead(2)
    keep(0)
    lax.fori_loop(tiles // 2, tiles, prepare, 0)
    spread(2)
    ahead(3)
    keep(1)
    spread(3)
    ahead(4)
    keep(2)
    for part in range(4):
        e = 2 * part + 1 - x
        arrived(att_ref.at[m_y, e], att_sem.at[m_y, e])
        mail.send(att_ref.at[m_y, e], att_ref.at[m_y, e], att_sem.at[m_y, e], partner, piece)
    for step in range(2):
        other = 2 * step + 1 - c
        for e in range(n_dp):
            arrived(att_ref.at[other, e], att_sem.at[other, e])
    out = pltpu.make_async_copy(att_ref, weight_ref, local_sem.at[1])
    out.start()

    part = half // HEADS
    width = x_ref.shape[1]

    def weight(index):
        return att_ref[index].reshape(width, width)

    def rotate(i, carry):
        @pl.when(i < 3)
        def _():
            ahead(5 + i)

        keep(3 + i)
        t = pl.ds(pl.multiple_of(i * TILE, TILE), TILE)
        n1t = n1_ref[:, t]
        cosine = cos_ref[:, t]
        sine = sin_ref[:, t]
        for index, (ref, scale) in enumerate(((q_ref, 0.125), (k_ref, 1.0))):
            flat = dot(weight(index), n1t, 0, 0) + turned_ref[:, 2 + index : 3 + index]
            for head in range(HEADS):
                low, mid = 2 * part * head, 2 * part * head + part
                a = flat[low:mid]
                b = flat[mid : mid + part]
                cs = cosine[part * head : part * (head + 1)]
                sn = sine[part * head : part * (head + 1)]
                ref[low:mid, t] = (a * cs - b * sn).astype(BF) * jnp.asarray(scale, BF)
                ref[mid : mid + part, t] = (b * cs + a * sn).astype(BF) * jnp.asarray(scale, BF)
        v_ref[:, t] = (dot(weight(2), n1t, 0, 0) + turned_ref[:, 4:5]).astype(BF)
        return carry

    lax.fori_loop(0, tiles, rotate, 0)
    keep(7)
    last_out = pltpu.make_async_copy(zland_ref, zone_ref, local_sem.at[2])
    last_out.start()
    mail.finish()
    for kind in range(3):
        for step in range(4):
            arrived(piece, relay_sem.at[far, kind, step])

            @pl.when(inner)
            def _():
                arrived(piece, relay_sem.at[near, kind, step])

    out.wait()
    last_out.wait()


def enter(owner, heights, widths, slot, x, segment, patch_rows, patch_cols, vec):
    rows, width = x.shape
    half = width // 2
    n_dp, share, _ = slot.shape
    n_mlp = owner.shape[0]
    smem = pl.BlockSpec(memory_space=pltpu.SMEM)
    vmem = pl.BlockSpec(memory_space=pltpu.VMEM)
    hbm = pl.BlockSpec(memory_space=pl.ANY)
    out = lambda n, dtype: jax.ShapeDtypeStruct((n, rows), dtype)
    return pl.pallas_call(
        enter_kernel,
        in_specs=[smem, smem, smem, hbm] + [vmem] * 5,
        out_specs=[vmem] * 9 + [hbm] * 2,
        out_shape=[out(width, BF)] * 4
        + [out(half, F32)] * 2
        + [out(16, BF)] * 2
        + [out(8, F32)]
        + [
            jax.ShapeDtypeStruct((n_mlp, n_dp, share, width), BF),
            jax.ShapeDtypeStruct((2, 4, share, width), BF),
        ],
        scratch_shapes=[
            pltpu.VMEM((16, width), F32),
            pltpu.VMEM((width, 16), F32),
            pltpu.VMEM((n_dp, share, width), F32),
            pltpu.VMEM((n_dp, share, width), BF),
            pltpu.VMEM((4, share, width), BF),
            pltpu.VMEM((2, 3, 4, share, width), BF),
            pltpu.VMEM((n_mlp, n_dp, share, width), BF),
            pltpu.VMEM((2, 4, share, width), BF),
            pltpu.SemaphoreType.DMA((4,)),
            pltpu.SemaphoreType.DMA((2, 3, 4)),
            pltpu.SemaphoreType.DMA((2, 3, 4)),
            pltpu.SemaphoreType.DMA((n_mlp, n_dp)),
            pltpu.SemaphoreType.DMA((48,)),
            pltpu.SemaphoreType.DMA((3,)),
        ],
        compiler_params=pltpu.CompilerParams(
            vmem_limit_bytes=31 * 1024 * 1024, collective_id=0, has_side_effects=True
        ),
        name="enter",
    )(
        owner, heights, widths, slot, x,
        *(a.reshape(1, rows) for a in (segment, patch_rows, patch_cols)), vec,
    )


def project_kernel(
    x_ref, pos_ref, vec_ref, turned_ref, weight_ref,
    n1_ref, q_ref, k_ref, v_ref, cos_ref, sin_ref, qmark_ref, kmark_ref,
):
    unit, _ = normed(x_ref[...].astype(F32))
    n1 = (unit * vec_ref[0:1, :] + vec_ref[1:2, :]).astype(BF)
    n1t = n1.T
    n1_ref[...] = n1t
    px = pos_ref[0:1, :]
    py = pos_ref[1:2, :]
    half = cos_ref.shape[0]
    last = turned_ref.shape[1] - 1
    angle = turned_ref[half:, last:] * py + turned_ref[:half, last:] * px
    cosine = jnp.cos(angle)
    sine = jnp.sin(angle)
    cos_ref[...] = cosine
    sin_ref[...] = sine
    seg = pos_ref[2:3, :].astype(jnp.int32)
    row = lax.broadcasted_iota(jnp.int32, qmark_ref.shape, 0)
    qmark_ref[...] = jnp.where(row == seg, 1.0, 0.0).astype(BF)
    kmark_ref[...] = jnp.where(row == seg, 0.0, MASK_SHIFT).astype(BF)
    part = half // HEADS
    for index, (out, scale) in enumerate(((q_ref, 0.125), (k_ref, 1.0))):
        flat = dot(weight_ref[index], n1t, 0, 0) + turned_ref[:, 2 + index : 3 + index]
        for head in range(HEADS):
            low, mid = 2 * part * head, 2 * part * head + part
            a = flat[low:mid]
            b = flat[mid : mid + part]
            c = cosine[part * head : part * (head + 1)]
            s = sine[part * head : part * (head + 1)]
            out[low:mid, :] = (a * c - b * s).astype(BF) * jnp.asarray(scale, BF)
            out[mid : mid + part, :] = (b * c + a * s).astype(BF) * jnp.asarray(scale, BF)
    v_ref[...] = (dot(weight_ref[2], n1t, 0, 0) + turned_ref[:, 4:5]).astype(BF)


def project(x, pos, vec, turned, weights):
    rows, width = x.shape
    half = width // 2
    whole = lambda a: pl.BlockSpec(a.shape, lambda i: (0,) * a.ndim)
    col = lambda n: pl.BlockSpec((n, TILE), lambda i: (0, i))
    out = lambda n, d: jax.ShapeDtypeStruct((n, rows), d)
    return pl.pallas_call(
        project_kernel,
        grid=(rows // TILE,),
        in_specs=[
            pl.BlockSpec((TILE, width), lambda i: (i, 0)),
            col(8),
            whole(vec),
            whole(turned),
            whole(weights),
        ],
        out_specs=[col(width)] * 4 + [col(half)] * 2 + [col(16)] * 2,
        out_shape=[out(width, BF)] * 4 + [out(half, F32)] * 2 + [out(16, BF)] * 2,
        compiler_params=pltpu.CompilerParams(vmem_limit_bytes=VMEM_LIMIT),
        name="project",
    )(x, pos, vec, turned, weights)


def key_window(height_ref, width_ref, block):
    first = block * BLOCK
    last = first + BLOCK - 1
    start = jnp.int32(0)
    low = jnp.int32(0)
    high = jnp.int32(0)
    for image in range(height_ref.shape[0]):
        end = start + height_ref[image] * width_ref[image]
        low = jnp.where((start <= first) & (first < end), start, low)
        high = jnp.where((start <= last) & (last < end), end, high)
        start = end
    base = low // BLOCK
    return base, (high + BLOCK - 1) // BLOCK - base


def attend_kernel(height_ref, width_ref, q_ref, k_ref, v_ref, qmark_ref, kmark_ref, o_ref, log_ref):
    tokens = q_ref.shape[1]
    blocks = tokens // BLOCK
    size = q_ref.shape[0] // HEADS
    group = 4

    def one(block, part, base, count):
        here = pl.ds(pl.multiple_of(block * BLOCK, BLOCK), BLOCK)
        keys = pl.ds(pl.multiple_of(base * BLOCK, BLOCK), BLOCK * count)
        qmark = qmark_ref[:, here]
        kmark = kmark_ref[:, keys]
        for j in range(group):
            head = part * group + j
            rows = pl.ds(pl.multiple_of(head * size, size), size)
            q = jnp.concatenate([q_ref[rows, here], qmark], axis=0)
            k = jnp.concatenate([k_ref[rows, keys], kmark], axis=0)
            scores = dot(k, q, 0, 0)
            peak = jnp.max(scores, axis=0, keepdims=True)
            powers = jnp.exp(scores - peak)
            total = jnp.sum(powers, axis=0, keepdims=True)
            mixed = dot(v_ref[rows, keys], powers.astype(BF), 1, 0)
            o_ref[rows, here] = (mixed * (1.0 / total)).astype(BF)
            log_ref[pl.ds(pl.multiple_of(head * 8, 8), 8), here] = jnp.broadcast_to(
                peak + jnp.log(total), (8, BLOCK)
            )

    def step(block, carry):
        base, count = key_window(height_ref, width_ref, block)
        for n in range(1, min(blocks, WINDOW) + 1):

            @pl.when(count == n)
            def _():
                def inner(part, c):
                    one(block, part, base, n)
                    return c

                lax.fori_loop(0, HEADS // group, inner, 0)

        return carry

    lax.fori_loop(0, blocks, step, 0)


def attend(heights, widths, q, k, v, qmark, kmark):
    smem = pl.BlockSpec(memory_space=pltpu.SMEM)
    vmem = pl.BlockSpec(memory_space=pltpu.VMEM)
    return pl.pallas_call(
        attend_kernel,
        in_specs=[smem, smem] + [vmem] * 5,
        out_specs=[vmem, vmem],
        out_shape=[
            jax.ShapeDtypeStruct(q.shape, BF),
            jax.ShapeDtypeStruct((8 * HEADS, q.shape[1]), F32),
        ],
        compiler_params=pltpu.CompilerParams(vmem_limit_bytes=9 * 1024 * 1024),
        name="attend",
    )(heights, widths, q, k, v, qmark, kmark)


def attend_back_kernel(
    height_ref, width_ref, q_ref, k_ref, v_ref, qmark_ref, kmark_ref, log_ref, do_ref,
    pos_ref, cos_ref, sin_ref,
    dq_ref, dk_ref, dv_ref, freq_ref, bias_ref,
    gq_ref, gk_ref, gv_ref, turn_ref,
):
    tokens = q_ref.shape[1]
    blocks = tokens // BLOCK
    heads = log_ref.shape[0] // 8
    size = q_ref.shape[0] // heads
    half = size // 2
    group = 2
    gk_ref[...] = jnp.zeros_like(gk_ref)
    gv_ref[...] = jnp.zeros_like(gv_ref)

    def one(block, part, base, count):
        here = pl.ds(pl.multiple_of(block * BLOCK, BLOCK), BLOCK)
        keys = pl.ds(pl.multiple_of(base * BLOCK, BLOCK), BLOCK * count)
        qmark = qmark_ref[:, here]
        kmark = kmark_ref[:, keys]
        for j in range(group):
            head = part * group + j
            rows = pl.ds(pl.multiple_of(head * size, size), size)
            q = q_ref[rows, here]
            k = k_ref[rows, keys]
            do = do_ref[rows, here]
            scores = dot(
                jnp.concatenate([k, kmark], axis=0), jnp.concatenate([q, qmark], axis=0), 0, 0
            )
            log_row = log_ref[pl.ds(pl.multiple_of(head * 8, 8), 8), here][0:1]
            probs = jnp.exp(scores - log_row)
            dp = dot(v_ref[rows, keys], do, 0, 0)
            inner = jnp.sum(probs * dp, axis=0, keepdims=True)
            ds = (probs * (dp - inner)).astype(BF)
            gq_ref[rows, here] = dot(k, ds, 1, 0) * 0.125
            gk_ref[rows, keys] += dot(q, ds, 1, 1)
            gv_ref[rows, keys] += dot(do, probs.astype(BF), 1, 1)

    def step(block, carry):
        base, count = key_window(height_ref, width_ref, block)
        for n in range(1, min(blocks, WINDOW) + 1):

            @pl.when(count == n)
            def _():
                def inner(part, c):
                    one(block, part, base, n)
                    return c

                lax.fori_loop(0, heads // group, inner, 0)

        return carry

    lax.fori_loop(0, blocks, step, 0)

    def unturn(head, carry):
        low = pl.ds(pl.multiple_of(head * size, size), half)
        high = pl.ds(pl.multiple_of(head * size + half, half), half)
        table = pl.ds(pl.multiple_of(head * half, half), half)
        c = cos_ref[table, :]
        s = sin_ref[table, :]
        turn = None
        for grad_ref, rot_ref, scale, out_ref in (
            (gq_ref, q_ref, 8.0, dq_ref),
            (gk_ref, k_ref, 1.0, dk_ref),
        ):
            ga = grad_ref[low, :]
            gb = grad_ref[high, :]
            out_ref[low, :] = (ga * c + gb * s).astype(BF)
            out_ref[high, :] = (gb * c - ga * s).astype(BF)
            ra = rot_ref[low, :].astype(F32) * scale
            rb = rot_ref[high, :].astype(F32) * scale
            piece = gb * ra - ga * rb
            turn = piece if turn is None else turn + piece
        turn_ref[table, :] = turn
        both = pl.ds(pl.multiple_of(head * size, size), size)
        dv_ref[both, :] = gv_ref[both, :].astype(BF)
        return carry

    lax.fori_loop(0, heads, unturn, 0)
    freq_ref[...] = dot(pos_ref[...], turn_ref[...], 1, 1, lax.Precision.HIGHEST)
    ones = jnp.ones((8, tokens), BF)
    for index, ref in enumerate((dq_ref, dk_ref, dv_ref)):
        bias_ref[8 * index : 8 * index + 8, :] = dot(ones, ref[...], 1, 1)


def attend_back(heights, widths, q, k, v, qmark, kmark, log_totals, do, pos, cosine, sine, part):
    smem = pl.BlockSpec(memory_space=pltpu.SMEM)
    width, tokens = q.shape
    half = width // PARTS
    cut = lambda a: pl.BlockSpec((a.shape[0] // PARTS, tokens), lambda i: (part, 0))
    whole = lambda a: pl.BlockSpec(a.shape, lambda i: (0, 0))
    out = lambda n, cols, dtype: jax.ShapeDtypeStruct((n, cols), dtype)
    outs = [out(half, tokens, BF)] * 3 + [out(8, half // 2, F32), out(24, half, F32)]
    return pl.pallas_call(
        attend_back_kernel,
        grid=(1,),
        in_specs=[smem, smem, cut(q), cut(k), cut(v), whole(qmark), whole(kmark), cut(log_totals)]
        + [cut(do), whole(pos), cut(cosine), cut(sine)],
        out_specs=[whole(a) for a in outs],
        out_shape=outs,
        scratch_shapes=[pltpu.VMEM((half, tokens), F32)] * 3
        + [pltpu.VMEM((half // 2, tokens), F32)],
        compiler_params=pltpu.CompilerParams(vmem_limit_bytes=18 * 1024 * 1024),
        name="attend_back",
    )(heights, widths, q, k, v, qmark, kmark, log_totals, do, pos, cosine, sine)


def middle_kernel(
    x_ref, g_ref, o_ref, vec_ref, wo_ref, up_ref, down_ref,
    y_ref, dh_ref, do_ref, dwo_ref, dup_ref, ddown_ref, rows_ref, dc_ref,
    h_ref, n2_ref, n2t_ref, acc_ref, dn_ref, a_ref, dz_ref, dr_ref,
):
    groups = vec_ref.shape[0] - 10
    step = pl.program_id(0)
    tokens, width = x_ref.shape
    tiles = tokens // TILE

    def tile(i):
        return pl.ds(pl.multiple_of(i * TILE, TILE), TILE)

    @pl.when(step == 0)
    def _():
        def first(i, c):
            t = tile(i)
            branch = dot(o_ref[:, t], wo_ref[...], 0, 0) + vec_ref[5:6, :]
            h = x_ref[t, :].astype(F32) + branch
            h_ref[t, :] = h
            unit, _ = normed(h)
            n2 = (unit * vec_ref[6:7, :] + vec_ref[7:8, :]).astype(BF)
            n2_ref[t, :] = n2
            n2t_ref[:, t] = n2.T
            acc_ref[t, :] = h + vec_ref[8 + groups : 9 + groups, :]
            dn_ref[t, :] = jnp.zeros((TILE, width), F32)
            return c

        lax.fori_loop(0, tiles, first, 0)

    up_bias = vec_ref[pl.ds(8 + step, 1), :]

    def second(i, c):
        t = tile(i)
        z = dot(n2_ref[t, :], up_ref[0], 1, 0) + up_bias
        cdf = 0.5 * (1.0 + lax.erf(z * math.sqrt(0.5)))
        a = (z * cdf).astype(BF)
        a_ref[t, :] = a
        acc_ref[t, :] += dot(a, down_ref[0], 1, 0)
        da = dot(g_ref[t, :], down_ref[0], 1, 1)
        slope = cdf + z * (jnp.exp(-0.5 * z * z) * (1.0 / math.sqrt(2.0 * math.pi)))
        dz = (da * slope).astype(BF)
        dz_ref[t, :] = dz
        dn_ref[t, :] += dot(dz, up_ref[0], 1, 1)
        return c

    lax.fori_loop(0, tiles, second, 0)
    dc_ref[0] = dot(jnp.ones((8, tokens), BF), dz_ref[...], 1, 0)
    dup_ref[0] = dot(n2t_ref[...], dz_ref[...], 1, 0).astype(BF)
    ddown_ref[0] = dot(a_ref[...], g_ref[...], 0, 0).astype(BF)

    @pl.when(step == groups - 1)
    def _():
        rows_ref[...] = jnp.zeros_like(rows_ref)

        def third(i, c):
            t = tile(i)
            y_ref[t, :] = acc_ref[t, :].astype(BF)
            g = g_ref[t, :].astype(F32)
            unit, scale = normed(h_ref[t, :])
            dn = dn_ref[t, :]
            dh = g + norm_back(dn, unit, scale, vec_ref[6:7, :])
            dh_ref[t, :] = dh
            dr = dh.astype(BF)
            dr_ref[t, :] = dr
            do_ref[:, t] = dot(wo_ref[...], dr, 1, 1).astype(BF)
            rows_ref[0:8, :] += fold_rows(dr.astype(F32))
            rows_ref[8:16, :] += fold_rows(dn * unit)
            rows_ref[16:24, :] += fold_rows(dn)
            rows_ref[24:32, :] += fold_rows(g)
            return c

        lax.fori_loop(0, tiles, third, 0)
        dwo_ref[...] = dot(o_ref[...], dr_ref[...], 1, 0).astype(BF)


def middle_part(x, g, o, vec, wo, up, down):
    tokens, width = x.shape
    groups = up.shape[0]
    whole = lambda s: pl.BlockSpec(s, lambda i: (0,) * len(s))
    block = pl.BlockSpec((1, width, width), lambda i: (i, 0, 0))
    return pl.pallas_call(
        middle_kernel,
        grid=(groups,),
        in_specs=[
            whole(x.shape),
            whole(g.shape),
            whole(o.shape),
            whole(vec.shape),
            whole(wo.shape),
            block,
            block,
        ],
        out_specs=[
            whole((tokens, width)),
            whole((tokens, width)),
            whole((width, tokens)),
            whole((width, width)),
            block,
            block,
            whole((32, width)),
            pl.BlockSpec((1, 8, width), lambda i: (i, 0, 0)),
        ],
        out_shape=[
            jax.ShapeDtypeStruct((tokens, width), BF),
            jax.ShapeDtypeStruct((tokens, width), F32),
            jax.ShapeDtypeStruct((width, tokens), BF),
            jax.ShapeDtypeStruct((width, width), BF),
            jax.ShapeDtypeStruct((groups, width, width), BF),
            jax.ShapeDtypeStruct((groups, width, width), BF),
            jax.ShapeDtypeStruct((32, width), F32),
            jax.ShapeDtypeStruct((groups, 8, width), F32),
        ],
        scratch_shapes=[
            pltpu.VMEM((tokens, width), F32),
            pltpu.VMEM((tokens, width), BF),
            pltpu.VMEM((width, tokens), BF),
            pltpu.VMEM((tokens, width), F32),
            pltpu.VMEM((tokens, width), F32),
            pltpu.VMEM((tokens, width), BF),
            pltpu.VMEM((tokens, width), BF),
            pltpu.VMEM((tokens, width), BF),
        ],
        compiler_params=pltpu.CompilerParams(vmem_limit_bytes=VMEM_LIMIT),
        name="middle",
    )(x, g, o, vec, wo, up, down)


def final_kernel(
    x_ref, dh_ref, n1_ref, dq_ref, dk_ref, dv_ref, vec_ref, weight_ref, dwo_ref,
    dx_ref, dw_ref, rows_ref,
):
    tokens, width = x_ref.shape
    dw_ref[3] = dwo_ref[...]
    for index, ref in enumerate((dq_ref, dk_ref, dv_ref)):
        dw_ref[index] = dot(n1_ref[...], ref[...], 1, 1).astype(BF)
    rows_ref[...] = jnp.zeros_like(rows_ref)

    def loop(i, c):
        t = pl.ds(pl.multiple_of(i * TILE, TILE), TILE)
        dn = dot(dq_ref[:, t], weight_ref[0], 0, 1)
        dn += dot(dk_ref[:, t], weight_ref[1], 0, 1)
        dn += dot(dv_ref[:, t], weight_ref[2], 0, 1)
        unit, scale = normed(x_ref[t, :].astype(F32))
        dx_ref[t, :] = dh_ref[t, :] + norm_back(dn, unit, scale, vec_ref[0:1, :])
        rows_ref[0:8, :] += fold_rows(dn * unit)
        rows_ref[8:16, :] += fold_rows(dn)
        return c

    lax.fori_loop(0, tokens // TILE, loop, 0)


def final_part(x, dh, n1, dq, dk, dv, vec, weights, dwo):
    tokens, width = x.shape
    vmem = pl.BlockSpec(memory_space=pltpu.VMEM)
    return pl.pallas_call(
        final_kernel,
        in_specs=[vmem] * 9,
        out_specs=[vmem] * 3,
        out_shape=[
            jax.ShapeDtypeStruct((tokens, width), F32),
            jax.ShapeDtypeStruct((4, width, width), BF),
            jax.ShapeDtypeStruct((16, width), F32),
        ],
        compiler_params=pltpu.CompilerParams(vmem_limit_bytes=VMEM_LIMIT),
        name="final",
    )(x, dh, n1, dq, dk, dv, vec, weights, dwo)


def center_kernel(
    x_ref, g_ref, o_ref, vec_ref, weight_ref, zone_ref, xzone_ref, yzone_ref,
    y_ref, dh_ref, do_ref, dwo_ref, rows_ref, dc_ref, upgo_ref, upstay_ref, downgo_ref, downstay_ref,
    h_ref, n2_ref, n2t_ref, acc_ref, dn_ref, a_ref, dz_ref, wo_ref, w_ref, near_ref,
    land_sem, near_sem, send_sem, local_sem, out_sem,
):
    z, x, y, c = place()
    m = 2 * y + c
    m_y = 2 * (1 - y) + c
    right_x, right_y, partner = at(z, 1 - x, y, c), at(z, x, 1 - y, c), at(z, x, y, 1 - c)
    tokens, width = x_ref.shape
    tiles = tokens // TILE
    n_dp = w_ref.shape[2]
    fetch = pltpu.make_async_copy(weight_ref.at[3], wo_ref, local_sem.at[24])
    fetch.start()
    greet([right_x, right_y, partner])
    mail = Mail(send_sem)
    piece = w_ref.at[0, 0, 0]
    column_like = near_ref.at[0, 0]
    kept = []
    for kind in range(2):
        to = w_ref.at[kind]
        sem = land_sem.at[kind]
        for part in range(4):
            own, from_x = 2 * part + x, 2 * part + 1 - x
            if part < 2:
                mail.send(xzone_ref.at[kind, part], to.at[m, from_x], sem.at[m, from_x], right_y, piece)
            else:
                mail.send(yzone_ref.at[kind, part], to.at[m_y, own], sem.at[m_y, own], right_x, piece)
    for ref, column, shift in ((zone_ref, m, 0), (xzone_ref, m, 1), (yzone_ref, m_y, 0)):
        for kind in range(2):
            to = w_ref.at[kind]
            sem = land_sem.at[kind]
            for part in range(4):
                e = 2 * part + (x + shift) % 2
                mail.send(ref.at[kind, part], to.at[column, e], sem.at[column, e], partner, piece)
                copy = pltpu.make_async_copy(
                    ref.at[kind, part], to.at[column, e], local_sem.at[len(kept)]
                )
                copy.start()
                kept.append(copy)

    def tile(i):
        return pl.ds(pl.multiple_of(i * TILE, TILE), TILE)

    fetch.wait()
    wo = wo_ref.reshape(width, width)

    def first(i, carry):
        t = tile(i)
        branch = dot(o_ref[:, t], wo[...], 0, 0) + vec_ref[5:6, :]
        h = x_ref[t, :].astype(F32) + branch
        h_ref[t, :] = h
        unit, _ = normed(h)
        n2 = (unit * vec_ref[6:7, :] + vec_ref[7:8, :]).astype(BF)
        n2_ref[t, :] = n2
        n2t_ref[:, t] = n2.T
        acc_ref[t, :] = h + vec_ref[12:13, :]
        dn_ref[t, :] = jnp.zeros((TILE, width), F32)
        return carry

    lax.fori_loop(0, tiles, first, 0)
    for copy in kept:
        copy.wait()
    forwards = []

    def work(step, carry):
        column = 2 * ((y + step // 2) % 2) + (c + (step + 1) // 2) % 2

        @pl.when(step == 1)
        def _():
            for kind in range(2):
                sem = land_sem.at[kind]
                for part in range(4):
                    e = 2 * part + 1 - x
                    arrived(w_ref.at[kind, m_y, e], sem.at[m_y, e])
                    forwards.append(
                        mail.send(
                            w_ref.at[kind, m_y, e], w_ref.at[kind, m_y, e], sem.at[m_y, e], partner, piece
                        )
                    )
                for e in range(n_dp):
                    arrived(w_ref.at[kind, 2 * y + 1 - c, e], sem.at[2 * y + 1 - c, e])

        @pl.when(step == 2)
        def _():
            for kind in range(2):
                for e in range(n_dp):
                    other = 2 * (1 - y) + 1 - c
                    arrived(w_ref.at[kind, other, e], land_sem.at[kind, other, e])
            for slot in forwards:
                arrived(w_ref.at[0, 0, 0], send_sem.at[slot])
                mail.like[slot] = None

        up = w_ref.at[0, column].reshape(width, width)
        down = w_ref.at[1, column].reshape(width, width)
        up_bias = vec_ref[pl.ds(8 + column, 1), :]

        def second(i, c):
            t = tile(i)
            zed = dot(n2_ref[t, :], up[...], 1, 0) + up_bias
            cdf = 0.5 * (1.0 + lax.erf(zed * math.sqrt(0.5)))
            a = (zed * cdf).astype(BF)
            a_ref[t, :] = a
            acc_ref[t, :] += dot(a, down[...], 1, 0)
            da = dot(g_ref[t, :], down[...], 1, 1)
            slope = cdf + zed * (jnp.exp(-0.5 * zed * zed) * (1.0 / math.sqrt(2.0 * math.pi)))
            dz = (da * slope).astype(BF)
            dz_ref[t, :] = dz
            dn_ref[t, :] += dot(dz, up[...], 1, 1)
            return c

        lax.fori_loop(0, tiles, second, 0)
        dc_ref[column] = dot(jnp.ones((8, tokens), BF), dz_ref[...], 1, 0)
        up[...] = dot(n2t_ref[...], dz_ref[...], 1, 0).astype(BF)
        down[...] = dot(a_ref[...], g_ref[...], 0, 0).astype(BF)
        for s, row in ((1, y), (2, 1 - y)):

            @pl.when(step == s)
            def _():
                for kind in range(2):
                    mail.send(
                        w_ref.at[kind, 2 * row + 1 - c], near_ref.at[kind, row],
                        near_sem.at[kind, row], partner, column_like,
                    )

        return carry

    lax.fori_loop(0, 4, work, 0)

    outs = []

    def emit(source, target):
        copy = pltpu.make_async_copy(source, target, out_sem.at[len(outs)])
        copy.start()
        outs.append(copy)

    for row in (y, 1 - y):
        for kind in range(2):
            arrived(near_ref.at[kind, row], near_sem.at[kind, row])

            def summed(e, carry):
                total = w_ref[kind, 2 * row + c, e].astype(F32) + near_ref[kind, row, e].astype(F32)
                near_ref[kind, row, e] = total.astype(BF)
                return carry

            lax.fori_loop(0, n_dp, summed, 0)
    for row in range(2):
        for part in range(4):
            emit(near_ref.at[0, row, 2 * part + 1 - x], upgo_ref.at[row, part])
            emit(near_ref.at[0, row, 2 * part + x], upstay_ref.at[row, part])
    emit(near_ref.at[1, 1 - y], downgo_ref)
    emit(near_ref.at[1, y], downstay_ref)

    rows_ref[...] = jnp.zeros_like(rows_ref)

    def third(i, carry):
        t = tile(i)
        y_ref[t, :] = acc_ref[t, :].astype(BF)
        g = g_ref[t, :].astype(F32)
        unit, scale = normed(h_ref[t, :])
        dn = dn_ref[t, :]
        dh = g + norm_back(dn, unit, scale, vec_ref[6:7, :])
        dh_ref[t, :] = dh
        dr = dh.astype(BF)
        a_ref[t, :] = dr
        do_ref[:, t] = dot(wo[...], dr, 1, 1).astype(BF)
        rows_ref[0:8, :] += fold_rows(dr.astype(F32))
        rows_ref[8:16, :] += fold_rows(dn * unit)
        rows_ref[16:24, :] += fold_rows(dn)
        rows_ref[24:32, :] += fold_rows(g)
        return carry

    lax.fori_loop(0, tiles, third, 0)
    dwo_ref[...] = dot(o_ref[...], a_ref[...], 1, 0).astype(BF)
    for copy in outs:
        copy.wait()
    mail.finish()


def center(x, g, o, vec, weights, zone, xzone, yzone):
    tokens, width = x.shape
    n_mlp, n_dp, share, _ = weights.shape
    vmem = pl.BlockSpec(memory_space=pltpu.VMEM)
    hbm = pl.BlockSpec(memory_space=pl.ANY)
    shape = jax.ShapeDtypeStruct
    dma = pltpu.SemaphoreType.DMA
    return pl.pallas_call(
        center_kernel,
        in_specs=[vmem] * 4 + [hbm] * 4,
        out_specs=[vmem] * 6 + [hbm] * 4,
        out_shape=[
            shape((tokens, width), BF),
            shape((tokens, width), F32),
            shape((width, tokens), BF),
            shape((width, width), BF),
            shape((32, width), F32),
            shape((n_mlp, 8, width), F32),
        ]
        + [shape((2, 4, share, width), BF)] * 2
        + [shape((n_dp, share, width), BF)] * 2,
        scratch_shapes=[
            pltpu.VMEM((tokens, width), F32),
            pltpu.VMEM((tokens, width), BF),
            pltpu.VMEM((width, tokens), BF),
            pltpu.VMEM((tokens, width), F32),
            pltpu.VMEM((tokens, width), F32),
            pltpu.VMEM((tokens, width), BF),
            pltpu.VMEM((tokens, width), BF),
            pltpu.VMEM((n_dp, share, width), BF),
            pltpu.VMEM((2, n_mlp, n_dp, share, width), BF),
            pltpu.VMEM((2, 2, n_dp, share, width), BF),
            dma((2, n_mlp, n_dp)), dma((2, 2)), dma((48,)), dma((25,)), dma((18,)),
        ],
        compiler_params=pltpu.CompilerParams(
            vmem_limit_bytes=48 * 1024 * 1024, collective_id=1, has_side_effects=True
        ),
        name="center",
    )(x, g, o, vec, weights, zone, xzone, yzone)


def added(*values):
    total = values[0].astype(F32)
    for value in values[1:]:
        total = total + value.astype(F32)
    return total.astype(BF)


def merge_kernel(
    upstay_ref, upgot_ref, downstay_ref, downgot_ref, upgo_out, upstay_out, downgo_out, downstay_out
):
    _, x, y, _ = place()
    for part in range(4):
        upgo_out[part] = added(upstay_ref[1 - y, part], upgot_ref[1 - y, part])
        upstay_out[part] = added(upstay_ref[y, part], upgot_ref[y, part])
        e = 2 * part + 1 - x
        downgo_out[part] = added(downstay_ref[e], downgot_ref[e])
        f = 2 * part + x
        downstay_out[part] = added(downstay_ref[f], downgot_ref[f])


def merge(upstay, upgot, downstay, downgot):
    vmem = pl.BlockSpec(memory_space=pltpu.VMEM)
    return pl.pallas_call(
        merge_kernel,
        in_specs=[vmem] * 4,
        out_specs=[vmem] * 4,
        out_shape=[jax.ShapeDtypeStruct((4,) + upstay.shape[2:], BF)] * 4,
        compiler_params=pltpu.CompilerParams(vmem_limit_bytes=6 * 1024 * 1024),
        name="merge",
    )(upstay, upgot, downstay, downgot)


def leave_kernel(
    owner_ref, n1_ref, dq0_ref, dq1_ref, dk0_ref, dk1_ref, dv0_ref, dv1_ref, vec_ref,
    freq0_ref, freq1_ref, bias0_ref, bias1_ref, mid_ref, dc_ref,
    upstay_ref, upgot_ref, downstay_ref, downgot_ref, x_hbm, dh_hbm, weight_hbm, dwo_hbm,
    dx_ref, grad_ref, total_ref,
    x_ref, dh_ref, weight_ref, rows_ref,
    dw_ref, near_ref, fromx_ref, fromy_ref, diagx_ref, diagy_ref, third_ref, chain_ref, done_ref,
    pack_ref, side_ref, sums_ref,
    near_sem, x_sem, y_sem, dx_sem, dy_sem, chain_sem, relay_sem, grad_sem, side_sem, send_sem, local_sem,
):
    z, x, y, c = place()
    m = 2 * y + c
    d = 2 * z + x
    n_dp = grad_ref.shape[0]
    right_x, right_y, partner = at(z, 1 - x, y, c), at(z, x, 1 - y, c), at(z, x, y, 1 - c)
    tokens, width = x_ref.shape
    loads = []
    for source, target in (
        (dwo_hbm, dw_ref.at[3]), (x_hbm, x_ref), (dh_hbm, dh_ref), (weight_hbm, weight_ref)
    ):
        load = pltpu.make_async_copy(source, target, local_sem.at[len(loads)])
        load.start()
        loads.append(load)
    greet([right_x, right_y, partner] + [at((z + off) % 4, x, y, c) for off in range(1, 4)])
    mail = Mail(send_sem)
    piece = pack_ref.at[0]

    edge = z % 3 == 0
    inner = z % 3 != 0
    far = z // 2
    near = 1 - far

    def relay(direction, kind, part):
        ref = chain_ref.at[direction, kind, part]
        return pltpu.make_async_remote_copy(
            src_ref=ref,
            dst_ref=ref,
            send_sem=relay_sem.at[direction, kind, part],
            recv_sem=chain_sem.at[direction, kind, part],
            device_id=at(z + 1 - 2 * direction, x, y, c),
            device_id_type=pl.DeviceIdType.MESH,
        )

    def opening(kind, part):
        chain_ref[far, kind, part] = third_ref[kind, part]
        relay(far, kind, part).start()

    def outward(kind, part):
        ref = chain_ref.at[far, kind, part]
        arrived(ref, chain_sem.at[far, kind, part])
        ref[...] = added(third_ref[kind, part], ref[...])
        relay(far, kind, part).start()

    def inward(kind, part):
        ref = chain_ref.at[near, kind, part]
        arrived(ref, chain_sem.at[near, kind, part])
        total = added(chain_ref[far, kind, part], ref[...])

        @pl.when(inner)
        def _():
            ref[...] = added(third_ref[kind, part], ref[...])
            relay(near, kind, part).start()

        return total

    def ahead(s):
        @pl.when(inner)
        def _():
            outward(1 + s // 4, s % 4)

    def keep(s):
        done_ref[s // 4, s % 4] = inward(1 + s // 4, s % 4)

    for kind, (stay_ref, got_ref) in enumerate(
        ((upstay_ref, upgot_ref), (downstay_ref, downgot_ref))
    ):
        for part in range(4):
            third_ref[1 + kind, part] = added(stay_ref[part], got_ref[part])

    @pl.when(edge)
    def _():
        def rest(s, carry):
            opening(1 + s // 4, s % 4)
            return carry

        lax.fori_loop(0, 8, rest, 0)

    pairs = ((dq0_ref, dq1_ref), (dk0_ref, dk1_ref), (dv0_ref, dv1_ref))
    half = width // PARTS
    groups = ((0, 2), (1, 3))
    share = near_ref.shape[2]
    twin = near_ref.at[0, pl.ds(0, 2)]

    def products(group):
        rows = [slice(2 * share * part, 2 * share * (part + 1)) for part in group]
        left = jnp.concatenate([n1_ref[r, :] for r in rows], axis=0)
        for index, pair in enumerate(pairs):
            out = dw_ref.at[index].reshape(width, width)
            for side, ref in enumerate(pair):
                value = dot(left, ref[...], 1, 1).astype(BF)
                for place_in, r in enumerate(rows):
                    out[r, side * half : (side + 1) * half] = value[
                        2 * share * place_in : 2 * share * (place_in + 1)
                    ]

    def pass_over(group):
        for part in group:
            for row in range(2):
                mail.send(
                    dw_ref.at[2 * row + 1 - c, pl.ds(2 * part, 2)], near_ref.at[row, pl.ds(2 * part, 2)],
                    near_sem.at[row, part], partner, twin,
                )

    def summed(group):
        for part in group:
            for row in range(2):
                arrived(twin, near_sem.at[row, part])

            def one(i, carry):
                row, e = i // 2, 2 * part + i % 2
                near_ref[row, e] = added(near_ref[row, e], dw_ref[2 * row + c, e])
                return carry

            lax.fori_loop(0, 4, one, 0)

    def issue(group):
        low, high = group
        mail.send(
            near_ref.at[1 - y, 2 * low + 1 - x], diagy_ref.at[low], dy_sem.at[low], right_y, piece
        )
        mail.send(
            near_ref.at[1 - y, 2 * high + 1 - x], diagx_ref.at[high - 2], dx_sem.at[high - 2],
            right_x, piece,
        )
        mail.send(near_ref.at[1 - y, 2 * low + x], fromy_ref.at[low], y_sem.at[low], right_y, piece)
        mail.send(near_ref.at[y, 2 * high + 1 - x], fromx_ref.at[high], x_sem.at[high], right_x, piece)

    def forward(group):
        low, high = group
        turn = high - 2
        arrived(diagy_ref.at[low], dy_sem.at[low])
        diagy_ref[low] = added(near_ref[y, 2 * low + 1 - x], diagy_ref[low])
        mail.send(diagy_ref.at[low], fromx_ref.at[low], x_sem.at[low], right_x, piece)
        arrived(diagx_ref.at[turn], dx_sem.at[turn])
        diagx_ref[turn] = added(near_ref[1 - y, 2 * high + x], diagx_ref[turn])
        mail.send(diagx_ref.at[turn], fromy_ref.at[high], y_sem.at[high], right_y, piece)

    products(groups[0])
    loads[0].wait()
    pass_over(groups[0])
    products(groups[1])
    pass_over(groups[1])
    for load in loads[1:]:
        load.wait()
    rows_ref[...] = jnp.zeros_like(rows_ref)
    flat = [weight_ref.at[index].reshape(width, width) for index in range(3)]

    def back(i, carry):
        t = pl.ds(pl.multiple_of(i * TILE, TILE), TILE)
        dn = jnp.zeros((TILE, width), F32)
        for index, pair in enumerate(pairs):
            for part, ref in enumerate(pair):
                dn += dot(ref[:, t], flat[index][:, part * half : (part + 1) * half], 0, 1)
        unit, scale = normed(x_ref[t, :].astype(F32))
        dx_ref[t, :] = dh_ref[t, :] + norm_back(dn, unit, scale, vec_ref[0:1, :])
        rows_ref[0:8, :] += fold_rows(dn * unit)
        rows_ref[8:16, :] += fold_rows(dn)
        return carry

    def gathered(part):
        arrived(fromx_ref.at[part], x_sem.at[part])
        arrived(fromy_ref.at[part], y_sem.at[part])
        third_ref[0, part] = added(near_ref[y, 2 * part + x], fromx_ref[part], fromy_ref[part])

    def wanted(e, part, first):
        second = lax.select(owner_ref[m, 2] == e, done_ref[1, part], first)
        return lax.select(owner_ref[m, 1] == e, done_ref[0, part], second)

    def close(part):
        first = inward(0, part)
        e = 2 * part + x
        pack_ref[part] = wanted(2 * z + 1 - x, part, first)
        mail.send(pack_ref.at[part], grad_ref.at[e], grad_sem.at[part], right_x, piece)
        grad_ref[e] = wanted(d, part, first)

    def begin(group):
        @pl.when(edge)
        def _():
            for part in group[::-1]:
                gathered(part)
                opening(0, part)

    def early(part):
        @pl.when(inner)
        def _():
            gathered(part)
            outward(0, part)

    def hop(index, peer):
        mail.send(
            sums_ref.at[index], side_ref.at[index], side_sem.at[index], peer, sums_ref.at[0]
        )

    def landed(index):
        arrived(side_ref.at[index], side_sem.at[index])
        sums_ref[index + 1] = sums_ref[index] + side_ref[index]

    ahead(0)
    summed(groups[0])
    issue(groups[0])
    ahead(1)
    lax.fori_loop(0, 1, back, 0)
    summed(groups[1])
    ahead(2)
    keep(0)
    forward(groups[0])
    issue(groups[1])

    def middle(i, carry):
        ahead(2 + i)
        keep(i)
        return back(i, carry)

    lax.fori_loop(1, 3, middle, 0)
    begin(groups[0])
    lax.fori_loop(3, tokens // TILE, middle, 0)

    def eight(ref, index):
        return jnp.sum(ref[8 * index : 8 * index + 8, :], axis=0, keepdims=True)

    ups = dc_ref.shape[0]
    sums_ref[0, 0:1, :] = eight(rows_ref, 0)
    sums_ref[0, 1:2, :] = eight(rows_ref, 1)
    for index in range(3):
        sums_ref[0, 2 + index : 3 + index, 0:half] = bias0_ref[8 * index : 8 * index + 1, :]
        sums_ref[0, 2 + index : 3 + index, half:width] = bias1_ref[8 * index : 8 * index + 1, :]
        sums_ref[0, 5 + index : 6 + index, :] = eight(mid_ref, index)
    for index in range(ups):
        sums_ref[0, 8 + index : 9 + index, :] = dc_ref[index, 0:1, :]
    sums_ref[0, 8 + ups : 9 + ups, :] = eight(mid_ref, 3)
    sums_ref[0, 9 + ups : 10 + ups, :] = jnp.concatenate(
        [freq0_ref[0:1, :], freq1_ref[0:1, :], freq0_ref[1:2, :], freq1_ref[1:2, :]], axis=1
    )
    hop(0, partner)
    forward(groups[1])
    ahead(6)
    keep(4)
    landed(0)
    hop(1, right_x)
    ahead(7)
    keep(5)
    landed(1)
    hop(2, right_y)
    begin(groups[1])
    keep(6)
    landed(2)
    for off in range(1, 4):
        mail.send(
            sums_ref.at[3], side_ref.at[3 + z], side_sem.at[3 + z], at((z + off) % 4, x, y, c),
            sums_ref.at[0],
        )
    side_ref[3 + z] = sums_ref[3]
    early(2)
    keep(7)
    early(0)
    close(2)
    early(3)
    close(0)
    early(1)
    close(3)
    close(1)
    for off in range(1, 4):
        e = (z + off) % 4
        arrived(side_ref.at[3 + e], side_sem.at[3 + e])
    total_ref[...] = (side_ref[3] + side_ref[4]) + (side_ref[5] + side_ref[6])
    for part in (2, 3, 0, 1):
        arrived(grad_ref.at[2 * part + 1 - x], grad_sem.at[part])
    mail.finish()
    for kind in range(3):
        for part in range(4):
            arrived(piece, relay_sem.at[far, kind, part])

            @pl.when(inner)
            def _():
                arrived(piece, relay_sem.at[near, kind, part])


def leave(owner, x, dh, n1, flows, vec, weights, dwo, smalls, rest):
    tokens, width = x.shape
    n_mlp, n_dp, share, _ = weights.shape
    smem = pl.BlockSpec(memory_space=pltpu.SMEM)
    vmem = pl.BlockSpec(memory_space=pltpu.VMEM)
    hbm = pl.BlockSpec(memory_space=pl.ANY)
    dma = pltpu.SemaphoreType.DMA
    part = lambda *lead: pltpu.VMEM(lead + (share, width), BF)
    flat = [ref for pair in flows for ref in pair]
    return pl.pallas_call(
        leave_kernel,
        in_specs=[smem] + [vmem] * 18 + [hbm] * 4,
        out_specs=[vmem] * 3,
        out_shape=[
            jax.ShapeDtypeStruct((tokens, width), F32),
            jax.ShapeDtypeStruct((n_dp, share, width), BF),
            jax.ShapeDtypeStruct(vec.shape, F32),
        ],
        scratch_shapes=[
            pltpu.VMEM((tokens, width), BF),
            pltpu.VMEM((tokens, width), F32),
            part(n_mlp, n_dp),
            pltpu.VMEM((16, width), F32),
            part(n_mlp, n_dp), part(2, n_dp), part(4), part(4), part(2), part(2), part(3, 4),
            part(2, 3, 4), part(2, 4), part(4),
            pltpu.VMEM((7,) + vec.shape, F32),
            pltpu.VMEM((4,) + vec.shape, F32),
            dma((2, 4)), dma((4,)), dma((4,)), dma((2,)), dma((2,)), dma((2, 3, 4)), dma((2, 3, 4)),
            dma((4,)), dma((7,)), dma((32,)), dma((4,)),
        ],
        compiler_params=pltpu.CompilerParams(
            vmem_limit_bytes=38 * 1024 * 1024, collective_id=2, has_side_effects=True
        ),
        name="leave",
    )(
        owner, n1, *flat, vec, *smalls, *rest, x, dh, weights,
        dwo.reshape(n_dp, share, width),
    )


def update_kernel(
    owner_ref, decay_ref, grad_ref, total_ref, moment_ref, vec_ref,
    left_hbm, right_hbm, lroot_hbm, rroot_hbm, master_hbm, y_hbm, dx_hbm,
    small_out, moment_out, vec_out, slot_out, left_out, right_out, master_out, y_out, dx_out,
    left_ref, right_ref, lroot_ref, rroot_ref, master_ref, y_ref, dx_ref, slot_ref, turn_ref,
    in_sem, out_sem,
):
    loads = []
    for source, target in (
        (left_hbm, left_ref), (right_hbm, right_ref), (lroot_hbm, lroot_ref), (rroot_hbm, rroot_ref),
        (master_hbm, master_ref), (y_hbm, y_ref), (dx_hbm, dx_ref),
    ):
        loads.append(pltpu.make_async_copy(source, target, in_sem.at[len(loads)]))
        loads[-1].start()
    outs = []

    def emit(source, target):
        outs.append(pltpu.make_async_copy(source, target, out_sem.at[len(outs)]))
        outs[-1].start()

    d = lax.axis_index("dp")
    m = lax.axis_index("mlp")
    held = (owner_ref[m, 0] == d) | (owner_ref[m, 1] == d) | (owner_ref[m, 2] == d)
    decay = decay_ref[0]
    width = grad_ref.shape[0]
    tall = width // 3

    def strip(i):
        return pl.ds(pl.multiple_of(i * tall, tall), tall)

    @pl.when(held)
    def _():
        slot_ref[...] = grad_ref[...].astype(F32)

    @pl.when(jnp.logical_not(held))
    def _():
        slot_ref[...] = jnp.zeros_like(slot_ref)

    emit(slot_ref, slot_out)

    def own(ref):
        cut = small_out.shape[1]
        value = ref[:, 0:cut]
        for index in range(1, owner_ref.shape[0]):
            value = lax.select(m == index, ref[:, index * cut : (index + 1) * cut], value)
        return value

    slow = decay_ref[1]
    small = own(total_ref)
    moment = slow * own(moment_ref) + (1.0 - slow) * small * small
    small_out[...] = small
    moment_out[...] = moment
    vec_out[...] = own(vec_ref) - RATE_VECTOR * small / (jnp.sqrt(moment) + STEP_EPSILON)
    loads[0].wait()

    @pl.when(held)
    def _():
        def rows(i, carry):
            r = strip(i)
            gram = dot(grad_ref[r, :], grad_ref[...], 1, 1)
            left_ref[r, :] = decay * left_ref[r, :] + (1.0 - decay) * gram
            return carry

        lax.fori_loop(0, 3, rows, 0)

    emit(left_ref, left_out)
    loads[1].wait()

    @pl.when(held)
    def _():
        turn_ref[...] = grad_ref[...].T

        def rows(i, carry):
            r = strip(i)
            gram = dot(turn_ref[r, :], grad_ref[...], 1, 0)
            right_ref[r, :] = decay * right_ref[r, :] + (1.0 - decay) * gram
            return carry

        lax.fori_loop(0, 3, rows, 0)

    emit(right_ref, right_out)
    for index, source, target in ((5, y_ref, y_out), (6, dx_ref, dx_out)):
        loads[index].wait()
        emit(source, target)
    for load in loads[2:5]:
        load.wait()

    @pl.when(held)
    def _():
        turn_ref[...] = rroot_ref[...].astype(BF)

        def rows(i, total):
            r = strip(i)
            inner = dot(lroot_ref[r, :].astype(BF), grad_ref[...], 1, 0).astype(BF)
            direction = dot(inner, turn_ref[...], 1, 0)
            lroot_ref[r, :] = direction
            return total + jnp.sum(direction * direction, axis=0, keepdims=True)

        total = jnp.sum(lax.fori_loop(0, 3, rows, jnp.zeros((1, width), F32)), keepdims=True)
        mean = total * (1.0 / (width * width))
        master_ref[...] -= lroot_ref[...] * (RATE_MATRIX * lax.rsqrt(mean + GRAFT_EPSILON))

    emit(master_ref, master_out)
    for copy in outs:
        copy.wait()


def update(
    owner, decays, grad, total, moments, vectors, left, right, lroot, rroot, master, output, input_grad
):
    smem = pl.BlockSpec(memory_space=pltpu.SMEM)
    vmem = pl.BlockSpec(memory_space=pltpu.VMEM)
    hbm = pl.BlockSpec(memory_space=pl.ANY)
    shape = lambda a: jax.ShapeDtypeStruct(a.shape, a.dtype)
    room = lambda a: pltpu.VMEM(a.shape, a.dtype)
    return pl.pallas_call(
        update_kernel,
        in_specs=[smem, smem] + [vmem] * 4 + [hbm] * 7,
        out_specs=[vmem] * 3 + [hbm] * 6,
        out_shape=[jax.ShapeDtypeStruct((total.shape[0], total.shape[1] // owner.shape[0]), F32)] * 3
        + [shape(a) for a in (left, left, right, master, output, input_grad)],
        scratch_shapes=[room(a) for a in (left, right, lroot, rroot, master, output, input_grad, left, grad)]
        + [pltpu.SemaphoreType.DMA((7,)), pltpu.SemaphoreType.DMA((6,))],
        compiler_params=pltpu.CompilerParams(vmem_limit_bytes=26 * 1024 * 1024),
        name="update",
    )(
        owner, decays, grad, total, moments, vectors, left, right, lroot, rroot, master, output, input_grad
    )


def positions(segment, heights, widths, patch_rows, patch_cols):
    images = heights.shape[0]
    matches = segment[None, :] == jnp.arange(images, dtype=jnp.int32)[:, None]
    tall = jnp.sum(jnp.where(matches, heights[:, None], 0), axis=0).astype(F32)
    wide = jnp.sum(jnp.where(matches, widths[:, None], 0), axis=0).astype(F32)
    py = patch_rows.astype(F32) * GRID_BASE / tall
    px = patch_cols.astype(F32) * GRID_BASE / wide
    zero = jnp.zeros_like(px)
    return jnp.stack([px, py, segment.astype(F32), zero, zero, zero, zero, zero])


def local(
    tokens, cotangent, vectors, vector_moments, decays, owner, master_slots, left_slots,
    right_slots, left_roots, right_roots, grid_height, grid_width, patch_rows, patch_cols, segment,
):
    mlp_index = lax.axis_index("mlp")
    n_dp = lax.axis_size("dp")
    n_mlp = lax.axis_size("mlp")
    width = tokens.shape[1]
    share = width // n_dp
    owner_row = jnp.take(owner, mlp_index, axis=0)
    master = master_slots[0, 0]
    direct = n_dp == 8 and n_mlp == 4
    if direct:
        n1t, q, k, v, cosine, sine, qmark, kmark, pos, attention, zone = enter(
            owner, grid_height, grid_width, master.reshape(n_dp, share, width), tokens, segment,
            patch_rows, patch_cols, vectors,
        )
        over_x = [(i, i ^ 1) for i in range(n_dp)]
        over_y = [(i, i ^ 2) for i in range(n_mlp)]
        xzone = lax.ppermute(zone, "dp", over_x)
        yzone = lax.ppermute(zone, "mlp", over_y)
    else:
        turned = vectors.T
        pos = positions(segment, grid_height, grid_width, patch_rows, patch_cols)
        slot = master.astype(BF).reshape(n_dp, share, width)
        pieces = lax.all_to_all(slot, "dp", 0, 0, tiled=True)
        mine = jnp.take(pieces, owner_row, axis=0)
        every = lax.all_gather(mine[None], ("dp", "mlp"), axis=0, tiled=True)
        blocks = every.reshape(n_dp, n_mlp, 3, share, width).transpose(2, 1, 0, 3, 4)
        attention, up, down = blocks.reshape(3, n_mlp, width, width)
        n1t, q, k, v, cosine, sine, qmark, kmark = project(tokens, pos, vectors, turned, attention)
    o, log_totals = attend(grid_height, grid_width, q, k, v, qmark, kmark)
    fine = (n_mlp, n_dp, share, width)
    back = functools.partial(attend_back, grid_height, grid_width)
    if direct:
        output, dh, do, dwo, mid_rows, dc, upgo, upstay, downgo, downstay = center(
            tokens, cotangent, o, vectors, attention, zone, xzone, yzone
        )
        upgot = lax.ppermute(upgo, "dp", over_x)
        downgot = lax.ppermute(downgo, "mlp", over_y)
        first = back(q, k, v, qmark, kmark, log_totals, do, pos, cosine, sine, 0)
        first, upgot, downgot = lax.optimization_barrier((first, upgot, downgot))
        upgo, upstay, downgo, downstay = merge(upstay, upgot, downstay, downgot)
        upgot = lax.ppermute(upgo, "mlp", over_y)
        downgot = lax.ppermute(downgo, "dp", over_x)
        do, upstay, downstay = lax.optimization_barrier((do, upstay, downstay))
    else:
        output, dh, do, dwo, dup, ddown, mid_rows, dc = middle_part(
            tokens, cotangent, o, vectors, attention[3], up, down
        )
        first = back(q, k, v, qmark, kmark, log_totals, do, pos, cosine, sine, 0)
    second = back(q, k, v, qmark, kmark, log_totals, do, pos, cosine, sine, 1)
    both = list(zip(first, second))
    if direct:
        input_grad, gradient, total = leave(
            owner, tokens, dh, n1t, both[0:3], vectors, attention.reshape(fine), dwo,
            (*both[3], *both[4], mid_rows, dc),
            (upstay, upgot, downstay, downgot),
        )
    else:
        freq = jnp.concatenate(both[3], axis=1)[0:2].reshape(1, width)
        bias = jnp.concatenate(both[4], axis=1)[0::8]
        eights = lambda rows: jnp.sum(rows.reshape(-1, 8, width), axis=1)
        mid = eights(mid_rows)
        tail = [bias, mid[0:3], dc[:, 0, :], mid[3:4], freq]
        dq, dk, dv = (jnp.concatenate(pair, axis=0) for pair in both[0:3])
        input_grad, datt, fin_rows = final_part(
            tokens, dh, n1t, dq, dk, dv, vectors, attention, dwo
        )
        grads = jnp.stack([datt, dup, ddown], axis=1)
        grads = grads.reshape(n_mlp, 3, n_dp, share, width).transpose(2, 0, 1, 3, 4)
        grads = grads.reshape(n_dp * n_mlp * 3, share, width)
        reduced = lax.psum_scatter(grads, ("dp", "mlp"), scatter_dimension=0, tiled=True)
        takers = owner_row[None, :] == jnp.arange(n_dp, dtype=jnp.int32)[:, None]
        kind_of = jnp.sum(jnp.where(takers, jnp.arange(3, dtype=jnp.int32)[None, :], 0), axis=1)
        gradient = lax.all_to_all(jnp.take(reduced, kind_of, axis=0), "dp", 0, 0, tiled=True)
        total = lax.psum(jnp.concatenate([eights(fin_rows)] + tail, axis=0), ("dp", "mlp"))
    gradient = gradient.reshape(width, width)
    grad_share, moment_next, vector_next, slot_grad, left_out, right_out, master_out, output, input_grad = (
        update(
            owner, decays, gradient, total, vector_moments, vectors, left_slots[0, 0], right_slots[0, 0],
            left_roots[0, 0], right_roots[0, 0], master, output, input_grad,
        )
    )
    lift = lambda a: a[None, None]
    return (
        output, input_grad, lift(slot_grad), lift(left_out), lift(right_out), lift(master_out),
        grad_share, moment_next, vector_next,
    )


def solution(mesh):
    both = P(("dp", "mlp"))
    flat = P(("dp", "mlp"), None)
    slots = P("dp", "mlp", None, None)
    split = P(None, "mlp")
    return jax.shard_map(
        local,
        mesh=mesh,
        in_specs=(flat, flat, P(), P(), P(), P(), slots, slots, slots, slots, slots)
        + (both,) * 5,
        out_specs=(flat, flat, slots, slots, slots, slots, split, split, split),
        check_vma=False,
    )
```

```python
import functools
import math

import jax
import jax.numpy as jnp
from jax import lax
from jax.experimental import pallas as pl
from jax.experimental.pallas import tpu as pltpu
from jax.sharding import PartitionSpec as P

HEADS = 12
GRID_BASE = 16
NORM_EPSILON = 1e-06
GRAFT_EPSILON = 1e-06
STEP_EPSILON = 1e-08
RATE_MATRIX = 0.04
RATE_VECTOR = 0.02
MASK_SHIFT = -(2.0**100)
BLOCK = 128
TILE = 256
PARTS = 2
WINDOW = 6
F32 = jnp.float32
BF = jnp.bfloat16
VMEM_LIMIT = 60 * 1024 * 1024


def dot(left, right, left_dim, right_dim, precision=None):
    return lax.dot_general(
        left,
        right,
        (((left_dim,), (right_dim,)), ((), ())),
        preferred_element_type=F32,
        precision=precision,
    )


def normed(values):
    mean = jnp.mean(values, axis=-1, keepdims=True)
    centred = values - mean
    spread = jnp.mean(centred * centred, axis=-1, keepdims=True)
    scale = lax.rsqrt(spread + NORM_EPSILON)
    return centred * scale, scale


def norm_back(grad, unit, scale, gain):
    scaled = grad * gain
    first = jnp.mean(scaled, axis=-1, keepdims=True)
    second = jnp.mean(scaled * unit, axis=-1, keepdims=True)
    return scale * (scaled - first - unit * second)


def fold_rows(values):
    return jnp.sum(values.reshape(values.shape[0] // 8, 8, values.shape[1]), axis=0)


def place():
    d = lax.axis_index("dp")
    m = lax.axis_index("mlp")
    return d // 2, d % 2, m // 2, m % 2


def at(z, x, y, c):
    return (2 * z + x, 2 * y + c)


def greet(peers):
    barrier = pltpu.get_barrier_semaphore()
    for peer in peers:
        pl.semaphore_signal(barrier, inc=1, device_id=peer, device_id_type=pl.DeviceIdType.MESH)
    pl.semaphore_wait(barrier, len(peers))


class Mail:
    def __init__(self, sems):
        self.sems = sems
        self.like = []

    def send(self, source, target, arrival, peer, like):
        slot = len(self.like)
        pltpu.make_async_remote_copy(
            src_ref=source,
            dst_ref=target,
            send_sem=self.sems.at[slot],
            recv_sem=arrival,
            device_id=peer,
            device_id_type=pl.DeviceIdType.MESH,
        ).start()
        self.like.append(like)
        return slot

    def settle(self, slot):
        arrived(self.like[slot], self.sems.at[slot])
        self.like[slot] = None

    def finish(self):
        for slot, like in enumerate(self.like):
            if like is not None:
                self.settle(slot)


def arrived(target, arrival):
    pltpu.make_async_copy(target, target, arrival).wait()


def enter_kernel(
    owner_ref, height_ref, width_ref, slot_hbm, x_ref, seg_ref, patch_rows_ref, patch_cols_ref, vec_ref,
    n1_ref, q_ref, k_ref, v_ref, cos_ref, sin_ref, qmark_ref, kmark_ref, pos_ref, weight_ref, zone_ref,
    wide_ref, turned_ref, raw_ref, slot_ref, cross_ref, chain_ref, att_ref, zland_ref,
    cross_sem, chain_sem, relay_sem, att_sem, send_sem, local_sem,
):
    z, x, y, c = place()
    m = 2 * y + c
    n_dp = slot_ref.shape[0]
    right_x, right_y, partner = at(z, 1 - x, y, c), at(z, x, 1 - y, c), at(z, x, y, 1 - c)
    own = pltpu.make_async_copy(slot_hbm, raw_ref, local_sem.at[0])
    own.start()
    greet([right_x, right_y, partner, at((z + 1) % 4, x, y, c), at((z + 3) % 4, x, y, c)])
    mail = Mail(send_sem)
    piece = slot_ref.at[0]
    own.wait()
    for part in range(4):
        e = 2 * part + 1 - x
        slot_ref[e] = raw_ref[e].astype(BF)
        mail.send(slot_ref.at[e], cross_ref.at[part], cross_sem.at[part], right_x, piece)
    for part in range(4):
        e = 2 * part + x
        slot_ref[e] = raw_ref[e].astype(BF)

    tokens = x_ref.shape[0]
    half = cos_ref.shape[0]
    last = vec_ref.shape[0] - 1
    tiles = tokens // TILE
    wide_ref[...] = jnp.zeros_like(wide_ref)
    wide_ref[0 : last + 1, :] = vec_ref[...]
    turned_ref[...] = wide_ref[...].T
    tall = jnp.zeros(seg_ref.shape, F32)
    broad = jnp.zeros(seg_ref.shape, F32)
    for image in range(height_ref.shape[0]):
        match = seg_ref[...] == image
        tall = jnp.where(match, height_ref[image].astype(F32), tall)
        broad = jnp.where(match, width_ref[image].astype(F32), broad)
    pos_ref[...] = jnp.zeros_like(pos_ref)
    pos_ref[0:1, :] = patch_cols_ref[...].astype(F32) * GRID_BASE / broad
    pos_ref[1:2, :] = patch_rows_ref[...].astype(F32) * GRID_BASE / tall
    pos_ref[2:3, :] = seg_ref[...].astype(F32)

    def prepare(i, carry):
        t = pl.ds(pl.multiple_of(i * TILE, TILE), TILE)
        unit, _ = normed(x_ref[t, :].astype(F32))
        n1_ref[:, t] = (unit * vec_ref[0:1, :] + vec_ref[1:2, :]).astype(BF).T
        angle = turned_ref[half:, last : last + 1] * pos_ref[1:2, t] + turned_ref[:half, last : last + 1] * pos_ref[0:1, t]
        cos_ref[:, t] = jnp.cos(angle)
        sin_ref[:, t] = jnp.sin(angle)
        seg = pos_ref[2:3, t].astype(jnp.int32)
        row = lax.broadcasted_iota(jnp.int32, (qmark_ref.shape[0], TILE), 0)
        qmark_ref[:, t] = jnp.where(row == seg, 1.0, 0.0).astype(BF)
        kmark_ref[:, t] = jnp.where(row == seg, 0.0, MASK_SHIFT).astype(BF)
        return carry

    lax.fori_loop(0, tiles // 2, prepare, 0)

    edge = z % 3 == 0
    inner = z % 3 != 0
    far = z // 2
    near = 1 - far

    def relay(direction, kind, part):
        ref = chain_ref.at[direction, kind, part]
        return pltpu.make_async_remote_copy(
            src_ref=ref,
            dst_ref=ref,
            send_sem=relay_sem.at[direction, kind, part],
            recv_sem=chain_sem.at[direction, kind, part],
            device_id=at(z + 1 - 2 * direction, x, y, c),
            device_id_type=pl.DeviceIdType.MESH,
        )

    def merged(direction, kind, part, opening):
        ref = chain_ref.at[direction, kind, part]
        home = owner_ref[m, kind]
        value = lax.select(home % 2 == x, slot_ref[2 * part + x], cross_ref[part])
        if not opening:
            arrived(ref, chain_sem.at[direction, kind, part])
            value = lax.select(home // 2 == z, value, ref[...])
        ref[...] = value

    def crossed(part):
        arrived(cross_ref.at[part], cross_sem.at[part])

    def outward(kind, part):
        merged(far, kind, part, False)
        relay(far, kind, part).start()

    def inward(kind, part):
        merged(near, kind, part, False)

        @pl.when(inner)
        def _():
            relay(near, kind, part).start()

        return lax.select(
            owner_ref[m, kind] // 2 <= z, chain_ref[0, kind, part], chain_ref[1, kind, part]
        )

    def bring(part):
        e = 2 * part + x
        att_ref[m, e] = inward(0, part)
        for peer in (right_x, right_y, partner):
            mail.send(att_ref.at[m, e], att_ref.at[m, e], att_sem.at[m, e], peer, piece)

    @pl.when(edge)
    def _():
        def opening(part, carry):
            crossed(part)
            merged(far, 0, part, True)
            relay(far, 0, part).start()
            return carry

        lax.fori_loop(0, 4, opening, 0)

        def rest(s, carry):
            merged(far, 1 + s // 4, s % 4, True)
            relay(far, 1 + s // 4, s % 4).start()
            return carry

        lax.fori_loop(0, 8, rest, 0)

    def early(part):
        @pl.when(inner)
        def _():
            crossed(part)
            outward(0, part)

    def ahead(s):
        @pl.when(inner)
        def _():
            outward(1 + s // 4, s % 4)

    def keep(s):
        zland_ref[s // 4, s % 4] = inward(1 + s // 4, s % 4)

    m_y = 2 * (1 - y) + c

    def spread(part):
        e = 2 * part + 1 - x
        arrived(att_ref.at[m, e], att_sem.at[m, e])
        if part < 2:
            mail.send(att_ref.at[m, e], att_ref.at[m, e], att_sem.at[m, e], right_y, piece)
        mail.send(att_ref.at[m, e], att_ref.at[m, e], att_sem.at[m, e], partner, piece)
        f = 2 * part + x
        arrived(att_ref.at[m_y, f], att_sem.at[m_y, f])
        if part >= 2:
            mail.send(att_ref.at[m_y, f], att_ref.at[m_y, f], att_sem.at[m_y, f], right_x, piece)
        mail.send(att_ref.at[m_y, f], att_ref.at[m_y, f], att_sem.at[m_y, f], partner, piece)

    early(0)
    early(1)
    bring(0)
    early(2)
    bring(1)
    early(3)
    bring(2)
    ahead(0)
    spread(0)
    bring(3)
    ahead(1)
    spread(1)
    ahead(2)
    keep(0)
    lax.fori_loop(tiles // 2, tiles, prepare, 0)
    spread(2)
    ahead(3)
    keep(1)
    spread(3)
    ahead(4)
    keep(2)
    for part in range(4):
        e = 2 * part + 1 - x
        arrived(att_ref.at[m_y, e], att_sem.at[m_y, e])
        mail.send(att_ref.at[m_y, e], att_ref.at[m_y, e], att_sem.at[m_y, e], partner, piece)
    for step in range(2):
        other = 2 * step + 1 - c
        for e in range(n_dp):
            arrived(att_ref.at[other, e], att_sem.at[other, e])
    out = pltpu.make_async_copy(att_ref, weight_ref, local_sem.at[1])
    out.start()

    part = half // HEADS
    width = x_ref.shape[1]

    def weight(index):
        return att_ref[index].reshape(width, width)

    def rotate(i, carry):
        @pl.when(i < 3)
        def _():
            ahead(5 + i)

        keep(3 + i)
        t = pl.ds(pl.multiple_of(i * TILE, TILE), TILE)
        n1t = n1_ref[:, t]
        cosine = cos_ref[:, t]
        sine = sin_ref[:, t]
        for index, (ref, scale) in enumerate(((q_ref, 0.125), (k_ref, 1.0))):
            flat = dot(weight(index), n1t, 0, 0) + turned_ref[:, 2 + index : 3 + index]
            for head in range(HEADS):
                low, mid = 2 * part * head, 2 * part * head + part
                a = flat[low:mid]
                b = flat[mid : mid + part]
                cs = cosine[part * head : part * (head + 1)]
                sn = sine[part * head : part * (head + 1)]
                ref[low:mid, t] = (a * cs - b * sn).astype(BF) * jnp.asarray(scale, BF)
                ref[mid : mid + part, t] = (b * cs + a * sn).astype(BF) * jnp.asarray(scale, BF)
        v_ref[:, t] = (dot(weight(2), n1t, 0, 0) + turned_ref[:, 4:5]).astype(BF)
        return carry

    lax.fori_loop(0, tiles, rotate, 0)
    keep(7)
    last_out = pltpu.make_async_copy(zland_ref, zone_ref, local_sem.at[2])
    last_out.start()
    mail.finish()
    for kind in range(3):
        for step in range(4):
            arrived(piece, relay_sem.at[far, kind, step])

            @pl.when(inner)
            def _():
                arrived(piece, relay_sem.at[near, kind, step])

    out.wait()
    last_out.wait()


def enter(owner, heights, widths, slot, x, segment, patch_rows, patch_cols, vec):
    rows, width = x.shape
    half = width // 2
    n_dp, share, _ = slot.shape
    n_mlp = owner.shape[0]
    smem = pl.BlockSpec(memory_space=pltpu.SMEM)
    vmem = pl.BlockSpec(memory_space=pltpu.VMEM)
    hbm = pl.BlockSpec(memory_space=pl.ANY)
    out = lambda n, dtype: jax.ShapeDtypeStruct((n, rows), dtype)
    return pl.pallas_call(
        enter_kernel,
        in_specs=[smem, smem, smem, hbm] + [vmem] * 5,
        out_specs=[vmem] * 9 + [hbm] * 2,
        out_shape=[out(width, BF)] * 4
        + [out(half, F32)] * 2
        + [out(16, BF)] * 2
        + [out(8, F32)]
        + [
            jax.ShapeDtypeStruct((n_mlp, n_dp, share, width), BF),
            jax.ShapeDtypeStruct((2, 4, share, width), BF),
        ],
        scratch_shapes=[
            pltpu.VMEM((16, width), F32),
            pltpu.VMEM((width, 16), F32),
            pltpu.VMEM((n_dp, share, width), F32),
            pltpu.VMEM((n_dp, share, width), BF),
            pltpu.VMEM((4, share, width), BF),
            pltpu.VMEM((2, 3, 4, share, width), BF),
            pltpu.VMEM((n_mlp, n_dp, share, width), BF),
            pltpu.VMEM((2, 4, share, width), BF),
            pltpu.SemaphoreType.DMA((4,)),
            pltpu.SemaphoreType.DMA((2, 3, 4)),
            pltpu.SemaphoreType.DMA((2, 3, 4)),
            pltpu.SemaphoreType.DMA((n_mlp, n_dp)),
            pltpu.SemaphoreType.DMA((48,)),
            pltpu.SemaphoreType.DMA((3,)),
        ],
        compiler_params=pltpu.CompilerParams(
            vmem_limit_bytes=60 * 1024 * 1024, collective_id=0, has_side_effects=True
        ),
        name="enter",
    )(
        owner, heights, widths, slot, x,
        *(a.reshape(1, rows) for a in (segment, patch_rows, patch_cols)), vec,
    )


def project_kernel(
    x_ref, pos_ref, vec_ref, turned_ref, weight_ref,
    n1_ref, q_ref, k_ref, v_ref, cos_ref, sin_ref, qmark_ref, kmark_ref,
):
    unit, _ = normed(x_ref[...].astype(F32))
    n1 = (unit * vec_ref[0:1, :] + vec_ref[1:2, :]).astype(BF)
    n1t = n1.T
    n1_ref[...] = n1t
    px = pos_ref[0:1, :]
    py = pos_ref[1:2, :]
    half = cos_ref.shape[0]
    last = turned_ref.shape[1] - 1
    angle = turned_ref[half:, last:] * py + turned_ref[:half, last:] * px
    cosine = jnp.cos(angle)
    sine = jnp.sin(angle)
    cos_ref[...] = cosine
    sin_ref[...] = sine
    seg = pos_ref[2:3, :].astype(jnp.int32)
    row = lax.broadcasted_iota(jnp.int32, qmark_ref.shape, 0)
    qmark_ref[...] = jnp.where(row == seg, 1.0, 0.0).astype(BF)
    kmark_ref[...] = jnp.where(row == seg, 0.0, MASK_SHIFT).astype(BF)
    part = half // HEADS
    for index, (out, scale) in enumerate(((q_ref, 0.125), (k_ref, 1.0))):
        flat = dot(weight_ref[index], n1t, 0, 0) + turned_ref[:, 2 + index : 3 + index]
        for head in range(HEADS):
            low, mid = 2 * part * head, 2 * part * head + part
            a = flat[low:mid]
            b = flat[mid : mid + part]
            c = cosine[part * head : part * (head + 1)]
            s = sine[part * head : part * (head + 1)]
            out[low:mid, :] = (a * c - b * s).astype(BF) * jnp.asarray(scale, BF)
            out[mid : mid + part, :] = (b * c + a * s).astype(BF) * jnp.asarray(scale, BF)
    v_ref[...] = (dot(weight_ref[2], n1t, 0, 0) + turned_ref[:, 4:5]).astype(BF)


def project(x, pos, vec, turned, weights):
    rows, width = x.shape
    half = width // 2
    whole = lambda a: pl.BlockSpec(a.shape, lambda i: (0,) * a.ndim)
    col = lambda n: pl.BlockSpec((n, TILE), lambda i: (0, i))
    out = lambda n, d: jax.ShapeDtypeStruct((n, rows), d)
    return pl.pallas_call(
        project_kernel,
        grid=(rows // TILE,),
        in_specs=[
            pl.BlockSpec((TILE, width), lambda i: (i, 0)),
            col(8),
            whole(vec),
            whole(turned),
            whole(weights),
        ],
        out_specs=[col(width)] * 4 + [col(half)] * 2 + [col(16)] * 2,
        out_shape=[out(width, BF)] * 4 + [out(half, F32)] * 2 + [out(16, BF)] * 2,
        compiler_params=pltpu.CompilerParams(vmem_limit_bytes=VMEM_LIMIT),
        name="project",
    )(x, pos, vec, turned, weights)


def key_window(height_ref, width_ref, block):
    first = block * BLOCK
    last = first + BLOCK - 1
    start = jnp.int32(0)
    low = jnp.int32(0)
    high = jnp.int32(0)
    for image in range(height_ref.shape[0]):
        end = start + height_ref[image] * width_ref[image]
        low = jnp.where((start <= first) & (first < end), start, low)
        high = jnp.where((start <= last) & (last < end), end, high)
        start = end
    base = low // BLOCK
    return base, (high + BLOCK - 1) // BLOCK - base


def attend_kernel(height_ref, width_ref, q_ref, k_ref, v_ref, qmark_ref, kmark_ref, o_ref, log_ref):
    tokens = q_ref.shape[1]
    blocks = tokens // BLOCK
    size = q_ref.shape[0] // HEADS
    group = 4

    def one(block, part, base, count):
        here = pl.ds(pl.multiple_of(block * BLOCK, BLOCK), BLOCK)
        keys = pl.ds(pl.multiple_of(base * BLOCK, BLOCK), BLOCK * count)
        qmark = qmark_ref[:, here]
        kmark = kmark_ref[:, keys]
        for j in range(group):
            head = part * group + j
            rows = pl.ds(pl.multiple_of(head * size, size), size)
            q = jnp.concatenate([q_ref[rows, here], qmark], axis=0)
            k = jnp.concatenate([k_ref[rows, keys], kmark], axis=0)
            scores = dot(k, q, 0, 0)
            peak = jnp.max(scores, axis=0, keepdims=True)
            powers = jnp.exp(scores - peak)
            total = jnp.sum(powers, axis=0, keepdims=True)
            mixed = dot(v_ref[rows, keys], powers.astype(BF), 1, 0)
            o_ref[rows, here] = (mixed * (1.0 / total)).astype(BF)
            log_ref[pl.ds(pl.multiple_of(head * 8, 8), 8), here] = jnp.broadcast_to(
                peak + jnp.log(total), (8, BLOCK)
            )

    def step(block, carry):
        base, count = key_window(height_ref, width_ref, block)
        for n in range(1, min(blocks, WINDOW) + 1):

            @pl.when(count == n)
            def _():
                def inner(part, c):
                    one(block, part, base, n)
                    return c

                lax.fori_loop(0, HEADS // group, inner, 0)

        return carry

    lax.fori_loop(0, blocks, step, 0)


def attend(heights, widths, q, k, v, qmark, kmark):
    smem = pl.BlockSpec(memory_space=pltpu.SMEM)
    vmem = pl.BlockSpec(memory_space=pltpu.VMEM)
    return pl.pallas_call(
        attend_kernel,
        in_specs=[smem, smem] + [vmem] * 5,
        out_specs=[vmem, vmem],
        out_shape=[
            jax.ShapeDtypeStruct(q.shape, BF),
            jax.ShapeDtypeStruct((8 * HEADS, q.shape[1]), F32),
        ],
        compiler_params=pltpu.CompilerParams(vmem_limit_bytes=60 * 1024 * 1024),
        name="attend",
    )(heights, widths, q, k, v, qmark, kmark)


def attend_back_kernel(
    height_ref, width_ref, q_ref, k_ref, v_ref, qmark_ref, kmark_ref, log_ref, do_ref,
    pos_ref, cos_ref, sin_ref,
    dq_ref, dk_ref, dv_ref, freq_ref, bias_ref,
    gq_ref, gk_ref, gv_ref, turn_ref,
):
    tokens = q_ref.shape[1]
    blocks = tokens // BLOCK
    heads = log_ref.shape[0] // 8
    size = q_ref.shape[0] // heads
    half = size // 2
    group = 2
    gk_ref[...] = jnp.zeros_like(gk_ref)
    gv_ref[...] = jnp.zeros_like(gv_ref)

    def one(block, part, base, count):
        here = pl.ds(pl.multiple_of(block * BLOCK, BLOCK), BLOCK)
        keys = pl.ds(pl.multiple_of(base * BLOCK, BLOCK), BLOCK * count)
        qmark = qmark_ref[:, here]
        kmark = kmark_ref[:, keys]
        for j in range(group):
            head = part * group + j
            rows = pl.ds(pl.multiple_of(head * size, size), size)
            q = q_ref[rows, here]
            k = k_ref[rows, keys]
            do = do_ref[rows, here]
            scores = dot(
                jnp.concatenate([k, kmark], axis=0), jnp.concatenate([q, qmark], axis=0), 0, 0
            )
            log_row = log_ref[pl.ds(pl.multiple_of(head * 8, 8), 8), here][0:1]
            probs = jnp.exp(scores - log_row)
            dp = dot(v_ref[rows, keys], do, 0, 0)
            inner = jnp.sum(probs * dp, axis=0, keepdims=True)
            ds = (probs * (dp - inner)).astype(BF)
            gq_ref[rows, here] = dot(k, ds, 1, 0) * 0.125
            gk_ref[rows, keys] += dot(q, ds, 1, 1)
            gv_ref[rows, keys] += dot(do, probs.astype(BF), 1, 1)

    def step(block, carry):
        base, count = key_window(height_ref, width_ref, block)
        for n in range(1, min(blocks, WINDOW) + 1):

            @pl.when(count == n)
            def _():
                def inner(part, c):
                    one(block, part, base, n)
                    return c

                lax.fori_loop(0, heads // group, inner, 0)

        return carry

    lax.fori_loop(0, blocks, step, 0)

    def unturn(head, carry):
        low = pl.ds(pl.multiple_of(head * size, size), half)
        high = pl.ds(pl.multiple_of(head * size + half, half), half)
        table = pl.ds(pl.multiple_of(head * half, half), half)
        c = cos_ref[table, :]
        s = sin_ref[table, :]
        turn = None
        for grad_ref, rot_ref, scale, out_ref in (
            (gq_ref, q_ref, 8.0, dq_ref),
            (gk_ref, k_ref, 1.0, dk_ref),
        ):
            ga = grad_ref[low, :]
            gb = grad_ref[high, :]
            out_ref[low, :] = (ga * c + gb * s).astype(BF)
            out_ref[high, :] = (gb * c - ga * s).astype(BF)
            ra = rot_ref[low, :].astype(F32) * scale
            rb = rot_ref[high, :].astype(F32) * scale
            piece = gb * ra - ga * rb
            turn = piece if turn is None else turn + piece
        turn_ref[table, :] = turn
        both = pl.ds(pl.multiple_of(head * size, size), size)
        dv_ref[both, :] = gv_ref[both, :].astype(BF)
        return carry

    lax.fori_loop(0, heads, unturn, 0)
    freq_ref[...] = dot(pos_ref[...], turn_ref[...], 1, 1, lax.Precision.HIGHEST)
    ones = jnp.ones((8, tokens), BF)
    for index, ref in enumerate((dq_ref, dk_ref, dv_ref)):
        bias_ref[8 * index : 8 * index + 8, :] = dot(ones, ref[...], 1, 1)


def attend_back(heights, widths, q, k, v, qmark, kmark, log_totals, do, pos, cosine, sine, part):
    smem = pl.BlockSpec(memory_space=pltpu.SMEM)
    width, tokens = q.shape
    half = width // PARTS
    cut = lambda a: pl.BlockSpec((a.shape[0] // PARTS, tokens), lambda i: (part, 0))
    whole = lambda a: pl.BlockSpec(a.shape, lambda i: (0, 0))
    out = lambda n, cols, dtype: jax.ShapeDtypeStruct((n, cols), dtype)
    outs = [out(half, tokens, BF)] * 3 + [out(8, half // 2, F32), out(24, half, F32)]
    return pl.pallas_call(
        attend_back_kernel,
        grid=(1,),
        in_specs=[smem, smem, cut(q), cut(k), cut(v), whole(qmark), whole(kmark), cut(log_totals)]
        + [cut(do), whole(pos), cut(cosine), cut(sine)],
        out_specs=[whole(a) for a in outs],
        out_shape=outs,
        scratch_shapes=[pltpu.VMEM((half, tokens), F32)] * 3
        + [pltpu.VMEM((half // 2, tokens), F32)],
        compiler_params=pltpu.CompilerParams(vmem_limit_bytes=18 * 1024 * 1024),
        name="attend_back",
    )(heights, widths, q, k, v, qmark, kmark, log_totals, do, pos, cosine, sine)


def middle_kernel(
    x_ref, g_ref, o_ref, vec_ref, wo_ref, up_ref, down_ref,
    y_ref, dh_ref, do_ref, dwo_ref, dup_ref, ddown_ref, rows_ref, dc_ref,
    h_ref, n2_ref, n2t_ref, acc_ref, dn_ref, a_ref, dz_ref, dr_ref,
):
    groups = vec_ref.shape[0] - 10
    step = pl.program_id(0)
    tokens, width = x_ref.shape
    tiles = tokens // TILE

    def tile(i):
        return pl.ds(pl.multiple_of(i * TILE, TILE), TILE)

    @pl.when(step == 0)
    def _():
        def first(i, c):
            t = tile(i)
            branch = dot(o_ref[:, t], wo_ref[...], 0, 0) + vec_ref[5:6, :]
            h = x_ref[t, :].astype(F32) + branch
            h_ref[t, :] = h
            unit, _ = normed(h)
            n2 = (unit * vec_ref[6:7, :] + vec_ref[7:8, :]).astype(BF)
            n2_ref[t, :] = n2
            n2t_ref[:, t] = n2.T
            acc_ref[t, :] = h + vec_ref[8 + groups : 9 + groups, :]
            dn_ref[t, :] = jnp.zeros((TILE, width), F32)
            return c

        lax.fori_loop(0, tiles, first, 0)

    up_bias = vec_ref[pl.ds(8 + step, 1), :]

    def second(i, c):
        t = tile(i)
        z = dot(n2_ref[t, :], up_ref[0], 1, 0) + up_bias
        cdf = 0.5 * (1.0 + lax.erf(z * math.sqrt(0.5)))
        a = (z * cdf).astype(BF)
        a_ref[t, :] = a
        acc_ref[t, :] += dot(a, down_ref[0], 1, 0)
        da = dot(g_ref[t, :], down_ref[0], 1, 1)
        slope = cdf + z * (jnp.exp(-0.5 * z * z) * (1.0 / math.sqrt(2.0 * math.pi)))
        dz = (da * slope).astype(BF)
        dz_ref[t, :] = dz
        dn_ref[t, :] += dot(dz, up_ref[0], 1, 1)
        return c

    lax.fori_loop(0, tiles, second, 0)
    dc_ref[0] = dot(jnp.ones((8, tokens), BF), dz_ref[...], 1, 0)
    dup_ref[0] = dot(n2t_ref[...], dz_ref[...], 1, 0).astype(BF)
    ddown_ref[0] = dot(a_ref[...], g_ref[...], 0, 0).astype(BF)

    @pl.when(step == groups - 1)
    def _():
        rows_ref[...] = jnp.zeros_like(rows_ref)

        def third(i, c):
            t = tile(i)
            y_ref[t, :] = acc_ref[t, :].astype(BF)
            g = g_ref[t, :].astype(F32)
            unit, scale = normed(h_ref[t, :])
            dn = dn_ref[t, :]
            dh = g + norm_back(dn, unit, scale, vec_ref[6:7, :])
            dh_ref[t, :] = dh
            dr = dh.astype(BF)
            dr_ref[t, :] = dr
            do_ref[:, t] = dot(wo_ref[...], dr, 1, 1).astype(BF)
            rows_ref[0:8, :] += fold_rows(dr.astype(F32))
            rows_ref[8:16, :] += fold_rows(dn * unit)
            rows_ref[16:24, :] += fold_rows(dn)
            rows_ref[24:32, :] += fold_rows(g)
            return c

        lax.fori_loop(0, tiles, third, 0)
        dwo_ref[...] = dot(o_ref[...], dr_ref[...], 1, 0).astype(BF)


def middle_part(x, g, o, vec, wo, up, down):
    tokens, width = x.shape
    groups = up.shape[0]
    whole = lambda s: pl.BlockSpec(s, lambda i: (0,) * len(s))
    block = pl.BlockSpec((1, width, width), lambda i: (i, 0, 0))
    return pl.pallas_call(
        middle_kernel,
        grid=(groups,),
        in_specs=[
            whole(x.shape),
            whole(g.shape),
            whole(o.shape),
            whole(vec.shape),
            whole(wo.shape),
            block,
            block,
        ],
        out_specs=[
            whole((tokens, width)),
            whole((tokens, width)),
            whole((width, tokens)),
            whole((width, width)),
            block,
            block,
            whole((32, width)),
            pl.BlockSpec((1, 8, width), lambda i: (i, 0, 0)),
        ],
        out_shape=[
            jax.ShapeDtypeStruct((tokens, width), BF),
            jax.ShapeDtypeStruct((tokens, width), F32),
            jax.ShapeDtypeStruct((width, tokens), BF),
            jax.ShapeDtypeStruct((width, width), BF),
            jax.ShapeDtypeStruct((groups, width, width), BF),
            jax.ShapeDtypeStruct((groups, width, width), BF),
            jax.ShapeDtypeStruct((32, width), F32),
            jax.ShapeDtypeStruct((groups, 8, width), F32),
        ],
        scratch_shapes=[
            pltpu.VMEM((tokens, width), F32),
            pltpu.VMEM((tokens, width), BF),
            pltpu.VMEM((width, tokens), BF),
            pltpu.VMEM((tokens, width), F32),
            pltpu.VMEM((tokens, width), F32),
            pltpu.VMEM((tokens, width), BF),
            pltpu.VMEM((tokens, width), BF),
            pltpu.VMEM((tokens, width), BF),
        ],
        compiler_params=pltpu.CompilerParams(vmem_limit_bytes=VMEM_LIMIT),
        name="middle",
    )(x, g, o, vec, wo, up, down)


def final_kernel(
    x_ref, dh_ref, n1_ref, dq_ref, dk_ref, dv_ref, vec_ref, weight_ref, dwo_ref,
    dx_ref, dw_ref, rows_ref,
):
    tokens, width = x_ref.shape
    dw_ref[3] = dwo_ref[...]
    for index, ref in enumerate((dq_ref, dk_ref, dv_ref)):
        dw_ref[index] = dot(n1_ref[...], ref[...], 1, 1).astype(BF)
    rows_ref[...] = jnp.zeros_like(rows_ref)

    def loop(i, c):
        t = pl.ds(pl.multiple_of(i * TILE, TILE), TILE)
        dn = dot(dq_ref[:, t], weight_ref[0], 0, 1)
        dn += dot(dk_ref[:, t], weight_ref[1], 0, 1)
        dn += dot(dv_ref[:, t], weight_ref[2], 0, 1)
        unit, scale = normed(x_ref[t, :].astype(F32))
        dx_ref[t, :] = dh_ref[t, :] + norm_back(dn, unit, scale, vec_ref[0:1, :])
        rows_ref[0:8, :] += fold_rows(dn * unit)
        rows_ref[8:16, :] += fold_rows(dn)
        return c

    lax.fori_loop(0, tokens // TILE, loop, 0)


def final_part(x, dh, n1, dq, dk, dv, vec, weights, dwo):
    tokens, width = x.shape
    vmem = pl.BlockSpec(memory_space=pltpu.VMEM)
    return pl.pallas_call(
        final_kernel,
        in_specs=[vmem] * 9,
        out_specs=[vmem] * 3,
        out_shape=[
            jax.ShapeDtypeStruct((tokens, width), F32),
            jax.ShapeDtypeStruct((4, width, width), BF),
            jax.ShapeDtypeStruct((16, width), F32),
        ],
        compiler_params=pltpu.CompilerParams(vmem_limit_bytes=VMEM_LIMIT),
        name="final",
    )(x, dh, n1, dq, dk, dv, vec, weights, dwo)


def center_kernel(
    x_ref, g_ref, o_ref, vec_ref, weight_ref, zone_ref, xzone_ref, yzone_ref,
    y_ref, dh_ref, do_ref, dwo_ref, rows_ref, dc_ref, upgo_ref, upstay_ref, downgo_ref, downstay_ref,
    h_ref, n2_ref, n2t_ref, acc_ref, dn_ref, a_ref, dz_ref, wo_ref, w_ref, near_ref,
    land_sem, near_sem, send_sem, local_sem, out_sem,
):
    z, x, y, c = place()
    m = 2 * y + c
    m_y = 2 * (1 - y) + c
    right_x, right_y, partner = at(z, 1 - x, y, c), at(z, x, 1 - y, c), at(z, x, y, 1 - c)
    tokens, width = x_ref.shape
    tiles = tokens // TILE
    n_dp = w_ref.shape[2]
    fetch = pltpu.make_async_copy(weight_ref.at[3], wo_ref, local_sem.at[24])
    fetch.start()
    greet([right_x, right_y, partner])
    mail = Mail(send_sem)
    piece = w_ref.at[0, 0, 0]
    column_like = near_ref.at[0, 0]
    kept = []
    for kind in range(2):
        to = w_ref.at[kind]
        sem = land_sem.at[kind]
        for part in range(4):
            own, from_x = 2 * part + x, 2 * part + 1 - x
            if part < 2:
                mail.send(xzone_ref.at[kind, part], to.at[m, from_x], sem.at[m, from_x], right_y, piece)
            else:
                mail.send(yzone_ref.at[kind, part], to.at[m_y, own], sem.at[m_y, own], right_x, piece)
    for ref, column, shift in ((zone_ref, m, 0), (xzone_ref, m, 1), (yzone_ref, m_y, 0)):
        for kind in range(2):
            to = w_ref.at[kind]
            sem = land_sem.at[kind]
            for part in range(4):
                e = 2 * part + (x + shift) % 2
                mail.send(ref.at[kind, part], to.at[column, e], sem.at[column, e], partner, piece)
                copy = pltpu.make_async_copy(
                    ref.at[kind, part], to.at[column, e], local_sem.at[len(kept)]
                )
                copy.start()
                kept.append(copy)

    def tile(i):
        return pl.ds(pl.multiple_of(i * TILE, TILE), TILE)

    fetch.wait()
    wo = wo_ref.reshape(width, width)

    def first(i, carry):
        t = tile(i)
        branch = dot(o_ref[:, t], wo[...], 0, 0) + vec_ref[5:6, :]
        h = x_ref[t, :].astype(F32) + branch
        h_ref[t, :] = h
        unit, _ = normed(h)
        n2 = (unit * vec_ref[6:7, :] + vec_ref[7:8, :]).astype(BF)
        n2_ref[t, :] = n2
        n2t_ref[:, t] = n2.T
        acc_ref[t, :] = h + vec_ref[12:13, :]
        dn_ref[t, :] = jnp.zeros((TILE, width), F32)
        return carry

    lax.fori_loop(0, tiles, first, 0)
    for copy in kept:
        copy.wait()
    forwards = []

    def work(step, carry):
        column = 2 * ((y + step // 2) % 2) + (c + (step + 1) // 2) % 2

        @pl.when(step == 1)
        def _():
            for kind in range(2):
                sem = land_sem.at[kind]
                for part in range(4):
                    e = 2 * part + 1 - x
                    arrived(w_ref.at[kind, m_y, e], sem.at[m_y, e])
                    forwards.append(
                        mail.send(
                            w_ref.at[kind, m_y, e], w_ref.at[kind, m_y, e], sem.at[m_y, e], partner, piece
                        )
                    )
                for e in range(n_dp):
                    arrived(w_ref.at[kind, 2 * y + 1 - c, e], sem.at[2 * y + 1 - c, e])

        @pl.when(step == 2)
        def _():
            for kind in range(2):
                for e in range(n_dp):
                    other = 2 * (1 - y) + 1 - c
                    arrived(w_ref.at[kind, other, e], land_sem.at[kind, other, e])
            for slot in forwards:
                arrived(w_ref.at[0, 0, 0], send_sem.at[slot])
                mail.like[slot] = None

        up = w_ref.at[0, column].reshape(width, width)
        down = w_ref.at[1, column].reshape(width, width)
        up_bias = vec_ref[pl.ds(8 + column, 1), :]

        def second(i, c):
            t = tile(i)
            zed = dot(n2_ref[t, :], up[...], 1, 0) + up_bias
            cdf = 0.5 * (1.0 + lax.erf(zed * math.sqrt(0.5)))
            a = (zed * cdf).astype(BF)
            a_ref[t, :] = a
            acc_ref[t, :] += dot(a, down[...], 1, 0)
            da = dot(g_ref[t, :], down[...], 1, 1)
            slope = cdf + zed * (jnp.exp(-0.5 * zed * zed) * (1.0 / math.sqrt(2.0 * math.pi)))
            dz = (da * slope).astype(BF)
            dz_ref[t, :] = dz
            dn_ref[t, :] += dot(dz, up[...], 1, 1)
            return c

        lax.fori_loop(0, tiles, second, 0)
        dc_ref[column] = dot(jnp.ones((8, tokens), BF), dz_ref[...], 1, 0)
        up[...] = dot(n2t_ref[...], dz_ref[...], 1, 0).astype(BF)
        down[...] = dot(a_ref[...], g_ref[...], 0, 0).astype(BF)
        for s, row in ((1, y), (2, 1 - y)):

            @pl.when(step == s)
            def _():
                for kind in range(2):
                    mail.send(
                        w_ref.at[kind, 2 * row + 1 - c], near_ref.at[kind, row],
                        near_sem.at[kind, row], partner, column_like,
                    )

        return carry

    lax.fori_loop(0, 4, work, 0)

    outs = []

    def emit(source, target):
        copy = pltpu.make_async_copy(source, target, out_sem.at[len(outs)])
        copy.start()
        outs.append(copy)

    for row in (y, 1 - y):
        for kind in range(2):
            arrived(near_ref.at[kind, row], near_sem.at[kind, row])

            def summed(e, carry):
                total = w_ref[kind, 2 * row + c, e].astype(F32) + near_ref[kind, row, e].astype(F32)
                near_ref[kind, row, e] = total.astype(BF)
                return carry

            lax.fori_loop(0, n_dp, summed, 0)
    for row in range(2):
        for part in range(4):
            emit(near_ref.at[0, row, 2 * part + 1 - x], upgo_ref.at[row, part])
            emit(near_ref.at[0, row, 2 * part + x], upstay_ref.at[row, part])
    emit(near_ref.at[1, 1 - y], downgo_ref)
    emit(near_ref.at[1, y], downstay_ref)

    rows_ref[...] = jnp.zeros_like(rows_ref)

    def third(i, carry):
        t = tile(i)
        y_ref[t, :] = acc_ref[t, :].astype(BF)
        g = g_ref[t, :].astype(F32)
        unit, scale = normed(h_ref[t, :])
        dn = dn_ref[t, :]
        dh = g + norm_back(dn, unit, scale, vec_ref[6:7, :])
        dh_ref[t, :] = dh
        dr = dh.astype(BF)
        a_ref[t, :] = dr
        do_ref[:, t] = dot(wo[...], dr, 1, 1).astype(BF)
        rows_ref[0:8, :] += fold_rows(dr.astype(F32))
        rows_ref[8:16, :] += fold_rows(dn * unit)
        rows_ref[16:24, :] += fold_rows(dn)
        rows_ref[24:32, :] += fold_rows(g)
        return carry

    lax.fori_loop(0, tiles, third, 0)
    dwo_ref[...] = dot(o_ref[...], a_ref[...], 1, 0).astype(BF)
    for copy in outs:
        copy.wait()
    mail.finish()


def center(x, g, o, vec, weights, zone, xzone, yzone):
    tokens, width = x.shape
    n_mlp, n_dp, share, _ = weights.shape
    vmem = pl.BlockSpec(memory_space=pltpu.VMEM)
    hbm = pl.BlockSpec(memory_space=pl.ANY)
    shape = jax.ShapeDtypeStruct
    dma = pltpu.SemaphoreType.DMA
    return pl.pallas_call(
        center_kernel,
        in_specs=[vmem] * 4 + [hbm] * 4,
        out_specs=[vmem] * 6 + [hbm] * 4,
        out_shape=[
            shape((tokens, width), BF),
            shape((tokens, width), F32),
            shape((width, tokens), BF),
            shape((width, width), BF),
            shape((32, width), F32),
            shape((n_mlp, 8, width), F32),
        ]
        + [shape((2, 4, share, width), BF)] * 2
        + [shape((n_dp, share, width), BF)] * 2,
        scratch_shapes=[
            pltpu.VMEM((tokens, width), F32),
            pltpu.VMEM((tokens, width), BF),
            pltpu.VMEM((width, tokens), BF),
            pltpu.VMEM((tokens, width), F32),
            pltpu.VMEM((tokens, width), F32),
            pltpu.VMEM((tokens, width), BF),
            pltpu.VMEM((tokens, width), BF),
            pltpu.VMEM((n_dp, share, width), BF),
            pltpu.VMEM((2, n_mlp, n_dp, share, width), BF),
            pltpu.VMEM((2, 2, n_dp, share, width), BF),
            dma((2, n_mlp, n_dp)), dma((2, 2)), dma((48,)), dma((25,)), dma((18,)),
        ],
        compiler_params=pltpu.CompilerParams(
            vmem_limit_bytes=48 * 1024 * 1024, collective_id=1, has_side_effects=True
        ),
        name="center",
    )(x, g, o, vec, weights, zone, xzone, yzone)


def added(*values):
    total = values[0].astype(F32)
    for value in values[1:]:
        total = total + value.astype(F32)
    return total.astype(BF)


def merge_kernel(
    upstay_ref, upgot_ref, downstay_ref, downgot_ref, upgo_out, upstay_out, downgo_out, downstay_out
):
    _, x, y, _ = place()
    for part in range(4):
        upgo_out[part] = added(upstay_ref[1 - y, part], upgot_ref[1 - y, part])
        upstay_out[part] = added(upstay_ref[y, part], upgot_ref[y, part])
        e = 2 * part + 1 - x
        downgo_out[part] = added(downstay_ref[e], downgot_ref[e])
        f = 2 * part + x
        downstay_out[part] = added(downstay_ref[f], downgot_ref[f])


def merge(upstay, upgot, downstay, downgot):
    vmem = pl.BlockSpec(memory_space=pltpu.VMEM)
    return pl.pallas_call(
        merge_kernel,
        in_specs=[vmem] * 4,
        out_specs=[vmem] * 4,
        out_shape=[jax.ShapeDtypeStruct((4,) + upstay.shape[2:], BF)] * 4,
        compiler_params=pltpu.CompilerParams(vmem_limit_bytes=6 * 1024 * 1024),
        name="merge",
    )(upstay, upgot, downstay, downgot)


def leave_kernel(
    owner_ref, n1_ref, dq0_ref, dq1_ref, dk0_ref, dk1_ref, dv0_ref, dv1_ref, vec_ref,
    freq0_ref, freq1_ref, bias0_ref, bias1_ref, mid_ref, dc_ref,
    upstay_ref, upgot_ref, downstay_ref, downgot_ref, x_hbm, dh_hbm, weight_hbm, dwo_hbm,
    dx_ref, grad_ref, total_ref,
    x_ref, dh_ref, weight_ref, rows_ref,
    dw_ref, near_ref, fromx_ref, fromy_ref, diagx_ref, diagy_ref, third_ref, chain_ref, done_ref,
    pack_ref, side_ref, sums_ref,
    near_sem, x_sem, y_sem, dx_sem, dy_sem, chain_sem, relay_sem, grad_sem, side_sem, send_sem, local_sem,
):
    z, x, y, c = place()
    m = 2 * y + c
    d = 2 * z + x
    n_dp = grad_ref.shape[0]
    right_x, right_y, partner = at(z, 1 - x, y, c), at(z, x, 1 - y, c), at(z, x, y, 1 - c)
    tokens, width = x_ref.shape
    loads = []
    for source, target in (
        (dwo_hbm, dw_ref.at[3]), (x_hbm, x_ref), (dh_hbm, dh_ref), (weight_hbm, weight_ref)
    ):
        load = pltpu.make_async_copy(source, target, local_sem.at[len(loads)])
        load.start()
        loads.append(load)
    greet([right_x, right_y, partner] + [at((z + off) % 4, x, y, c) for off in range(1, 4)])
    mail = Mail(send_sem)
    piece = pack_ref.at[0]

    edge = z % 3 == 0
    inner = z % 3 != 0
    far = z // 2
    near = 1 - far

    def relay(direction, kind, part):
        ref = chain_ref.at[direction, kind, part]
        return pltpu.make_async_remote_copy(
            src_ref=ref,
            dst_ref=ref,
            send_sem=relay_sem.at[direction, kind, part],
            recv_sem=chain_sem.at[direction, kind, part],
            device_id=at(z + 1 - 2 * direction, x, y, c),
            device_id_type=pl.DeviceIdType.MESH,
        )

    def opening(kind, part):
        chain_ref[far, kind, part] = third_ref[kind, part]
        relay(far, kind, part).start()

    def outward(kind, part):
        ref = chain_ref.at[far, kind, part]
        arrived(ref, chain_sem.at[far, kind, part])
        ref[...] = added(third_ref[kind, part], ref[...])
        relay(far, kind, part).start()

    def inward(kind, part):
        ref = chain_ref.at[near, kind, part]
        arrived(ref, chain_sem.at[near, kind, part])
        total = added(chain_ref[far, kind, part], ref[...])

        @pl.when(inner)
        def _():
            ref[...] = added(third_ref[kind, part], ref[...])
            relay(near, kind, part).start()

        return total

    def ahead(s):
        @pl.when(inner)
        def _():
            outward(1 + s // 4, s % 4)

    def keep(s):
        done_ref[s // 4, s % 4] = inward(1 + s // 4, s % 4)

    for kind, (stay_ref, got_ref) in enumerate(
        ((upstay_ref, upgot_ref), (downstay_ref, downgot_ref))
    ):
        for part in range(4):
            third_ref[1 + kind, part] = added(stay_ref[part], got_ref[part])

    @pl.when(edge)
    def _():
        def rest(s, carry):
            opening(1 + s // 4, s % 4)
            return carry

        lax.fori_loop(0, 8, rest, 0)

    pairs = ((dq0_ref, dq1_ref), (dk0_ref, dk1_ref), (dv0_ref, dv1_ref))
    half = width // PARTS
    groups = ((0, 2), (1, 3))
    share = near_ref.shape[2]
    twin = near_ref.at[0, pl.ds(0, 2)]

    def products(group):
        rows = [slice(2 * share * part, 2 * share * (part + 1)) for part in group]
        left = jnp.concatenate([n1_ref[r, :] for r in rows], axis=0)
        for index, pair in enumerate(pairs):
            out = dw_ref.at[index].reshape(width, width)
            for side, ref in enumerate(pair):
                value = dot(left, ref[...], 1, 1).astype(BF)
                for place_in, r in enumerate(rows):
                    out[r, side * half : (side + 1) * half] = value[
                        2 * share * place_in : 2 * share * (place_in + 1)
                    ]

    def pass_over(group):
        for part in group:
            for row in range(2):
                mail.send(
                    dw_ref.at[2 * row + 1 - c, pl.ds(2 * part, 2)], near_ref.at[row, pl.ds(2 * part, 2)],
                    near_sem.at[row, part], partner, twin,
                )

    def summed(group):
        for part in group:
            for row in range(2):
                arrived(twin, near_sem.at[row, part])

            def one(i, carry):
                row, e = i // 2, 2 * part + i % 2
                near_ref[row, e] = added(near_ref[row, e], dw_ref[2 * row + c, e])
                return carry

            lax.fori_loop(0, 4, one, 0)

    def issue(group):
        low, high = group
        mail.send(
            near_ref.at[1 - y, 2 * low + 1 - x], diagy_ref.at[low], dy_sem.at[low], right_y, piece
        )
        mail.send(
            near_ref.at[1 - y, 2 * high + 1 - x], diagx_ref.at[high - 2], dx_sem.at[high - 2],
            right_x, piece,
        )
        mail.send(near_ref.at[1 - y, 2 * low + x], fromy_ref.at[low], y_sem.at[low], right_y, piece)
        mail.send(near_ref.at[y, 2 * high + 1 - x], fromx_ref.at[high], x_sem.at[high], right_x, piece)

    def forward(group):
        low, high = group
        turn = high - 2
        arrived(diagy_ref.at[low], dy_sem.at[low])
        diagy_ref[low] = added(near_ref[y, 2 * low + 1 - x], diagy_ref[low])
        mail.send(diagy_ref.at[low], fromx_ref.at[low], x_sem.at[low], right_x, piece)
        arrived(diagx_ref.at[turn], dx_sem.at[turn])
        diagx_ref[turn] = added(near_ref[1 - y, 2 * high + x], diagx_ref[turn])
        mail.send(diagx_ref.at[turn], fromy_ref.at[high], y_sem.at[high], right_y, piece)

    products(groups[0])
    loads[0].wait()
    pass_over(groups[0])
    products(groups[1])
    pass_over(groups[1])
    for load in loads[1:]:
        load.wait()
    rows_ref[...] = jnp.zeros_like(rows_ref)
    flat = [weight_ref.at[index].reshape(width, width) for index in range(3)]

    def back(i, carry):
        t = pl.ds(pl.multiple_of(i * TILE, TILE), TILE)
        dn = jnp.zeros((TILE, width), F32)
        for index, pair in enumerate(pairs):
            for part, ref in enumerate(pair):
                dn += dot(ref[:, t], flat[index][:, part * half : (part + 1) * half], 0, 1)
        unit, scale = normed(x_ref[t, :].astype(F32))
        dx_ref[t, :] = dh_ref[t, :] + norm_back(dn, unit, scale, vec_ref[0:1, :])
        rows_ref[0:8, :] += fold_rows(dn * unit)
        rows_ref[8:16, :] += fold_rows(dn)
        return carry

    def gathered(part):
        arrived(fromx_ref.at[part], x_sem.at[part])
        arrived(fromy_ref.at[part], y_sem.at[part])
        third_ref[0, part] = added(near_ref[y, 2 * part + x], fromx_ref[part], fromy_ref[part])

    def wanted(e, part, first):
        second = lax.select(owner_ref[m, 2] == e, done_ref[1, part], first)
        return lax.select(owner_ref[m, 1] == e, done_ref[0, part], second)

    def close(part):
        first = inward(0, part)
        e = 2 * part + x
        pack_ref[part] = wanted(2 * z + 1 - x, part, first)
        mail.send(pack_ref.at[part], grad_ref.at[e], grad_sem.at[part], right_x, piece)
        grad_ref[e] = wanted(d, part, first)

    def begin(group):
        @pl.when(edge)
        def _():
            for part in group[::-1]:
                gathered(part)
                opening(0, part)

    def early(part):
        @pl.when(inner)
        def _():
            gathered(part)
            outward(0, part)

    def hop(index, peer):
        mail.send(
            sums_ref.at[index], side_ref.at[index], side_sem.at[index], peer, sums_ref.at[0]
        )

    def landed(index):
        arrived(side_ref.at[index], side_sem.at[index])
        sums_ref[index + 1] = sums_ref[index] + side_ref[index]

    ahead(0)
    summed(groups[0])
    issue(groups[0])
    ahead(1)
    lax.fori_loop(0, 1, back, 0)
    summed(groups[1])
    ahead(2)
    keep(0)
    forward(groups[0])
    issue(groups[1])

    def middle(i, carry):
        ahead(2 + i)
        keep(i)
        return back(i, carry)

    lax.fori_loop(1, 3, middle, 0)
    begin(groups[0])
    lax.fori_loop(3, tokens // TILE, middle, 0)

    def eight(ref, index):
        return jnp.sum(ref[8 * index : 8 * index + 8, :], axis=0, keepdims=True)

    ups = dc_ref.shape[0]
    sums_ref[0, 0:1, :] = eight(rows_ref, 0)
    sums_ref[0, 1:2, :] = eight(rows_ref, 1)
    for index in range(3):
        sums_ref[0, 2 + index : 3 + index, 0:half] = bias0_ref[8 * index : 8 * index + 1, :]
        sums_ref[0, 2 + index : 3 + index, half:width] = bias1_ref[8 * index : 8 * index + 1, :]
        sums_ref[0, 5 + index : 6 + index, :] = eight(mid_ref, index)
    for index in range(ups):
        sums_ref[0, 8 + index : 9 + index, :] = dc_ref[index, 0:1, :]
    sums_ref[0, 8 + ups : 9 + ups, :] = eight(mid_ref, 3)
    sums_ref[0, 9 + ups : 10 + ups, :] = jnp.concatenate(
        [freq0_ref[0:1, :], freq1_ref[0:1, :], freq0_ref[1:2, :], freq1_ref[1:2, :]], axis=1
    )
    hop(0, partner)
    forward(groups[1])
    ahead(6)
    keep(4)
    landed(0)
    hop(1, right_x)
    ahead(7)
    keep(5)
    landed(1)
    hop(2, right_y)
    begin(groups[1])
    keep(6)
    landed(2)
    for off in range(1, 4):
        mail.send(
            sums_ref.at[3], side_ref.at[3 + z], side_sem.at[3 + z], at((z + off) % 4, x, y, c),
            sums_ref.at[0],
        )
    side_ref[3 + z] = sums_ref[3]
    early(2)
    keep(7)
    early(0)
    close(2)
    early(3)
    close(0)
    early(1)
    close(3)
    close(1)
    for off in range(1, 4):
        e = (z + off) % 4
        arrived(side_ref.at[3 + e], side_sem.at[3 + e])
    total_ref[...] = (side_ref[3] + side_ref[4]) + (side_ref[5] + side_ref[6])
    for part in (2, 3, 0, 1):
        arrived(grad_ref.at[2 * part + 1 - x], grad_sem.at[part])
    mail.finish()
    for kind in range(3):
        for part in range(4):
            arrived(piece, relay_sem.at[far, kind, part])

            @pl.when(inner)
            def _():
                arrived(piece, relay_sem.at[near, kind, part])


def leave(owner, x, dh, n1, flows, vec, weights, dwo, smalls, rest):
    tokens, width = x.shape
    n_mlp, n_dp, share, _ = weights.shape
    smem = pl.BlockSpec(memory_space=pltpu.SMEM)
    vmem = pl.BlockSpec(memory_space=pltpu.VMEM)
    hbm = pl.BlockSpec(memory_space=pl.ANY)
    dma = pltpu.SemaphoreType.DMA
    part = lambda *lead: pltpu.VMEM(lead + (share, width), BF)
    flat = [ref for pair in flows for ref in pair]
    return pl.pallas_call(
        leave_kernel,
        in_specs=[smem] + [vmem] * 18 + [hbm] * 4,
        out_specs=[vmem] * 3,
        out_shape=[
            jax.ShapeDtypeStruct((tokens, width), F32),
            jax.ShapeDtypeStruct((n_dp, share, width), BF),
            jax.ShapeDtypeStruct(vec.shape, F32),
        ],
        scratch_shapes=[
            pltpu.VMEM((tokens, width), BF),
            pltpu.VMEM((tokens, width), F32),
            part(n_mlp, n_dp),
            pltpu.VMEM((16, width), F32),
            part(n_mlp, n_dp), part(2, n_dp), part(4), part(4), part(2), part(2), part(3, 4),
            part(2, 3, 4), part(2, 4), part(4),
            pltpu.VMEM((7,) + vec.shape, F32),
            pltpu.VMEM((4,) + vec.shape, F32),
            dma((2, 4)), dma((4,)), dma((4,)), dma((2,)), dma((2,)), dma((2, 3, 4)), dma((2, 3, 4)),
            dma((4,)), dma((7,)), dma((32,)), dma((4,)),
        ],
        compiler_params=pltpu.CompilerParams(
            vmem_limit_bytes=38 * 1024 * 1024, collective_id=2, has_side_effects=True
        ),
        name="leave",
    )(
        owner, n1, *flat, vec, *smalls, *rest, x, dh, weights,
        dwo.reshape(n_dp, share, width),
    )


def update_kernel(
    owner_ref, decay_ref, grad_ref, total_ref, moment_ref, vec_ref,
    left_hbm, right_hbm, lroot_hbm, rroot_hbm, master_hbm, y_hbm, dx_hbm,
    small_out, moment_out, vec_out, slot_out, left_out, right_out, master_out, y_out, dx_out,
    left_ref, right_ref, lroot_ref, rroot_ref, master_ref, y_ref, dx_ref, slot_ref, turn_ref,
    in_sem, out_sem,
):
    loads = []
    for source, target in (
        (left_hbm, left_ref), (right_hbm, right_ref), (lroot_hbm, lroot_ref), (rroot_hbm, rroot_ref),
        (master_hbm, master_ref), (y_hbm, y_ref), (dx_hbm, dx_ref),
    ):
        loads.append(pltpu.make_async_copy(source, target, in_sem.at[len(loads)]))
        loads[-1].start()
    outs = []

    def emit(source, target):
        outs.append(pltpu.make_async_copy(source, target, out_sem.at[len(outs)]))
        outs[-1].start()

    d = lax.axis_index("dp")
    m = lax.axis_index("mlp")
    held = (owner_ref[m, 0] == d) | (owner_ref[m, 1] == d) | (owner_ref[m, 2] == d)
    decay = decay_ref[0]
    width = grad_ref.shape[0]
    tall = width // 3

    def strip(i):
        return pl.ds(pl.multiple_of(i * tall, tall), tall)

    @pl.when(held)
    def _():
        slot_ref[...] = grad_ref[...].astype(F32)

    @pl.when(jnp.logical_not(held))
    def _():
        slot_ref[...] = jnp.zeros_like(slot_ref)

    emit(slot_ref, slot_out)

    def own(ref):
        cut = small_out.shape[1]
        value = ref[:, 0:cut]
        for index in range(1, owner_ref.shape[0]):
            value = lax.select(m == index, ref[:, index * cut : (index + 1) * cut], value)
        return value

    slow = decay_ref[1]
    small = own(total_ref)
    moment = slow * own(moment_ref) + (1.0 - slow) * small * small
    small_out[...] = small
    moment_out[...] = moment
    vec_out[...] = own(vec_ref) - RATE_VECTOR * small / (jnp.sqrt(moment) + STEP_EPSILON)
    loads[0].wait()

    @pl.when(held)
    def _():
        def rows(i, carry):
            r = strip(i)
            gram = dot(grad_ref[r, :], grad_ref[...], 1, 1)
            left_ref[r, :] = decay * left_ref[r, :] + (1.0 - decay) * gram
            return carry

        lax.fori_loop(0, 3, rows, 0)

    emit(left_ref, left_out)
    loads[1].wait()

    @pl.when(held)
    def _():
        turn_ref[...] = grad_ref[...].T

        def rows(i, carry):
            r = strip(i)
            gram = dot(turn_ref[r, :], grad_ref[...], 1, 0)
            right_ref[r, :] = decay * right_ref[r, :] + (1.0 - decay) * gram
            return carry

        lax.fori_loop(0, 3, rows, 0)

    emit(right_ref, right_out)
    for index, source, target in ((5, y_ref, y_out), (6, dx_ref, dx_out)):
        loads[index].wait()
        emit(source, target)
    for load in loads[2:5]:
        load.wait()

    @pl.when(held)
    def _():
        turn_ref[...] = rroot_ref[...].astype(BF)

        def rows(i, total):
            r = strip(i)
            inner = dot(lroot_ref[r, :].astype(BF), grad_ref[...], 1, 0).astype(BF)
            direction = dot(inner, turn_ref[...], 1, 0)
            lroot_ref[r, :] = direction
            return total + jnp.sum(direction * direction, axis=0, keepdims=True)

        total = jnp.sum(lax.fori_loop(0, 3, rows, jnp.zeros((1, width), F32)), keepdims=True)
        mean = total * (1.0 / (width * width))
        master_ref[...] -= lroot_ref[...] * (RATE_MATRIX * lax.rsqrt(mean + GRAFT_EPSILON))

    emit(master_ref, master_out)
    for copy in outs:
        copy.wait()


def update(
    owner, decays, grad, total, moments, vectors, left, right, lroot, rroot, master, output, input_grad
):
    smem = pl.BlockSpec(memory_space=pltpu.SMEM)
    vmem = pl.BlockSpec(memory_space=pltpu.VMEM)
    hbm = pl.BlockSpec(memory_space=pl.ANY)
    shape = lambda a: jax.ShapeDtypeStruct(a.shape, a.dtype)
    room = lambda a: pltpu.VMEM(a.shape, a.dtype)
    return pl.pallas_call(
        update_kernel,
        in_specs=[smem, smem] + [vmem] * 4 + [hbm] * 7,
        out_specs=[vmem] * 3 + [hbm] * 6,
        out_shape=[jax.ShapeDtypeStruct((total.shape[0], total.shape[1] // owner.shape[0]), F32)] * 3
        + [shape(a) for a in (left, left, right, master, output, input_grad)],
        scratch_shapes=[room(a) for a in (left, right, lroot, rroot, master, output, input_grad, left, grad)]
        + [pltpu.SemaphoreType.DMA((7,)), pltpu.SemaphoreType.DMA((6,))],
        compiler_params=pltpu.CompilerParams(vmem_limit_bytes=26 * 1024 * 1024),
        name="update",
    )(
        owner, decays, grad, total, moments, vectors, left, right, lroot, rroot, master, output, input_grad
    )


def positions(segment, heights, widths, patch_rows, patch_cols):
    images = heights.shape[0]
    matches = segment[None, :] == jnp.arange(images, dtype=jnp.int32)[:, None]
    tall = jnp.sum(jnp.where(matches, heights[:, None], 0), axis=0).astype(F32)
    wide = jnp.sum(jnp.where(matches, widths[:, None], 0), axis=0).astype(F32)
    py = patch_rows.astype(F32) * GRID_BASE / tall
    px = patch_cols.astype(F32) * GRID_BASE / wide
    zero = jnp.zeros_like(px)
    return jnp.stack([px, py, segment.astype(F32), zero, zero, zero, zero, zero])


def local(
    tokens, cotangent, vectors, vector_moments, decays, owner, master_slots, left_slots,
    right_slots, left_roots, right_roots, grid_height, grid_width, patch_rows, patch_cols, segment,
):
    mlp_index = lax.axis_index("mlp")
    n_dp = lax.axis_size("dp")
    n_mlp = lax.axis_size("mlp")
    width = tokens.shape[1]
    share = width // n_dp
    owner_row = jnp.take(owner, mlp_index, axis=0)
    master = master_slots[0, 0]
    direct = n_dp == 8 and n_mlp == 4
    if direct:
        n1t, q, k, v, cosine, sine, qmark, kmark, pos, attention, zone = enter(
            owner, grid_height, grid_width, master.reshape(n_dp, share, width), tokens, segment,
            patch_rows, patch_cols, vectors,
        )
        over_x = [(i, i ^ 1) for i in range(n_dp)]
        over_y = [(i, i ^ 2) for i in range(n_mlp)]
        xzone = lax.ppermute(zone, "dp", over_x)
        yzone = lax.ppermute(zone, "mlp", over_y)
    else:
        turned = vectors.T
        pos = positions(segment, grid_height, grid_width, patch_rows, patch_cols)
        slot = master.astype(BF).reshape(n_dp, share, width)
        pieces = lax.all_to_all(slot, "dp", 0, 0, tiled=True)
        mine = jnp.take(pieces, owner_row, axis=0)
        every = lax.all_gather(mine[None], ("dp", "mlp"), axis=0, tiled=True)
        blocks = every.reshape(n_dp, n_mlp, 3, share, width).transpose(2, 1, 0, 3, 4)
        attention, up, down = blocks.reshape(3, n_mlp, width, width)
        n1t, q, k, v, cosine, sine, qmark, kmark = project(tokens, pos, vectors, turned, attention)
    o, log_totals = attend(grid_height, grid_width, q, k, v, qmark, kmark)
    fine = (n_mlp, n_dp, share, width)
    back = functools.partial(attend_back, grid_height, grid_width)
    if direct:
        output, dh, do, dwo, mid_rows, dc, upgo, upstay, downgo, downstay = center(
            tokens, cotangent, o, vectors, attention, zone, xzone, yzone
        )
        upgot = lax.ppermute(upgo, "dp", over_x)
        downgot = lax.ppermute(downgo, "mlp", over_y)
        first = back(q, k, v, qmark, kmark, log_totals, do, pos, cosine, sine, 0)
        first, upgot, downgot = lax.optimization_barrier((first, upgot, downgot))
        upgo, upstay, downgo, downstay = merge(upstay, upgot, downstay, downgot)
        upgot = lax.ppermute(upgo, "mlp", over_y)
        downgot = lax.ppermute(downgo, "dp", over_x)
        do, upstay, downstay = lax.optimization_barrier((do, upstay, downstay))
    else:
        output, dh, do, dwo, dup, ddown, mid_rows, dc = middle_part(
            tokens, cotangent, o, vectors, attention[3], up, down
        )
        first = back(q, k, v, qmark, kmark, log_totals, do, pos, cosine, sine, 0)
    second = back(q, k, v, qmark, kmark, log_totals, do, pos, cosine, sine, 1)
    both = list(zip(first, second))
    if direct:
        input_grad, gradient, total = leave(
            owner, tokens, dh, n1t, both[0:3], vectors, attention.reshape(fine), dwo,
            (*both[3], *both[4], mid_rows, dc),
            (upstay, upgot, downstay, downgot),
        )
    else:
        freq = jnp.concatenate(both[3], axis=1)[0:2].reshape(1, width)
        bias = jnp.concatenate(both[4], axis=1)[0::8]
        eights = lambda rows: jnp.sum(rows.reshape(-1, 8, width), axis=1)
        mid = eights(mid_rows)
        tail = [bias, mid[0:3], dc[:, 0, :], mid[3:4], freq]
        dq, dk, dv = (jnp.concatenate(pair, axis=0) for pair in both[0:3])
        input_grad, datt, fin_rows = final_part(
            tokens, dh, n1t, dq, dk, dv, vectors, attention, dwo
        )
        grads = jnp.stack([datt, dup, ddown], axis=1)
        grads = grads.reshape(n_mlp, 3, n_dp, share, width).transpose(2, 0, 1, 3, 4)
        grads = grads.reshape(n_dp * n_mlp * 3, share, width)
        reduced = lax.psum_scatter(grads, ("dp", "mlp"), scatter_dimension=0, tiled=True)
        takers = owner_row[None, :] == jnp.arange(n_dp, dtype=jnp.int32)[:, None]
        kind_of = jnp.sum(jnp.where(takers, jnp.arange(3, dtype=jnp.int32)[None, :], 0), axis=1)
        gradient = lax.all_to_all(jnp.take(reduced, kind_of, axis=0), "dp", 0, 0, tiled=True)
        total = lax.psum(jnp.concatenate([eights(fin_rows)] + tail, axis=0), ("dp", "mlp"))
    gradient = gradient.reshape(width, width)
    grad_share, moment_next, vector_next, slot_grad, left_out, right_out, master_out, output, input_grad = (
        update(
            owner, decays, gradient, total, vector_moments, vectors, left_slots[0, 0], right_slots[0, 0],
            left_roots[0, 0], right_roots[0, 0], master, output, input_grad,
        )
    )
    lift = lambda a: a[None, None]
    return (
        output, input_grad, lift(slot_grad), lift(left_out), lift(right_out), lift(master_out),
        grad_share, moment_next, vector_next,
    )


def solution(mesh):
    both = P(("dp", "mlp"))
    flat = P(("dp", "mlp"), None)
    slots = P("dp", "mlp", None, None)
    split = P(None, "mlp")
    return jax.shard_map(
        local,
        mesh=mesh,
        in_specs=(flat, flat, P(), P(), P(), P(), slots, slots, slots, slots, slots)
        + (both,) * 5,
        out_specs=(flat, flat, slots, slots, slots, slots, split, split, split),
        check_vma=False,
    )
```

```python
import functools
import math

import jax
import jax.numpy as jnp
from jax import lax
from jax.experimental import pallas as pl
from jax.experimental.pallas import tpu as pltpu
from jax.sharding import PartitionSpec as P

HEADS = 12
GRID_BASE = 16
NORM_EPSILON = 1e-06
GRAFT_EPSILON = 1e-06
STEP_EPSILON = 1e-08
RATE_MATRIX = 0.04
RATE_VECTOR = 0.02
MASK_SHIFT = -(2.0**100)
BLOCK = 128
TILE = 256
PARTS = 2
WINDOW = 6
F32 = jnp.float32
BF = jnp.bfloat16
VMEM_LIMIT = 60 * 1024 * 1024


def dot(left, right, left_dim, right_dim, precision=None):
    return lax.dot_general(
        left,
        right,
        (((left_dim,), (right_dim,)), ((), ())),
        preferred_element_type=F32,
        precision=precision,
    )


def normed(values):
    mean = jnp.mean(values, axis=-1, keepdims=True)
    centred = values - mean
    spread = jnp.mean(centred * centred, axis=-1, keepdims=True)
    scale = lax.rsqrt(spread + NORM_EPSILON)
    return centred * scale, scale


def norm_back(grad, unit, scale, gain):
    scaled = grad * gain
    first = jnp.mean(scaled, axis=-1, keepdims=True)
    second = jnp.mean(scaled * unit, axis=-1, keepdims=True)
    return scale * (scaled - first - unit * second)


def fold_rows(values):
    return jnp.sum(values.reshape(values.shape[0] // 8, 8, values.shape[1]), axis=0)


def place():
    d = lax.axis_index("dp")
    m = lax.axis_index("mlp")
    return d // 2, d % 2, m // 2, m % 2


def at(z, x, y, c):
    return (2 * z + x, 2 * y + c)


def greet(peers):
    barrier = pltpu.get_barrier_semaphore()
    for peer in peers:
        pl.semaphore_signal(barrier, inc=1, device_id=peer, device_id_type=pl.DeviceIdType.MESH)
    pl.semaphore_wait(barrier, len(peers))


class Mail:
    def __init__(self, sems):
        self.sems = sems
        self.like = []

    def send(self, source, target, arrival, peer, like):
        slot = len(self.like)
        pltpu.make_async_remote_copy(
            src_ref=source,
            dst_ref=target,
            send_sem=self.sems.at[slot],
            recv_sem=arrival,
            device_id=peer,
            device_id_type=pl.DeviceIdType.MESH,
        ).start()
        self.like.append(like)
        return slot

    def settle(self, slot):
        arrived(self.like[slot], self.sems.at[slot])
        self.like[slot] = None

    def finish(self):
        for slot, like in enumerate(self.like):
            if like is not None:
                self.settle(slot)


def arrived(target, arrival):
    pltpu.make_async_copy(target, target, arrival).wait()


def enter_kernel(
    owner_ref, height_ref, width_ref, slot_hbm, x_ref, seg_ref, patch_rows_ref, patch_cols_ref, vec_ref,
    n1_ref, q_ref, k_ref, v_ref, cos_ref, sin_ref, qmark_ref, kmark_ref, pos_ref, weight_ref, zone_ref,
    wide_ref, turned_ref, raw_ref, slot_ref, cross_ref, chain_ref, att_ref, zland_ref,
    cross_sem, chain_sem, relay_sem, att_sem, send_sem, local_sem,
):
    z, x, y, c = place()
    m = 2 * y + c
    n_dp = slot_ref.shape[0]
    right_x, right_y, partner = at(z, 1 - x, y, c), at(z, x, 1 - y, c), at(z, x, y, 1 - c)
    own = pltpu.make_async_copy(slot_hbm, raw_ref, local_sem.at[0])
    own.start()
    greet([right_x, right_y, partner, at((z + 1) % 4, x, y, c), at((z + 3) % 4, x, y, c)])
    mail = Mail(send_sem)
    piece = slot_ref.at[0]
    own.wait()
    for part in range(4):
        e = 2 * part + 1 - x
        slot_ref[e] = raw_ref[e].astype(BF)
        mail.send(slot_ref.at[e], cross_ref.at[part], cross_sem.at[part], right_x, piece)
    for part in range(4):
        e = 2 * part + x
        slot_ref[e] = raw_ref[e].astype(BF)

    tokens = x_ref.shape[0]
    half = cos_ref.shape[0]
    last = vec_ref.shape[0] - 1
    tiles = tokens // TILE
    wide_ref[...] = jnp.zeros_like(wide_ref)
    wide_ref[0 : last + 1, :] = vec_ref[...]
    turned_ref[...] = wide_ref[...].T
    tall = jnp.zeros(seg_ref.shape, F32)
    broad = jnp.zeros(seg_ref.shape, F32)
    for image in range(height_ref.shape[0]):
        match = seg_ref[...] == image
        tall = jnp.where(match, height_ref[image].astype(F32), tall)
        broad = jnp.where(match, width_ref[image].astype(F32), broad)
    pos_ref[...] = jnp.zeros_like(pos_ref)
    pos_ref[0:1, :] = patch_cols_ref[...].astype(F32) * GRID_BASE / broad
    pos_ref[1:2, :] = patch_rows_ref[...].astype(F32) * GRID_BASE / tall
    pos_ref[2:3, :] = seg_ref[...].astype(F32)

    def prepare(i, carry):
        t = pl.ds(pl.multiple_of(i * TILE, TILE), TILE)
        unit, _ = normed(x_ref[t, :].astype(F32))
        n1_ref[:, t] = (unit * vec_ref[0:1, :] + vec_ref[1:2, :]).astype(BF).T
        angle = turned_ref[half:, last : last + 1] * pos_ref[1:2, t] + turned_ref[:half, last : last + 1] * pos_ref[0:1, t]
        cos_ref[:, t] = jnp.cos(angle)
        sin_ref[:, t] = jnp.sin(angle)
        seg = pos_ref[2:3, t].astype(jnp.int32)
        row = lax.broadcasted_iota(jnp.int32, (qmark_ref.shape[0], TILE), 0)
        qmark_ref[:, t] = jnp.where(row == seg, 1.0, 0.0).astype(BF)
        kmark_ref[:, t] = jnp.where(row == seg, 0.0, MASK_SHIFT).astype(BF)
        return carry

    lax.fori_loop(0, tiles // 2, prepare, 0)

    edge = z % 3 == 0
    inner = z % 3 != 0
    far = z // 2
    near = 1 - far

    def relay(direction, kind, part):
        ref = chain_ref.at[direction, kind, part]
        return pltpu.make_async_remote_copy(
            src_ref=ref,
            dst_ref=ref,
            send_sem=relay_sem.at[direction, kind, part],
            recv_sem=chain_sem.at[direction, kind, part],
            device_id=at(z + 1 - 2 * direction, x, y, c),
            device_id_type=pl.DeviceIdType.MESH,
        )

    def merged(direction, kind, part, opening):
        ref = chain_ref.at[direction, kind, part]
        home = owner_ref[m, kind]
        value = lax.select(home % 2 == x, slot_ref[2 * part + x], cross_ref[part])
        if not opening:
            arrived(ref, chain_sem.at[direction, kind, part])
            value = lax.select(home // 2 == z, value, ref[...])
        ref[...] = value

    def crossed(part):
        arrived(cross_ref.at[part], cross_sem.at[part])

    def outward(kind, part):
        merged(far, kind, part, False)
        relay(far, kind, part).start()

    def inward(kind, part):
        merged(near, kind, part, False)

        @pl.when(inner)
        def _():
            relay(near, kind, part).start()

        return lax.select(
            owner_ref[m, kind] // 2 <= z, chain_ref[0, kind, part], chain_ref[1, kind, part]
        )

    def bring(part):
        e = 2 * part + x
        att_ref[m, e] = inward(0, part)
        for peer in (right_x, right_y, partner):
            mail.send(att_ref.at[m, e], att_ref.at[m, e], att_sem.at[m, e], peer, piece)

    @pl.when(edge)
    def _():
        def opening(part, carry):
            crossed(part)
            merged(far, 0, part, True)
            relay(far, 0, part).start()
            return carry

        lax.fori_loop(0, 4, opening, 0)

        def rest(s, carry):
            merged(far, 1 + s // 4, s % 4, True)
            relay(far, 1 + s // 4, s % 4).start()
            return carry

        lax.fori_loop(0, 8, rest, 0)

    def early(part):
        @pl.when(inner)
        def _():
            crossed(part)
            outward(0, part)

    def ahead(s):
        @pl.when(inner)
        def _():
            outward(1 + s // 4, s % 4)

    def keep(s):
        zland_ref[s // 4, s % 4] = inward(1 + s // 4, s % 4)

    m_y = 2 * (1 - y) + c

    def spread(part):
        e = 2 * part + 1 - x
        arrived(att_ref.at[m, e], att_sem.at[m, e])
        if part < 2:
            mail.send(att_ref.at[m, e], att_ref.at[m, e], att_sem.at[m, e], right_y, piece)
        mail.send(att_ref.at[m, e], att_ref.at[m, e], att_sem.at[m, e], partner, piece)
        f = 2 * part + x
        arrived(att_ref.at[m_y, f], att_sem.at[m_y, f])
        if part >= 2:
            mail.send(att_ref.at[m_y, f], att_ref.at[m_y, f], att_sem.at[m_y, f], right_x, piece)
        mail.send(att_ref.at[m_y, f], att_ref.at[m_y, f], att_sem.at[m_y, f], partner, piece)

    early(0)
    early(1)
    bring(0)
    early(2)
    bring(1)
    early(3)
    bring(2)
    ahead(0)
    spread(0)
    bring(3)
    ahead(1)
    spread(1)
    ahead(2)
    keep(0)
    lax.fori_loop(tiles // 2, tiles, prepare, 0)
    spread(2)
    ahead(3)
    keep(1)
    spread(3)
    ahead(4)
    keep(2)
    for part in range(4):
        e = 2 * part + 1 - x
        arrived(att_ref.at[m_y, e], att_sem.at[m_y, e])
        mail.send(att_ref.at[m_y, e], att_ref.at[m_y, e], att_sem.at[m_y, e], partner, piece)
    for step in range(2):
        other = 2 * step + 1 - c
        for e in range(n_dp):
            arrived(att_ref.at[other, e], att_sem.at[other, e])
    out = pltpu.make_async_copy(att_ref, weight_ref, local_sem.at[1])
    out.start()

    part = half // HEADS
    width = x_ref.shape[1]

    def weight(index):
        return att_ref[index].reshape(width, width)

    def rotate(i, carry):
        @pl.when(i < 3)
        def _():
            ahead(5 + i)

        keep(3 + i)
        t = pl.ds(pl.multiple_of(i * TILE, TILE), TILE)
        n1t = n1_ref[:, t]
        cosine = cos_ref[:, t]
        sine = sin_ref[:, t]
        for index, (ref, scale) in enumerate(((q_ref, 0.125), (k_ref, 1.0))):
            flat = dot(weight(index), n1t, 0, 0) + turned_ref[:, 2 + index : 3 + index]
            for head in range(HEADS):
                low, mid = 2 * part * head, 2 * part * head + part
                a = flat[low:mid]
                b = flat[mid : mid + part]
                cs = cosine[part * head : part * (head + 1)]
                sn = sine[part * head : part * (head + 1)]
                ref[low:mid, t] = (a * cs - b * sn).astype(BF) * jnp.asarray(scale, BF)
                ref[mid : mid + part, t] = (b * cs + a * sn).astype(BF) * jnp.asarray(scale, BF)
        v_ref[:, t] = (dot(weight(2), n1t, 0, 0) + turned_ref[:, 4:5]).astype(BF)
        return carry

    lax.fori_loop(0, tiles, rotate, 0)
    keep(7)
    last_out = pltpu.make_async_copy(zland_ref, zone_ref, local_sem.at[2])
    last_out.start()
    mail.finish()
    for kind in range(3):
        for step in range(4):
            arrived(piece, relay_sem.at[far, kind, step])

            @pl.when(inner)
            def _():
                arrived(piece, relay_sem.at[near, kind, step])

    out.wait()
    last_out.wait()


def enter(owner, heights, widths, slot, x, segment, patch_rows, patch_cols, vec):
    rows, width = x.shape
    half = width // 2
    n_dp, share, _ = slot.shape
    n_mlp = owner.shape[0]
    smem = pl.BlockSpec(memory_space=pltpu.SMEM)
    vmem = pl.BlockSpec(memory_space=pltpu.VMEM)
    hbm = pl.BlockSpec(memory_space=pl.ANY)
    out = lambda n, dtype: jax.ShapeDtypeStruct((n, rows), dtype)
    return pl.pallas_call(
        enter_kernel,
        in_specs=[smem, smem, smem, hbm] + [vmem] * 5,
        out_specs=[vmem] * 9 + [hbm] * 2,
        out_shape=[out(width, BF)] * 4
        + [out(half, F32)] * 2
        + [out(16, BF)] * 2
        + [out(8, F32)]
        + [
            jax.ShapeDtypeStruct((n_mlp, n_dp, share, width), BF),
            jax.ShapeDtypeStruct((2, 4, share, width), BF),
        ],
        scratch_shapes=[
            pltpu.VMEM((16, width), F32),
            pltpu.VMEM((width, 16), F32),
            pltpu.VMEM((n_dp, share, width), F32),
            pltpu.VMEM((n_dp, share, width), BF),
            pltpu.VMEM((4, share, width), BF),
            pltpu.VMEM((2, 3, 4, share, width), BF),
            pltpu.VMEM((n_mlp, n_dp, share, width), BF),
            pltpu.VMEM((2, 4, share, width), BF),
            pltpu.SemaphoreType.DMA((4,)),
            pltpu.SemaphoreType.DMA((2, 3, 4)),
            pltpu.SemaphoreType.DMA((2, 3, 4)),
            pltpu.SemaphoreType.DMA((n_mlp, n_dp)),
            pltpu.SemaphoreType.DMA((48,)),
            pltpu.SemaphoreType.DMA((3,)),
        ],
        compiler_params=pltpu.CompilerParams(
            vmem_limit_bytes=31 * 1024 * 1024, collective_id=0, has_side_effects=True
        ),
        name="enter",
    )(
        owner, heights, widths, slot, x,
        *(a.reshape(1, rows) for a in (segment, patch_rows, patch_cols)), vec,
    )


def project_kernel(
    x_ref, pos_ref, vec_ref, turned_ref, weight_ref,
    n1_ref, q_ref, k_ref, v_ref, cos_ref, sin_ref, qmark_ref, kmark_ref,
):
    unit, _ = normed(x_ref[...].astype(F32))
    n1 = (unit * vec_ref[0:1, :] + vec_ref[1:2, :]).astype(BF)
    n1t = n1.T
    n1_ref[...] = n1t
    px = pos_ref[0:1, :]
    py = pos_ref[1:2, :]
    half = cos_ref.shape[0]
    last = turned_ref.shape[1] - 1
    angle = turned_ref[half:, last:] * py + turned_ref[:half, last:] * px
    cosine = jnp.cos(angle)
    sine = jnp.sin(angle)
    cos_ref[...] = cosine
    sin_ref[...] = sine
    seg = pos_ref[2:3, :].astype(jnp.int32)
    row = lax.broadcasted_iota(jnp.int32, qmark_ref.shape, 0)
    qmark_ref[...] = jnp.where(row == seg, 1.0, 0.0).astype(BF)
    kmark_ref[...] = jnp.where(row == seg, 0.0, MASK_SHIFT).astype(BF)
    part = half // HEADS
    for index, (out, scale) in enumerate(((q_ref, 0.125), (k_ref, 1.0))):
        flat = dot(weight_ref[index], n1t, 0, 0) + turned_ref[:, 2 + index : 3 + index]
        for head in range(HEADS):
            low, mid = 2 * part * head, 2 * part * head + part
            a = flat[low:mid]
            b = flat[mid : mid + part]
            c = cosine[part * head : part * (head + 1)]
            s = sine[part * head : part * (head + 1)]
            out[low:mid, :] = (a * c - b * s).astype(BF) * jnp.asarray(scale, BF)
            out[mid : mid + part, :] = (b * c + a * s).astype(BF) * jnp.asarray(scale, BF)
    v_ref[...] = (dot(weight_ref[2], n1t, 0, 0) + turned_ref[:, 4:5]).astype(BF)


def project(x, pos, vec, turned, weights):
    rows, width = x.shape
    half = width // 2
    whole = lambda a: pl.BlockSpec(a.shape, lambda i: (0,) * a.ndim)
    col = lambda n: pl.BlockSpec((n, TILE), lambda i: (0, i))
    out = lambda n, d: jax.ShapeDtypeStruct((n, rows), d)
    return pl.pallas_call(
        project_kernel,
        grid=(rows // TILE,),
        in_specs=[
            pl.BlockSpec((TILE, width), lambda i: (i, 0)),
            col(8),
            whole(vec),
            whole(turned),
            whole(weights),
        ],
        out_specs=[col(width)] * 4 + [col(half)] * 2 + [col(16)] * 2,
        out_shape=[out(width, BF)] * 4 + [out(half, F32)] * 2 + [out(16, BF)] * 2,
        compiler_params=pltpu.CompilerParams(vmem_limit_bytes=VMEM_LIMIT),
        name="project",
    )(x, pos, vec, turned, weights)


def key_window(height_ref, width_ref, block):
    first = block * BLOCK
    last = first + BLOCK - 1
    start = jnp.int32(0)
    low = jnp.int32(0)
    high = jnp.int32(0)
    for image in range(height_ref.shape[0]):
        end = start + height_ref[image] * width_ref[image]
        low = jnp.where((start <= first) & (first < end), start, low)
        high = jnp.where((start <= last) & (last < end), end, high)
        start = end
    base = low // BLOCK
    return base, (high + BLOCK - 1) // BLOCK - base


def attend_kernel(height_ref, width_ref, q_ref, k_ref, v_ref, qmark_ref, kmark_ref, o_ref, log_ref):
    tokens = q_ref.shape[1]
    blocks = tokens // BLOCK
    size = q_ref.shape[0] // HEADS
    group = 4

    def one(block, part, base, count):
        here = pl.ds(pl.multiple_of(block * BLOCK, BLOCK), BLOCK)
        keys = pl.ds(pl.multiple_of(base * BLOCK, BLOCK), BLOCK * count)
        qmark = qmark_ref[:, here]
        kmark = kmark_ref[:, keys]
        for j in range(group):
            head = part * group + j
            rows = pl.ds(pl.multiple_of(head * size, size), size)
            q = jnp.concatenate([q_ref[rows, here], qmark], axis=0)
            k = jnp.concatenate([k_ref[rows, keys], kmark], axis=0)
            scores = dot(k, q, 0, 0)
            peak = jnp.max(scores, axis=0, keepdims=True)
            powers = jnp.exp(scores - peak)
            total = jnp.sum(powers, axis=0, keepdims=True)
            mixed = dot(v_ref[rows, keys], powers.astype(BF), 1, 0)
            o_ref[rows, here] = (mixed * (1.0 / total)).astype(BF)
            log_ref[pl.ds(pl.multiple_of(head * 8, 8), 8), here] = jnp.broadcast_to(
                peak + jnp.log(total), (8, BLOCK)
            )

    def step(block, carry):
        base, count = key_window(height_ref, width_ref, block)
        for n in range(1, min(blocks, WINDOW) + 1):

            @pl.when(count == n)
            def _():
                def inner(part, c):
                    one(block, part, base, n)
                    return c

                lax.fori_loop(0, HEADS // group, inner, 0)

        return carry

    lax.fori_loop(0, blocks, step, 0)


def attend(heights, widths, q, k, v, qmark, kmark):
    smem = pl.BlockSpec(memory_space=pltpu.SMEM)
    vmem = pl.BlockSpec(memory_space=pltpu.VMEM)
    return pl.pallas_call(
        attend_kernel,
        in_specs=[smem, smem] + [vmem] * 5,
        out_specs=[vmem, vmem],
        out_shape=[
            jax.ShapeDtypeStruct(q.shape, BF),
            jax.ShapeDtypeStruct((8 * HEADS, q.shape[1]), F32),
        ],
        compiler_params=pltpu.CompilerParams(vmem_limit_bytes=9 * 1024 * 1024),
        name="attend",
    )(heights, widths, q, k, v, qmark, kmark)


def attend_back_kernel(
    height_ref, width_ref, q_ref, k_ref, v_ref, qmark_ref, kmark_ref, log_ref, do_ref,
    pos_ref, cos_ref, sin_ref,
    dq_ref, dk_ref, dv_ref, freq_ref, bias_ref,
    gq_ref, gk_ref, gv_ref, turn_ref,
):
    tokens = q_ref.shape[1]
    blocks = tokens // BLOCK
    heads = log_ref.shape[0] // 8
    size = q_ref.shape[0] // heads
    half = size // 2
    group = 2
    gk_ref[...] = jnp.zeros_like(gk_ref)
    gv_ref[...] = jnp.zeros_like(gv_ref)

    def one(block, part, base, count):
        here = pl.ds(pl.multiple_of(block * BLOCK, BLOCK), BLOCK)
        keys = pl.ds(pl.multiple_of(base * BLOCK, BLOCK), BLOCK * count)
        qmark = qmark_ref[:, here]
        kmark = kmark_ref[:, keys]
        for j in range(group):
            head = part * group + j
            rows = pl.ds(pl.multiple_of(head * size, size), size)
            q = q_ref[rows, here]
            k = k_ref[rows, keys]
            do = do_ref[rows, here]
            scores = dot(
                jnp.concatenate([k, kmark], axis=0), jnp.concatenate([q, qmark], axis=0), 0, 0
            )
            log_row = log_ref[pl.ds(pl.multiple_of(head * 8, 8), 8), here][0:1]
            probs = jnp.exp(scores - log_row)
            dp = dot(v_ref[rows, keys], do, 0, 0)
            inner = jnp.sum(probs * dp, axis=0, keepdims=True)
            ds = (probs * (dp - inner)).astype(BF)
            gq_ref[rows, here] = dot(k, ds, 1, 0) * 0.125
            gk_ref[rows, keys] += dot(q, ds, 1, 1)
            gv_ref[rows, keys] += dot(do, probs.astype(BF), 1, 1)

    def step(block, carry):
        base, count = key_window(height_ref, width_ref, block)
        for n in range(1, min(blocks, WINDOW) + 1):

            @pl.when(count == n)
            def _():
                def inner(part, c):
                    one(block, part, base, n)
                    return c

                lax.fori_loop(0, heads // group, inner, 0)

        return carry

    lax.fori_loop(0, blocks, step, 0)

    def unturn(head, carry):
        low = pl.ds(pl.multiple_of(head * size, size), half)
        high = pl.ds(pl.multiple_of(head * size + half, half), half)
        table = pl.ds(pl.multiple_of(head * half, half), half)
        c = cos_ref[table, :]
        s = sin_ref[table, :]
        turn = None
        for grad_ref, rot_ref, scale, out_ref in (
            (gq_ref, q_ref, 8.0, dq_ref),
            (gk_ref, k_ref, 1.0, dk_ref),
        ):
            ga = grad_ref[low, :]
            gb = grad_ref[high, :]
            out_ref[low, :] = (ga * c + gb * s).astype(BF)
            out_ref[high, :] = (gb * c - ga * s).astype(BF)
            ra = rot_ref[low, :].astype(F32) * scale
            rb = rot_ref[high, :].astype(F32) * scale
            piece = gb * ra - ga * rb
            turn = piece if turn is None else turn + piece
        turn_ref[table, :] = turn
        both = pl.ds(pl.multiple_of(head * size, size), size)
        dv_ref[both, :] = gv_ref[both, :].astype(BF)
        return carry

    lax.fori_loop(0, heads, unturn, 0)
    freq_ref[...] = dot(pos_ref[...], turn_ref[...], 1, 1, lax.Precision.HIGHEST)
    ones = jnp.ones((8, tokens), BF)
    for index, ref in enumerate((dq_ref, dk_ref, dv_ref)):
        bias_ref[8 * index : 8 * index + 8, :] = dot(ones, ref[...], 1, 1)


def attend_back(heights, widths, q, k, v, qmark, kmark, log_totals, do, pos, cosine, sine, part):
    smem = pl.BlockSpec(memory_space=pltpu.SMEM)
    width, tokens = q.shape
    half = width // PARTS
    cut = lambda a: pl.BlockSpec((a.shape[0] // PARTS, tokens), lambda i: (part, 0))
    whole = lambda a: pl.BlockSpec(a.shape, lambda i: (0, 0))
    out = lambda n, cols, dtype: jax.ShapeDtypeStruct((n, cols), dtype)
    outs = [out(half, tokens, BF)] * 3 + [out(8, half // 2, F32), out(24, half, F32)]
    return pl.pallas_call(
        attend_back_kernel,
        grid=(1,),
        in_specs=[smem, smem, cut(q), cut(k), cut(v), whole(qmark), whole(kmark), cut(log_totals)]
        + [cut(do), whole(pos), cut(cosine), cut(sine)],
        out_specs=[whole(a) for a in outs],
        out_shape=outs,
        scratch_shapes=[pltpu.VMEM((half, tokens), F32)] * 3
        + [pltpu.VMEM((half // 2, tokens), F32)],
        compiler_params=pltpu.CompilerParams(vmem_limit_bytes=18 * 1024 * 1024),
        name="attend_back",
    )(heights, widths, q, k, v, qmark, kmark, log_totals, do, pos, cosine, sine)


def middle_kernel(
    x_ref, g_ref, o_ref, vec_ref, wo_ref, up_ref, down_ref,
    y_ref, dh_ref, do_ref, dwo_ref, dup_ref, ddown_ref, rows_ref, dc_ref,
    h_ref, n2_ref, n2t_ref, acc_ref, dn_ref, a_ref, dz_ref, dr_ref,
):
    groups = vec_ref.shape[0] - 10
    step = pl.program_id(0)
    tokens, width = x_ref.shape
    tiles = tokens // TILE

    def tile(i):
        return pl.ds(pl.multiple_of(i * TILE, TILE), TILE)

    @pl.when(step == 0)
    def _():
        def first(i, c):
            t = tile(i)
            branch = dot(o_ref[:, t], wo_ref[...], 0, 0) + vec_ref[5:6, :]
            h = x_ref[t, :].astype(F32) + branch
            h_ref[t, :] = h
            unit, _ = normed(h)
            n2 = (unit * vec_ref[6:7, :] + vec_ref[7:8, :]).astype(BF)
            n2_ref[t, :] = n2
            n2t_ref[:, t] = n2.T
            acc_ref[t, :] = h + vec_ref[8 + groups : 9 + groups, :]
            dn_ref[t, :] = jnp.zeros((TILE, width), F32)
            return c

        lax.fori_loop(0, tiles, first, 0)

    up_bias = vec_ref[pl.ds(8 + step, 1), :]

    def second(i, c):
        t = tile(i)
        z = dot(n2_ref[t, :], up_ref[0], 1, 0) + up_bias
        cdf = 0.5 * (1.0 + lax.erf(z * math.sqrt(0.5)))
        a = (z * cdf).astype(BF)
        a_ref[t, :] = a
        acc_ref[t, :] += dot(a, down_ref[0], 1, 0)
        da = dot(g_ref[t, :], down_ref[0], 1, 1)
        slope = cdf + z * (jnp.exp(-0.5 * z * z) * (1.0 / math.sqrt(2.0 * math.pi)))
        dz = (da * slope).astype(BF)
        dz_ref[t, :] = dz
        dn_ref[t, :] += dot(dz, up_ref[0], 1, 1)
        return c

    lax.fori_loop(0, tiles, second, 0)
    dc_ref[0] = dot(jnp.ones((8, tokens), BF), dz_ref[...], 1, 0)
    dup_ref[0] = dot(n2t_ref[...], dz_ref[...], 1, 0).astype(BF)
    ddown_ref[0] = dot(a_ref[...], g_ref[...], 0, 0).astype(BF)

    @pl.when(step == groups - 1)
    def _():
        rows_ref[...] = jnp.zeros_like(rows_ref)

        def third(i, c):
            t = tile(i)
            y_ref[t, :] = acc_ref[t, :].astype(BF)
            g = g_ref[t, :].astype(F32)
            unit, scale = normed(h_ref[t, :])
            dn = dn_ref[t, :]
            dh = g + norm_back(dn, unit, scale, vec_ref[6:7, :])
            dh_ref[t, :] = dh
            dr = dh.astype(BF)
            dr_ref[t, :] = dr
            do_ref[:, t] = dot(wo_ref[...], dr, 1, 1).astype(BF)
            rows_ref[0:8, :] += fold_rows(dr.astype(F32))
            rows_ref[8:16, :] += fold_rows(dn * unit)
            rows_ref[16:24, :] += fold_rows(dn)
            rows_ref[24:32, :] += fold_rows(g)
            return c

        lax.fori_loop(0, tiles, third, 0)
        dwo_ref[...] = dot(o_ref[...], dr_ref[...], 1, 0).astype(BF)


def middle_part(x, g, o, vec, wo, up, down):
    tokens, width = x.shape
    groups = up.shape[0]
    whole = lambda s: pl.BlockSpec(s, lambda i: (0,) * len(s))
    block = pl.BlockSpec((1, width, width), lambda i: (i, 0, 0))
    return pl.pallas_call(
        middle_kernel,
        grid=(groups,),
        in_specs=[
            whole(x.shape),
            whole(g.shape),
            whole(o.shape),
            whole(vec.shape),
            whole(wo.shape),
            block,
            block,
        ],
        out_specs=[
            whole((tokens, width)),
            whole((tokens, width)),
            whole((width, tokens)),
            whole((width, width)),
            block,
            block,
            whole((32, width)),
            pl.BlockSpec((1, 8, width), lambda i: (i, 0, 0)),
        ],
        out_shape=[
            jax.ShapeDtypeStruct((tokens, width), BF),
            jax.ShapeDtypeStruct((tokens, width), F32),
            jax.ShapeDtypeStruct((width, tokens), BF),
            jax.ShapeDtypeStruct((width, width), BF),
            jax.ShapeDtypeStruct((groups, width, width), BF),
            jax.ShapeDtypeStruct((groups, width, width), BF),
            jax.ShapeDtypeStruct((32, width), F32),
            jax.ShapeDtypeStruct((groups, 8, width), F32),
        ],
        scratch_shapes=[
            pltpu.VMEM((tokens, width), F32),
            pltpu.VMEM((tokens, width), BF),
            pltpu.VMEM((width, tokens), BF),
            pltpu.VMEM((tokens, width), F32),
            pltpu.VMEM((tokens, width), F32),
            pltpu.VMEM((tokens, width), BF),
            pltpu.VMEM((tokens, width), BF),
            pltpu.VMEM((tokens, width), BF),
        ],
        compiler_params=pltpu.CompilerParams(vmem_limit_bytes=VMEM_LIMIT),
        name="middle",
    )(x, g, o, vec, wo, up, down)


def final_kernel(
    x_ref, dh_ref, n1_ref, dq_ref, dk_ref, dv_ref, vec_ref, weight_ref, dwo_ref,
    dx_ref, dw_ref, rows_ref,
):
    tokens, width = x_ref.shape
    dw_ref[3] = dwo_ref[...]
    for index, ref in enumerate((dq_ref, dk_ref, dv_ref)):
        dw_ref[index] = dot(n1_ref[...], ref[...], 1, 1).astype(BF)
    rows_ref[...] = jnp.zeros_like(rows_ref)

    def loop(i, c):
        t = pl.ds(pl.multiple_of(i * TILE, TILE), TILE)
        dn = dot(dq_ref[:, t], weight_ref[0], 0, 1)
        dn += dot(dk_ref[:, t], weight_ref[1], 0, 1)
        dn += dot(dv_ref[:, t], weight_ref[2], 0, 1)
        unit, scale = normed(x_ref[t, :].astype(F32))
        dx_ref[t, :] = dh_ref[t, :] + norm_back(dn, unit, scale, vec_ref[0:1, :])
        rows_ref[0:8, :] += fold_rows(dn * unit)
        rows_ref[8:16, :] += fold_rows(dn)
        return c

    lax.fori_loop(0, tokens // TILE, loop, 0)


def final_part(x, dh, n1, dq, dk, dv, vec, weights, dwo):
    tokens, width = x.shape
    vmem = pl.BlockSpec(memory_space=pltpu.VMEM)
    return pl.pallas_call(
        final_kernel,
        in_specs=[vmem] * 9,
        out_specs=[vmem] * 3,
        out_shape=[
            jax.ShapeDtypeStruct((tokens, width), F32),
            jax.ShapeDtypeStruct((4, width, width), BF),
            jax.ShapeDtypeStruct((16, width), F32),
        ],
        compiler_params=pltpu.CompilerParams(vmem_limit_bytes=VMEM_LIMIT),
        name="final",
    )(x, dh, n1, dq, dk, dv, vec, weights, dwo)


def center_kernel(
    x_ref, g_ref, o_ref, vec_ref, weight_ref, zone_ref, xzone_ref, yzone_ref,
    y_ref, dh_ref, do_ref, dwo_ref, rows_ref, dc_ref, upgo_ref, upstay_ref, downgo_ref, downstay_ref,
    h_ref, n2_ref, n2t_ref, acc_ref, dn_ref, a_ref, dz_ref, wo_ref, w_ref, near_ref,
    land_sem, near_sem, send_sem, local_sem, out_sem,
):
    z, x, y, c = place()
    m = 2 * y + c
    m_y = 2 * (1 - y) + c
    right_x, right_y, partner = at(z, 1 - x, y, c), at(z, x, 1 - y, c), at(z, x, y, 1 - c)
    tokens, width = x_ref.shape
    tiles = tokens // TILE
    n_dp = w_ref.shape[2]
    fetch = pltpu.make_async_copy(weight_ref.at[3], wo_ref, local_sem.at[24])
    fetch.start()
    greet([right_x, right_y, partner])
    mail = Mail(send_sem)
    piece = w_ref.at[0, 0, 0]
    column_like = near_ref.at[0, 0]
    kept = []
    for kind in range(2):
        to = w_ref.at[kind]
        sem = land_sem.at[kind]
        for part in range(4):
            own, from_x = 2 * part + x, 2 * part + 1 - x
            if part < 2:
                mail.send(xzone_ref.at[kind, part], to.at[m, from_x], sem.at[m, from_x], right_y, piece)
            else:
                mail.send(yzone_ref.at[kind, part], to.at[m_y, own], sem.at[m_y, own], right_x, piece)
    for ref, column, shift in ((zone_ref, m, 0), (xzone_ref, m, 1), (yzone_ref, m_y, 0)):
        for kind in range(2):
            to = w_ref.at[kind]
            sem = land_sem.at[kind]
            for part in range(4):
                e = 2 * part + (x + shift) % 2
                mail.send(ref.at[kind, part], to.at[column, e], sem.at[column, e], partner, piece)
                copy = pltpu.make_async_copy(
                    ref.at[kind, part], to.at[column, e], local_sem.at[len(kept)]
                )
                copy.start()
                kept.append(copy)

    def tile(i):
        return pl.ds(pl.multiple_of(i * TILE, TILE), TILE)

    fetch.wait()
    wo = wo_ref.reshape(width, width)

    def first(i, carry):
        t = tile(i)
        branch = dot(o_ref[:, t], wo[...], 0, 0) + vec_ref[5:6, :]
        h = x_ref[t, :].astype(F32) + branch
        h_ref[t, :] = h
        unit, _ = normed(h)
        n2 = (unit * vec_ref[6:7, :] + vec_ref[7:8, :]).astype(BF)
        n2_ref[t, :] = n2
        n2t_ref[:, t] = n2.T
        acc_ref[t, :] = h + vec_ref[12:13, :]
        dn_ref[t, :] = jnp.zeros((TILE, width), F32)
        return carry

    lax.fori_loop(0, tiles, first, 0)
    for copy in kept:
        copy.wait()
    forwards = []

    def work(step, carry):
        column = 2 * ((y + step // 2) % 2) + (c + (step + 1) // 2) % 2

        @pl.when(step == 1)
        def _():
            for kind in range(2):
                sem = land_sem.at[kind]
                for part in range(4):
                    e = 2 * part + 1 - x
                    arrived(w_ref.at[kind, m_y, e], sem.at[m_y, e])
                    forwards.append(
                        mail.send(
                            w_ref.at[kind, m_y, e], w_ref.at[kind, m_y, e], sem.at[m_y, e], partner, piece
                        )
                    )
                for e in range(n_dp):
                    arrived(w_ref.at[kind, 2 * y + 1 - c, e], sem.at[2 * y + 1 - c, e])

        @pl.when(step == 2)
        def _():
            for kind in range(2):
                for e in range(n_dp):
                    other = 2 * (1 - y) + 1 - c
                    arrived(w_ref.at[kind, other, e], land_sem.at[kind, other, e])
            for slot in forwards:
                arrived(w_ref.at[0, 0, 0], send_sem.at[slot])
                mail.like[slot] = None

        up = w_ref.at[0, column].reshape(width, width)
        down = w_ref.at[1, column].reshape(width, width)
        up_bias = vec_ref[pl.ds(8 + column, 1), :]

        def second(i, c):
            t = tile(i)
            zed = dot(n2_ref[t, :], up[...], 1, 0) + up_bias
            cdf = 0.5 * (1.0 + lax.erf(zed * math.sqrt(0.5)))
            a = (zed * cdf).astype(BF)
            a_ref[t, :] = a
            acc_ref[t, :] += dot(a, down[...], 1, 0)
            da = dot(g_ref[t, :], down[...], 1, 1)
            slope = cdf + zed * (jnp.exp(-0.5 * zed * zed) * (1.0 / math.sqrt(2.0 * math.pi)))
            dz = (da * slope).astype(BF)
            dz_ref[t, :] = dz
            dn_ref[t, :] += dot(dz, up[...], 1, 1)
            return c

        lax.fori_loop(0, tiles, second, 0)
        dc_ref[column] = dot(jnp.ones((8, tokens), BF), dz_ref[...], 1, 0)
        up[...] = dot(n2t_ref[...], dz_ref[...], 1, 0).astype(BF)
        down[...] = dot(a_ref[...], g_ref[...], 0, 0).astype(BF)
        for s, row in ((1, y), (2, 1 - y)):

            @pl.when(step == s)
            def _():
                for kind in range(2):
                    mail.send(
                        w_ref.at[kind, 2 * row + 1 - c], near_ref.at[kind, row],
                        near_sem.at[kind, row], partner, column_like,
                    )

        return carry

    lax.fori_loop(0, 4, work, 0)

    outs = []

    def emit(source, target):
        copy = pltpu.make_async_copy(source, target, out_sem.at[len(outs)])
        copy.start()
        outs.append(copy)

    for row in (y, 1 - y):
        for kind in range(2):
            arrived(near_ref.at[kind, row], near_sem.at[kind, row])

            def summed(e, carry):
                total = w_ref[kind, 2 * row + c, e].astype(F32) + near_ref[kind, row, e].astype(F32)
                near_ref[kind, row, e] = total.astype(BF)
                return carry

            lax.fori_loop(0, n_dp, summed, 0)
    for row in range(2):
        for part in range(4):
            emit(near_ref.at[0, row, 2 * part + 1 - x], upgo_ref.at[row, part])
            emit(near_ref.at[0, row, 2 * part + x], upstay_ref.at[row, part])
    emit(near_ref.at[1, 1 - y], downgo_ref)
    emit(near_ref.at[1, y], downstay_ref)

    rows_ref[...] = jnp.zeros_like(rows_ref)

    def third(i, carry):
        t = tile(i)
        y_ref[t, :] = acc_ref[t, :].astype(BF)
        g = g_ref[t, :].astype(F32)
        unit, scale = normed(h_ref[t, :])
        dn = dn_ref[t, :]
        dh = g + norm_back(dn, unit, scale, vec_ref[6:7, :])
        dh_ref[t, :] = dh
        dr = dh.astype(BF)
        a_ref[t, :] = dr
        do_ref[:, t] = dot(wo[...], dr, 1, 1).astype(BF)
        rows_ref[0:8, :] += fold_rows(dr.astype(F32))
        rows_ref[8:16, :] += fold_rows(dn * unit)
        rows_ref[16:24, :] += fold_rows(dn)
        rows_ref[24:32, :] += fold_rows(g)
        return carry

    lax.fori_loop(0, tiles, third, 0)
    dwo_ref[...] = dot(o_ref[...], a_ref[...], 1, 0).astype(BF)
    for copy in outs:
        copy.wait()
    mail.finish()


def center(x, g, o, vec, weights, zone, xzone, yzone):
    tokens, width = x.shape
    n_mlp, n_dp, share, _ = weights.shape
    vmem = pl.BlockSpec(memory_space=pltpu.VMEM)
    hbm = pl.BlockSpec(memory_space=pl.ANY)
    shape = jax.ShapeDtypeStruct
    dma = pltpu.SemaphoreType.DMA
    return pl.pallas_call(
        center_kernel,
        in_specs=[vmem] * 4 + [hbm] * 4,
        out_specs=[vmem] * 6 + [hbm] * 4,
        out_shape=[
            shape((tokens, width), BF),
            shape((tokens, width), F32),
            shape((width, tokens), BF),
            shape((width, width), BF),
            shape((32, width), F32),
            shape((n_mlp, 8, width), F32),
        ]
        + [shape((2, 4, share, width), BF)] * 2
        + [shape((n_dp, share, width), BF)] * 2,
        scratch_shapes=[
            pltpu.VMEM((tokens, width), F32),
            pltpu.VMEM((tokens, width), BF),
            pltpu.VMEM((width, tokens), BF),
            pltpu.VMEM((tokens, width), F32),
            pltpu.VMEM((tokens, width), F32),
            pltpu.VMEM((tokens, width), BF),
            pltpu.VMEM((tokens, width), BF),
            pltpu.VMEM((n_dp, share, width), BF),
            pltpu.VMEM((2, n_mlp, n_dp, share, width), BF),
            pltpu.VMEM((2, 2, n_dp, share, width), BF),
            dma((2, n_mlp, n_dp)), dma((2, 2)), dma((48,)), dma((25,)), dma((18,)),
        ],
        compiler_params=pltpu.CompilerParams(
            vmem_limit_bytes=60 * 1024 * 1024, collective_id=1, has_side_effects=True
        ),
        name="center",
    )(x, g, o, vec, weights, zone, xzone, yzone)


def added(*values):
    total = values[0].astype(F32)
    for value in values[1:]:
        total = total + value.astype(F32)
    return total.astype(BF)


def merge_kernel(
    upstay_ref, upgot_ref, downstay_ref, downgot_ref, upgo_out, upstay_out, downgo_out, downstay_out
):
    _, x, y, _ = place()
    for part in range(4):
        upgo_out[part] = added(upstay_ref[1 - y, part], upgot_ref[1 - y, part])
        upstay_out[part] = added(upstay_ref[y, part], upgot_ref[y, part])
        e = 2 * part + 1 - x
        downgo_out[part] = added(downstay_ref[e], downgot_ref[e])
        f = 2 * part + x
        downstay_out[part] = added(downstay_ref[f], downgot_ref[f])


def merge(upstay, upgot, downstay, downgot):
    vmem = pl.BlockSpec(memory_space=pltpu.VMEM)
    return pl.pallas_call(
        merge_kernel,
        in_specs=[vmem] * 4,
        out_specs=[vmem] * 4,
        out_shape=[jax.ShapeDtypeStruct((4,) + upstay.shape[2:], BF)] * 4,
        compiler_params=pltpu.CompilerParams(vmem_limit_bytes=6 * 1024 * 1024),
        name="merge",
    )(upstay, upgot, downstay, downgot)


def leave_kernel(
    owner_ref, n1_ref, dq0_ref, dq1_ref, dk0_ref, dk1_ref, dv0_ref, dv1_ref, vec_ref,
    freq0_ref, freq1_ref, bias0_ref, bias1_ref, mid_ref, dc_ref,
    upstay_ref, upgot_ref, downstay_ref, downgot_ref, x_hbm, dh_hbm, weight_hbm, dwo_hbm,
    dx_ref, grad_ref, total_ref,
    x_ref, dh_ref, weight_ref, rows_ref,
    dw_ref, near_ref, fromx_ref, fromy_ref, diagx_ref, diagy_ref, third_ref, chain_ref, done_ref,
    pack_ref, side_ref, sums_ref,
    near_sem, x_sem, y_sem, dx_sem, dy_sem, chain_sem, relay_sem, grad_sem, side_sem, send_sem, local_sem,
):
    z, x, y, c = place()
    m = 2 * y + c
    d = 2 * z + x
    n_dp = grad_ref.shape[0]
    right_x, right_y, partner = at(z, 1 - x, y, c), at(z, x, 1 - y, c), at(z, x, y, 1 - c)
    tokens, width = x_ref.shape
    loads = []
    for source, target in (
        (dwo_hbm, dw_ref.at[3]), (x_hbm, x_ref), (dh_hbm, dh_ref), (weight_hbm, weight_ref)
    ):
        load = pltpu.make_async_copy(source, target, local_sem.at[len(loads)])
        load.start()
        loads.append(load)
    greet([right_x, right_y, partner] + [at((z + off) % 4, x, y, c) for off in range(1, 4)])
    mail = Mail(send_sem)
    piece = pack_ref.at[0]

    edge = z % 3 == 0
    inner = z % 3 != 0
    far = z // 2
    near = 1 - far

    def relay(direction, kind, part):
        ref = chain_ref.at[direction, kind, part]
        return pltpu.make_async_remote_copy(
            src_ref=ref,
            dst_ref=ref,
            send_sem=relay_sem.at[direction, kind, part],
            recv_sem=chain_sem.at[direction, kind, part],
            device_id=at(z + 1 - 2 * direction, x, y, c),
            device_id_type=pl.DeviceIdType.MESH,
        )

    def opening(kind, part):
        chain_ref[far, kind, part] = third_ref[kind, part]
        relay(far, kind, part).start()

    def outward(kind, part):
        ref = chain_ref.at[far, kind, part]
        arrived(ref, chain_sem.at[far, kind, part])
        ref[...] = added(third_ref[kind, part], ref[...])
        relay(far, kind, part).start()

    def inward(kind, part):
        ref = chain_ref.at[near, kind, part]
        arrived(ref, chain_sem.at[near, kind, part])
        total = added(chain_ref[far, kind, part], ref[...])

        @pl.when(inner)
        def _():
            ref[...] = added(third_ref[kind, part], ref[...])
            relay(near, kind, part).start()

        return total

    def ahead(s):
        @pl.when(inner)
        def _():
            outward(1 + s // 4, s % 4)

    def keep(s):
        done_ref[s // 4, s % 4] = inward(1 + s // 4, s % 4)

    for kind, (stay_ref, got_ref) in enumerate(
        ((upstay_ref, upgot_ref), (downstay_ref, downgot_ref))
    ):
        for part in range(4):
            third_ref[1 + kind, part] = added(stay_ref[part], got_ref[part])

    @pl.when(edge)
    def _():
        def rest(s, carry):
            opening(1 + s // 4, s % 4)
            return carry

        lax.fori_loop(0, 8, rest, 0)

    pairs = ((dq0_ref, dq1_ref), (dk0_ref, dk1_ref), (dv0_ref, dv1_ref))
    half = width // PARTS
    groups = ((0, 2), (1, 3))
    share = near_ref.shape[2]
    twin = near_ref.at[0, pl.ds(0, 2)]

    def products(group):
        rows = [slice(2 * share * part, 2 * share * (part + 1)) for part in group]
        left = jnp.concatenate([n1_ref[r, :] for r in rows], axis=0)
        for index, pair in enumerate(pairs):
            out = dw_ref.at[index].reshape(width, width)
            for side, ref in enumerate(pair):
                value = dot(left, ref[...], 1, 1).astype(BF)
                for place_in, r in enumerate(rows):
                    out[r, side * half : (side + 1) * half] = value[
                        2 * share * place_in : 2 * share * (place_in + 1)
                    ]

    def pass_over(group):
        for part in group:
            for row in range(2):
                mail.send(
                    dw_ref.at[2 * row + 1 - c, pl.ds(2 * part, 2)], near_ref.at[row, pl.ds(2 * part, 2)],
                    near_sem.at[row, part], partner, twin,
                )

    def summed(group):
        for part in group:
            for row in range(2):
                arrived(twin, near_sem.at[row, part])

            def one(i, carry):
                row, e = i // 2, 2 * part + i % 2
                near_ref[row, e] = added(near_ref[row, e], dw_ref[2 * row + c, e])
                return carry

            lax.fori_loop(0, 4, one, 0)

    def issue(group):
        low, high = group
        mail.send(
            near_ref.at[1 - y, 2 * low + 1 - x], diagy_ref.at[low], dy_sem.at[low], right_y, piece
        )
        mail.send(
            near_ref.at[1 - y, 2 * high + 1 - x], diagx_ref.at[high - 2], dx_sem.at[high - 2],
            right_x, piece,
        )
        mail.send(near_ref.at[1 - y, 2 * low + x], fromy_ref.at[low], y_sem.at[low], right_y, piece)
        mail.send(near_ref.at[y, 2 * high + 1 - x], fromx_ref.at[high], x_sem.at[high], right_x, piece)

    def forward(group):
        low, high = group
        turn = high - 2
        arrived(diagy_ref.at[low], dy_sem.at[low])
        diagy_ref[low] = added(near_ref[y, 2 * low + 1 - x], diagy_ref[low])
        mail.send(diagy_ref.at[low], fromx_ref.at[low], x_sem.at[low], right_x, piece)
        arrived(diagx_ref.at[turn], dx_sem.at[turn])
        diagx_ref[turn] = added(near_ref[1 - y, 2 * high + x], diagx_ref[turn])
        mail.send(diagx_ref.at[turn], fromy_ref.at[high], y_sem.at[high], right_y, piece)

    products(groups[0])
    loads[0].wait()
    pass_over(groups[0])
    products(groups[1])
    pass_over(groups[1])
    for load in loads[1:]:
        load.wait()
    rows_ref[...] = jnp.zeros_like(rows_ref)
    flat = [weight_ref.at[index].reshape(width, width) for index in range(3)]

    def back(i, carry):
        t = pl.ds(pl.multiple_of(i * TILE, TILE), TILE)
        dn = jnp.zeros((TILE, width), F32)
        for index, pair in enumerate(pairs):
            for part, ref in enumerate(pair):
                dn += dot(ref[:, t], flat[index][:, part * half : (part + 1) * half], 0, 1)
        unit, scale = normed(x_ref[t, :].astype(F32))
        dx_ref[t, :] = dh_ref[t, :] + norm_back(dn, unit, scale, vec_ref[0:1, :])
        rows_ref[0:8, :] += fold_rows(dn * unit)
        rows_ref[8:16, :] += fold_rows(dn)
        return carry

    def gathered(part):
        arrived(fromx_ref.at[part], x_sem.at[part])
        arrived(fromy_ref.at[part], y_sem.at[part])
        third_ref[0, part] = added(near_ref[y, 2 * part + x], fromx_ref[part], fromy_ref[part])

    def wanted(e, part, first):
        second = lax.select(owner_ref[m, 2] == e, done_ref[1, part], first)
        return lax.select(owner_ref[m, 1] == e, done_ref[0, part], second)

    def close(part):
        first = inward(0, part)
        e = 2 * part + x
        pack_ref[part] = wanted(2 * z + 1 - x, part, first)
        mail.send(pack_ref.at[part], grad_ref.at[e], grad_sem.at[part], right_x, piece)
        grad_ref[e] = wanted(d, part, first)

    def begin(group):
        @pl.when(edge)
        def _():
            for part in group[::-1]:
                gathered(part)
                opening(0, part)

    def early(part):
        @pl.when(inner)
        def _():
            gathered(part)
            outward(0, part)

    def hop(index, peer):
        mail.send(
            sums_ref.at[index], side_ref.at[index], side_sem.at[index], peer, sums_ref.at[0]
        )

    def landed(index):
        arrived(side_ref.at[index], side_sem.at[index])
        sums_ref[index + 1] = sums_ref[index] + side_ref[index]

    ahead(0)
    summed(groups[0])
    issue(groups[0])
    ahead(1)
    lax.fori_loop(0, 1, back, 0)
    summed(groups[1])
    ahead(2)
    keep(0)
    forward(groups[0])
    issue(groups[1])

    def middle(i, carry):
        ahead(2 + i)
        keep(i)
        return back(i, carry)

    lax.fori_loop(1, 3, middle, 0)
    begin(groups[0])
    lax.fori_loop(3, tokens // TILE, middle, 0)

    def eight(ref, index):
        return jnp.sum(ref[8 * index : 8 * index + 8, :], axis=0, keepdims=True)

    ups = dc_ref.shape[0]
    sums_ref[0, 0:1, :] = eight(rows_ref, 0)
    sums_ref[0, 1:2, :] = eight(rows_ref, 1)
    for index in range(3):
        sums_ref[0, 2 + index : 3 + index, 0:half] = bias0_ref[8 * index : 8 * index + 1, :]
        sums_ref[0, 2 + index : 3 + index, half:width] = bias1_ref[8 * index : 8 * index + 1, :]
        sums_ref[0, 5 + index : 6 + index, :] = eight(mid_ref, index)
    for index in range(ups):
        sums_ref[0, 8 + index : 9 + index, :] = dc_ref[index, 0:1, :]
    sums_ref[0, 8 + ups : 9 + ups, :] = eight(mid_ref, 3)
    sums_ref[0, 9 + ups : 10 + ups, :] = jnp.concatenate(
        [freq0_ref[0:1, :], freq1_ref[0:1, :], freq0_ref[1:2, :], freq1_ref[1:2, :]], axis=1
    )
    hop(0, partner)
    forward(groups[1])
    ahead(6)
    keep(4)
    landed(0)
    hop(1, right_x)
    ahead(7)
    keep(5)
    landed(1)
    hop(2, right_y)
    begin(groups[1])
    keep(6)
    landed(2)
    for off in range(1, 4):
        mail.send(
            sums_ref.at[3], side_ref.at[3 + z], side_sem.at[3 + z], at((z + off) % 4, x, y, c),
            sums_ref.at[0],
        )
    side_ref[3 + z] = sums_ref[3]
    early(2)
    keep(7)
    early(0)
    close(2)
    early(3)
    close(0)
    early(1)
    close(3)
    close(1)
    for off in range(1, 4):
        e = (z + off) % 4
        arrived(side_ref.at[3 + e], side_sem.at[3 + e])
    total_ref[...] = (side_ref[3] + side_ref[4]) + (side_ref[5] + side_ref[6])
    for part in (2, 3, 0, 1):
        arrived(grad_ref.at[2 * part + 1 - x], grad_sem.at[part])
    mail.finish()
    for kind in range(3):
        for part in range(4):
            arrived(piece, relay_sem.at[far, kind, part])

            @pl.when(inner)
            def _():
                arrived(piece, relay_sem.at[near, kind, part])


def leave(owner, x, dh, n1, flows, vec, weights, dwo, smalls, rest):
    tokens, width = x.shape
    n_mlp, n_dp, share, _ = weights.shape
    smem = pl.BlockSpec(memory_space=pltpu.SMEM)
    vmem = pl.BlockSpec(memory_space=pltpu.VMEM)
    hbm = pl.BlockSpec(memory_space=pl.ANY)
    dma = pltpu.SemaphoreType.DMA
    part = lambda *lead: pltpu.VMEM(lead + (share, width), BF)
    flat = [ref for pair in flows for ref in pair]
    return pl.pallas_call(
        leave_kernel,
        in_specs=[smem] + [vmem] * 18 + [hbm] * 4,
        out_specs=[vmem] * 3,
        out_shape=[
            jax.ShapeDtypeStruct((tokens, width), F32),
            jax.ShapeDtypeStruct((n_dp, share, width), BF),
            jax.ShapeDtypeStruct(vec.shape, F32),
        ],
        scratch_shapes=[
            pltpu.VMEM((tokens, width), BF),
            pltpu.VMEM((tokens, width), F32),
            part(n_mlp, n_dp),
            pltpu.VMEM((16, width), F32),
            part(n_mlp, n_dp), part(2, n_dp), part(4), part(4), part(2), part(2), part(3, 4),
            part(2, 3, 4), part(2, 4), part(4),
            pltpu.VMEM((7,) + vec.shape, F32),
            pltpu.VMEM((4,) + vec.shape, F32),
            dma((2, 4)), dma((4,)), dma((4,)), dma((2,)), dma((2,)), dma((2, 3, 4)), dma((2, 3, 4)),
            dma((4,)), dma((7,)), dma((32,)), dma((4,)),
        ],
        compiler_params=pltpu.CompilerParams(
            vmem_limit_bytes=38 * 1024 * 1024, collective_id=2, has_side_effects=True
        ),
        name="leave",
    )(
        owner, n1, *flat, vec, *smalls, *rest, x, dh, weights,
        dwo.reshape(n_dp, share, width),
    )


def update_kernel(
    owner_ref, decay_ref, grad_ref, total_ref, moment_ref, vec_ref,
    left_hbm, right_hbm, lroot_hbm, rroot_hbm, master_hbm, y_hbm, dx_hbm,
    small_out, moment_out, vec_out, slot_out, left_out, right_out, master_out, y_out, dx_out,
    left_ref, right_ref, lroot_ref, rroot_ref, master_ref, y_ref, dx_ref, slot_ref, turn_ref,
    in_sem, out_sem,
):
    loads = []
    for source, target in (
        (left_hbm, left_ref), (right_hbm, right_ref), (lroot_hbm, lroot_ref), (rroot_hbm, rroot_ref),
        (master_hbm, master_ref), (y_hbm, y_ref), (dx_hbm, dx_ref),
    ):
        loads.append(pltpu.make_async_copy(source, target, in_sem.at[len(loads)]))
        loads[-1].start()
    outs = []

    def emit(source, target):
        outs.append(pltpu.make_async_copy(source, target, out_sem.at[len(outs)]))
        outs[-1].start()

    d = lax.axis_index("dp")
    m = lax.axis_index("mlp")
    held = (owner_ref[m, 0] == d) | (owner_ref[m, 1] == d) | (owner_ref[m, 2] == d)
    decay = decay_ref[0]
    width = grad_ref.shape[0]
    tall = width // 3

    def strip(i):
        return pl.ds(pl.multiple_of(i * tall, tall), tall)

    @pl.when(held)
    def _():
        slot_ref[...] = grad_ref[...].astype(F32)

    @pl.when(jnp.logical_not(held))
    def _():
        slot_ref[...] = jnp.zeros_like(slot_ref)

    emit(slot_ref, slot_out)

    def own(ref):
        cut = small_out.shape[1]
        value = ref[:, 0:cut]
        for index in range(1, owner_ref.shape[0]):
            value = lax.select(m == index, ref[:, index * cut : (index + 1) * cut], value)
        return value

    slow = decay_ref[1]
    small = own(total_ref)
    moment = slow * own(moment_ref) + (1.0 - slow) * small * small
    small_out[...] = small
    moment_out[...] = moment
    vec_out[...] = own(vec_ref) - RATE_VECTOR * small / (jnp.sqrt(moment) + STEP_EPSILON)
    loads[0].wait()

    @pl.when(held)
    def _():
        def rows(i, carry):
            r = strip(i)
            gram = dot(grad_ref[r, :], grad_ref[...], 1, 1)
            left_ref[r, :] = decay * left_ref[r, :] + (1.0 - decay) * gram
            return carry

        lax.fori_loop(0, 3, rows, 0)

    emit(left_ref, left_out)
    loads[1].wait()

    @pl.when(held)
    def _():
        turn_ref[...] = grad_ref[...].T

        def rows(i, carry):
            r = strip(i)
            gram = dot(turn_ref[r, :], grad_ref[...], 1, 0)
            right_ref[r, :] = decay * right_ref[r, :] + (1.0 - decay) * gram
            return carry

        lax.fori_loop(0, 3, rows, 0)

    emit(right_ref, right_out)
    for index, source, target in ((5, y_ref, y_out), (6, dx_ref, dx_out)):
        loads[index].wait()
        emit(source, target)
    for load in loads[2:5]:
        load.wait()

    @pl.when(held)
    def _():
        turn_ref[...] = rroot_ref[...].astype(BF)

        def rows(i, total):
            r = strip(i)
            inner = dot(lroot_ref[r, :].astype(BF), grad_ref[...], 1, 0).astype(BF)
            direction = dot(inner, turn_ref[...], 1, 0)
            lroot_ref[r, :] = direction
            return total + jnp.sum(direction * direction, axis=0, keepdims=True)

        total = jnp.sum(lax.fori_loop(0, 3, rows, jnp.zeros((1, width), F32)), keepdims=True)
        mean = total * (1.0 / (width * width))
        master_ref[...] -= lroot_ref[...] * (RATE_MATRIX * lax.rsqrt(mean + GRAFT_EPSILON))

    emit(master_ref, master_out)
    for copy in outs:
        copy.wait()


def update(
    owner, decays, grad, total, moments, vectors, left, right, lroot, rroot, master, output, input_grad
):
    smem = pl.BlockSpec(memory_space=pltpu.SMEM)
    vmem = pl.BlockSpec(memory_space=pltpu.VMEM)
    hbm = pl.BlockSpec(memory_space=pl.ANY)
    shape = lambda a: jax.ShapeDtypeStruct(a.shape, a.dtype)
    room = lambda a: pltpu.VMEM(a.shape, a.dtype)
    return pl.pallas_call(
        update_kernel,
        in_specs=[smem, smem] + [vmem] * 4 + [hbm] * 7,
        out_specs=[vmem] * 3 + [hbm] * 6,
        out_shape=[jax.ShapeDtypeStruct((total.shape[0], total.shape[1] // owner.shape[0]), F32)] * 3
        + [shape(a) for a in (left, left, right, master, output, input_grad)],
        scratch_shapes=[room(a) for a in (left, right, lroot, rroot, master, output, input_grad, left, grad)]
        + [pltpu.SemaphoreType.DMA((7,)), pltpu.SemaphoreType.DMA((6,))],
        compiler_params=pltpu.CompilerParams(vmem_limit_bytes=26 * 1024 * 1024),
        name="update",
    )(
        owner, decays, grad, total, moments, vectors, left, right, lroot, rroot, master, output, input_grad
    )


def positions(segment, heights, widths, patch_rows, patch_cols):
    images = heights.shape[0]
    matches = segment[None, :] == jnp.arange(images, dtype=jnp.int32)[:, None]
    tall = jnp.sum(jnp.where(matches, heights[:, None], 0), axis=0).astype(F32)
    wide = jnp.sum(jnp.where(matches, widths[:, None], 0), axis=0).astype(F32)
    py = patch_rows.astype(F32) * GRID_BASE / tall
    px = patch_cols.astype(F32) * GRID_BASE / wide
    zero = jnp.zeros_like(px)
    return jnp.stack([px, py, segment.astype(F32), zero, zero, zero, zero, zero])


def local(
    tokens, cotangent, vectors, vector_moments, decays, owner, master_slots, left_slots,
    right_slots, left_roots, right_roots, grid_height, grid_width, patch_rows, patch_cols, segment,
):
    mlp_index = lax.axis_index("mlp")
    n_dp = lax.axis_size("dp")
    n_mlp = lax.axis_size("mlp")
    width = tokens.shape[1]
    share = width // n_dp
    owner_row = jnp.take(owner, mlp_index, axis=0)
    master = master_slots[0, 0]
    direct = n_dp == 8 and n_mlp == 4
    if direct:
        n1t, q, k, v, cosine, sine, qmark, kmark, pos, attention, zone = enter(
            owner, grid_height, grid_width, master.reshape(n_dp, share, width), tokens, segment,
            patch_rows, patch_cols, vectors,
        )
        over_x = [(i, i ^ 1) for i in range(n_dp)]
        over_y = [(i, i ^ 2) for i in range(n_mlp)]
        xzone = lax.ppermute(zone, "dp", over_x)
        yzone = lax.ppermute(zone, "mlp", over_y)
    else:
        turned = vectors.T
        pos = positions(segment, grid_height, grid_width, patch_rows, patch_cols)
        slot = master.astype(BF).reshape(n_dp, share, width)
        pieces = lax.all_to_all(slot, "dp", 0, 0, tiled=True)
        mine = jnp.take(pieces, owner_row, axis=0)
        every = lax.all_gather(mine[None], ("dp", "mlp"), axis=0, tiled=True)
        blocks = every.reshape(n_dp, n_mlp, 3, share, width).transpose(2, 1, 0, 3, 4)
        attention, up, down = blocks.reshape(3, n_mlp, width, width)
        n1t, q, k, v, cosine, sine, qmark, kmark = project(tokens, pos, vectors, turned, attention)
    o, log_totals = attend(grid_height, grid_width, q, k, v, qmark, kmark)
    fine = (n_mlp, n_dp, share, width)
    back = functools.partial(attend_back, grid_height, grid_width)
    if direct:
        output, dh, do, dwo, mid_rows, dc, upgo, upstay, downgo, downstay = center(
            tokens, cotangent, o, vectors, attention, zone, xzone, yzone
        )
        upgot = lax.ppermute(upgo, "dp", over_x)
        downgot = lax.ppermute(downgo, "mlp", over_y)
        first = back(q, k, v, qmark, kmark, log_totals, do, pos, cosine, sine, 0)
        first, upgot, downgot = lax.optimization_barrier((first, upgot, downgot))
        upgo, upstay, downgo, downstay = merge(upstay, upgot, downstay, downgot)
        upgot = lax.ppermute(upgo, "mlp", over_y)
        downgot = lax.ppermute(downgo, "dp", over_x)
        do, upstay, downstay = lax.optimization_barrier((do, upstay, downstay))
    else:
        output, dh, do, dwo, dup, ddown, mid_rows, dc = middle_part(
            tokens, cotangent, o, vectors, attention[3], up, down
        )
        first = back(q, k, v, qmark, kmark, log_totals, do, pos, cosine, sine, 0)
    second = back(q, k, v, qmark, kmark, log_totals, do, pos, cosine, sine, 1)
    both = list(zip(first, second))
    if direct:
        input_grad, gradient, total = leave(
            owner, tokens, dh, n1t, both[0:3], vectors, attention.reshape(fine), dwo,
            (*both[3], *both[4], mid_rows, dc),
            (upstay, upgot, downstay, downgot),
        )
    else:
        freq = jnp.concatenate(both[3], axis=1)[0:2].reshape(1, width)
        bias = jnp.concatenate(both[4], axis=1)[0::8]
        eights = lambda rows: jnp.sum(rows.reshape(-1, 8, width), axis=1)
        mid = eights(mid_rows)
        tail = [bias, mid[0:3], dc[:, 0, :], mid[3:4], freq]
        dq, dk, dv = (jnp.concatenate(pair, axis=0) for pair in both[0:3])
        input_grad, datt, fin_rows = final_part(
            tokens, dh, n1t, dq, dk, dv, vectors, attention, dwo
        )
        grads = jnp.stack([datt, dup, ddown], axis=1)
        grads = grads.reshape(n_mlp, 3, n_dp, share, width).transpose(2, 0, 1, 3, 4)
        grads = grads.reshape(n_dp * n_mlp * 3, share, width)
        reduced = lax.psum_scatter(grads, ("dp", "mlp"), scatter_dimension=0, tiled=True)
        takers = owner_row[None, :] == jnp.arange(n_dp, dtype=jnp.int32)[:, None]
        kind_of = jnp.sum(jnp.where(takers, jnp.arange(3, dtype=jnp.int32)[None, :], 0), axis=1)
        gradient = lax.all_to_all(jnp.take(reduced, kind_of, axis=0), "dp", 0, 0, tiled=True)
        total = lax.psum(jnp.concatenate([eights(fin_rows)] + tail, axis=0), ("dp", "mlp"))
    gradient = gradient.reshape(width, width)
    grad_share, moment_next, vector_next, slot_grad, left_out, right_out, master_out, output, input_grad = (
        update(
            owner, decays, gradient, total, vector_moments, vectors, left_slots[0, 0], right_slots[0, 0],
            left_roots[0, 0], right_roots[0, 0], master, output, input_grad,
        )
    )
    lift = lambda a: a[None, None]
    return (
        output, input_grad, lift(slot_grad), lift(left_out), lift(right_out), lift(master_out),
        grad_share, moment_next, vector_next,
    )


def solution(mesh):
    both = P(("dp", "mlp"))
    flat = P(("dp", "mlp"), None)
    slots = P("dp", "mlp", None, None)
    split = P(None, "mlp")
    return jax.shard_map(
        local,
        mesh=mesh,
        in_specs=(flat, flat, P(), P(), P(), P(), slots, slots, slots, slots, slots)
        + (both,) * 5,
        out_specs=(flat, flat, slots, slots, slots, slots, split, split, split),
        check_vma=False,
    )
```
